32 devices in a mesh: seq: 2 (over x), fsdp: 16 (over z, y, core).
Axes of the slice: x: 2, y: 2, z: 4, core: 2. Of those that a mesh axis runs over, the one named last changes fastest.
Arguments:
- tokens_in: bfloat16 [32, 2048, 768], P('fsdp', 'seq')
- segment_ids: int32 [32, 2048], P('fsdp'), may hold values from 0 to 15, never falling along the last dimension, each value on 1 to 1024 neighbouring positions
- random_blocks: int32 [32, 32, 3], P('fsdp'), may hold values from 0 to 31
- global_blocks: int32 [32, 2], P('fsdp'), may hold values from 0 to 31
- w_query: bfloat16 [768, 768], P('fsdp'), may hold values from -0.15625 to 0.15625
- b_query: bfloat16 [768], P('fsdp'), may hold values from -1.5 to 1.5
- w_key: bfloat16 [768, 768], P('fsdp'), may hold values from -0.15625 to 0.15625
- w_value: bfloat16 [768, 768], P('fsdp'), may hold values from -0.21875 to 0.21875
- b_value: bfloat16 [768], P('fsdp'), may hold values from -1.5 to 1.5
- w_attn_out: bfloat16 [768, 768], P('fsdp'), may hold values from -0.875 to 0.875
- b_attn_out: bfloat16 [768], P('fsdp'), may hold values from -1.5 to 1.5
- ln1_gain: bfloat16 [768], P('fsdp'), may hold values from 0.5 to 1.5
- ln1_bias: bfloat16 [768], P('fsdp'), may hold values from -1.5 to 1.5
- w_inner: bfloat16 [768, 3072], P('fsdp')
- b_inner: bfloat16 [3072], P('fsdp'), may hold values from -1.5 to 1.5
- w_outer: bfloat16 [3072, 768], P('fsdp'), may hold values from -0.109375 to 0.109375
- b_outer: bfloat16 [768], P('fsdp'), may hold values from -1.5 to 1.5
- ln2_gain: bfloat16 [768], P('fsdp'), may hold values from 0.5 to 1.5
- ln2_bias: bfloat16 [768], P('fsdp'), may hold values from -1.5 to 1.5
- out_grad: bfloat16 [32, 2048, 768], P('fsdp', 'seq'), may hold values from -6 to 6
Outputs:
- out_tokens: bfloat16 [32, 2048, 768], P('fsdp', 'seq')
- d_tokens_in: bfloat16 [32, 2048, 768], P('fsdp', 'seq')
- d_w_query: float32 [768, 768], P('fsdp')
- d_b_query: float32 [768], P('fsdp')
- d_w_key: float32 [768, 768], P('fsdp')
- d_w_value: float32 [768, 768], P('fsdp')
- d_b_value: float32 [768], P('fsdp')
- d_w_attn_out: float32 [768, 768], P('fsdp')
- d_b_attn_out: float32 [768], P('fsdp')
- d_ln1_gain: float32 [768], P('fsdp')
- d_ln1_bias: float32 [768], P('fsdp')
- d_w_inner: float32 [768, 3072], P('fsdp')
- d_b_inner: float32 [3072], P('fsdp')
- d_w_outer: float32 [3072, 768], P('fsdp')
- d_b_outer: float32 [768], P('fsdp')
- d_ln2_gain: float32 [768], P('fsdp')
- d_ln2_bias: float32 [768], P('fsdp')
- rms_values: float32 [3], replicated
The draws below stay inside these ranges and needn't reach their ends.
Inputs may be any that keep to these rules, and one draw needn't show every extreme that they name: `segment_ids`: along a sequence the ids never fall; each id marks one document. `random_blocks`: block numbers of the same sequence, repeats allowed. `global_blocks`: block numbers of the same sequence, the two may coincide.
All inputs are finite; a program needn't handle non-finite values.
Results may differ from the reference program's by a relative error of at most 0.015.
Values may be sent and summed in bfloat16 or wider, within the bound.
A program may use at most 320 MiB of HBM per device.

```python
import math
import jax
import jax.numpy as jnp
import numpy as np
from jax import lax

D = 768
HEADS = 12
HD = 64
FF = 3072
BLK = 64
NRAND = 3
NGLOB = 2
LEN = 2048
NB = 32
ROWS = 32


def feature_tilt(key):
    return jax.random.uniform(jax.random.fold_in(key, 7), (D,), jnp.float32, -1.0, 1.0)


def draw_tokens_in(key, part):
    tilt = feature_tilt(key)
    row_pos = jnp.arange(ROWS, dtype=jnp.float32)[:, None, None] / max(ROWS - 1, 1)
    tok_pos = jnp.arange(LEN, dtype=jnp.float32)[None, :, None] / (LEN - 1)
    row_scale = 0.7 * jnp.exp(0.5 * math.log(3.0) * (row_pos + tok_pos))
    lean = jnp.exp(1.15 * tilt[None, None, :] * (1.0 - 2.0 * row_pos))
    base_key = jax.random.fold_in(key, 11)
    base_vals = jax.random.normal(base_key, (ROWS, LEN, D), jnp.float32)
    return (base_vals * row_scale * lean).astype(jnp.bfloat16)


def draw_w_inner(key, part):
    tilt = feature_tilt(key)
    row_gain = jnp.exp(1.15 * tilt) / math.sqrt(math.sinh(2.3) / 2.3)
    base_key = jax.random.fold_in(key, 13)
    base_vals = jax.random.normal(base_key, (D, FF), jnp.float32)
    return (base_vals * D ** (-0.5) * row_gain[:, None]).astype(jnp.bfloat16)


def with_ends(drawn, own_key, least, largest):
    longest = drawn.shape.index(max(drawn.shape))
    spots = []
    for shift in (0, 1):
        where = [jax.random.randint(jax.random.fold_in(own_key, axis), (), 0, length) for axis, length in enumerate(drawn.shape)]
        where[longest] = (where[longest] + shift) % drawn.shape[longest]
        spots.append(tuple(where))
    return drawn.at[spots[0]].set(least).at[spots[1]].set(largest)


def level_of(own_key, shape, pieces, least, high):
    gain, own = 1.0, jax.random.fold_in(own_key, 6)
    for position, blocks in pieces:
        steps = jnp.exp(jax.random.uniform(jax.random.fold_in(own, position), (blocks,), jnp.float32, least / len(pieces), high / len(pieces)))
        gain = gain * jnp.repeat(steps, shape[position] // blocks).reshape([-1 if axis == position else 1 for axis in range(len(shape))])
    return gain


def length_profile(number_of, total, bound, skew):
    weights = [(1 << 20) // math.isqrt(grade ** skew) + 1 for grade in range(2, number_of + 1)]
    rest, holding = total - bound - (number_of - 1), [1] * (number_of - 1)
    while rest > 0:
        movable = [i for i in range(number_of - 1) if holding[i] < bound]
        whole, budget = sum([weights[i] for i in movable]), rest
        for i in movable:
            addition = min(bound - holding[i], max(1, budget * weights[i] // whole), rest)
            holding[i] = holding[i] + addition
            rest = rest - addition
    return np.array([bound] + holding)


def ragged_sizes(rng, amount, total, bound, slope):
    if amount == 2:
        one = jax.random.randint(rng, (), max(1, total - bound), min(bound, total - 1) + 1)
        return jnp.stack([one, total - one])
    tallies = jnp.asarray(length_profile(amount, total, bound, slope), jnp.int32)
    twos = (amount - 1) // 2
    source_of, receiver = tallies[1:1 + 2 * twos:2], tallies[2:2 + 2 * twos:2]
    margin = jnp.minimum(source_of - 1, bound - receiver)
    passed = jax.random.randint(jax.random.fold_in(rng, 1), (twos,), 0, 1 << 20) % (margin + 1)
    tallies = tallies.at[1:1 + 2 * twos:2].set(source_of - passed).at[2:2 + 2 * twos:2].set(receiver + passed)
    return tallies[jax.random.permutation(jax.random.fold_in(rng, 2), amount)]


def scatter_about(key, extent, deviation, most, split=(), kind=jnp.bfloat16):
    values = deviation * jax.random.normal(key, extent, jnp.float32)
    if split:
        values = values * level_of(key, extent, split, -0.22, 0.18)
    return jnp.clip(values, -most, most).astype(kind)


def setup_inputs(seed: int = 0) -> dict:
    arg_keys = jax.random.split(jax.random.key(seed), 21)
    return {
        "tokens_in": draw_tokens_in(jax.random.fold_in(arg_keys[20], 71), 0),
        "segment_ids": jax.vmap(lambda own: jnp.searchsorted(jnp.cumsum(ragged_sizes(own, LEN // (2 * BLK), LEN, LEN // 2, 2)), jnp.arange(LEN), side="right"))(jax.random.split(arg_keys[1], ROWS)).reshape((ROWS, LEN)).astype(jnp.int32),
        "random_blocks": with_ends(jax.random.randint(arg_keys[2], (ROWS, NB, NRAND), 0, NB), jax.random.fold_in(arg_keys[2], 1), 0, NB - 1).astype(jnp.int32),
        "global_blocks": with_ends(jax.random.randint(arg_keys[3], (ROWS, NGLOB), 0, NB), jax.random.fold_in(arg_keys[3], 1), 0, NB - 1).astype(jnp.int32),
        "w_query": scatter_about(arg_keys[4], (D, D), (2 * D) ** -0.5, 0.15625, ((0, 16),)),
        "b_query": scatter_about(arg_keys[5], (D,), 0.3, 1.5, ((0, 16),)),
        "w_key": scatter_about(arg_keys[6], (D, D), (2 * D) ** -0.5, 0.15625, ((0, 16),)),
        "w_value": scatter_about(arg_keys[7], (D, D), D ** -0.5, 0.21875, ((0, 16),)),
        "b_value": scatter_about(arg_keys[8], (D,), 0.3, 1.5, ((0, 16),)),
        "w_attn_out": scatter_about(arg_keys[9], (D, D), (D // 16) ** -0.5, 0.875, ((0, 16),)),
        "b_attn_out": scatter_about(arg_keys[10], (D,), 0.3, 1.5, ((0, 16),)),
        "ln1_gain": jnp.clip(1.0 + 0.1 * jax.random.normal(arg_keys[11], (D,), jnp.float32), 0.5, 1.5).astype(jnp.bfloat16),
        "ln1_bias": scatter_about(arg_keys[12], (D,), 0.3, 1.5, ((0, 16),)),
        "w_inner": draw_w_inner(jax.random.fold_in(arg_keys[20], 71), 0),
        "b_inner": scatter_about(arg_keys[14], (FF,), 0.3, 1.5, ((0, 16),)),
        "w_outer": scatter_about(arg_keys[15], (FF, D), FF ** -0.5, 0.109375, ((0, 16),)),
        "b_outer": scatter_about(arg_keys[16], (D,), 0.3, 1.5, ((0, 16),)),
        "ln2_gain": jnp.clip(1.0 + 0.1 * jax.random.normal(arg_keys[17], (D,), jnp.float32), 0.5, 1.5).astype(jnp.bfloat16),
        "ln2_bias": scatter_about(arg_keys[18], (D,), 0.3, 1.5, ((0, 16),)),
        "out_grad": scatter_about(arg_keys[19], (ROWS, LEN, D), 1.0, 6.0, ((0, 16), (1, 2))),
    }


@jax.custom_vjp
def low(v):
    return lax.optimization_barrier(v.astype(jnp.bfloat16)).astype(jnp.float32)

@jax.custom_vjp
def low_back(v):
    return v

def low_keep(v):
    return (low(v), None)

def low_pass(kept, grad):
    return (grad,)

def back_keep(v):
    return (v, None)

def back_low(kept, grad):
    return (low(grad),)
low.defvjp(low_keep, low_pass)
low_back.defvjp(back_keep, back_low)
eps_norm = 1e-06
high_prec = lax.Precision.HIGHEST

def layer_norm(hidden, gain_vec, shift_vec):
    mean_val = lax.optimization_barrier(jnp.mean(hidden, axis=-1, keepdims=True))
    centred = hidden - mean_val
    var_val = lax.optimization_barrier(jnp.mean(centred * centred, axis=-1, keepdims=True))
    return centred * lax.rsqrt(var_val + eps_norm) * gain_vec + shift_vec

def allowed_mask(seg_row, rand_row, glob_row, start_at, span_len):
    full_len = seg_row.shape[0]
    block_ids = jnp.arange(full_len // BLK, dtype=jnp.int32)
    is_global = jnp.any(block_ids[:, None] == glob_row[None, :], axis=1)
    picked = jnp.any(rand_row[:, :, None] == block_ids[None, None, :], axis=1)
    nearby = jnp.abs(block_ids[:, None] - block_ids[None, :]) <= 1
    block_mask = nearby | picked | is_global[:, None] | is_global[None, :]
    block_rows = lax.dynamic_slice_in_dim(block_mask, start_at // BLK, span_len // BLK, 0)
    token_mask = jnp.repeat(jnp.repeat(block_rows, BLK, axis=0), BLK, axis=1)
    seg_query = lax.dynamic_slice_in_dim(seg_row, start_at, span_len, 0)
    return token_mask & (seg_query[:, None] == seg_row[None, :])

def matmul_high(left, right):
    return jnp.dot(left, right, preferred_element_type=jnp.float32, precision=high_prec)

def layer_fn(tokens, seg_row, rand_row, glob_row, params):
    query_w, query_b, key_w, value_w, value_b, out_w, out_b, gain_one, bias_one, inner_w, inner_b, outer_w, outer_b, gain_two, bias_two = params
    q_rows = min(512, LEN)
    block_count = LEN // q_rows
    score_scale = HD ** (-0.5)
    queries = low(low_back(matmul_high(tokens, query_w) + query_b)).reshape(LEN, HEADS, HD)
    keys_all = low(low_back(matmul_high(tokens, key_w))).reshape(LEN, HEADS, HD)
    values_all = low(low_back(matmul_high(tokens, value_w) + value_b)).reshape(LEN, HEADS, HD)

    def attend(block_idx):
        start_at = block_idx * q_rows
        q_block = lax.dynamic_slice_in_dim(queries, start_at, q_rows, 0)
        allowed = allowed_mask(seg_row, rand_row, glob_row, start_at, q_rows)
        scores = jnp.einsum('qhd,khd->hqk', q_block, keys_all, precision=high_prec) * score_scale
        scores = low_back(jnp.where(allowed[None], scores, -1e+30))
        softmax_w = jax.nn.softmax(scores, axis=-1)
        return low(low_back(jnp.einsum('hqk,khd->qhd', low(softmax_w), values_all, precision=high_prec)))
    attended = lax.map(jax.checkpoint(attend), jnp.arange(block_count, dtype=jnp.int32)).reshape(LEN, D)
    attn_out = low_back(matmul_high(attended, out_w) + out_b)
    resid_one = tokens + attn_out
    normed_one = layer_norm(resid_one, gain_one, bias_one)
    pre_act = low_back(matmul_high(low(normed_one), inner_w) + inner_b)
    act_low = low(jax.nn.gelu(pre_act, approximate=True))
    mlp_out = low_back(matmul_high(act_low, outer_w) + outer_b)
    result = layer_norm(normed_one + mlp_out, gain_two, bias_two)
    return (result, (jnp.sum(resid_one * resid_one), jnp.sum(attn_out * attn_out), jnp.sum(mlp_out * mlp_out)))

def reference(tokens_in, segment_ids, random_blocks, global_blocks, w_query, b_query, w_key, w_value, b_value, w_attn_out, b_attn_out, ln1_gain, ln1_bias, w_inner, b_inner, w_outer, b_outer, ln2_gain, ln2_bias, out_grad):
    weights = tuple((item.astype(jnp.float32) for item in (w_query, b_query, w_key, w_value, b_value, w_attn_out, b_attn_out, ln1_gain, ln1_bias, w_inner, b_inner, w_outer, b_outer, ln2_gain, ln2_bias)))

    def one_row(totals, packed):
        tokens, seg_row, rand_row, glob_row, cotangent = packed

        def row_layer(row_tokens, params):
            return layer_fn(row_tokens, seg_row, rand_row, glob_row, params)
        result, pullback, sum_trio = jax.vjp(row_layer, tokens.astype(jnp.float32), weights, has_aux=True)
        d_tokens, d_params = pullback(cotangent.astype(jnp.float32))
        grad_totals, stat_totals = totals
        updated = (jax.tree.map(jnp.add, grad_totals, d_params), (stat_totals[0] + sum_trio[0], stat_totals[1] + sum_trio[1], stat_totals[2] + sum_trio[2]))
        return (updated, (result.astype(jnp.bfloat16), d_tokens.astype(jnp.bfloat16)))
    zero_val = jnp.zeros((), jnp.float32)
    start_totals = (tuple((jnp.zeros_like(item) for item in weights)), (zero_val, zero_val, zero_val))
    final_totals, stacked = lax.scan(one_row, start_totals, (tokens_in, segment_ids, random_blocks, global_blocks, out_grad))
    grads, stat_totals = final_totals
    out_tokens, d_tokens_in = stacked
    rms_values = jnp.sqrt(jnp.stack([stat_totals[0], stat_totals[1], stat_totals[2]]) / (ROWS * LEN * D))
    return (out_tokens, d_tokens_in, grads[0], grads[1], grads[2], grads[3], grads[4], grads[5], grads[6], grads[7], grads[8], grads[9], grads[10], grads[11], grads[12], grads[13], grads[14], rms_values)
```

```python
import functools
import math

import jax
import jax.numpy as jnp
from jax import lax
from jax.experimental import pallas as pl
from jax.experimental.pallas import tpu as pltpu
from jax.sharding import PartitionSpec as P

HD = 64
BLK = 64
CHUNK = 4
NEG = -1e30


def plan_blocks(seg, rand, glob):
    rows, full_len = seg.shape
    nb = full_len // BLK
    ids = jnp.arange(nb, dtype=jnp.int32)
    is_global = jnp.any(ids[None, :, None] == glob[:, None, :], axis=-1)
    picked = jnp.any(rand[:, :, None, :] == ids[None, None, :, None], axis=-1)
    nearby = jnp.abs(ids[:, None] - ids[None, :]) <= 1
    admitted = nearby[None] | picked | is_global[:, :, None] | is_global[:, None, :]
    by_block = seg.reshape(rows, nb, BLK)
    low, high = by_block[:, :, 0], by_block[:, :, BLK - 1]
    meets = (low[:, :, None] <= high[:, None, :]) & (low[:, None, :] <= high[:, :, None])
    active = (admitted & meets).astype(jnp.int32)
    upto = (ids[:, None] <= ids[None, :]).astype(jnp.int32)
    place = jnp.sum(active[:, :, :, None] * upto[None, None], axis=2) - 1
    count = jnp.sum(active, axis=2)
    hit = (place[:, :, :, None] == ids[None, None, None, :]) & (active[:, :, :, None] > 0)
    listed = jnp.sum(jnp.where(hit, ids[None, None, :, None], 0), axis=2)
    listed = jnp.where(ids[None, None, :] < count[:, :, None], listed, nb)
    chunks = (count + (CHUNK - 1)) // CHUNK
    seg_cols = jnp.concatenate([seg, jnp.full((rows, BLK), -1, jnp.int32)], axis=1)
    seg_cols = jnp.broadcast_to(seg_cols[:, :, None], (rows, full_len + BLK, 128))
    seg_rows = jnp.concatenate([by_block, by_block], axis=2)[:, :, None, :]
    return chunks, listed.reshape(rows, nb * nb), seg_cols, seg_rows


def lane_low(rows):
    return lax.broadcasted_iota(jnp.int32, (rows, 128), 1) < HD


def diag128(dup_t):
    row = lax.broadcasted_iota(jnp.int32, (128, 128), 0) < HD
    col = lax.broadcasted_iota(jnp.int32, (128, 128), 1) < HD
    return jnp.where(row == col, dup_t, jnp.zeros_like(dup_t))


def transposed_twice(tile):
    both = jnp.concatenate([tile, tile], axis=0)
    return both.T


def head_rows(acc):
    turned = jnp.concatenate([acc, acc], axis=0).T
    return jnp.where(lane_low(HD), turned[:HD], turned[HD:])


def pick_diag(full, half):
    lanes = slice(half * 128, half * 128 + 128)
    top = full[half * 128 : half * 128 + HD, lanes]
    low = full[half * 128 + HD : half * 128 + 128, lanes]
    return jnp.where(lane_low(HD), top, low)


def chunk_ids(list_ref, row, base, nb):
    ids = [list_ref[row, base + j] for j in range(CHUNK)]
    safe = [jnp.where(b == nb, 0, b) for b in ids]
    return ids, safe


def block_rows(ref, blocks, lanes):
    return jnp.concatenate(
        [ref[0, pl.ds(pl.multiple_of(b * BLK, BLK), BLK), lanes] for b in blocks], axis=0
    )


def turned_blocks(ref, blocks, rows):
    low = lane_low(rows.stop - rows.start)
    tiles = [ref[b, rows, :] for b in blocks]
    return jnp.concatenate(
        [jnp.where(low, tiles[i], tiles[i + 1]) for i in range(0, CHUNK, 2)], axis=1
    )


def turn_all(src_ref, dst_ref, nb, width):
    def body(b, _):
        start = pl.multiple_of(b * BLK, BLK)
        for t in range(width // 128):
            tile = src_ref[0, pl.ds(start, BLK), t * 128 : t * 128 + 128]
            dst_ref[b, t * 128 : t * 128 + 128, :] = transposed_twice(tile)
        return 0

    lax.fori_loop(0, nb, body, 0)


def dot_f32(left, right):
    return lax.dot_general(
        left, right, (((1,), (0,)), ((), ())), preferred_element_type=jnp.float32
    )


def forward_kernel(group, n_ref, list_ref, q_ref, k_ref, v_ref, segc_ref, segr_ref,
                   o_ref, lse_ref, vt_ref, qst_ref, m_ref, l_ref, acc_ref):
    row = pl.program_id(0)
    width = q_ref.shape[2]
    nb = q_ref.shape[1] // BLK
    groups, halves = width // group, group // 128
    turn_all(v_ref, vt_ref, nb, width)
    qst_ref[...] = jnp.zeros_like(qst_ref)

    def per_query(a, _):
        start = pl.multiple_of(a * BLK, BLK)
        for t in range(width // 128):
            tile = q_ref[0, pl.ds(start, BLK), t * 128 : t * 128 + 128] * 0.125
            g, u = t // halves, t % halves
            qst_ref[g, u * 128 : u * 128 + 128, u * 128 : u * 128 + 128] = diag128(
                transposed_twice(tile.astype(jnp.bfloat16))
            )
        seg_q = segr_ref[0, a]
        m_ref[...] = jnp.full_like(m_ref, NEG)
        l_ref[...] = jnp.zeros_like(l_ref)
        acc_ref[...] = jnp.zeros_like(acc_ref)

        def per_chunk(c, _):
            ids, safe = chunk_ids(list_ref, row, a * nb + c * CHUNK, nb)
            seg_k = block_rows(segc_ref, ids, slice(0, 128))
            allowed = seg_k == seg_q
            for g in range(groups):
                lanes = slice(g * group, g * group + group)
                s_t = dot_f32(block_rows(k_ref, safe, lanes), qst_ref[g])
                weights, alphas = [], []
                for u in range(halves):
                    t = g * halves + u
                    s = jnp.where(allowed, s_t[:, u * 128 : u * 128 + 128], NEG)
                    m_old = m_ref[t]
                    m_new = jnp.maximum(m_old, jnp.max(s, axis=0, keepdims=True))
                    p = jnp.exp(s - m_new)
                    alpha = jnp.exp(m_old - m_new)
                    l_ref[t] = alpha * l_ref[t] + jnp.sum(p, axis=0, keepdims=True)
                    m_ref[t] = m_new
                    weights.append(p.astype(jnp.bfloat16))
                    alphas.append(alpha)
                p_t = jnp.concatenate(weights, axis=1) if halves > 1 else weights[0]
                o_t = dot_f32(turned_blocks(vt_ref, safe, lanes), p_t)
                for u in range(halves):
                    t = g * halves + u
                    acc_ref[t] = alphas[u] * acc_ref[t] + pick_diag(o_t, u)
            return 0

        lax.fori_loop(0, n_ref[row, a], per_chunk, 0)
        for t in range(width // 128):
            total = l_ref[t]
            out = acc_ref[t] / total
            o_ref[0, pl.ds(start, BLK), t * 128 : t * 128 + 128] = head_rows(out).astype(
                jnp.bfloat16
            )
            lse_ref[0, a, :, t * 128 : t * 128 + 128] = m_ref[t] + jnp.log(total)
        return 0

    lax.fori_loop(0, nb, per_query, 0)


def group_of(width):
    return 256 if width % 256 == 0 else 128


def whole_spec(shape):
    rest = (0,) * (len(shape) - 1)
    return pl.BlockSpec((1,) + tuple(shape[1:]), lambda r, *_: (r,) + rest)


def one_spec(shape):
    rest = (0,) * (len(shape) - 1)
    return pl.BlockSpec((1,) + tuple(shape[1:]), lambda r, *_: (r,) + rest,
                        pipeline_mode=pl.Buffered(1))


def attention_forward(q, k, v, plan):
    chunks, listed, seg_cols, seg_rows = plan
    rows, full_len, width = q.shape
    nb, group = full_len // BLK, group_of(width)
    tiles = width // 128
    pairs = rows * full_len * full_len // 4 * width
    args = (q, k, v, seg_cols, seg_rows)
    return pl.pallas_call(
        functools.partial(forward_kernel, group),
        out_shape=(
            jax.ShapeDtypeStruct((rows, full_len, width), jnp.bfloat16),
            jax.ShapeDtypeStruct((rows, nb, 1, width), jnp.float32),
        ),
        grid_spec=pltpu.PrefetchScalarGridSpec(
            num_scalar_prefetch=2,
            grid=(rows,),
            in_specs=[one_spec(x.shape) for x in args],
            out_specs=(one_spec((rows, full_len, width)), one_spec((rows, nb, 1, width))),
            scratch_shapes=[
                pltpu.VMEM((nb, width, 128), jnp.bfloat16),
                pltpu.VMEM((width // group, group, group), jnp.bfloat16),
                pltpu.VMEM((tiles, 1, 128), jnp.float32),
                pltpu.VMEM((tiles, 1, 128), jnp.float32),
                pltpu.VMEM((tiles, HD, 128), jnp.float32),
            ],
        ),
        compiler_params=pltpu.CompilerParams(vmem_limit_bytes=48 << 20),
        cost_estimate=pl.CostEstimate(
            flops=4 * pairs, transcendentals=pairs // HD, bytes_accessed=8 * q.size
        ),
        name="attention_forward",
    )(chunks, listed, *args)


def backward_kernel(group, n_ref, list_ref, q_ref, k_ref, v_ref, o_ref, do_ref, lse_ref,
                    segc_ref, segr_ref, dq_ref, dk_ref, dv_ref,
                    kt_ref, qst_ref, qs_ref, dost_ref, dos_ref, delta_ref, acc_ref,
                    dk_acc, dv_acc):
    row = pl.program_id(0)
    full_len, width = q_ref.shape[1], q_ref.shape[2]
    nb = full_len // BLK
    groups, halves = width // group, group // 128
    turn_all(k_ref, kt_ref, nb, width)
    for ref in (qst_ref, qs_ref, dost_ref, dos_ref, dk_acc, dv_acc):
        ref[...] = jnp.zeros_like(ref)
    low = lane_low(HD)

    def per_query(a, _):
        start = pl.multiple_of(a * BLK, BLK)
        for t in range(width // 128):
            g, u = t // halves, t % halves
            lanes = slice(t * 128, t * 128 + 128)
            square = slice(u * 128, u * 128 + 128)
            q_tile = (q_ref[0, pl.ds(start, BLK), lanes] * 0.125).astype(jnp.bfloat16)
            g_tile = do_ref[0, pl.ds(start, BLK), lanes]
            o_tile = o_ref[0, pl.ds(start, BLK), lanes]
            g_turn = transposed_twice(g_tile)
            qst_ref[g, square, square] = diag128(transposed_twice(q_tile))
            dost_ref[g, square, square] = diag128(g_turn)
            qs_ref[g, square, square] = diag128(jnp.concatenate([q_tile, q_tile], axis=0))
            dos_ref[g, square, square] = diag128(jnp.concatenate([g_tile, g_tile], axis=0))
            product = g_turn.astype(jnp.float32) * transposed_twice(o_tile).astype(jnp.float32)
            delta_ref[t] = jnp.where(
                low[:1],
                jnp.sum(product[:HD], axis=0, keepdims=True),
                jnp.sum(product[HD:], axis=0, keepdims=True),
            )
        seg_q = segr_ref[0, a]
        acc_ref[...] = jnp.zeros_like(acc_ref)

        def per_chunk(c, _):
            ids, safe = chunk_ids(list_ref, row, a * nb + c * CHUNK, nb)
            seg_k = block_rows(segc_ref, ids, slice(0, 128))
            allowed = seg_k == seg_q
            for g in range(groups):
                lanes = slice(g * group, g * group + group)
                s_t = dot_f32(block_rows(k_ref, safe, lanes), qst_ref[g])
                dp_t = dot_f32(block_rows(v_ref, safe, lanes), dost_ref[g])
                p_parts, ds_parts = [], []
                for u in range(halves):
                    t = g * halves + u
                    half = slice(u * 128, u * 128 + 128)
                    lse = lse_ref[0, a, :, t * 128 : t * 128 + 128]
                    p = jnp.exp(jnp.where(allowed, s_t[:, half], NEG) - lse)
                    ds = p * (dp_t[:, half] - delta_ref[t])
                    p_parts.append(p.astype(jnp.bfloat16))
                    ds_parts.append(ds.astype(jnp.bfloat16))
                p_t = jnp.concatenate(p_parts, axis=1) if halves > 1 else p_parts[0]
                ds_t = jnp.concatenate(ds_parts, axis=1) if halves > 1 else ds_parts[0]
                dv = dot_f32(p_t, dos_ref[g])
                dk = dot_f32(ds_t, qs_ref[g])
                dq_t = dot_f32(turned_blocks(kt_ref, safe, lanes), ds_t)
                for j in range(CHUNK):
                    where = pl.ds(pl.multiple_of(safe[j] * BLK, BLK), BLK)
                    part = slice(j * BLK, j * BLK + BLK)
                    dv_acc[where, lanes] += dv[part]
                    dk_acc[where, lanes] += dk[part]
                for u in range(halves):
                    acc_ref[g * halves + u] += pick_diag(dq_t, u)
            return 0

        lax.fori_loop(0, n_ref[row, a], per_chunk, 0)
        for t in range(width // 128):
            dq_ref[0, pl.ds(start, BLK), t * 128 : t * 128 + 128] = (
                head_rows(acc_ref[t]) * 0.125
            ).astype(jnp.bfloat16)
        return 0

    lax.fori_loop(0, nb, per_query, 0)

    def flush(a, _):
        where = pl.ds(pl.multiple_of(a * BLK, BLK), BLK)
        dk_ref[0, where, :] = dk_acc[where, :].astype(jnp.bfloat16)
        dv_ref[0, where, :] = dv_acc[where, :].astype(jnp.bfloat16)
        return 0

    lax.fori_loop(0, nb, flush, 0)


def attention_backward(q, k, v, o, do, lse, plan):
    chunks, listed, seg_cols, seg_rows = plan
    rows, full_len, width = q.shape
    nb, group = full_len // BLK, group_of(width)
    tiles, groups = width // 128, width // group
    pairs = rows * full_len * full_len // 4 * width
    args = (q, k, v, o, do, lse, seg_cols, seg_rows)
    like = jax.ShapeDtypeStruct((rows, full_len, width), jnp.bfloat16)
    square = pltpu.VMEM((groups, group, group), jnp.bfloat16)
    return pl.pallas_call(
        functools.partial(backward_kernel, group),
        out_shape=(like, like, like),
        grid_spec=pltpu.PrefetchScalarGridSpec(
            num_scalar_prefetch=2,
            grid=(rows,),
            in_specs=[one_spec(x.shape) for x in args],
            out_specs=tuple(one_spec(like.shape) for _ in range(3)),
            scratch_shapes=[
                pltpu.VMEM((nb, width, 128), jnp.bfloat16),
                square, square, square, square,
                pltpu.VMEM((tiles, 1, 128), jnp.float32),
                pltpu.VMEM((tiles, HD, 128), jnp.float32),
                pltpu.VMEM((full_len, width), jnp.float32),
                pltpu.VMEM((full_len, width), jnp.float32),
            ],
        ),
        compiler_params=pltpu.CompilerParams(vmem_limit_bytes=58 << 20),
        cost_estimate=pl.CostEstimate(
            flops=10 * pairs, transcendentals=pairs // HD, bytes_accessed=16 * q.size
        ),
        name="attention_backward",
    )(chunks, listed, *args)


eps_norm = 1e-06


def layer_norm(hidden, gain_vec, shift_vec):
    mean_val = jnp.mean(hidden, axis=-1, keepdims=True)
    centred = hidden - mean_val
    var_val = jnp.mean(centred * centred, axis=-1, keepdims=True)
    return centred * lax.rsqrt(var_val + eps_norm) * gain_vec + shift_vec


def gelu_tanh(values):
    return jax.nn.gelu(values, approximate=True)


def contract_rows(left, right):
    return lax.dot_general(
        left, right, (((0,), (0,)), ((), ())), preferred_element_type=jnp.float32
    )


def times_transpose(left, right):
    return lax.dot_general(
        left, right, (((1,), (1,)), ((), ())), preferred_element_type=jnp.float32
    )


def butterfly_sum(values, axis):
    size = lax.axis_size(axis)
    if size & (size - 1):
        return lax.psum(values, axis)
    step = 1
    while step < size:
        pairs = [(i, i ^ step) for i in range(size)]
        values = values + lax.ppermute(values, axis, pairs)
        step *= 2
    return values


def sum_seq(values):
    if lax.axis_size("seq") == 2:
        other = lax.ppermute(values, "seq", [(0, 1), (1, 0)])
        return values.astype(jnp.float32) + other.astype(jnp.float32)
    return lax.psum(values, "seq").astype(jnp.float32)


class Regroup:
    def __init__(self, row_count):
        self.size = lax.axis_size("seq")
        self.ways = math.gcd(row_count, self.size)
        self.parts = self.size // self.ways
        self.rows = row_count // self.ways
        me = lax.axis_index("seq")
        self.place = lax.rem(me, self.ways)
        self.row_group = me // self.parts

    def targets(self, turn):
        ways, parts = self.ways, self.parts
        return [
            (s, ((s % ways + turn) % ways) * parts + s // ways) for s in range(self.size)
        ]

    def move(self, values, pairs):
        if all(a == b for a, b in pairs):
            return values
        return lax.ppermute(values, "seq", pairs)

    def gather(self, values):
        rows, local, width = self.rows, values.shape[1], values.shape[2]
        out = jnp.zeros((rows, self.ways, local, width), values.dtype)
        for turn in range(self.ways):
            pick = lax.rem(self.place + turn, self.ways)
            chunk = lax.dynamic_slice_in_dim(values, pick * rows, rows, 0)
            chunk = self.move(chunk, self.targets(turn))
            spot = lax.rem(self.row_group - turn + self.ways, self.ways)
            out = lax.dynamic_update_slice_in_dim(out, chunk[:, None], spot, 1)
        return out.reshape(rows, self.ways * local, width)

    def scatter(self, values):
        rows, width = self.rows, values.shape[2]
        local = values.shape[1] // self.ways
        values = values.reshape(rows, self.ways, local, width)
        out = jnp.zeros((rows * self.ways, local, width), values.dtype)
        for turn in range(self.ways):
            spot = lax.rem(self.row_group - turn + self.ways, self.ways)
            chunk = lax.dynamic_slice_in_dim(values, spot, 1, 1)[:, 0]
            chunk = self.move(chunk, [(b, a) for a, b in self.targets(turn)])
            pick = lax.rem(self.place + turn, self.ways)
            out = lax.dynamic_update_slice_in_dim(out, chunk, pick * rows, 0)
        return out

    def pick_rows(self, values):
        return lax.dynamic_slice_in_dim(values, self.row_group * self.rows, self.rows, 0)

    def groups(self):
        return [
            [r * self.parts + j for j in range(self.parts)] for r in range(self.ways)
        ]

    def to_heads(self, values):
        if self.parts == 1:
            return values
        return lax.all_to_all(
            values, "seq", split_axis=2, concat_axis=1, tiled=True,
            axis_index_groups=self.groups(),
        )

    def from_heads(self, values):
        if self.parts == 1:
            return values
        return lax.all_to_all(
            values, "seq", split_axis=1, concat_axis=2, tiled=True,
            axis_index_groups=self.groups(),
        )


def shards(
    tokens_in,
    segment_ids,
    random_blocks,
    global_blocks,
    w_query,
    b_query,
    w_key,
    w_value,
    b_value,
    w_attn_out,
    b_attn_out,
    ln1_gain,
    ln1_bias,
    w_inner,
    b_inner,
    w_outer,
    b_outer,
    ln2_gain,
    ln2_bias,
    out_grad,
):
    row_count, local_len, width = tokens_in.shape
    seq_count = lax.axis_size("seq")
    fsdp_count = lax.axis_size("fsdp")
    tok_count = row_count * local_len
    own = w_query.shape[0]
    per_own = b_inner.shape[0] // own
    regroup = Regroup(row_count)

    vectors = [b_query, b_value, b_attn_out, ln1_gain, ln1_bias, b_outer, ln2_gain, ln2_bias]
    columns = [x[:, None] for x in vectors] + [b_inner.reshape(own, per_own)]
    used = len(vectors) + per_own
    columns.append(jnp.zeros((own, 128 - used), jnp.bfloat16))
    first = jnp.concatenate([w_query, w_key, w_value] + columns, axis=1)
    first = lax.all_gather(first, "fsdp", axis=0, tiled=True)
    qkv_w = first[:, : 3 * width]
    small = first[:, 3 * width : 3 * width + used].astype(jnp.float32).T
    query_b, value_b, out_b, gain_one, bias_one, outer_b, gain_two, bias_two = small[:8]
    inner_b = small[8:].T.reshape(-1)
    second = lax.all_gather(
        jnp.concatenate([w_attn_out, w_inner], axis=1), "fsdp", axis=0, tiled=True
    )
    out_w, inner_w = second[:, :width], second[:, width:]
    outer_w = lax.all_gather(w_outer, "fsdp", axis=0, tiled=True)

    flat_in = regroup.gather(tokens_in).reshape(tok_count, width)
    flat_grad = regroup.gather(out_grad).reshape(tok_count, width)
    plan = plan_blocks(
        regroup.pick_rows(segment_ids),
        regroup.pick_rows(random_blocks),
        regroup.pick_rows(global_blocks),
    )

    def split_rows(values):
        return values.reshape(regroup.rows, tok_count // regroup.rows, width)

    qkv_bias = jnp.concatenate([query_b, jnp.zeros_like(query_b), value_b])
    qkv = (jnp.dot(flat_in, qkv_w, preferred_element_type=jnp.float32) + qkv_bias).astype(
        jnp.bfloat16
    )
    q, k, v = (
        regroup.to_heads(split_rows(qkv[:, i * width : (i + 1) * width])) for i in range(3)
    )
    att, lse = attention_forward(q, k, v, plan)
    att_flat = regroup.from_heads(att).reshape(tok_count, width)
    attn_branch = jnp.dot(att_flat, out_w, preferred_element_type=jnp.float32) + out_b
    resid_one = flat_in.astype(jnp.float32) + attn_branch
    normed_one, norm_one_pull = jax.vjp(layer_norm, resid_one, gain_one, bias_one)
    normed_low = normed_one.astype(jnp.bfloat16)
    inner_pre = jnp.dot(normed_low, inner_w, preferred_element_type=jnp.float32) + inner_b
    inner_act, gelu_pull = jax.vjp(gelu_tanh, inner_pre)
    inner_low = inner_act.astype(jnp.bfloat16)
    mlp_branch = jnp.dot(inner_low, outer_w, preferred_element_type=jnp.float32) + outer_b
    normed_two, norm_two_pull = jax.vjp(layer_norm, normed_one + mlp_branch, gain_two, bias_two)
    out_tokens = regroup.scatter(split_rows(normed_two.astype(jnp.bfloat16)))

    sums = jnp.stack(
        [
            jnp.sum(resid_one * resid_one),
            jnp.sum(attn_branch * attn_branch),
            jnp.sum(mlp_branch * mlp_branch),
        ]
    )
    sums = jnp.broadcast_to(sums[:, None], (3, 128))
    sums = butterfly_sum(butterfly_sum(sums, "fsdp"), "seq")[:, 0]
    rms_values = jnp.sqrt(sums / (tok_count * width * seq_count * fsdp_count))

    def reduced(values):
        return lax.psum_scatter(
            values.astype(jnp.bfloat16), "fsdp", scatter_dimension=0, tiled=True
        )

    d_resid_two, d_gain_two, d_bias_two = norm_two_pull(flat_grad.astype(jnp.float32))
    d_mlp = d_resid_two.astype(jnp.bfloat16)
    d_outer_b = jnp.sum(d_mlp.astype(jnp.float32), axis=0)
    d_outer_w = sum_seq(reduced(contract_rows(inner_low, d_mlp)))
    (d_pre_full,) = gelu_pull(times_transpose(d_mlp, outer_w))
    d_pre = d_pre_full.astype(jnp.bfloat16)
    d_inner_b = jnp.sum(d_pre.astype(jnp.float32), axis=0)
    d_inner_w = contract_rows(normed_low, d_pre)
    d_normed_one = d_resid_two + times_transpose(d_pre, inner_w)
    d_resid_one, d_gain_one, d_bias_one = norm_one_pull(d_normed_one)
    d_attn = d_resid_one.astype(jnp.bfloat16)
    d_out_b = jnp.sum(d_attn.astype(jnp.float32), axis=0)
    d_out_w = contract_rows(att_flat, d_attn)
    d_second = sum_seq(reduced(jnp.concatenate([d_out_w, d_inner_w], axis=1)))
    d_att = times_transpose(d_attn, out_w).astype(jnp.bfloat16)
    dq, dk, dv = attention_backward(
        q, k, v, att, regroup.to_heads(split_rows(d_att)), lse, plan
    )
    dq, dk, dv = (regroup.from_heads(x).reshape(tok_count, width) for x in (dq, dk, dv))
    d_query_b = jnp.sum(dq.astype(jnp.float32), axis=0)
    d_value_b = jnp.sum(dv.astype(jnp.float32), axis=0)
    grads = [
        d_query_b, d_value_b, d_out_b, d_gain_one, d_bias_one, d_outer_b, d_gain_two, d_bias_two,
    ]
    d_small = jnp.concatenate(
        [jnp.stack(grads), d_inner_b.reshape(width, per_own).T,
         jnp.zeros((128 - used, width), jnp.float32)], axis=0
    ).T
    d_first = sum_seq(
        reduced(jnp.concatenate([contract_rows(flat_in, x) for x in (dq, dk, dv)] + [d_small], axis=1))
    )
    d_tokens = d_resid_one
    for i, part in enumerate((dq, dk, dv)):
        d_tokens = d_tokens + times_transpose(part, qkv_w[:, i * width : (i + 1) * width])
    d_tokens_in = regroup.scatter(split_rows(d_tokens.astype(jnp.bfloat16)))
    d_cols = d_first[:, 3 * width :].T
    d_vec = [d_cols[i] for i in range(len(vectors))]
    return (
        out_tokens,
        d_tokens_in,
        d_first[:, :width],
        d_vec[0],
        d_first[:, width : 2 * width],
        d_first[:, 2 * width : 3 * width],
        d_vec[1],
        d_second[:, :width],
        d_vec[2],
        d_vec[3],
        d_vec[4],
        d_second[:, width:],
        d_cols[len(vectors) : used].T.reshape(-1),
        d_outer_w,
        d_vec[5],
        d_vec[6],
        d_vec[7],
        rms_values,
    )


def solution(mesh):
    in_specs = (
        P("fsdp", "seq", None),
        P("fsdp", None),
        P("fsdp", None, None),
        P("fsdp", None),
        P("fsdp", None),
        P("fsdp"),
        P("fsdp", None),
        P("fsdp", None),
        P("fsdp"),
        P("fsdp", None),
        P("fsdp"),
        P("fsdp"),
        P("fsdp"),
        P("fsdp", None),
        P("fsdp"),
        P("fsdp", None),
        P("fsdp"),
        P("fsdp"),
        P("fsdp"),
        P("fsdp", "seq", None),
    )
    out_specs = (
        P("fsdp", "seq", None),
        P("fsdp", "seq", None),
        P("fsdp", None),
        P("fsdp"),
        P("fsdp", None),
        P("fsdp", None),
        P("fsdp"),
        P("fsdp", None),
        P("fsdp"),
        P("fsdp"),
        P("fsdp"),
        P("fsdp", None),
        P("fsdp"),
        P("fsdp", None),
        P("fsdp"),
        P("fsdp"),
        P("fsdp"),
        P(),
    )
    return jax.shard_map(shards, mesh=mesh, in_specs=in_specs, out_specs=out_specs, check_vma=False)
```

```python
import functools
import math

import jax
import jax.numpy as jnp
from jax import lax
from jax.experimental import pallas as pl
from jax.experimental.pallas import tpu as pltpu
from jax.sharding import PartitionSpec as P

HD = 64
BLK = 64
CHUNK = 4
NEG = -1e30


def plan_blocks(seg, rand, glob):
    rows, full_len = seg.shape
    nb = full_len // BLK
    ids = jnp.arange(nb, dtype=jnp.int32)
    is_global = jnp.any(ids[None, :, None] == glob[:, None, :], axis=-1)
    picked = jnp.any(rand[:, :, None, :] == ids[None, None, :, None], axis=-1)
    nearby = jnp.abs(ids[:, None] - ids[None, :]) <= 1
    admitted = nearby[None] | picked | is_global[:, :, None] | is_global[:, None, :]
    by_block = seg.reshape(rows, nb, BLK)
    low, high = by_block[:, :, 0], by_block[:, :, BLK - 1]
    meets = (low[:, :, None] <= high[:, None, :]) & (low[:, None, :] <= high[:, :, None])
    active = (admitted & meets).astype(jnp.int32)
    upto = (ids[:, None] <= ids[None, :]).astype(jnp.int32)
    place = jnp.sum(active[:, :, :, None] * upto[None, None], axis=2) - 1
    count = jnp.sum(active, axis=2)
    hit = (place[:, :, :, None] == ids[None, None, None, :]) & (active[:, :, :, None] > 0)
    listed = jnp.sum(jnp.where(hit, ids[None, None, :, None], 0), axis=2)
    listed = jnp.where(ids[None, None, :] < count[:, :, None], listed, nb)
    chunks = (count + (CHUNK - 1)) // CHUNK
    seg_cols = jnp.concatenate([seg, jnp.full((rows, BLK), -1, jnp.int32)], axis=1)
    seg_cols = jnp.broadcast_to(seg_cols[:, :, None], (rows, full_len + BLK, 128))
    seg_rows = jnp.concatenate([by_block, by_block], axis=2)[:, :, None, :]
    return chunks, listed.reshape(rows, nb * nb), seg_cols, seg_rows


def lane_low(rows):
    return lax.broadcasted_iota(jnp.int32, (rows, 128), 1) < HD


def diag128(dup_t):
    row = lax.broadcasted_iota(jnp.int32, (128, 128), 0) < HD
    col = lax.broadcasted_iota(jnp.int32, (128, 128), 1) < HD
    return jnp.where(row == col, dup_t, jnp.zeros_like(dup_t))


def transposed_twice(tile):
    both = jnp.concatenate([tile, tile], axis=0)
    return both.T


def head_rows(acc):
    turned = jnp.concatenate([acc, acc], axis=0).T
    return jnp.where(lane_low(HD), turned[:HD], turned[HD:])


def pick_diag(full, half):
    lanes = slice(half * 128, half * 128 + 128)
    top = full[half * 128 : half * 128 + HD, lanes]
    low = full[half * 128 + HD : half * 128 + 128, lanes]
    return jnp.where(lane_low(HD), top, low)


def chunk_ids(list_ref, row, base, nb):
    ids = [list_ref[row, base + j] for j in range(CHUNK)]
    safe = [jnp.where(b == nb, 0, b) for b in ids]
    return ids, safe


def block_rows(ref, blocks, lanes):
    return jnp.concatenate(
        [ref[0, pl.ds(pl.multiple_of(b * BLK, BLK), BLK), lanes] for b in blocks], axis=0
    )


def turned_blocks(ref, blocks, rows):
    low = lane_low(rows.stop - rows.start)
    tiles = [ref[b, rows, :] for b in blocks]
    return jnp.concatenate(
        [jnp.where(low, tiles[i], tiles[i + 1]) for i in range(0, CHUNK, 2)], axis=1
    )


def turn_all(src_ref, dst_ref, nb, width):
    def body(b, _):
        start = pl.multiple_of(b * BLK, BLK)
        for t in range(width // 128):
            tile = src_ref[0, pl.ds(start, BLK), t * 128 : t * 128 + 128]
            dst_ref[b, t * 128 : t * 128 + 128, :] = transposed_twice(tile)
        return 0

    lax.fori_loop(0, nb, body, 0)


def dot_f32(left, right):
    return lax.dot_general(
        left, right, (((1,), (0,)), ((), ())), preferred_element_type=jnp.float32
    )


def forward_kernel(group, n_ref, list_ref, q_ref, k_ref, v_ref, segc_ref, segr_ref,
                   o_ref, lse_ref, vt_ref, qst_ref, m_ref, l_ref, acc_ref):
    row = pl.program_id(0)
    width = q_ref.shape[2]
    nb = q_ref.shape[1] // BLK
    groups, halves = width // group, group // 128
    turn_all(v_ref, vt_ref, nb, width)
    qst_ref[...] = jnp.zeros_like(qst_ref)

    def per_query(a, _):
        start = pl.multiple_of(a * BLK, BLK)
        for t in range(width // 128):
            tile = q_ref[0, pl.ds(start, BLK), t * 128 : t * 128 + 128] * 0.125
            g, u = t // halves, t % halves
            qst_ref[g, u * 128 : u * 128 + 128, u * 128 : u * 128 + 128] = diag128(
                transposed_twice(tile.astype(jnp.bfloat16))
            )
        seg_q = segr_ref[0, a]
        m_ref[...] = jnp.full_like(m_ref, NEG)
        l_ref[...] = jnp.zeros_like(l_ref)
        acc_ref[...] = jnp.zeros_like(acc_ref)

        def per_chunk(c, _):
            ids, safe = chunk_ids(list_ref, row, a * nb + c * CHUNK, nb)
            seg_k = block_rows(segc_ref, ids, slice(0, 128))
            allowed = seg_k == seg_q
            for g in range(groups):
                lanes = slice(g * group, g * group + group)
                s_t = dot_f32(block_rows(k_ref, safe, lanes), qst_ref[g])
                weights, alphas = [], []
                for u in range(halves):
                    t = g * halves + u
                    s = jnp.where(allowed, s_t[:, u * 128 : u * 128 + 128], NEG)
                    m_old = m_ref[t]
                    m_new = jnp.maximum(m_old, jnp.max(s, axis=0, keepdims=True))
                    p = jnp.exp(s - m_new)
                    alpha = jnp.exp(m_old - m_new)
                    l_ref[t] = alpha * l_ref[t] + jnp.sum(p, axis=0, keepdims=True)
                    m_ref[t] = m_new
                    weights.append(p.astype(jnp.bfloat16))
                    alphas.append(alpha)
                p_t = jnp.concatenate(weights, axis=1) if halves > 1 else weights[0]
                o_t = dot_f32(turned_blocks(vt_ref, safe, lanes), p_t)
                for u in range(halves):
                    t = g * halves + u
                    acc_ref[t] = alphas[u] * acc_ref[t] + pick_diag(o_t, u)
            return 0

        lax.fori_loop(0, n_ref[row, a], per_chunk, 0)
        for t in range(width // 128):
            total = l_ref[t]
            out = acc_ref[t] / total
            o_ref[0, pl.ds(start, BLK), t * 128 : t * 128 + 128] = head_rows(out).astype(
                jnp.bfloat16
            )
            lse_ref[0, a, :, t * 128 : t * 128 + 128] = m_ref[t] + jnp.log(total)
        return 0

    lax.fori_loop(0, nb, per_query, 0)


def group_of(width):
    return 256 if width % 256 == 0 else 128


def whole_spec(shape):
    rest = (0,) * (len(shape) - 1)
    return pl.BlockSpec((1,) + tuple(shape[1:]), lambda r, *_: (r,) + rest)


def one_spec(shape):
    rest = (0,) * (len(shape) - 1)
    return pl.BlockSpec((1,) + tuple(shape[1:]), lambda r, *_: (r,) + rest,
                        pipeline_mode=pl.Buffered(1))


def attention_forward(q, k, v, plan):
    chunks, listed, seg_cols, seg_rows = plan
    rows, full_len, width = q.shape
    nb, group = full_len // BLK, group_of(width)
    tiles = width // 128
    pairs = rows * full_len * full_len // 4 * width
    args = (q, k, v, seg_cols, seg_rows)
    return pl.pallas_call(
        functools.partial(forward_kernel, group),
        out_shape=(
            jax.ShapeDtypeStruct((rows, full_len, width), jnp.bfloat16),
            jax.ShapeDtypeStruct((rows, nb, 1, width), jnp.float32),
        ),
        grid_spec=pltpu.PrefetchScalarGridSpec(
            num_scalar_prefetch=2,
            grid=(rows,),
            in_specs=[one_spec(x.shape) for x in args],
            out_specs=(one_spec((rows, full_len, width)), one_spec((rows, nb, 1, width))),
            scratch_shapes=[
                pltpu.VMEM((nb, width, 128), jnp.bfloat16),
                pltpu.VMEM((width // group, group, group), jnp.bfloat16),
                pltpu.VMEM((tiles, 1, 128), jnp.float32),
                pltpu.VMEM((tiles, 1, 128), jnp.float32),
                pltpu.VMEM((tiles, HD, 128), jnp.float32),
            ],
        ),
        compiler_params=pltpu.CompilerParams(vmem_limit_bytes=48 << 20),
        cost_estimate=pl.CostEstimate(
            flops=64 * pairs, transcendentals=pairs // HD, bytes_accessed=8 * q.size
        ),
        name="attention_forward",
    )(chunks, listed, *args)


def backward_kernel(group, n_ref, list_ref, q_ref, k_ref, v_ref, o_ref, do_ref, lse_ref,
                    segc_ref, segr_ref, dq_ref, dk_ref, dv_ref,
                    kt_ref, qst_ref, qs_ref, dost_ref, dos_ref, delta_ref, acc_ref,
                    dk_acc, dv_acc):
    row = pl.program_id(0)
    full_len, width = q_ref.shape[1], q_ref.shape[2]
    nb = full_len // BLK
    groups, halves = width // group, group // 128
    turn_all(k_ref, kt_ref, nb, width)
    for ref in (qst_ref, qs_ref, dost_ref, dos_ref, dk_acc, dv_acc):
        ref[...] = jnp.zeros_like(ref)
    low = lane_low(HD)

    def per_query(a, _):
        start = pl.multiple_of(a * BLK, BLK)
        for t in range(width // 128):
            g, u = t // halves, t % halves
            lanes = slice(t * 128, t * 128 + 128)
            square = slice(u * 128, u * 128 + 128)
            q_tile = (q_ref[0, pl.ds(start, BLK), lanes] * 0.125).astype(jnp.bfloat16)
            g_tile = do_ref[0, pl.ds(start, BLK), lanes]
            o_tile = o_ref[0, pl.ds(start, BLK), lanes]
            g_turn = transposed_twice(g_tile)
            qst_ref[g, square, square] = diag128(transposed_twice(q_tile))
            dost_ref[g, square, square] = diag128(g_turn)
            qs_ref[g, square, square] = diag128(jnp.concatenate([q_tile, q_tile], axis=0))
            dos_ref[g, square, square] = diag128(jnp.concatenate([g_tile, g_tile], axis=0))
            product = g_turn.astype(jnp.float32) * transposed_twice(o_tile).astype(jnp.float32)
            delta_ref[t] = jnp.where(
                low[:1],
                jnp.sum(product[:HD], axis=0, keepdims=True),
                jnp.sum(product[HD:], axis=0, keepdims=True),
            )
        seg_q = segr_ref[0, a]
        acc_ref[...] = jnp.zeros_like(acc_ref)

        def per_chunk(c, _):
            ids, safe = chunk_ids(list_ref, row, a * nb + c * CHUNK, nb)
            seg_k = block_rows(segc_ref, ids, slice(0, 128))
            allowed = seg_k == seg_q
            for g in range(groups):
                lanes = slice(g * group, g * group + group)
                s_t = dot_f32(block_rows(k_ref, safe, lanes), qst_ref[g])
                dp_t = dot_f32(block_rows(v_ref, safe, lanes), dost_ref[g])
                p_parts, ds_parts = [], []
                for u in range(halves):
                    t = g * halves + u
                    half = slice(u * 128, u * 128 + 128)
                    lse = lse_ref[0, a, :, t * 128 : t * 128 + 128]
                    p = jnp.exp(jnp.where(allowed, s_t[:, half], NEG) - lse)
                    ds = p * (dp_t[:, half] - delta_ref[t])
                    p_parts.append(p.astype(jnp.bfloat16))
                    ds_parts.append(ds.astype(jnp.bfloat16))
                p_t = jnp.concatenate(p_parts, axis=1) if halves > 1 else p_parts[0]
                ds_t = jnp.concatenate(ds_parts, axis=1) if halves > 1 else ds_parts[0]
                dv = dot_f32(p_t, dos_ref[g])
                dk = dot_f32(ds_t, qs_ref[g])
                dq_t = dot_f32(turned_blocks(kt_ref, safe, lanes), ds_t)
                for j in range(CHUNK):
                    where = pl.ds(pl.multiple_of(safe[j] * BLK, BLK), BLK)
                    part = slice(j * BLK, j * BLK + BLK)
                    dv_acc[where, lanes] += dv[part]
                    dk_acc[where, lanes] += dk[part]
                for u in range(halves):
                    acc_ref[g * halves + u] += pick_diag(dq_t, u)
            return 0

        lax.fori_loop(0, n_ref[row, a], per_chunk, 0)
        for t in range(width // 128):
            dq_ref[0, pl.ds(start, BLK), t * 128 : t * 128 + 128] = (
                head_rows(acc_ref[t]) * 0.125
            ).astype(jnp.bfloat16)
        return 0

    lax.fori_loop(0, nb, per_query, 0)

    def flush(a, _):
        where = pl.ds(pl.multiple_of(a * BLK, BLK), BLK)
        dk_ref[0, where, :] = dk_acc[where, :].astype(jnp.bfloat16)
        dv_ref[0, where, :] = dv_acc[where, :].astype(jnp.bfloat16)
        return 0

    lax.fori_loop(0, nb, flush, 0)


def attention_backward(q, k, v, o, do, lse, plan):
    chunks, listed, seg_cols, seg_rows = plan
    rows, full_len, width = q.shape
    nb, group = full_len // BLK, group_of(width)
    tiles, groups = width // 128, width // group
    pairs = rows * full_len * full_len // 4 * width
    args = (q, k, v, o, do, lse, seg_cols, seg_rows)
    like = jax.ShapeDtypeStruct((rows, full_len, width), jnp.bfloat16)
    square = pltpu.VMEM((groups, group, group), jnp.bfloat16)
    return pl.pallas_call(
        functools.partial(backward_kernel, group),
        out_shape=(like, like, like),
        grid_spec=pltpu.PrefetchScalarGridSpec(
            num_scalar_prefetch=2,
            grid=(rows,),
            in_specs=[one_spec(x.shape) for x in args],
            out_specs=tuple(one_spec(like.shape) for _ in range(3)),
            scratch_shapes=[
                pltpu.VMEM((nb, width, 128), jnp.bfloat16),
                square, square, square, square,
                pltpu.VMEM((tiles, 1, 128), jnp.float32),
                pltpu.VMEM((tiles, HD, 128), jnp.float32),
                pltpu.VMEM((full_len, width), jnp.float32),
                pltpu.VMEM((full_len, width), jnp.float32),
            ],
        ),
        compiler_params=pltpu.CompilerParams(vmem_limit_bytes=58 << 20),
        cost_estimate=pl.CostEstimate(
            flops=100 * pairs, transcendentals=pairs // HD, bytes_accessed=16 * q.size
        ),
        name="attention_backward",
    )(chunks, listed, *args)


eps_norm = 1e-06


def layer_norm(hidden, gain_vec, shift_vec):
    mean_val = jnp.mean(hidden, axis=-1, keepdims=True)
    centred = hidden - mean_val
    var_val = jnp.mean(centred * centred, axis=-1, keepdims=True)
    return centred * lax.rsqrt(var_val + eps_norm) * gain_vec + shift_vec


def gelu_tanh(values):
    return jax.nn.gelu(values, approximate=True)


def contract_rows(left, right):
    return lax.dot_general(
        left, right, (((0,), (0,)), ((), ())), preferred_element_type=jnp.float32
    )


def times_transpose(left, right):
    return lax.dot_general(
        left, right, (((1,), (1,)), ((), ())), preferred_element_type=jnp.float32
    )


def butterfly_sum(values, axis):
    size = lax.axis_size(axis)
    if size & (size - 1):
        return lax.psum(values, axis)
    step = 1
    while step < size:
        pairs = [(i, i ^ step) for i in range(size)]
        values = values + lax.ppermute(values, axis, pairs)
        step *= 2
    return values


def sum_seq(values):
    if lax.axis_size("seq") == 2:
        other = lax.ppermute(values, "seq", [(0, 1), (1, 0)])
        return values.astype(jnp.float32) + other.astype(jnp.float32)
    return lax.psum(values, "seq").astype(jnp.float32)


class Regroup:
    def __init__(self, row_count):
        self.size = lax.axis_size("seq")
        self.ways = math.gcd(row_count, self.size)
        self.parts = self.size // self.ways
        self.rows = row_count // self.ways
        me = lax.axis_index("seq")
        self.place = lax.rem(me, self.ways)
        self.row_group = me // self.parts

    def targets(self, turn):
        ways, parts = self.ways, self.parts
        return [
            (s, ((s % ways + turn) % ways) * parts + s // ways) for s in range(self.size)
        ]

    def move(self, values, pairs):
        if all(a == b for a, b in pairs):
            return values
        return lax.ppermute(values, "seq", pairs)

    def gather(self, values):
        rows, local, width = self.rows, values.shape[1], values.shape[2]
        out = jnp.zeros((rows, self.ways, local, width), values.dtype)
        for turn in range(self.ways):
            pick = lax.rem(self.place + turn, self.ways)
            chunk = lax.dynamic_slice_in_dim(values, pick * rows, rows, 0)
            chunk = self.move(chunk, self.targets(turn))
            spot = lax.rem(self.row_group - turn + self.ways, self.ways)
            out = lax.dynamic_update_slice_in_dim(out, chunk[:, None], spot, 1)
        return out.reshape(rows, self.ways * local, width)

    def scatter(self, values):
        rows, width = self.rows, values.shape[2]
        local = values.shape[1] // self.ways
        values = values.reshape(rows, self.ways, local, width)
        out = jnp.zeros((rows * self.ways, local, width), values.dtype)
        for turn in range(self.ways):
            spot = lax.rem(self.row_group - turn + self.ways, self.ways)
            chunk = lax.dynamic_slice_in_dim(values, spot, 1, 1)[:, 0]
            chunk = self.move(chunk, [(b, a) for a, b in self.targets(turn)])
            pick = lax.rem(self.place + turn, self.ways)
            out = lax.dynamic_update_slice_in_dim(out, chunk, pick * rows, 0)
        return out

    def pick_rows(self, values):
        return lax.dynamic_slice_in_dim(values, self.row_group * self.rows, self.rows, 0)

    def groups(self):
        return [
            [r * self.parts + j for j in range(self.parts)] for r in range(self.ways)
        ]

    def to_heads(self, values):
        if self.parts == 1:
            return values
        return lax.all_to_all(
            values, "seq", split_axis=2, concat_axis=1, tiled=True,
            axis_index_groups=self.groups(),
        )

    def from_heads(self, values):
        if self.parts == 1:
            return values
        return lax.all_to_all(
            values, "seq", split_axis=1, concat_axis=2, tiled=True,
            axis_index_groups=self.groups(),
        )


def shards(
    tokens_in,
    segment_ids,
    random_blocks,
    global_blocks,
    w_query,
    b_query,
    w_key,
    w_value,
    b_value,
    w_attn_out,
    b_attn_out,
    ln1_gain,
    ln1_bias,
    w_inner,
    b_inner,
    w_outer,
    b_outer,
    ln2_gain,
    ln2_bias,
    out_grad,
):
    row_count, local_len, width = tokens_in.shape
    seq_count = lax.axis_size("seq")
    fsdp_count = lax.axis_size("fsdp")
    tok_count = row_count * local_len
    own = w_query.shape[0]
    per_own = b_inner.shape[0] // own
    regroup = Regroup(row_count)

    vectors = [b_query, b_value, b_attn_out, ln1_gain, ln1_bias, b_outer, ln2_gain, ln2_bias]
    columns = [x[:, None] for x in vectors] + [b_inner.reshape(own, per_own)]
    used = len(vectors) + per_own
    columns.append(jnp.zeros((own, 128 - used), jnp.bfloat16))
    first = jnp.concatenate([w_query, w_key, w_value] + columns, axis=1)
    first = lax.all_gather(first, "fsdp", axis=0, tiled=True)
    qkv_w = first[:, : 3 * width]
    small = first[:, 3 * width : 3 * width + used].astype(jnp.float32).T
    query_b, value_b, out_b, gain_one, bias_one, outer_b, gain_two, bias_two = small[:8]
    inner_b = small[8:].T.reshape(-1)
    second = lax.all_gather(
        jnp.concatenate([w_attn_out, w_inner], axis=1), "fsdp", axis=0, tiled=True
    )
    out_w, inner_w = second[:, :width], second[:, width:]
    outer_w = lax.all_gather(w_outer, "fsdp", axis=0, tiled=True)

    flat_in = regroup.gather(tokens_in).reshape(tok_count, width)
    plan = plan_blocks(
        regroup.pick_rows(segment_ids),
        regroup.pick_rows(random_blocks),
        regroup.pick_rows(global_blocks),
    )

    def split_rows(values):
        return values.reshape(regroup.rows, tok_count // regroup.rows, width)

    qkv_bias = jnp.concatenate([query_b, jnp.zeros_like(query_b), value_b])
    qkv = (jnp.dot(flat_in, qkv_w, preferred_element_type=jnp.float32) + qkv_bias).astype(
        jnp.bfloat16
    )
    qkv, out_grad = lax.optimization_barrier((qkv, out_grad))
    flat_grad = regroup.gather(out_grad).reshape(tok_count, width)
    q, k, v = (
        regroup.to_heads(split_rows(qkv[:, i * width : (i + 1) * width])) for i in range(3)
    )
    att, lse = attention_forward(q, k, v, plan)
    att_flat = regroup.from_heads(att).reshape(tok_count, width)
    attn_branch = jnp.dot(att_flat, out_w, preferred_element_type=jnp.float32) + out_b
    resid_one = flat_in.astype(jnp.float32) + attn_branch
    normed_one, norm_one_pull = jax.vjp(layer_norm, resid_one, gain_one, bias_one)
    normed_low = normed_one.astype(jnp.bfloat16)
    inner_pre = jnp.dot(normed_low, inner_w, preferred_element_type=jnp.float32) + inner_b
    inner_act, gelu_pull = jax.vjp(gelu_tanh, inner_pre)
    inner_low = inner_act.astype(jnp.bfloat16)
    mlp_branch = jnp.dot(inner_low, outer_w, preferred_element_type=jnp.float32) + outer_b
    normed_two, norm_two_pull = jax.vjp(layer_norm, normed_one + mlp_branch, gain_two, bias_two)
    out_tokens = regroup.scatter(split_rows(normed_two.astype(jnp.bfloat16)))

    sums = jnp.stack(
        [
            jnp.sum(resid_one * resid_one),
            jnp.sum(attn_branch * attn_branch),
            jnp.sum(mlp_branch * mlp_branch),
        ]
    )
    sums = jnp.broadcast_to(sums[:, None], (3, 128))
    sums = butterfly_sum(butterfly_sum(sums, "fsdp"), "seq")[:, 0]
    rms_values = jnp.sqrt(sums / (tok_count * width * seq_count * fsdp_count))

    def scattered(values):
        return lax.psum_scatter(values, "fsdp", scatter_dimension=0, tiled=True)

    d_resid_two, d_gain_two, d_bias_two = norm_two_pull(flat_grad.astype(jnp.float32))
    d_mlp = d_resid_two.astype(jnp.bfloat16)
    d_outer_b = jnp.sum(d_mlp.astype(jnp.float32), axis=0)
    outer_part = contract_rows(inner_low, d_mlp).astype(jnp.bfloat16)
    d_mlp, outer_part = lax.optimization_barrier((d_mlp, outer_part))
    d_outer_w = scattered(outer_part)
    (d_pre_full,) = gelu_pull(times_transpose(d_mlp, outer_w))
    d_pre = d_pre_full.astype(jnp.bfloat16)
    d_inner_b = jnp.sum(d_pre.astype(jnp.float32), axis=0)
    d_inner_w = contract_rows(normed_low, d_pre)
    d_normed_one = d_resid_two + times_transpose(d_pre, inner_w)
    d_resid_one, d_gain_one, d_bias_one = norm_one_pull(d_normed_one)
    d_attn = d_resid_one.astype(jnp.bfloat16)
    d_out_b = jnp.sum(d_attn.astype(jnp.float32), axis=0)
    d_out_w = contract_rows(att_flat, d_attn)
    second_part = jnp.concatenate(
        [d_out_w.astype(jnp.bfloat16), d_inner_w.astype(jnp.bfloat16)], axis=1
    )
    d_att = times_transpose(d_attn, out_w).astype(jnp.bfloat16)
    d_att, second_part = lax.optimization_barrier((d_att, second_part))
    d_outer_w, second_part = lax.optimization_barrier((d_outer_w, second_part))
    d_second = scattered(second_part)
    dq, dk, dv = attention_backward(
        q, k, v, att, regroup.to_heads(split_rows(d_att)), lse, plan
    )
    dq, dk, dv = (regroup.from_heads(x).reshape(tok_count, width) for x in (dq, dk, dv))
    d_query_b = jnp.sum(dq.astype(jnp.float32), axis=0)
    d_value_b = jnp.sum(dv.astype(jnp.float32), axis=0)
    grads = [
        d_query_b, d_value_b, d_out_b, d_gain_one, d_bias_one, d_outer_b, d_gain_two, d_bias_two,
    ]
    d_small = jnp.concatenate(
        [jnp.stack(grads), d_inner_b.reshape(width, per_own).T,
         jnp.zeros((128 - used, width), jnp.float32)], axis=0
    ).T
    parts = [contract_rows(flat_in, x) for x in (dq, dk, dv)] + [d_small]
    first_part = jnp.concatenate([x.astype(jnp.bfloat16) for x in parts], axis=1)
    dq, first_part = lax.optimization_barrier((dq, first_part))
    d_second, first_part = lax.optimization_barrier((d_second, first_part))
    d_first = sum_seq(scattered(first_part))
    d_outer_w, d_second = sum_seq(d_outer_w), sum_seq(d_second)
    d_tokens = d_resid_one
    for i, part in enumerate((dq, dk, dv)):
        d_tokens = d_tokens + times_transpose(part, qkv_w[:, i * width : (i + 1) * width])
    d_tokens_in = regroup.scatter(split_rows(d_tokens.astype(jnp.bfloat16)))
    d_cols = d_first[:, 3 * width :].T
    d_vec = [d_cols[i] for i in range(len(vectors))]
    return (
        out_tokens,
        d_tokens_in,
        d_first[:, :width],
        d_vec[0],
        d_first[:, width : 2 * width],
        d_first[:, 2 * width : 3 * width],
        d_vec[1],
        d_second[:, :width],
        d_vec[2],
        d_vec[3],
        d_vec[4],
        d_second[:, width:],
        d_cols[len(vectors) : used].T.reshape(-1),
        d_outer_w,
        d_vec[5],
        d_vec[6],
        d_vec[7],
        rms_values,
    )


def solution(mesh):
    in_specs = (
        P("fsdp", "seq", None),
        P("fsdp", None),
        P("fsdp", None, None),
        P("fsdp", None),
        P("fsdp", None),
        P("fsdp"),
        P("fsdp", None),
        P("fsdp", None),
        P("fsdp"),
        P("fsdp", None),
        P("fsdp"),
        P("fsdp"),
        P("fsdp"),
        P("fsdp", None),
        P("fsdp"),
        P("fsdp", None),
        P("fsdp"),
        P("fsdp"),
        P("fsdp"),
        P("fsdp", "seq", None),
    )
    out_specs = (
        P("fsdp", "seq", None),
        P("fsdp", "seq", None),
        P("fsdp", None),
        P("fsdp"),
        P("fsdp", None),
        P("fsdp", None),
        P("fsdp"),
        P("fsdp", None),
        P("fsdp"),
        P("fsdp"),
        P("fsdp"),
        P("fsdp", None),
        P("fsdp"),
        P("fsdp", None),
        P("fsdp"),
        P("fsdp"),
        P("fsdp"),
        P(),
    )
    return jax.shard_map(shards, mesh=mesh, in_specs=in_specs, out_specs=out_specs, check_vma=False)
```

```python
import functools
import math

import jax
import jax.numpy as jnp
from jax import lax
from jax.experimental import pallas as pl
from jax.experimental.pallas import tpu as pltpu
from jax.sharding import PartitionSpec as P

HD = 64
BLK = 64
CHUNK = 4
NEG = -1e30


def plan_blocks(seg, rand, glob):
    rows, full_len = seg.shape
    nb = full_len // BLK
    ids = jnp.arange(nb, dtype=jnp.int32)
    is_global = jnp.any(ids[None, :, None] == glob[:, None, :], axis=-1)
    picked = jnp.any(rand[:, :, None, :] == ids[None, None, :, None], axis=-1)
    nearby = jnp.abs(ids[:, None] - ids[None, :]) <= 1
    admitted = nearby[None] | picked | is_global[:, :, None] | is_global[:, None, :]
    by_block = seg.reshape(rows, nb, BLK)
    low, high = by_block[:, :, 0], by_block[:, :, BLK - 1]
    meets = (low[:, :, None] <= high[:, None, :]) & (low[:, None, :] <= high[:, :, None])
    active = (admitted & meets).astype(jnp.int32)
    upto = (ids[:, None] <= ids[None, :]).astype(jnp.int32)
    place = jnp.sum(active[:, :, :, None] * upto[None, None], axis=2) - 1
    count = jnp.sum(active, axis=2)
    hit = (place[:, :, :, None] == ids[None, None, None, :]) & (active[:, :, :, None] > 0)
    listed = jnp.sum(jnp.where(hit, ids[None, None, :, None], 0), axis=2)
    listed = jnp.where(ids[None, None, :] < count[:, :, None], listed, nb)
    chunks = (count + (CHUNK - 1)) // CHUNK
    seg_cols = jnp.concatenate([seg, jnp.full((rows, BLK), -1, jnp.int32)], axis=1)
    seg_cols = jnp.broadcast_to(seg_cols[:, :, None], (rows, full_len + BLK, 128))
    seg_rows = jnp.concatenate([by_block, by_block], axis=2)[:, :, None, :]
    return chunks, listed.reshape(rows, nb * nb), seg_cols, seg_rows


def lane_low(rows):
    return lax.broadcasted_iota(jnp.int32, (rows, 128), 1) < HD


def diag128(dup_t):
    row = lax.broadcasted_iota(jnp.int32, (128, 128), 0) < HD
    col = lax.broadcasted_iota(jnp.int32, (128, 128), 1) < HD
    return jnp.where(row == col, dup_t, jnp.zeros_like(dup_t))


def transposed_twice(tile):
    both = jnp.concatenate([tile, tile], axis=0)
    return both.T


def head_rows(acc):
    turned = jnp.concatenate([acc, acc], axis=0).T
    return jnp.where(lane_low(HD), turned[:HD], turned[HD:])


def pick_diag(full, half):
    lanes = slice(half * 128, half * 128 + 128)
    top = full[half * 128 : half * 128 + HD, lanes]
    low = full[half * 128 + HD : half * 128 + 128, lanes]
    return jnp.where(lane_low(HD), top, low)


def chunk_ids(list_ref, row, base, nb):
    ids = [list_ref[row, base + j] for j in range(CHUNK)]
    safe = [jnp.where(b == nb, 0, b) for b in ids]
    return ids, safe


def block_rows(ref, blocks, lanes):
    return jnp.concatenate(
        [ref[0, pl.ds(pl.multiple_of(b * BLK, BLK), BLK), lanes] for b in blocks], axis=0
    )


def turned_blocks(ref, blocks, rows):
    low = lane_low(rows.stop - rows.start)
    tiles = [ref[b, rows, :] for b in blocks]
    return jnp.concatenate(
        [jnp.where(low, tiles[i], tiles[i + 1]) for i in range(0, CHUNK, 2)], axis=1
    )


def turn_all(src_ref, dst_ref, nb, width):
    def body(b, _):
        start = pl.multiple_of(b * BLK, BLK)
        for t in range(width // 128):
            tile = src_ref[0, pl.ds(start, BLK), t * 128 : t * 128 + 128]
            dst_ref[b, t * 128 : t * 128 + 128, :] = transposed_twice(tile)
        return 0

    lax.fori_loop(0, nb, body, 0)


def dot_f32(left, right):
    return lax.dot_general(
        left, right, (((1,), (0,)), ((), ())), preferred_element_type=jnp.float32
    )


def forward_kernel(group, n_ref, list_ref, q_ref, k_ref, v_ref, segc_ref, segr_ref,
                   o_ref, lse_ref, vt_ref, qst_ref, m_ref, l_ref, acc_ref):
    row = pl.program_id(0)
    width = q_ref.shape[2]
    nb = q_ref.shape[1] // BLK
    groups, halves = width // group, group // 128
    turn_all(v_ref, vt_ref, nb, width)
    qst_ref[...] = jnp.zeros_like(qst_ref)

    def per_query(a, _):
        start = pl.multiple_of(a * BLK, BLK)
        for t in range(width // 128):
            tile = q_ref[0, pl.ds(start, BLK), t * 128 : t * 128 + 128] * 0.125
            g, u = t // halves, t % halves
            qst_ref[g, u * 128 : u * 128 + 128, u * 128 : u * 128 + 128] = diag128(
                transposed_twice(tile.astype(jnp.bfloat16))
            )
        seg_q = segr_ref[0, a]
        m_ref[...] = jnp.full_like(m_ref, NEG)
        l_ref[...] = jnp.zeros_like(l_ref)
        acc_ref[...] = jnp.zeros_like(acc_ref)

        def per_chunk(c, _):
            ids, safe = chunk_ids(list_ref, row, a * nb + c * CHUNK, nb)
            seg_k = block_rows(segc_ref, ids, slice(0, 128))
            allowed = seg_k == seg_q
            for g in range(groups):
                lanes = slice(g * group, g * group + group)
                s_t = dot_f32(block_rows(k_ref, safe, lanes), qst_ref[g])
                weights, alphas = [], []
                for u in range(halves):
                    t = g * halves + u
                    s = jnp.where(allowed, s_t[:, u * 128 : u * 128 + 128], NEG)
                    m_old = m_ref[t]
                    m_new = jnp.maximum(m_old, jnp.max(s, axis=0, keepdims=True))
                    p = jnp.exp(s - m_new)
                    alpha = jnp.exp(m_old - m_new)
                    l_ref[t] = alpha * l_ref[t] + jnp.sum(p, axis=0, keepdims=True)
                    m_ref[t] = m_new
                    weights.append(p.astype(jnp.bfloat16))
                    alphas.append(alpha)
                p_t = jnp.concatenate(weights, axis=1) if halves > 1 else weights[0]
                o_t = dot_f32(turned_blocks(vt_ref, safe, lanes), p_t)
                for u in range(halves):
                    t = g * halves + u
                    acc_ref[t] = alphas[u] * acc_ref[t] + pick_diag(o_t, u)
            return 0

        lax.fori_loop(0, n_ref[row, a], per_chunk, 0)
        for t in range(width // 128):
            total = l_ref[t]
            out = acc_ref[t] / total
            o_ref[0, pl.ds(start, BLK), t * 128 : t * 128 + 128] = head_rows(out).astype(
                jnp.bfloat16
            )
            lse_ref[0, a, :, t * 128 : t * 128 + 128] = m_ref[t] + jnp.log(total)
        return 0

    lax.fori_loop(0, nb, per_query, 0)


def group_of(width):
    return 256 if width % 256 == 0 else 128


def whole_spec(shape):
    rest = (0,) * (len(shape) - 1)
    return pl.BlockSpec((1,) + tuple(shape[1:]), lambda r, *_: (r,) + rest)


def one_spec(shape):
    rest = (0,) * (len(shape) - 1)
    return pl.BlockSpec((1,) + tuple(shape[1:]), lambda r, *_: (r,) + rest,
                        pipeline_mode=pl.Buffered(1))


def attention_forward(q, k, v, plan):
    chunks, listed, seg_cols, seg_rows = plan
    rows, full_len, width = q.shape
    nb, group = full_len // BLK, group_of(width)
    tiles = width // 128
    pairs = rows * full_len * full_len // 4 * width
    args = (q, k, v, seg_cols, seg_rows)
    return pl.pallas_call(
        functools.partial(forward_kernel, group),
        out_shape=(
            jax.ShapeDtypeStruct((rows, full_len, width), jnp.bfloat16),
            jax.ShapeDtypeStruct((rows, nb, 1, width), jnp.float32),
        ),
        grid_spec=pltpu.PrefetchScalarGridSpec(
            num_scalar_prefetch=2,
            grid=(rows,),
            in_specs=[one_spec(x.shape) for x in args],
            out_specs=(one_spec((rows, full_len, width)), one_spec((rows, nb, 1, width))),
            scratch_shapes=[
                pltpu.VMEM((nb, width, 128), jnp.bfloat16),
                pltpu.VMEM((width // group, group, group), jnp.bfloat16),
                pltpu.VMEM((tiles, 1, 128), jnp.float32),
                pltpu.VMEM((tiles, 1, 128), jnp.float32),
                pltpu.VMEM((tiles, HD, 128), jnp.float32),
            ],
        ),
        compiler_params=pltpu.CompilerParams(vmem_limit_bytes=48 << 20),
        cost_estimate=pl.CostEstimate(
            flops=64 * pairs, transcendentals=pairs // HD, bytes_accessed=8 * q.size
        ),
        name="attention_forward",
    )(chunks, listed, *args)


def backward_kernel(group, n_ref, list_ref, q_ref, k_ref, v_ref, o_ref, do_ref, lse_ref,
                    segc_ref, segr_ref, dq_ref, dk_ref, dv_ref,
                    kt_ref, qst_ref, qs_ref, dost_ref, dos_ref, delta_ref, acc_ref,
                    dk_acc, dv_acc):
    row = pl.program_id(0)
    full_len, width = q_ref.shape[1], q_ref.shape[2]
    nb = full_len // BLK
    groups, halves = width // group, group // 128
    turn_all(k_ref, kt_ref, nb, width)
    for ref in (qst_ref, qs_ref, dost_ref, dos_ref, dk_acc, dv_acc):
        ref[...] = jnp.zeros_like(ref)
    low = lane_low(HD)

    def per_query(a, _):
        start = pl.multiple_of(a * BLK, BLK)
        for t in range(width // 128):
            g, u = t // halves, t % halves
            lanes = slice(t * 128, t * 128 + 128)
            square = slice(u * 128, u * 128 + 128)
            q_tile = (q_ref[0, pl.ds(start, BLK), lanes] * 0.125).astype(jnp.bfloat16)
            g_tile = do_ref[0, pl.ds(start, BLK), lanes]
            o_tile = o_ref[0, pl.ds(start, BLK), lanes]
            g_turn = transposed_twice(g_tile)
            qst_ref[g, square, square] = diag128(transposed_twice(q_tile))
            dost_ref[g, square, square] = diag128(g_turn)
            qs_ref[g, square, square] = diag128(jnp.concatenate([q_tile, q_tile], axis=0))
            dos_ref[g, square, square] = diag128(jnp.concatenate([g_tile, g_tile], axis=0))
            product = g_turn.astype(jnp.float32) * transposed_twice(o_tile).astype(jnp.float32)
            delta_ref[t] = jnp.where(
                low[:1],
                jnp.sum(product[:HD], axis=0, keepdims=True),
                jnp.sum(product[HD:], axis=0, keepdims=True),
            )
        seg_q = segr_ref[0, a]
        acc_ref[...] = jnp.zeros_like(acc_ref)

        def per_chunk(c, _):
            ids, safe = chunk_ids(list_ref, row, a * nb + c * CHUNK, nb)
            seg_k = block_rows(segc_ref, ids, slice(0, 128))
            allowed = seg_k == seg_q
            for g in range(groups):
                lanes = slice(g * group, g * group + group)
                s_t = dot_f32(block_rows(k_ref, safe, lanes), qst_ref[g])
                dp_t = dot_f32(block_rows(v_ref, safe, lanes), dost_ref[g])
                p_parts, ds_parts = [], []
                for u in range(halves):
                    t = g * halves + u
                    half = slice(u * 128, u * 128 + 128)
                    lse = lse_ref[0, a, :, t * 128 : t * 128 + 128]
                    p = jnp.exp(jnp.where(allowed, s_t[:, half], NEG) - lse)
                    ds = p * (dp_t[:, half] - delta_ref[t])
                    p_parts.append(p.astype(jnp.bfloat16))
                    ds_parts.append(ds.astype(jnp.bfloat16))
                p_t = jnp.concatenate(p_parts, axis=1) if halves > 1 else p_parts[0]
                ds_t = jnp.concatenate(ds_parts, axis=1) if halves > 1 else ds_parts[0]
                dv = dot_f32(p_t, dos_ref[g])
                dk = dot_f32(ds_t, qs_ref[g])
                dq_t = dot_f32(turned_blocks(kt_ref, safe, lanes), ds_t)
                for j in range(CHUNK):
                    where = pl.ds(pl.multiple_of(safe[j] * BLK, BLK), BLK)
                    part = slice(j * BLK, j * BLK + BLK)
                    dv_acc[where, lanes] += dv[part]
                    dk_acc[where, lanes] += dk[part]
                for u in range(halves):
                    acc_ref[g * halves + u] += pick_diag(dq_t, u)
            return 0

        lax.fori_loop(0, n_ref[row, a], per_chunk, 0)
        for t in range(width // 128):
            dq_ref[0, pl.ds(start, BLK), t * 128 : t * 128 + 128] = (
                head_rows(acc_ref[t]) * 0.125
            ).astype(jnp.bfloat16)
        return 0

    lax.fori_loop(0, nb, per_query, 0)

    def flush(a, _):
        where = pl.ds(pl.multiple_of(a * BLK, BLK), BLK)
        dk_ref[0, where, :] = dk_acc[where, :].astype(jnp.bfloat16)
        dv_ref[0, where, :] = dv_acc[where, :].astype(jnp.bfloat16)
        return 0

    lax.fori_loop(0, nb, flush, 0)


def attention_backward(q, k, v, o, do, lse, plan):
    chunks, listed, seg_cols, seg_rows = plan
    rows, full_len, width = q.shape
    nb, group = full_len // BLK, group_of(width)
    tiles, groups = width // 128, width // group
    pairs = rows * full_len * full_len // 4 * width
    args = (q, k, v, o, do, lse, seg_cols, seg_rows)
    like = jax.ShapeDtypeStruct((rows, full_len, width), jnp.bfloat16)
    square = pltpu.VMEM((groups, group, group), jnp.bfloat16)
    return pl.pallas_call(
        functools.partial(backward_kernel, group),
        out_shape=(like, like, like),
        grid_spec=pltpu.PrefetchScalarGridSpec(
            num_scalar_prefetch=2,
            grid=(rows,),
            in_specs=[one_spec(x.shape) for x in args],
            out_specs=tuple(one_spec(like.shape) for _ in range(3)),
            scratch_shapes=[
                pltpu.VMEM((nb, width, 128), jnp.bfloat16),
                square, square, square, square,
                pltpu.VMEM((tiles, 1, 128), jnp.float32),
                pltpu.VMEM((tiles, HD, 128), jnp.float32),
                pltpu.VMEM((full_len, width), jnp.float32),
                pltpu.VMEM((full_len, width), jnp.float32),
            ],
        ),
        compiler_params=pltpu.CompilerParams(vmem_limit_bytes=58 << 20),
        cost_estimate=pl.CostEstimate(
            flops=100 * pairs, transcendentals=pairs // HD, bytes_accessed=16 * q.size
        ),
        name="attention_backward",
    )(chunks, listed, *args)


def pair_bit(index, bit):
    return lax.rem(index // (1 << bit), 2)


def pair_of(index, bit):
    return index + (1 - 2 * pair_bit(index, bit)) * (1 << bit)


def all_arrived(bits):
    me = lax.axis_index("fsdp")
    barrier = pltpu.get_barrier_semaphore()
    for bit in range(bits):
        pl.semaphore_signal(
            barrier, inc=1, device_id={"fsdp": pair_of(me, bit)},
            device_id_type=pl.DeviceIdType.MESH,
        )
    pl.semaphore_signal(
        barrier, inc=1, device_id={"seq": 1 - lax.axis_index("seq")},
        device_id_type=pl.DeviceIdType.MESH,
    )
    pl.semaphore_wait(barrier, bits + 1)


def qkv_backward_kernel(
    bits, xt_in, dq_in, dk_in, dv_in, wt_in, res_in, small_in,
    wq_out, wk_out, wv_out, small_out, tok_out,
    xt, grads, wt, res, tok, kept, sends, lands, final, small, small_land, result,
    in_sem, tok_send, tok_land, own_sem, send_sem, land_sem, x_send, x_land,
    small_send, small_recv, out_sem,
):
    me, side = lax.axis_index("fsdp"), lax.axis_index("seq")
    half = tok.shape[2] * tok.shape[1]
    piece, pieces = tok.shape[2], tok.shape[1]
    own, width = wq_out.shape
    owners = 1 << bits
    sources = (dq_in, dk_in, dv_in)
    loads = [
        pltpu.make_async_copy(wt_in, wt, in_sem.at[0]),
        pltpu.make_async_copy(res_in, res, in_sem.at[1]),
        pltpu.make_async_copy(small_in, small.at[0], in_sem.at[2]),
        pltpu.make_async_copy(xt_in, xt, in_sem.at[3]),
    ] + [pltpu.make_async_copy(sources[i], grads.at[i], in_sem.at[4 + i]) for i in range(3)]
    for i in (4, 5, 6, 0, 1, 3, 2):
        loads[i].start()
    all_arrived(bits)
    for i in (4, 5, 6, 0, 1):
        loads[i].wait()

    def token_rows(start):
        total = res[pl.ds(start, piece), :]
        for i in range(3):
            total = total + dot_f32(
                grads[i, pl.ds(start, piece), :], wt[i * width : (i + 1) * width, :]
            )
        return total.astype(jnp.bfloat16)

    def sent(i):
        return pltpu.make_async_remote_copy(
            src_ref=tok.at[0, i],
            dst_ref=tok_out.at[side, pl.ds(pl.multiple_of(i * piece, piece), piece)],
            send_sem=tok_send.at[i], recv_sem=tok_land.at[i],
            device_id={"seq": 1 - side}, device_id_type=pl.DeviceIdType.MESH,
        )

    def landed(i):
        return pltpu.make_async_remote_copy(
            src_ref=tok.at[0, i],
            dst_ref=tok_out.at[1 - side, pl.ds(pl.multiple_of(i * piece, piece), piece)],
            send_sem=tok_send.at[i], recv_sem=tok_land.at[i],
            device_id={"seq": 1 - side}, device_id_type=pl.DeviceIdType.MESH,
        )

    def stays(i):
        return pltpu.make_async_copy(
            tok.at[1, i],
            tok_out.at[side, pl.ds(pl.multiple_of(i * piece, piece), piece)],
            own_sem.at[i],
        )

    def send_piece(i, _):
        start = pl.multiple_of((1 - side) * half + i * piece, piece)
        tok[0, i] = token_rows(start)
        sent(i).start()
        return 0

    lax.fori_loop(0, pieces, send_piece, 0)

    def keep_piece(i, _):
        start = pl.multiple_of(side * half + i * piece, piece)
        tok[1, i] = token_rows(start)
        stays(i).start()
        return 0

    low_bit = pair_bit(me, 0) == 0
    tile = 8 if owners % 8 == 0 else owners
    first_of = [0]
    for bit in range(bits):
        first_of.append(first_of[-1] + (owners >> (bit + 1)))

    def weights(i):
        def rows(m, _):
            block = dot_f32(
                xt[pl.ds(pl.multiple_of(m * tile * own, tile * own), tile * own), :], grads[i]
            ).reshape(tile // 2, 2, own, width)
            even, odd = block[:, 0], block[:, 1]
            spot = pl.ds(m * (tile // 2), tile // 2)
            kept[i, spot] = jnp.where(low_bit, even, odd)
            sends[i, spot] = jnp.where(low_bit, odd, even).astype(jnp.bfloat16)
            return 0

        lax.fori_loop(0, owners // tile, rows, 0)

    def hop(i, bit):
        count = owners >> (bit + 1)
        spot = pl.ds(first_of[bit], count)
        return pltpu.make_async_remote_copy(
            src_ref=sends.at[i, spot], dst_ref=lands.at[i, spot],
            send_sem=send_sem.at[i, bit], recv_sem=land_sem.at[i, bit],
            device_id={"fsdp": pair_of(me, bit)}, device_id_type=pl.DeviceIdType.MESH,
        )

    def cross(i):
        return pltpu.make_async_remote_copy(
            src_ref=final.at[0, i], dst_ref=final.at[1, i],
            send_sem=x_send.at[i], recv_sem=x_land.at[i],
            device_id={"seq": 1 - side}, device_id_type=pl.DeviceIdType.MESH,
        )

    def advance(i, bit):
        hop(i, bit).wait_recv()
        base = first_of[bit]
        if bit + 1 == bits:
            total = kept[i, base] + lands[i, base].astype(jnp.float32)
            final[0, i] = total.astype(jnp.bfloat16)
            cross(i).start()
            return
        nxt = pair_bit(me, bit + 1)

        def one(j, _):
            stay, go = 2 * j + nxt, 2 * j + 1 - nxt
            kept[i, first_of[bit + 1] + j] = kept[i, base + stay] + lands[
                i, base + stay
            ].astype(jnp.float32)
            sends[i, first_of[bit + 1] + j] = (
                kept[i, base + go] + lands[i, base + go].astype(jnp.float32)
            ).astype(jnp.bfloat16)
            return 0

        lax.fori_loop(0, owners >> (bit + 2), one, 0)
        hop(i, bit + 1).start()

    outs = (wq_out, wk_out, wv_out)

    def written(i):
        return pltpu.make_async_copy(result.at[i], outs[i], out_sem.at[i])

    def finish(i):
        cross(i).wait_recv()
        result[i] = final[0, i].astype(jnp.float32) + final[1, i].astype(jnp.float32)
        written(i).start()

    def small_hop(bit):
        where = {"fsdp": pair_of(me, bit)} if bit < bits else {"seq": 1 - side}
        return pltpu.make_async_remote_copy(
            src_ref=small.at[bit], dst_ref=small_land.at[bit],
            send_sem=small_send.at[bit], recv_sem=small_recv.at[bit],
            device_id=where, device_id_type=pl.DeviceIdType.MESH,
        )

    def small_advance(bit):
        small_hop(bit).wait_recv()
        small[bit + 1] = small[bit] + small_land[bit]
        if bit < bits:
            small_hop(bit + 1).start()

    loads[3].wait()
    loads[2].wait()
    weights(0)
    hop(0, 0).start()
    for spot, i in ((0, 0), (1, 2)):
        def column_sums(c, total):
            block = grads[i, pl.ds(pl.multiple_of(c * 128, 128), 128), :].astype(jnp.float32)
            return total + jnp.sum(block.reshape(16, 8, width), axis=0)

        total = lax.fori_loop(
            0, grads.shape[1] // 128, column_sums, jnp.zeros((8, width), jnp.float32)
        )
        small[0, spot : spot + 1] = jnp.sum(total, axis=0, keepdims=True)
    small_hop(0).start()
    weights(1)
    hop(1, 0).start()
    advance(0, 0)
    small_advance(0)
    weights(2)
    hop(2, 0).start()
    plan = []
    for step in range(1, bits + 2):
        todo = []
        for i in range(3):
            bit = step - i
            if 0 <= bit < bits:
                todo.append((i, bit))
        plan.append((todo, step))
    done = 0
    for todo, step in plan:
        for i, bit in todo:
            advance(i, bit)
        if step <= bits:
            small_advance(step)
        if done < pieces:
            keep_piece(done, 0)
            done += 1
    for i in range(3):
        finish(i)
    small_copy = pltpu.make_async_copy(small.at[bits + 1], small_out, out_sem.at[3])
    small_copy.start()
    while done < pieces:
        keep_piece(done, 0)
        done += 1
    for i in range(3):
        written(i).wait()
        cross(i).wait_send()
        for bit in range(bits):
            hop(i, bit).wait_send()
    for bit in range(bits + 1):
        small_hop(bit).wait_send()
    small_copy.wait()
    for i in range(pieces):
        stays(i).wait()
        sent(i).wait_send()
        landed(i).wait_recv()


def qkv_backward(xt, dq, dk, dv, wt, resid, small, own):
    tokens, width = dq.shape
    bits = lax.axis_size("fsdp").bit_length() - 1
    owners = 1 << bits
    pieces = 4
    piece = tokens // 2 // pieces
    dma = pltpu.SemaphoreType.DMA
    f32, bf16 = jnp.float32, jnp.bfloat16
    shard = jax.ShapeDtypeStruct((own, width), f32)
    anywhere = pl.BlockSpec(memory_space=pl.ANY)
    return pl.pallas_call(
        functools.partial(qkv_backward_kernel, bits),
        out_shape=(
            shard, shard, shard,
            jax.ShapeDtypeStruct(small.shape, f32),
            jax.ShapeDtypeStruct((2, tokens // 2, width), bf16),
        ),
        in_specs=[anywhere] * 7,
        out_specs=(anywhere,) * 5,
        scratch_shapes=[
            pltpu.VMEM(xt.shape, bf16),
            pltpu.VMEM((3, tokens, width), bf16),
            pltpu.VMEM(wt.shape, bf16),
            pltpu.VMEM((tokens, width), f32),
            pltpu.VMEM((2, pieces, piece, width), bf16),
            pltpu.VMEM((3, owners - 1, own, width), f32),
            pltpu.VMEM((3, owners - 1, own, width), bf16),
            pltpu.VMEM((3, owners - 1, own, width), bf16),
            pltpu.VMEM((2, 3, own, width), bf16),
            pltpu.VMEM((bits + 2,) + small.shape, f32),
            pltpu.VMEM((bits + 1,) + small.shape, f32),
            pltpu.VMEM((3, own, width), f32),
            dma((7,)), dma((pieces,)), dma((pieces,)), dma((pieces,)),
            dma((3, bits)), dma((3, bits)), dma((3,)), dma((3,)),
            dma((bits + 1,)), dma((bits + 1,)), dma((4,)),
        ],
        compiler_params=pltpu.CompilerParams(
            collective_id=1, has_side_effects=True, vmem_limit_bytes=60 << 20
        ),
        cost_estimate=pl.CostEstimate(
            flops=40 * tokens * width * width, transcendentals=0,
            bytes_accessed=16 * tokens * width,
        ),
        name="qkv_backward",
    )(xt, dq, dk, dv, wt, resid, small)


eps_norm = 1e-06


def layer_norm(hidden, gain_vec, shift_vec):
    mean_val = jnp.mean(hidden, axis=-1, keepdims=True)
    centred = hidden - mean_val
    var_val = jnp.mean(centred * centred, axis=-1, keepdims=True)
    return centred * lax.rsqrt(var_val + eps_norm) * gain_vec + shift_vec


def gelu_tanh(values):
    return jax.nn.gelu(values, approximate=True)


def contract_rows(left, right):
    return lax.dot_general(
        left, right, (((0,), (0,)), ((), ())), preferred_element_type=jnp.float32
    )


def times_transpose(left, right):
    return lax.dot_general(
        left, right, (((1,), (1,)), ((), ())), preferred_element_type=jnp.float32
    )


def butterfly_sum(values, axis):
    size = lax.axis_size(axis)
    if size & (size - 1):
        return lax.psum(values, axis)
    step = 1
    while step < size:
        pairs = [(i, i ^ step) for i in range(size)]
        values = values + lax.ppermute(values, axis, pairs)
        step *= 2
    return values


def sum_seq(values):
    if lax.axis_size("seq") == 2:
        other = lax.ppermute(values, "seq", [(0, 1), (1, 0)])
        return values.astype(jnp.float32) + other.astype(jnp.float32)
    return lax.psum(values, "seq").astype(jnp.float32)


class Regroup:
    def __init__(self, row_count):
        self.size = lax.axis_size("seq")
        self.ways = math.gcd(row_count, self.size)
        self.parts = self.size // self.ways
        self.rows = row_count // self.ways
        me = lax.axis_index("seq")
        self.place = lax.rem(me, self.ways)
        self.row_group = me // self.parts

    def targets(self, turn):
        ways, parts = self.ways, self.parts
        return [
            (s, ((s % ways + turn) % ways) * parts + s // ways) for s in range(self.size)
        ]

    def move(self, values, pairs):
        if all(a == b for a, b in pairs):
            return values
        return lax.ppermute(values, "seq", pairs)

    def gather(self, values):
        rows, local, width = self.rows, values.shape[1], values.shape[2]
        out = jnp.zeros((rows, self.ways, local, width), values.dtype)
        for turn in range(self.ways):
            pick = lax.rem(self.place + turn, self.ways)
            chunk = lax.dynamic_slice_in_dim(values, pick * rows, rows, 0)
            chunk = self.move(chunk, self.targets(turn))
            spot = lax.rem(self.row_group - turn + self.ways, self.ways)
            out = lax.dynamic_update_slice_in_dim(out, chunk[:, None], spot, 1)
        return out.reshape(rows, self.ways * local, width)

    def scatter(self, values):
        rows, width = self.rows, values.shape[2]
        local = values.shape[1] // self.ways
        values = values.reshape(rows, self.ways, local, width)
        out = jnp.zeros((rows * self.ways, local, width), values.dtype)
        for turn in range(self.ways):
            spot = lax.rem(self.row_group - turn + self.ways, self.ways)
            chunk = lax.dynamic_slice_in_dim(values, spot, 1, 1)[:, 0]
            chunk = self.move(chunk, [(b, a) for a, b in self.targets(turn)])
            pick = lax.rem(self.place + turn, self.ways)
            out = lax.dynamic_update_slice_in_dim(out, chunk, pick * rows, 0)
        return out

    def pick_rows(self, values):
        return lax.dynamic_slice_in_dim(values, self.row_group * self.rows, self.rows, 0)

    def groups(self):
        return [
            [r * self.parts + j for j in range(self.parts)] for r in range(self.ways)
        ]

    def to_heads(self, values):
        if self.parts == 1:
            return values
        return lax.all_to_all(
            values, "seq", split_axis=2, concat_axis=1, tiled=True,
            axis_index_groups=self.groups(),
        )

    def from_heads(self, values):
        if self.parts == 1:
            return values
        return lax.all_to_all(
            values, "seq", split_axis=1, concat_axis=2, tiled=True,
            axis_index_groups=self.groups(),
        )


def shards(
    tokens_in,
    segment_ids,
    random_blocks,
    global_blocks,
    w_query,
    b_query,
    w_key,
    w_value,
    b_value,
    w_attn_out,
    b_attn_out,
    ln1_gain,
    ln1_bias,
    w_inner,
    b_inner,
    w_outer,
    b_outer,
    ln2_gain,
    ln2_bias,
    out_grad,
):
    row_count, local_len, width = tokens_in.shape
    seq_count = lax.axis_size("seq")
    fsdp_count = lax.axis_size("fsdp")
    tok_count = row_count * local_len
    own = w_query.shape[0]
    per_own = b_inner.shape[0] // own
    regroup = Regroup(row_count)
    paired = row_count == 2 and seq_count == 2 and fsdp_count & (fsdp_count - 1) == 0

    vectors = [b_query, b_value, b_attn_out, ln1_gain, ln1_bias, b_outer, ln2_gain, ln2_bias]
    columns = [x[:, None] for x in vectors] + [b_inner.reshape(own, per_own)]
    used = len(vectors) + per_own
    columns.append(jnp.zeros((own, 128 - used), jnp.bfloat16))
    first = jnp.concatenate([w_query, w_key, w_value] + columns, axis=1)
    first = lax.all_gather(first, "fsdp", axis=0, tiled=True)
    qkv_w = first[:, : 3 * width]
    small = first[:, 3 * width : 3 * width + used].astype(jnp.float32).T
    query_b, value_b, out_b, gain_one, bias_one, outer_b, gain_two, bias_two = small[:8]
    inner_b = small[8:].T.reshape(-1)
    second = lax.all_gather(
        jnp.concatenate([w_attn_out, w_inner], axis=1), "fsdp", axis=0, tiled=True
    )
    out_w, inner_w = second[:, :width], second[:, width:]
    outer_w = lax.all_gather(w_outer, "fsdp", axis=0, tiled=True)

    flat_in = regroup.gather(tokens_in).reshape(tok_count, width)
    plan = plan_blocks(
        regroup.pick_rows(segment_ids),
        regroup.pick_rows(random_blocks),
        regroup.pick_rows(global_blocks),
    )

    def split_rows(values):
        return values.reshape(regroup.rows, tok_count // regroup.rows, width)

    qkv_bias = jnp.concatenate([query_b, jnp.zeros_like(query_b), value_b])
    qkv = (jnp.dot(flat_in, qkv_w, preferred_element_type=jnp.float32) + qkv_bias).astype(
        jnp.bfloat16
    )
    qkv, out_grad = lax.optimization_barrier((qkv, out_grad))
    flat_grad = regroup.gather(out_grad).reshape(tok_count, width)
    q, k, v = (
        regroup.to_heads(split_rows(qkv[:, i * width : (i + 1) * width])) for i in range(3)
    )
    att, lse = attention_forward(q, k, v, plan)
    att_flat = regroup.from_heads(att).reshape(tok_count, width)
    attn_branch = jnp.dot(att_flat, out_w, preferred_element_type=jnp.float32) + out_b
    resid_one = flat_in.astype(jnp.float32) + attn_branch
    normed_one, norm_one_pull = jax.vjp(layer_norm, resid_one, gain_one, bias_one)
    normed_low = normed_one.astype(jnp.bfloat16)
    inner_pre = jnp.dot(normed_low, inner_w, preferred_element_type=jnp.float32) + inner_b
    inner_act, gelu_pull = jax.vjp(gelu_tanh, inner_pre)
    inner_low = inner_act.astype(jnp.bfloat16)
    mlp_branch = jnp.dot(inner_low, outer_w, preferred_element_type=jnp.float32) + outer_b
    normed_two, norm_two_pull = jax.vjp(layer_norm, normed_one + mlp_branch, gain_two, bias_two)
    out_tokens = regroup.scatter(split_rows(normed_two.astype(jnp.bfloat16)))

    sums = jnp.stack(
        [
            jnp.sum(resid_one * resid_one),
            jnp.sum(attn_branch * attn_branch),
            jnp.sum(mlp_branch * mlp_branch),
        ]
    )
    def scattered(values):
        return lax.psum_scatter(values, "fsdp", scatter_dimension=0, tiled=True)

    d_resid_two, d_gain_two, d_bias_two = norm_two_pull(flat_grad.astype(jnp.float32))
    d_mlp = d_resid_two.astype(jnp.bfloat16)
    d_outer_b = jnp.sum(d_mlp.astype(jnp.float32), axis=0)
    outer_part = contract_rows(inner_low, d_mlp).astype(jnp.bfloat16)
    d_mlp, outer_part = lax.optimization_barrier((d_mlp, outer_part))
    d_outer_w = scattered(outer_part)
    (d_pre_full,) = gelu_pull(times_transpose(d_mlp, outer_w))
    d_pre = d_pre_full.astype(jnp.bfloat16)
    d_inner_b = jnp.sum(d_pre.astype(jnp.float32), axis=0)
    d_inner_w = contract_rows(normed_low, d_pre)
    d_normed_one = d_resid_two + times_transpose(d_pre, inner_w)
    d_resid_one, d_gain_one, d_bias_one = norm_one_pull(d_normed_one)
    d_attn = d_resid_one.astype(jnp.bfloat16)
    d_out_b = jnp.sum(d_attn.astype(jnp.float32), axis=0)
    d_out_w = contract_rows(att_flat, d_attn)
    second_part = jnp.concatenate(
        [d_out_w.astype(jnp.bfloat16), d_inner_w.astype(jnp.bfloat16)], axis=1
    )
    d_att = times_transpose(d_attn, out_w).astype(jnp.bfloat16)
    d_att, second_part = lax.optimization_barrier((d_att, second_part))
    d_outer_w, second_part = lax.optimization_barrier((d_outer_w, second_part))
    d_second = scattered(second_part)
    if paired:
        d_att, out_tokens = lax.optimization_barrier((d_att, out_tokens))
    dq, dk, dv = attention_backward(
        q, k, v, att, regroup.to_heads(split_rows(d_att)), lse, plan
    )
    dq, dk, dv = (regroup.from_heads(x).reshape(tok_count, width) for x in (dq, dk, dv))
    rms_scale = tok_count * width * seq_count * fsdp_count
    if paired:
        rows = jnp.concatenate(
            [
                jnp.zeros((2, width), jnp.float32),
                jnp.stack(
                    [d_out_b, d_gain_one, d_bias_one, d_outer_b, d_gain_two, d_bias_two]
                ),
                d_inner_b.reshape(per_own, width),
                jnp.pad(sums[None], ((0, 0), (0, width - 3))),
                jnp.zeros((3 + (-per_own) % 8, width), jnp.float32),
            ],
            axis=0,
        )[:16]
        d_outer_w = sum_seq(d_outer_w)
        dq, d_outer_w = lax.optimization_barrier((dq, d_outer_w))
        rows, d_second = lax.optimization_barrier((rows, d_second))
        d_query_w, d_key_w, d_value_w, rows, d_tokens_in = qkv_backward(
            flat_in.T, dq, dk, dv, qkv_w.T, d_resid_one, rows, own
        )
        d_second = sum_seq(d_second)
        mine = lax.axis_index("fsdp")
        d_vec = lax.dynamic_slice_in_dim(rows[:8], mine * own, own, 1)
        d_inner_b = lax.dynamic_slice_in_dim(
            rows[8 : 8 + per_own].reshape(-1), mine * own * per_own, own * per_own, 0
        )
        rms_values = jnp.sqrt(rows[8 + per_own, :3] / rms_scale)
        return (
            out_tokens,
            d_tokens_in,
            d_query_w,
            d_vec[0],
            d_key_w,
            d_value_w,
            d_vec[1],
            d_second[:, :width],
            d_vec[2],
            d_vec[3],
            d_vec[4],
            d_second[:, width:],
            d_inner_b,
            d_outer_w,
            d_vec[5],
            d_vec[6],
            d_vec[7],
            rms_values,
        )
    sums = jnp.broadcast_to(sums[:, None], (3, 128))
    sums = butterfly_sum(butterfly_sum(sums, "fsdp"), "seq")[:, 0]
    rms_values = jnp.sqrt(sums / rms_scale)
    d_query_b = jnp.sum(dq.astype(jnp.float32), axis=0)
    d_value_b = jnp.sum(dv.astype(jnp.float32), axis=0)
    grads = [
        d_query_b, d_value_b, d_out_b, d_gain_one, d_bias_one, d_outer_b, d_gain_two, d_bias_two,
    ]
    d_small = jnp.concatenate(
        [jnp.stack(grads), d_inner_b.reshape(width, per_own).T,
         jnp.zeros((128 - used, width), jnp.float32)], axis=0
    ).T
    parts = [contract_rows(flat_in, x) for x in (dq, dk, dv)] + [d_small]
    first_part = jnp.concatenate([x.astype(jnp.bfloat16) for x in parts], axis=1)
    dq, first_part = lax.optimization_barrier((dq, first_part))
    d_second, first_part = lax.optimization_barrier((d_second, first_part))
    d_first = sum_seq(scattered(first_part))
    d_outer_w, d_second = sum_seq(d_outer_w), sum_seq(d_second)
    d_tokens = d_resid_one
    for i, part in enumerate((dq, dk, dv)):
        d_tokens = d_tokens + times_transpose(part, qkv_w[:, i * width : (i + 1) * width])
    d_tokens_in = regroup.scatter(split_rows(d_tokens.astype(jnp.bfloat16)))
    d_cols = d_first[:, 3 * width :].T
    d_vec = [d_cols[i] for i in range(len(vectors))]
    return (
        out_tokens,
        d_tokens_in,
        d_first[:, :width],
        d_vec[0],
        d_first[:, width : 2 * width],
        d_first[:, 2 * width : 3 * width],
        d_vec[1],
        d_second[:, :width],
        d_vec[2],
        d_vec[3],
        d_vec[4],
        d_second[:, width:],
        d_cols[len(vectors) : used].T.reshape(-1),
        d_outer_w,
        d_vec[5],
        d_vec[6],
        d_vec[7],
        rms_values,
    )


def solution(mesh):
    in_specs = (
        P("fsdp", "seq", None),
        P("fsdp", None),
        P("fsdp", None, None),
        P("fsdp", None),
        P("fsdp", None),
        P("fsdp"),
        P("fsdp", None),
        P("fsdp", None),
        P("fsdp"),
        P("fsdp", None),
        P("fsdp"),
        P("fsdp"),
        P("fsdp"),
        P("fsdp", None),
        P("fsdp"),
        P("fsdp", None),
        P("fsdp"),
        P("fsdp"),
        P("fsdp"),
        P("fsdp", "seq", None),
    )
    out_specs = (
        P("fsdp", "seq", None),
        P("fsdp", "seq", None),
        P("fsdp", None),
        P("fsdp"),
        P("fsdp", None),
        P("fsdp", None),
        P("fsdp"),
        P("fsdp", None),
        P("fsdp"),
        P("fsdp"),
        P("fsdp"),
        P("fsdp", None),
        P("fsdp"),
        P("fsdp", None),
        P("fsdp"),
        P("fsdp"),
        P("fsdp"),
        P(),
    )
    return jax.shard_map(shards, mesh=mesh, in_specs=in_specs, out_specs=out_specs, check_vma=False)
```

```python
import functools
import math

import jax
import jax.numpy as jnp
from jax import lax
from jax.experimental import pallas as pl
from jax.experimental.pallas import tpu as pltpu
from jax.sharding import PartitionSpec as P

HD = 64
BLK = 64
CHUNK = 4
NEG = -1e30


def plan_blocks(seg, rand, glob):
    rows, full_len = seg.shape
    nb = full_len // BLK
    ids = jnp.arange(nb, dtype=jnp.int32)
    is_global = jnp.any(ids[None, :, None] == glob[:, None, :], axis=-1)
    picked = jnp.any(rand[:, :, None, :] == ids[None, None, :, None], axis=-1)
    nearby = jnp.abs(ids[:, None] - ids[None, :]) <= 1
    admitted = nearby[None] | picked | is_global[:, :, None] | is_global[:, None, :]
    by_block = seg.reshape(rows, nb, BLK)
    low, high = by_block[:, :, 0], by_block[:, :, BLK - 1]
    meets = (low[:, :, None] <= high[:, None, :]) & (low[:, None, :] <= high[:, :, None])
    active = (admitted & meets).astype(jnp.int32)
    upto = (ids[:, None] <= ids[None, :]).astype(jnp.int32)
    place = jnp.sum(active[:, :, :, None] * upto[None, None], axis=2) - 1
    count = jnp.sum(active, axis=2)
    hit = (place[:, :, :, None] == ids[None, None, None, :]) & (active[:, :, :, None] > 0)
    listed = jnp.sum(jnp.where(hit, ids[None, None, :, None], 0), axis=2)
    listed = jnp.where(ids[None, None, :] < count[:, :, None], listed, nb)
    chunks = (count + (CHUNK - 1)) // CHUNK
    seg_cols = jnp.concatenate([seg, jnp.full((rows, BLK), -1, jnp.int32)], axis=1)
    seg_cols = jnp.broadcast_to(seg_cols[:, :, None], (rows, full_len + BLK, 128))
    seg_rows = jnp.concatenate([by_block, by_block], axis=2)[:, :, None, :]
    return chunks, listed.reshape(rows, nb * nb), seg_cols, seg_rows


def lane_low(rows):
    return lax.broadcasted_iota(jnp.int32, (rows, 128), 1) < HD


def diag128(dup_t):
    row = lax.broadcasted_iota(jnp.int32, (128, 128), 0) < HD
    col = lax.broadcasted_iota(jnp.int32, (128, 128), 1) < HD
    return jnp.where(row == col, dup_t, jnp.zeros_like(dup_t))


def transposed_twice(tile):
    both = jnp.concatenate([tile, tile], axis=0)
    return both.T


def head_rows(acc):
    turned = jnp.concatenate([acc, acc], axis=0).T
    return jnp.where(lane_low(HD), turned[:HD], turned[HD:])


def pick_diag(full, half):
    lanes = slice(half * 128, half * 128 + 128)
    top = full[half * 128 : half * 128 + HD, lanes]
    low = full[half * 128 + HD : half * 128 + 128, lanes]
    return jnp.where(lane_low(HD), top, low)


def chunk_ids(list_ref, row, base, nb):
    ids = [list_ref[row, base + j] for j in range(CHUNK)]
    safe = [jnp.where(b == nb, 0, b) for b in ids]
    return ids, safe


def block_rows(ref, blocks, lanes):
    return jnp.concatenate(
        [ref[0, pl.ds(pl.multiple_of(b * BLK, BLK), BLK), lanes] for b in blocks], axis=0
    )


def turned_blocks(ref, blocks, rows):
    low = lane_low(rows.stop - rows.start)
    tiles = [ref[b, rows, :] for b in blocks]
    return jnp.concatenate(
        [jnp.where(low, tiles[i], tiles[i + 1]) for i in range(0, CHUNK, 2)], axis=1
    )


def turn_all(src_ref, dst_ref, nb, width):
    def body(b, _):
        start = pl.multiple_of(b * BLK, BLK)
        for t in range(width // 128):
            tile = src_ref[0, pl.ds(start, BLK), t * 128 : t * 128 + 128]
            dst_ref[b, t * 128 : t * 128 + 128, :] = transposed_twice(tile)
        return 0

    lax.fori_loop(0, nb, body, 0)


def dot_f32(left, right):
    return lax.dot_general(
        left, right, (((1,), (0,)), ((), ())), preferred_element_type=jnp.float32
    )


def forward_kernel(group, n_ref, list_ref, q_ref, k_ref, v_ref, segc_ref, segr_ref,
                   o_ref, lse_ref, vt_ref, qst_ref, m_ref, l_ref, acc_ref):
    row = pl.program_id(0)
    width = q_ref.shape[2]
    nb = q_ref.shape[1] // BLK
    groups, halves = width // group, group // 128
    turn_all(v_ref, vt_ref, nb, width)
    qst_ref[...] = jnp.zeros_like(qst_ref)

    def per_query(a, _):
        start = pl.multiple_of(a * BLK, BLK)
        for t in range(width // 128):
            tile = q_ref[0, pl.ds(start, BLK), t * 128 : t * 128 + 128] * 0.125
            g, u = t // halves, t % halves
            qst_ref[g, u * 128 : u * 128 + 128, u * 128 : u * 128 + 128] = diag128(
                transposed_twice(tile.astype(jnp.bfloat16))
            )
        seg_q = segr_ref[0, a]
        m_ref[...] = jnp.full_like(m_ref, NEG)
        l_ref[...] = jnp.zeros_like(l_ref)
        acc_ref[...] = jnp.zeros_like(acc_ref)

        def per_chunk(c, _):
            ids, safe = chunk_ids(list_ref, row, a * nb + c * CHUNK, nb)
            seg_k = block_rows(segc_ref, ids, slice(0, 128))
            allowed = seg_k == seg_q
            for g in range(groups):
                lanes = slice(g * group, g * group + group)
                s_t = dot_f32(block_rows(k_ref, safe, lanes), qst_ref[g])
                weights, alphas = [], []
                for u in range(halves):
                    t = g * halves + u
                    s = jnp.where(allowed, s_t[:, u * 128 : u * 128 + 128], NEG)
                    m_old = m_ref[t]
                    m_new = jnp.maximum(m_old, jnp.max(s, axis=0, keepdims=True))
                    p = jnp.exp(s - m_new)
                    alpha = jnp.exp(m_old - m_new)
                    l_ref[t] = alpha * l_ref[t] + jnp.sum(p, axis=0, keepdims=True)
                    m_ref[t] = m_new
                    weights.append(p.astype(jnp.bfloat16))
                    alphas.append(alpha)
                p_t = jnp.concatenate(weights, axis=1) if halves > 1 else weights[0]
                o_t = dot_f32(turned_blocks(vt_ref, safe, lanes), p_t)
                for u in range(halves):
                    t = g * halves + u
                    acc_ref[t] = alphas[u] * acc_ref[t] + pick_diag(o_t, u)
            return 0

        lax.fori_loop(0, n_ref[row, a], per_chunk, 0)
        for t in range(width // 128):
            total = l_ref[t]
            out = acc_ref[t] / total
            o_ref[0, pl.ds(start, BLK), t * 128 : t * 128 + 128] = head_rows(out).astype(
                jnp.bfloat16
            )
            lse_ref[0, a, :, t * 128 : t * 128 + 128] = m_ref[t] + jnp.log(total)
        return 0

    lax.fori_loop(0, nb, per_query, 0)


def group_of(width):
    return 256 if width % 256 == 0 else 128


def whole_spec(shape):
    rest = (0,) * (len(shape) - 1)
    return pl.BlockSpec((1,) + tuple(shape[1:]), lambda r, *_: (r,) + rest)


def one_spec(shape):
    rest = (0,) * (len(shape) - 1)
    return pl.BlockSpec((1,) + tuple(shape[1:]), lambda r, *_: (r,) + rest,
                        pipeline_mode=pl.Buffered(1))


def attention_forward(q, k, v, plan):
    chunks, listed, seg_cols, seg_rows = plan
    rows, full_len, width = q.shape
    nb, group = full_len // BLK, group_of(width)
    tiles = width // 128
    pairs = rows * full_len * full_len // 4 * width
    args = (q, k, v, seg_cols, seg_rows)
    return pl.pallas_call(
        functools.partial(forward_kernel, group),
        out_shape=(
            jax.ShapeDtypeStruct((rows, full_len, width), jnp.bfloat16),
            jax.ShapeDtypeStruct((rows, nb, 1, width), jnp.float32),
        ),
        grid_spec=pltpu.PrefetchScalarGridSpec(
            num_scalar_prefetch=2,
            grid=(rows,),
            in_specs=[one_spec(x.shape) for x in args],
            out_specs=(one_spec((rows, full_len, width)), one_spec((rows, nb, 1, width))),
            scratch_shapes=[
                pltpu.VMEM((nb, width, 128), jnp.bfloat16),
                pltpu.VMEM((width // group, group, group), jnp.bfloat16),
                pltpu.VMEM((tiles, 1, 128), jnp.float32),
                pltpu.VMEM((tiles, 1, 128), jnp.float32),
                pltpu.VMEM((tiles, HD, 128), jnp.float32),
            ],
        ),
        compiler_params=pltpu.CompilerParams(vmem_limit_bytes=48 << 20),
        cost_estimate=pl.CostEstimate(
            flops=64 * pairs, transcendentals=pairs // HD, bytes_accessed=8 * q.size
        ),
        name="attention_forward",
    )(chunks, listed, *args)


def backward_kernel(group, n_ref, list_ref, q_ref, k_ref, v_ref, o_ref, do_ref, lse_ref,
                    segc_ref, segr_ref, dq_ref, dk_ref, dv_ref,
                    kt_ref, qst_ref, qs_ref, dost_ref, dos_ref, delta_ref, acc_ref,
                    dk_acc, dv_acc):
    row = pl.program_id(0)
    full_len, width = q_ref.shape[1], q_ref.shape[2]
    nb = full_len // BLK
    groups, halves = width // group, group // 128
    turn_all(k_ref, kt_ref, nb, width)
    for ref in (qst_ref, qs_ref, dost_ref, dos_ref, dk_acc, dv_acc):
        ref[...] = jnp.zeros_like(ref)
    low = lane_low(HD)

    def per_query(a, _):
        start = pl.multiple_of(a * BLK, BLK)
        for t in range(width // 128):
            g, u = t // halves, t % halves
            lanes = slice(t * 128, t * 128 + 128)
            square = slice(u * 128, u * 128 + 128)
            q_tile = (q_ref[0, pl.ds(start, BLK), lanes] * 0.125).astype(jnp.bfloat16)
            g_tile = do_ref[0, pl.ds(start, BLK), lanes]
            o_tile = o_ref[0, pl.ds(start, BLK), lanes]
            g_turn = transposed_twice(g_tile)
            qst_ref[g, square, square] = diag128(transposed_twice(q_tile))
            dost_ref[g, square, square] = diag128(g_turn)
            qs_ref[g, square, square] = diag128(jnp.concatenate([q_tile, q_tile], axis=0))
            dos_ref[g, square, square] = diag128(jnp.concatenate([g_tile, g_tile], axis=0))
            product = g_turn.astype(jnp.float32) * transposed_twice(o_tile).astype(jnp.float32)
            delta_ref[t] = jnp.where(
                low[:1],
                jnp.sum(product[:HD], axis=0, keepdims=True),
                jnp.sum(product[HD:], axis=0, keepdims=True),
            )
        seg_q = segr_ref[0, a]
        acc_ref[...] = jnp.zeros_like(acc_ref)

        def per_chunk(c, _):
            ids, safe = chunk_ids(list_ref, row, a * nb + c * CHUNK, nb)
            seg_k = block_rows(segc_ref, ids, slice(0, 128))
            allowed = seg_k == seg_q
            for g in range(groups):
                lanes = slice(g * group, g * group + group)
                s_t = dot_f32(block_rows(k_ref, safe, lanes), qst_ref[g])
                dp_t = dot_f32(block_rows(v_ref, safe, lanes), dost_ref[g])
                p_parts, ds_parts = [], []
                for u in range(halves):
                    t = g * halves + u
                    half = slice(u * 128, u * 128 + 128)
                    lse = lse_ref[0, a, :, t * 128 : t * 128 + 128]
                    p = jnp.exp(jnp.where(allowed, s_t[:, half], NEG) - lse)
                    ds = p * (dp_t[:, half] - delta_ref[t])
                    p_parts.append(p.astype(jnp.bfloat16))
                    ds_parts.append(ds.astype(jnp.bfloat16))
                p_t = jnp.concatenate(p_parts, axis=1) if halves > 1 else p_parts[0]
                ds_t = jnp.concatenate(ds_parts, axis=1) if halves > 1 else ds_parts[0]
                dv = dot_f32(p_t, dos_ref[g])
                dk = dot_f32(ds_t, qs_ref[g])
                dq_t = dot_f32(turned_blocks(kt_ref, safe, lanes), ds_t)
                for j in range(CHUNK):
                    where = pl.ds(pl.multiple_of(safe[j] * BLK, BLK), BLK)
                    part = slice(j * BLK, j * BLK + BLK)
                    dv_acc[where, lanes] += dv[part]
                    dk_acc[where, lanes] += dk[part]
                for u in range(halves):
                    acc_ref[g * halves + u] += pick_diag(dq_t, u)
            return 0

        lax.fori_loop(0, n_ref[row, a], per_chunk, 0)
        for t in range(width // 128):
            dq_ref[0, pl.ds(start, BLK), t * 128 : t * 128 + 128] = (
                head_rows(acc_ref[t]) * 0.125
            ).astype(jnp.bfloat16)
        return 0

    lax.fori_loop(0, nb, per_query, 0)

    def flush(a, _):
        where = pl.ds(pl.multiple_of(a * BLK, BLK), BLK)
        dk_ref[0, where, :] = dk_acc[where, :].astype(jnp.bfloat16)
        dv_ref[0, where, :] = dv_acc[where, :].astype(jnp.bfloat16)
        return 0

    lax.fori_loop(0, nb, flush, 0)


def attention_backward(q, k, v, o, do, lse, plan):
    chunks, listed, seg_cols, seg_rows = plan
    rows, full_len, width = q.shape
    nb, group = full_len // BLK, group_of(width)
    tiles, groups = width // 128, width // group
    pairs = rows * full_len * full_len // 4 * width
    args = (q, k, v, o, do, lse, seg_cols, seg_rows)
    like = jax.ShapeDtypeStruct((rows, full_len, width), jnp.bfloat16)
    square = pltpu.VMEM((groups, group, group), jnp.bfloat16)
    return pl.pallas_call(
        functools.partial(backward_kernel, group),
        out_shape=(like, like, like),
        grid_spec=pltpu.PrefetchScalarGridSpec(
            num_scalar_prefetch=2,
            grid=(rows,),
            in_specs=[one_spec(x.shape) for x in args],
            out_specs=tuple(one_spec(like.shape) for _ in range(3)),
            scratch_shapes=[
                pltpu.VMEM((nb, width, 128), jnp.bfloat16),
                square, square, square, square,
                pltpu.VMEM((tiles, 1, 128), jnp.float32),
                pltpu.VMEM((tiles, HD, 128), jnp.float32),
                pltpu.VMEM((full_len, width), jnp.float32),
                pltpu.VMEM((full_len, width), jnp.float32),
            ],
        ),
        compiler_params=pltpu.CompilerParams(vmem_limit_bytes=58 << 20),
        cost_estimate=pl.CostEstimate(
            flops=100 * pairs, transcendentals=pairs // HD, bytes_accessed=16 * q.size
        ),
        name="attention_backward",
    )(chunks, listed, *args)


def pair_bit(index, bit):
    return lax.rem(index // (1 << bit), 2)


def pair_of(index, bit):
    return index + (1 - 2 * pair_bit(index, bit)) * (1 << bit)


def all_arrived(bits):
    me = lax.axis_index("fsdp")
    barrier = pltpu.get_barrier_semaphore()
    for bit in range(bits):
        pl.semaphore_signal(
            barrier, inc=1, device_id={"fsdp": pair_of(me, bit)},
            device_id_type=pl.DeviceIdType.MESH,
        )
    pl.semaphore_signal(
        barrier, inc=1, device_id={"seq": 1 - lax.axis_index("seq")},
        device_id_type=pl.DeviceIdType.MESH,
    )
    pl.semaphore_wait(barrier, bits + 1)


def qkv_backward_kernel(
    bits, x_in, dq_in, dk_in, dv_in, w_in, res_in, small_in,
    wq_out, wk_out, wv_out, small_out, tok_out,
    x, xt, grads, w, wt, res, tok, kept, sends, lands, final, small, small_land, result,
    in_sem, tok_send, tok_land, own_sem, send_sem, land_sem, x_send, x_land,
    small_send, small_recv, out_sem,
):
    me, side = lax.axis_index("fsdp"), lax.axis_index("seq")
    half = tok.shape[2] * tok.shape[1]
    piece, pieces = tok.shape[2], tok.shape[1]
    own, width = wq_out.shape
    owners = 1 << bits
    sources = (dq_in, dk_in, dv_in)
    loads = [
        pltpu.make_async_copy(w_in.at[:, pl.ds(0, 3 * width)], w, in_sem.at[0]),
        pltpu.make_async_copy(res_in, res, in_sem.at[1]),
        pltpu.make_async_copy(small_in, small.at[0], in_sem.at[2]),
        pltpu.make_async_copy(x_in, x, in_sem.at[3]),
    ] + [pltpu.make_async_copy(sources[i], grads.at[i], in_sem.at[4 + i]) for i in range(3)]
    for i in (0, 3, 4, 5, 6, 1, 2):
        loads[i].start()
    all_arrived(bits)
    loads[0].wait()
    for i in range(3):
        wt[i * width : (i + 1) * width, :] = w[:, i * width : (i + 1) * width].T
    loads[3].wait()

    def turn(r, _):
        xt[r] = x[pl.ds(pl.multiple_of(r * piece, piece), piece), :].T
        return 0

    lax.fori_loop(0, 2 * pieces, turn, 0)
    for i in (4, 5, 6, 1):
        loads[i].wait()

    def token_rows(start):
        total = res[pl.ds(start, piece), :].astype(jnp.float32)
        for i in range(3):
            total = total + dot_f32(
                grads[i, pl.ds(start, piece), :], wt[i * width : (i + 1) * width, :]
            )
        return total.astype(jnp.bfloat16)

    def sent(i):
        return pltpu.make_async_remote_copy(
            src_ref=tok.at[0, i],
            dst_ref=tok_out.at[side, pl.ds(pl.multiple_of(i * piece, piece), piece)],
            send_sem=tok_send.at[i], recv_sem=tok_land.at[i],
            device_id={"seq": 1 - side}, device_id_type=pl.DeviceIdType.MESH,
        )

    def landed(i):
        return pltpu.make_async_remote_copy(
            src_ref=tok.at[0, i],
            dst_ref=tok_out.at[1 - side, pl.ds(pl.multiple_of(i * piece, piece), piece)],
            send_sem=tok_send.at[i], recv_sem=tok_land.at[i],
            device_id={"seq": 1 - side}, device_id_type=pl.DeviceIdType.MESH,
        )

    def stays(i):
        return pltpu.make_async_copy(
            tok.at[1, i],
            tok_out.at[side, pl.ds(pl.multiple_of(i * piece, piece), piece)],
            own_sem.at[i],
        )

    def send_piece(i, _):
        start = pl.multiple_of((1 - side) * half + i * piece, piece)
        tok[0, i] = token_rows(start)
        sent(i).start()
        return 0

    lax.fori_loop(0, pieces, send_piece, 0)

    def keep_piece(i, _):
        start = pl.multiple_of(side * half + i * piece, piece)
        tok[1, i] = token_rows(start)
        stays(i).start()
        return 0

    low_bit = pair_bit(me, 0) == 0
    tile = 8 if owners % 8 == 0 else owners
    first_of = [0]
    for bit in range(bits):
        first_of.append(first_of[-1] + (owners >> (bit + 1)))

    def weights(i):
        def rows(m, _):
            rows_here = pl.ds(pl.multiple_of(m * tile * own, tile * own), tile * own)
            block = dot_f32(
                jnp.concatenate([xt[r, rows_here, :] for r in range(2 * pieces)], axis=1), grads[i]
            ).reshape(tile // 2, 2, own, width)
            even, odd = block[:, 0], block[:, 1]
            spot = pl.ds(m * (tile // 2), tile // 2)
            kept[i, spot] = jnp.where(low_bit, even, odd)
            sends[i, spot] = jnp.where(low_bit, odd, even).astype(jnp.bfloat16)
            return 0

        lax.fori_loop(0, owners // tile, rows, 0)

    def hop(i, bit):
        count = owners >> (bit + 1)
        spot = pl.ds(first_of[bit], count)
        return pltpu.make_async_remote_copy(
            src_ref=sends.at[i, spot], dst_ref=lands.at[i, spot],
            send_sem=send_sem.at[i, bit], recv_sem=land_sem.at[i, bit],
            device_id={"fsdp": pair_of(me, bit)}, device_id_type=pl.DeviceIdType.MESH,
        )

    def cross(i):
        return pltpu.make_async_remote_copy(
            src_ref=final.at[0, i], dst_ref=final.at[1, i],
            send_sem=x_send.at[i], recv_sem=x_land.at[i],
            device_id={"seq": 1 - side}, device_id_type=pl.DeviceIdType.MESH,
        )

    def advance(i, bit):
        hop(i, bit).wait_recv()
        base = first_of[bit]
        if bit + 1 == bits:
            total = kept[i, base] + lands[i, base].astype(jnp.float32)
            final[0, i] = total.astype(jnp.bfloat16)
            cross(i).start()
            return
        nxt = pair_bit(me, bit + 1)

        def one(j, _):
            stay, go = 2 * j + nxt, 2 * j + 1 - nxt
            kept[i, first_of[bit + 1] + j] = kept[i, base + stay] + lands[
                i, base + stay
            ].astype(jnp.float32)
            sends[i, first_of[bit + 1] + j] = (
                kept[i, base + go] + lands[i, base + go].astype(jnp.float32)
            ).astype(jnp.bfloat16)
            return 0

        lax.fori_loop(0, owners >> (bit + 2), one, 0)
        hop(i, bit + 1).start()

    outs = (wq_out, wk_out, wv_out)

    def written(i):
        return pltpu.make_async_copy(result.at[i], outs[i], out_sem.at[i])

    def finish(i):
        cross(i).wait_recv()
        result[i] = final[0, i].astype(jnp.float32) + final[1, i].astype(jnp.float32)
        written(i).start()

    def small_hop(bit):
        where = {"fsdp": pair_of(me, bit)} if bit < bits else {"seq": 1 - side}
        return pltpu.make_async_remote_copy(
            src_ref=small.at[bit], dst_ref=small_land.at[bit],
            send_sem=small_send.at[bit], recv_sem=small_recv.at[bit],
            device_id=where, device_id_type=pl.DeviceIdType.MESH,
        )

    def small_advance(bit):
        small_hop(bit).wait_recv()
        small[bit + 1] = small[bit] + small_land[bit]
        if bit < bits:
            small_hop(bit + 1).start()

    loads[2].wait()
    weights(0)
    hop(0, 0).start()
    for spot, i in ((0, 0), (1, 2)):
        def column_sums(c, total):
            block = grads[i, pl.ds(pl.multiple_of(c * 128, 128), 128), :].astype(jnp.float32)
            return total + jnp.sum(block.reshape(16, 8, width), axis=0)

        total = lax.fori_loop(
            0, grads.shape[1] // 128, column_sums, jnp.zeros((8, width), jnp.float32)
        )
        small[0, spot : spot + 1] = jnp.sum(total, axis=0, keepdims=True)
    small_hop(0).start()
    weights(1)
    hop(1, 0).start()
    advance(0, 0)
    small_advance(0)
    weights(2)
    hop(2, 0).start()
    plan = []
    for step in range(1, bits + 2):
        todo = []
        for i in range(3):
            bit = step - i
            if 0 <= bit < bits:
                todo.append((i, bit))
        plan.append((todo, step))
    done = 0
    for todo, step in plan:
        for i, bit in todo:
            advance(i, bit)
        if step <= bits:
            small_advance(step)
        if done < pieces:
            keep_piece(done, 0)
            done += 1
    for i in range(3):
        finish(i)
    small_copy = pltpu.make_async_copy(small.at[bits + 1], small_out, out_sem.at[3])
    small_copy.start()
    while done < pieces:
        keep_piece(done, 0)
        done += 1
    for i in range(3):
        written(i).wait()
        cross(i).wait_send()
        for bit in range(bits):
            hop(i, bit).wait_send()
    for bit in range(bits + 1):
        small_hop(bit).wait_send()
    small_copy.wait()
    for i in range(pieces):
        stays(i).wait()
        sent(i).wait_send()
        landed(i).wait_recv()


def qkv_backward(x, dq, dk, dv, w, resid, small, own):
    tokens, width = dq.shape
    bits = lax.axis_size("fsdp").bit_length() - 1
    owners = 1 << bits
    pieces = 4
    piece = tokens // 2 // pieces
    dma = pltpu.SemaphoreType.DMA
    f32, bf16 = jnp.float32, jnp.bfloat16
    shard = jax.ShapeDtypeStruct((own, width), f32)
    anywhere = pl.BlockSpec(memory_space=pl.ANY)
    return pl.pallas_call(
        functools.partial(qkv_backward_kernel, bits),
        out_shape=(
            shard, shard, shard,
            jax.ShapeDtypeStruct(small.shape, f32),
            jax.ShapeDtypeStruct((2, tokens // 2, width), bf16),
        ),
        in_specs=[anywhere] * 7,
        out_specs=(anywhere,) * 5,
        scratch_shapes=[
            pltpu.VMEM((tokens, width), bf16),
            pltpu.VMEM((2 * pieces, width, piece), bf16),
            pltpu.VMEM((3, tokens, width), bf16),
            pltpu.VMEM((width, 3 * width), bf16),
            pltpu.VMEM((3 * width, width), bf16),
            pltpu.VMEM((tokens, width), bf16),
            pltpu.VMEM((2, pieces, piece, width), bf16),
            pltpu.VMEM((3, owners - 1, own, width), f32),
            pltpu.VMEM((3, owners - 1, own, width), bf16),
            pltpu.VMEM((3, owners - 1, own, width), bf16),
            pltpu.VMEM((2, 3, own, width), bf16),
            pltpu.VMEM((bits + 2,) + small.shape, f32),
            pltpu.VMEM((bits + 1,) + small.shape, f32),
            pltpu.VMEM((3, own, width), f32),
            dma((7,)), dma((pieces,)), dma((pieces,)), dma((pieces,)),
            dma((3, bits)), dma((3, bits)), dma((3,)), dma((3,)),
            dma((bits + 1,)), dma((bits + 1,)), dma((4,)),
        ],
        compiler_params=pltpu.CompilerParams(
            collective_id=1, has_side_effects=True, vmem_limit_bytes=60 << 20
        ),
        cost_estimate=pl.CostEstimate(
            flops=40 * tokens * width * width, transcendentals=0,
            bytes_accessed=16 * tokens * width,
        ),
        name="qkv_backward",
    )(x, dq, dk, dv, w, resid, small)


eps_norm = 1e-06


def dot_rows(left, right):
    return lax.dot_general(
        left, right, (((0,), (0,)), ((), ())), preferred_element_type=jnp.float32
    )


def dot_nt(left, right):
    return lax.dot_general(
        left, right, (((1,), (1,)), ((), ())), preferred_element_type=jnp.float32
    )


def row_mean(values):
    return jnp.mean(values, axis=-1, keepdims=True)


GELU_K = math.sqrt(2.0 / math.pi)
GELU_A = 0.044715


def gelu_pair(u):
    square = u * u
    t = jnp.tanh(u * (GELU_K + (GELU_K * GELU_A) * square))
    half = 0.5 + 0.5 * t
    slope = half + (u * (half * (1.0 - t))) * (GELU_K + (3.0 * GELU_K * GELU_A) * square)
    return u * half, slope


OUT_B, GAIN_1, BIAS_1, OUTER_B, GAIN_2, BIAS_2, INNER_B = 2, 3, 4, 5, 6, 7, 8
STEP_ROWS = 64
SMALL_ROWS = 16


def middle_kernel(
    chunks, weights_in, small, att, tokens, cotangent,
    out, d_attn, d_att, d_weights, sums,
    w, acc, act, slope, z_one, flow, rs_one, normed, normed_t, d_mlp, load_sem, store_sem,
):
    step, steps = pl.program_id(0), pl.num_programs(0)
    rows, width = att.shape
    f32, bf16 = jnp.float32, jnp.bfloat16
    count = 2 * chunks + 1

    def load(i):
        return pltpu.make_async_copy(
            weights_in.at[:, pl.ds(i * width, width)], w.at[i], load_sem.at[i]
        )

    def store(i):
        return pltpu.make_async_copy(
            w.at[i], d_weights.at[:, pl.ds(i * width, width)], store_sem.at[i]
        )

    @pl.when(step == 0)
    def _():
        for i in range(count):
            load(i).start()
        sums[...] = jnp.zeros_like(sums)

        def clear(i, _):
            acc[i] = jnp.zeros_like(acc[i])
            return 0

        lax.fori_loop(0, count, clear, 0)
        for i in range(count):
            load(i).wait()

    def vector(i):
        return small[i : i + 1, :]

    def add_sum(i, values):
        sums[pl.ds(i, 1), :] += jnp.sum(values, axis=0, keepdims=True)

    def by_rows(body):
        def one(r, _):
            body(pl.ds(pl.multiple_of(r * STEP_ROWS, STEP_ROWS), STEP_ROWS))
            return 0

        lax.fori_loop(0, rows // STEP_ROWS, one, 0)

    flow[...] = dot_f32(att[...], w[0])

    def norm_one(r):
        attn = flow[r, :] + vector(OUT_B)
        resid = tokens[r, :].astype(f32) + attn
        add_sum(INNER_B + chunks, resid * resid)
        add_sum(INNER_B + chunks + 1, attn * attn)
        centred = resid - row_mean(resid)
        scale = lax.rsqrt(row_mean(centred * centred) + eps_norm)
        z = centred * scale
        z_one[r, :] = z
        rs_one[r, :] = scale
        normed[r, :] = (z * vector(GAIN_1) + vector(BIAS_1)).astype(bf16)

    by_rows(norm_one)
    normed_t[...] = normed[...].T

    def inner(c, _):
        for n in range(width // 256):
            cols = slice(n * 256, n * 256 + 256)
            pre = dot_f32(normed[...], w[1 + c, :, cols]) + small[pl.ds(INNER_B + c, 1), cols]
            value, grade = gelu_pair(pre)
            act[c, :, cols] = value.astype(bf16)
            slope[c, :, cols] = grade.astype(bf16)
        return 0

    lax.fori_loop(0, chunks, inner, 0)
    flow[...] = dot_f32(act[0], w[1 + chunks])

    def outer(c, _):
        flow[...] += dot_f32(act[c], w[1 + chunks + c])
        return 0

    lax.fori_loop(1, chunks, outer, 0)

    def norm_two(r):
        mlp = flow[r, :] + vector(OUTER_B)
        add_sum(INNER_B + chunks + 2, mlp * mlp)
        resid = z_one[r, :] * vector(GAIN_1) + vector(BIAS_1) + mlp
        centred = resid - row_mean(resid)
        scale = lax.rsqrt(row_mean(centred * centred) + eps_norm)
        z = centred * scale
        out[r, :] = (z * vector(GAIN_2) + vector(BIAS_2)).astype(bf16)
        grad = cotangent[r, :].astype(f32)
        add_sum(GAIN_2, grad * z)
        add_sum(BIAS_2, grad)
        grad = grad * vector(GAIN_2)
        d_resid = scale * (grad - row_mean(grad) - z * row_mean(grad * z))
        low = d_resid.astype(bf16)
        add_sum(OUTER_B, low.astype(f32))
        d_mlp[r, :] = low
        flow[r, :] = d_resid

    by_rows(norm_two)

    def back(c, _):
        for n in range(width // 256):
            cols = slice(n * 256, n * 256 + 256)
            d_act = dot_nt(d_mlp[...], w[1 + chunks + c, cols, :])
            d_pre = (slope[c, :, cols].astype(f32) * d_act).astype(bf16)
            sums[pl.ds(INNER_B + c, 1), cols] += jnp.sum(
                d_pre.astype(f32), axis=0, keepdims=True
            )
            slope[c, :, cols] = d_pre
        acc[1 + chunks + c] += dot_rows(act[c], d_mlp[...])
        acc[1 + c] += dot_f32(normed_t[...], slope[c])
        flow[...] += dot_nt(slope[c], w[1 + c])

        @pl.when(step == steps - 1)
        def _():
            for i in (1 + c, 1 + chunks + c):
                w[i] = acc[i].astype(bf16)
                store(i).start()

        return 0

    lax.fori_loop(0, chunks, back, 0)

    def norm_one_back(r):
        grad = flow[r, :]
        z = z_one[r, :]
        add_sum(GAIN_1, grad * z)
        add_sum(BIAS_1, grad)
        grad = grad * vector(GAIN_1)
        d_resid = rs_one[r, :] * (grad - row_mean(grad) - z * row_mean(grad * z))
        low = d_resid.astype(bf16)
        add_sum(OUT_B, low.astype(f32))
        d_attn[r, :] = low

    by_rows(norm_one_back)
    acc[0] += dot_rows(att[...], d_attn[...])
    d_att[...] = dot_nt(d_attn[...], w[0]).astype(bf16)

    @pl.when(step == steps - 1)
    def _():
        w[0] = acc[0].astype(bf16)
        store(0).start()
        for i in range(count):
            store(i).wait()


def middle(weights, small, att, tokens, cotangent):
    tok_count, width = att.shape
    chunks = (weights.shape[1] // width - 1) // 2
    count = 2 * chunks + 1
    rows = 512
    f32, bf16 = jnp.float32, jnp.bfloat16
    tile = pl.BlockSpec((rows, width), lambda i: (i, 0))
    fixed = pl.BlockSpec(small.shape, lambda i: (0, 0), pipeline_mode=pl.Buffered(1))
    anywhere = pl.BlockSpec(memory_space=pl.ANY)
    like = jax.ShapeDtypeStruct((tok_count, width), bf16)
    flops = 6 * tok_count * width * width * count
    return pl.pallas_call(
        functools.partial(middle_kernel, chunks),
        grid=(tok_count // rows,),
        out_shape=(
            like, like, like,
            jax.ShapeDtypeStruct(weights.shape, bf16),
            jax.ShapeDtypeStruct(small.shape, f32),
        ),
        in_specs=[anywhere, fixed, tile, tile, tile],
        out_specs=(tile, tile, tile, anywhere, pl.BlockSpec(small.shape, lambda i: (0, 0))),
        scratch_shapes=[
            pltpu.VMEM((count, width, width), bf16),
            pltpu.VMEM((count, width, width), f32),
            pltpu.VMEM((chunks, rows, width), bf16),
            pltpu.VMEM((chunks, rows, width), bf16),
            pltpu.VMEM((rows, width), f32),
            pltpu.VMEM((rows, width), f32),
            pltpu.VMEM((rows, 1), f32),
            pltpu.VMEM((rows, width), bf16),
            pltpu.VMEM((width, rows), bf16),
            pltpu.VMEM((rows, width), bf16),
            pltpu.SemaphoreType.DMA((count,)),
            pltpu.SemaphoreType.DMA((count,)),
        ],
        compiler_params=pltpu.CompilerParams(vmem_limit_bytes=62 << 20),
        cost_estimate=pl.CostEstimate(
            flops=2 * flops, transcendentals=tok_count * width * chunks,
            bytes_accessed=12 * tok_count * width + 4 * weights.size,
        ),
        name="middle",
    )(weights, small, att, tokens, cotangent)


def contract_rows(left, right):
    return lax.dot_general(
        left, right, (((0,), (0,)), ((), ())), preferred_element_type=jnp.float32
    )


def times_transpose(left, right):
    return lax.dot_general(
        left, right, (((1,), (1,)), ((), ())), preferred_element_type=jnp.float32
    )


def butterfly_sum(values, axis):
    size = lax.axis_size(axis)
    if size & (size - 1):
        return lax.psum(values, axis)
    step = 1
    while step < size:
        pairs = [(i, i ^ step) for i in range(size)]
        values = values + lax.ppermute(values, axis, pairs)
        step *= 2
    return values


def sum_seq(values):
    if lax.axis_size("seq") == 2:
        other = lax.ppermute(values, "seq", [(0, 1), (1, 0)])
        return values.astype(jnp.float32) + other.astype(jnp.float32)
    return lax.psum(values, "seq").astype(jnp.float32)


class Regroup:
    def __init__(self, row_count):
        self.size = lax.axis_size("seq")
        self.ways = math.gcd(row_count, self.size)
        self.parts = self.size // self.ways
        self.rows = row_count // self.ways
        me = lax.axis_index("seq")
        self.place = lax.rem(me, self.ways)
        self.row_group = me // self.parts

    def targets(self, turn):
        ways, parts = self.ways, self.parts
        return [
            (s, ((s % ways + turn) % ways) * parts + s // ways) for s in range(self.size)
        ]

    def move(self, values, pairs):
        if all(a == b for a, b in pairs):
            return values
        return lax.ppermute(values, "seq", pairs)

    def gather(self, values):
        rows, local, width = self.rows, values.shape[1], values.shape[2]
        out = jnp.zeros((rows, self.ways, local, width), values.dtype)
        for turn in range(self.ways):
            pick = lax.rem(self.place + turn, self.ways)
            chunk = lax.dynamic_slice_in_dim(values, pick * rows, rows, 0)
            chunk = self.move(chunk, self.targets(turn))
            spot = lax.rem(self.row_group - turn + self.ways, self.ways)
            out = lax.dynamic_update_slice_in_dim(out, chunk[:, None], spot, 1)
        return out.reshape(rows, self.ways * local, width)

    def scatter(self, values):
        rows, width = self.rows, values.shape[2]
        local = values.shape[1] // self.ways
        values = values.reshape(rows, self.ways, local, width)
        out = jnp.zeros((rows * self.ways, local, width), values.dtype)
        for turn in range(self.ways):
            spot = lax.rem(self.row_group - turn + self.ways, self.ways)
            chunk = lax.dynamic_slice_in_dim(values, spot, 1, 1)[:, 0]
            chunk = self.move(chunk, [(b, a) for a, b in self.targets(turn)])
            pick = lax.rem(self.place + turn, self.ways)
            out = lax.dynamic_update_slice_in_dim(out, chunk, pick * rows, 0)
        return out

    def pick_rows(self, values):
        return lax.dynamic_slice_in_dim(values, self.row_group * self.rows, self.rows, 0)

    def groups(self):
        return [
            [r * self.parts + j for j in range(self.parts)] for r in range(self.ways)
        ]

    def to_heads(self, values):
        if self.parts == 1:
            return values
        return lax.all_to_all(
            values, "seq", split_axis=2, concat_axis=1, tiled=True,
            axis_index_groups=self.groups(),
        )

    def from_heads(self, values):
        if self.parts == 1:
            return values
        return lax.all_to_all(
            values, "seq", split_axis=1, concat_axis=2, tiled=True,
            axis_index_groups=self.groups(),
        )


def shards(
    tokens_in,
    segment_ids,
    random_blocks,
    global_blocks,
    w_query,
    b_query,
    w_key,
    w_value,
    b_value,
    w_attn_out,
    b_attn_out,
    ln1_gain,
    ln1_bias,
    w_inner,
    b_inner,
    w_outer,
    b_outer,
    ln2_gain,
    ln2_bias,
    out_grad,
):
    row_count, local_len, width = tokens_in.shape
    seq_count = lax.axis_size("seq")
    fsdp_count = lax.axis_size("fsdp")
    tok_count = row_count * local_len
    own = w_query.shape[0]
    chunks = b_inner.shape[0] // own
    regroup = Regroup(row_count)
    paired = row_count == 2 and seq_count == 2 and fsdp_count & (fsdp_count - 1) == 0

    vectors = [b_query, b_value, b_attn_out, ln1_gain, ln1_bias, b_outer, ln2_gain, ln2_bias]
    columns = [x[:, None] for x in vectors] + [b_inner.reshape(own, chunks)]
    used = len(vectors) + chunks
    columns.append(jnp.zeros((own, 128 - used), jnp.bfloat16))
    first = jnp.concatenate([w_query, w_key, w_value] + columns, axis=1)
    first = lax.all_gather(first, "fsdp", axis=0, tiled=True)
    inner_own = w_inner.reshape(own, width, chunks).transpose(0, 2, 1).reshape(own, -1)
    second = jnp.concatenate([w_attn_out, inner_own, w_outer.reshape(own, -1)], axis=1)
    second = lax.all_gather(second, "fsdp", axis=0, tiled=True)
    qkv_w = first[:, : 3 * width]
    small = first[:, 3 * width : 3 * width + SMALL_ROWS].astype(jnp.float32).T

    flat_in = regroup.gather(tokens_in).reshape(tok_count, width)
    plan = plan_blocks(
        regroup.pick_rows(segment_ids),
        regroup.pick_rows(random_blocks),
        regroup.pick_rows(global_blocks),
    )

    def split_rows(values):
        return values.reshape(regroup.rows, tok_count // regroup.rows, width)

    qkv_bias = jnp.concatenate([small[0], jnp.zeros_like(small[0]), small[1]])
    qkv = (jnp.dot(flat_in, qkv_w, preferred_element_type=jnp.float32) + qkv_bias).astype(
        jnp.bfloat16
    )
    qkv, out_grad = lax.optimization_barrier((qkv, out_grad))
    flat_grad = regroup.gather(out_grad).reshape(tok_count, width)
    q, k, v = (
        regroup.to_heads(split_rows(qkv[:, i * width : (i + 1) * width])) for i in range(3)
    )
    att, lse = attention_forward(q, k, v, plan)
    att_flat = regroup.from_heads(att).reshape(tok_count, width)
    out_tokens, d_attn, d_att, d_second, sums = middle(
        second, small, att_flat, flat_in, flat_grad
    )
    out_tokens = regroup.scatter(split_rows(out_tokens))

    def scattered(values):
        return lax.psum_scatter(values, "fsdp", scatter_dimension=0, tiled=True)

    d_second = scattered(d_second)
    d_att, out_tokens = lax.optimization_barrier((d_att, out_tokens))
    dq, dk, dv = attention_backward(
        q, k, v, att, regroup.to_heads(split_rows(d_att)), lse, plan
    )
    dq, dk, dv = (regroup.from_heads(x).reshape(tok_count, width) for x in (dq, dk, dv))
    mine = lax.axis_index("fsdp")
    if paired:
        d_query_w, d_key_w, d_value_w, sums, d_tokens_in = qkv_backward(
            flat_in, dq, dk, dv, first, d_attn, sums, own
        )
    else:
        for spot, part in ((0, dq), (1, dv)):
            sums = sums.at[spot].set(jnp.sum(part.astype(jnp.float32), axis=0))
        sums = butterfly_sum(butterfly_sum(sums, "fsdp"), "seq")
        d_query_w, d_key_w, d_value_w = (
            sum_seq(scattered(contract_rows(flat_in, x).astype(jnp.bfloat16)))
            for x in (dq, dk, dv)
        )
        d_tokens = d_attn.astype(jnp.float32)
        for i, part in enumerate((dq, dk, dv)):
            d_tokens = d_tokens + times_transpose(part, qkv_w[:, i * width : (i + 1) * width])
        d_tokens_in = regroup.scatter(split_rows(d_tokens.astype(jnp.bfloat16)))
    d_second = sum_seq(d_second)
    d_inner_w = (
        d_second[:, width : (1 + chunks) * width]
        .reshape(own, chunks, width)
        .transpose(0, 2, 1)
        .reshape(own, -1)
    )
    d_outer_w = d_second[:, (1 + chunks) * width :].reshape(own * chunks, width)
    d_vec = lax.dynamic_slice_in_dim(sums, mine * own, own, 1)
    entry_total = tok_count * width * seq_count * fsdp_count
    rms_values = jnp.sqrt(
        jnp.sum(sums[INNER_B + chunks : INNER_B + chunks + 3], axis=1) / entry_total
    )
    return (
        out_tokens,
        d_tokens_in,
        d_query_w,
        d_vec[0],
        d_key_w,
        d_value_w,
        d_vec[1],
        d_second[:, :width],
        d_vec[OUT_B],
        d_vec[GAIN_1],
        d_vec[BIAS_1],
        d_inner_w,
        d_vec[INNER_B : INNER_B + chunks].T.reshape(-1),
        d_outer_w,
        d_vec[OUTER_B],
        d_vec[GAIN_2],
        d_vec[BIAS_2],
        rms_values,
    )


def solution(mesh):
    in_specs = (
        P("fsdp", "seq", None),
        P("fsdp", None),
        P("fsdp", None, None),
        P("fsdp", None),
        P("fsdp", None),
        P("fsdp"),
        P("fsdp", None),
        P("fsdp", None),
        P("fsdp"),
        P("fsdp", None),
        P("fsdp"),
        P("fsdp"),
        P("fsdp"),
        P("fsdp", None),
        P("fsdp"),
        P("fsdp", None),
        P("fsdp"),
        P("fsdp"),
        P("fsdp"),
        P("fsdp", "seq", None),
    )
    out_specs = (
        P("fsdp", "seq", None),
        P("fsdp", "seq", None),
        P("fsdp", None),
        P("fsdp"),
        P("fsdp", None),
        P("fsdp", None),
        P("fsdp"),
        P("fsdp", None),
        P("fsdp"),
        P("fsdp"),
        P("fsdp"),
        P("fsdp", None),
        P("fsdp"),
        P("fsdp", None),
        P("fsdp"),
        P("fsdp"),
        P("fsdp"),
        P(),
    )
    return jax.shard_map(shards, mesh=mesh, in_specs=in_specs, out_specs=out_specs, check_vma=False)
```

```python
import functools
import math

import jax
import jax.numpy as jnp
from jax import lax
from jax.experimental import pallas as pl
from jax.experimental.pallas import tpu as pltpu
from jax.sharding import PartitionSpec as P

HD = 64
BLK = 64
CHUNK = 4
NEG = -1e30


def plan_blocks(seg, rand, glob):
    rows, full_len = seg.shape
    nb = full_len // BLK
    ids = jnp.arange(nb, dtype=jnp.int32)
    is_global = jnp.any(ids[None, :, None] == glob[:, None, :], axis=-1)
    picked = jnp.any(rand[:, :, None, :] == ids[None, None, :, None], axis=-1)
    nearby = jnp.abs(ids[:, None] - ids[None, :]) <= 1
    admitted = nearby[None] | picked | is_global[:, :, None] | is_global[:, None, :]
    by_block = seg.reshape(rows, nb, BLK)
    low, high = by_block[:, :, 0], by_block[:, :, BLK - 1]
    meets = (low[:, :, None] <= high[:, None, :]) & (low[:, None, :] <= high[:, :, None])
    active = (admitted & meets).astype(jnp.int32)
    upto = (ids[:, None] <= ids[None, :]).astype(jnp.int32)
    place = jnp.sum(active[:, :, :, None] * upto[None, None], axis=2) - 1
    count = jnp.sum(active, axis=2)
    hit = (place[:, :, :, None] == ids[None, None, None, :]) & (active[:, :, :, None] > 0)
    listed = jnp.sum(jnp.where(hit, ids[None, None, :, None], 0), axis=2)
    listed = jnp.where(ids[None, None, :] < count[:, :, None], listed, nb)
    chunks = (count + (CHUNK - 1)) // CHUNK
    seg_cols = jnp.concatenate([seg, jnp.full((rows, BLK), -1, jnp.int32)], axis=1)
    seg_cols = jnp.broadcast_to(seg_cols[:, :, None], (rows, full_len + BLK, 128))
    seg_rows = jnp.concatenate([by_block, by_block], axis=2)[:, :, None, :]
    return chunks, listed.reshape(rows, nb * nb), seg_cols, seg_rows


def lane_low(rows):
    return lax.broadcasted_iota(jnp.int32, (rows, 128), 1) < HD


def diag128(dup_t):
    row = lax.broadcasted_iota(jnp.int32, (128, 128), 0) < HD
    col = lax.broadcasted_iota(jnp.int32, (128, 128), 1) < HD
    return jnp.where(row == col, dup_t, jnp.zeros_like(dup_t))


def transposed_twice(tile):
    both = jnp.concatenate([tile, tile], axis=0)
    return both.T


def head_rows(acc):
    turned = jnp.concatenate([acc, acc], axis=0).T
    return jnp.where(lane_low(HD), turned[:HD], turned[HD:])


def pick_diag(full, half):
    lanes = slice(half * 128, half * 128 + 128)
    top = full[half * 128 : half * 128 + HD, lanes]
    low = full[half * 128 + HD : half * 128 + 128, lanes]
    return jnp.where(lane_low(HD), top, low)


def chunk_ids(list_ref, row, base, nb):
    ids = [list_ref[row, base + j] for j in range(CHUNK)]
    safe = [jnp.where(b == nb, 0, b) for b in ids]
    return ids, safe


def block_rows(ref, blocks, lanes):
    return jnp.concatenate(
        [ref[0, pl.ds(pl.multiple_of(b * BLK, BLK), BLK), lanes] for b in blocks], axis=0
    )


def turned_blocks(ref, blocks, rows):
    low = lane_low(rows.stop - rows.start)
    tiles = [ref[b, rows, :] for b in blocks]
    return jnp.concatenate(
        [jnp.where(low, tiles[i], tiles[i + 1]) for i in range(0, CHUNK, 2)], axis=1
    )


def turn_all(src_ref, dst_ref, nb, width):
    def body(b, _):
        start = pl.multiple_of(b * BLK, BLK)
        for t in range(width // 128):
            tile = src_ref[0, pl.ds(start, BLK), t * 128 : t * 128 + 128]
            dst_ref[b, t * 128 : t * 128 + 128, :] = transposed_twice(tile)
        return 0

    lax.fori_loop(0, nb, body, 0)


def dot_f32(left, right):
    return lax.dot_general(
        left, right, (((1,), (0,)), ((), ())), preferred_element_type=jnp.float32
    )


def forward_kernel(group, n_ref, list_ref, q_ref, k_ref, v_ref, segc_ref, segr_ref,
                   o_ref, lse_ref, vt_ref, qst_ref, m_ref, l_ref, acc_ref):
    row = pl.program_id(0)
    width = q_ref.shape[2]
    nb = q_ref.shape[1] // BLK
    groups, halves = width // group, group // 128
    turn_all(v_ref, vt_ref, nb, width)
    qst_ref[...] = jnp.zeros_like(qst_ref)

    def per_query(a, _):
        start = pl.multiple_of(a * BLK, BLK)
        for t in range(width // 128):
            tile = q_ref[0, pl.ds(start, BLK), t * 128 : t * 128 + 128] * 0.125
            g, u = t // halves, t % halves
            qst_ref[g, u * 128 : u * 128 + 128, u * 128 : u * 128 + 128] = diag128(
                transposed_twice(tile.astype(jnp.bfloat16))
            )
        seg_q = segr_ref[0, a]
        m_ref[...] = jnp.full_like(m_ref, NEG)
        l_ref[...] = jnp.zeros_like(l_ref)
        acc_ref[...] = jnp.zeros_like(acc_ref)

        def per_chunk(c, _):
            ids, safe = chunk_ids(list_ref, row, a * nb + c * CHUNK, nb)
            seg_k = block_rows(segc_ref, ids, slice(0, 128))
            allowed = seg_k == seg_q
            for g in range(groups):
                lanes = slice(g * group, g * group + group)
                s_t = dot_f32(block_rows(k_ref, safe, lanes), qst_ref[g])
                weights, alphas = [], []
                for u in range(halves):
                    t = g * halves + u
                    s = jnp.where(allowed, s_t[:, u * 128 : u * 128 + 128], NEG)
                    m_old = m_ref[t]
                    m_new = jnp.maximum(m_old, jnp.max(s, axis=0, keepdims=True))
                    p = jnp.exp(s - m_new)
                    alpha = jnp.exp(m_old - m_new)
                    l_ref[t] = alpha * l_ref[t] + jnp.sum(p, axis=0, keepdims=True)
                    m_ref[t] = m_new
                    weights.append(p.astype(jnp.bfloat16))
                    alphas.append(alpha)
                p_t = jnp.concatenate(weights, axis=1) if halves > 1 else weights[0]
                o_t = dot_f32(turned_blocks(vt_ref, safe, lanes), p_t)
                for u in range(halves):
                    t = g * halves + u
                    acc_ref[t] = alphas[u] * acc_ref[t] + pick_diag(o_t, u)
            return 0

        lax.fori_loop(0, n_ref[row, a], per_chunk, 0)
        for t in range(width // 128):
            total = l_ref[t]
            out = acc_ref[t] / total
            o_ref[0, pl.ds(start, BLK), t * 128 : t * 128 + 128] = head_rows(out).astype(
                jnp.bfloat16
            )
            lse_ref[0, a, :, t * 128 : t * 128 + 128] = m_ref[t] + jnp.log(total)
        return 0

    lax.fori_loop(0, nb, per_query, 0)


def group_of(width):
    return 256 if width % 256 == 0 else 128


def whole_spec(shape):
    rest = (0,) * (len(shape) - 1)
    return pl.BlockSpec((1,) + tuple(shape[1:]), lambda r, *_: (r,) + rest)


def one_spec(shape):
    rest = (0,) * (len(shape) - 1)
    return pl.BlockSpec((1,) + tuple(shape[1:]), lambda r, *_: (r,) + rest,
                        pipeline_mode=pl.Buffered(1))


def attention_forward(q, k, v, plan):
    chunks, listed, seg_cols, seg_rows = plan
    rows, full_len, width = q.shape
    nb, group = full_len // BLK, group_of(width)
    tiles = width // 128
    pairs = rows * full_len * full_len // 4 * width
    args = (q, k, v, seg_cols, seg_rows)
    return pl.pallas_call(
        functools.partial(forward_kernel, group),
        out_shape=(
            jax.ShapeDtypeStruct((rows, full_len, width), jnp.bfloat16),
            jax.ShapeDtypeStruct((rows, nb, 1, width), jnp.float32),
        ),
        grid_spec=pltpu.PrefetchScalarGridSpec(
            num_scalar_prefetch=2,
            grid=(rows,),
            in_specs=[one_spec(x.shape) for x in args],
            out_specs=(one_spec((rows, full_len, width)), one_spec((rows, nb, 1, width))),
            scratch_shapes=[
                pltpu.VMEM((nb, width, 128), jnp.bfloat16),
                pltpu.VMEM((width // group, group, group), jnp.bfloat16),
                pltpu.VMEM((tiles, 1, 128), jnp.float32),
                pltpu.VMEM((tiles, 1, 128), jnp.float32),
                pltpu.VMEM((tiles, HD, 128), jnp.float32),
            ],
        ),
        compiler_params=pltpu.CompilerParams(vmem_limit_bytes=48 << 20),
        cost_estimate=pl.CostEstimate(
            flops=64 * pairs, transcendentals=pairs // HD, bytes_accessed=8 * q.size
        ),
        name="attention_forward",
    )(chunks, listed, *args)


def backward_kernel(group, n_ref, list_ref, q_ref, k_ref, v_ref, o_ref, do_ref, lse_ref,
                    segc_ref, segr_ref, dq_ref, dk_ref, dv_ref,
                    kt_ref, qst_ref, qs_ref, dost_ref, dos_ref, delta_ref, acc_ref,
                    dk_acc, dv_acc):
    row = pl.program_id(0)
    full_len, width = q_ref.shape[1], q_ref.shape[2]
    nb = full_len // BLK
    groups, halves = width // group, group // 128
    turn_all(k_ref, kt_ref, nb, width)
    for ref in (qst_ref, qs_ref, dost_ref, dos_ref, dk_acc, dv_acc):
        ref[...] = jnp.zeros_like(ref)
    low = lane_low(HD)

    def per_query(a, _):
        start = pl.multiple_of(a * BLK, BLK)
        for t in range(width // 128):
            g, u = t // halves, t % halves
            lanes = slice(t * 128, t * 128 + 128)
            square = slice(u * 128, u * 128 + 128)
            q_tile = (q_ref[0, pl.ds(start, BLK), lanes] * 0.125).astype(jnp.bfloat16)
            g_tile = do_ref[0, pl.ds(start, BLK), lanes]
            o_tile = o_ref[0, pl.ds(start, BLK), lanes]
            g_turn = transposed_twice(g_tile)
            qst_ref[g, square, square] = diag128(transposed_twice(q_tile))
            dost_ref[g, square, square] = diag128(g_turn)
            qs_ref[g, square, square] = diag128(jnp.concatenate([q_tile, q_tile], axis=0))
            dos_ref[g, square, square] = diag128(jnp.concatenate([g_tile, g_tile], axis=0))
            product = g_turn.astype(jnp.float32) * transposed_twice(o_tile).astype(jnp.float32)
            delta_ref[t] = jnp.where(
                low[:1],
                jnp.sum(product[:HD], axis=0, keepdims=True),
                jnp.sum(product[HD:], axis=0, keepdims=True),
            )
        seg_q = segr_ref[0, a]
        acc_ref[...] = jnp.zeros_like(acc_ref)

        def per_chunk(c, _):
            ids, safe = chunk_ids(list_ref, row, a * nb + c * CHUNK, nb)
            seg_k = block_rows(segc_ref, ids, slice(0, 128))
            allowed = seg_k == seg_q
            for g in range(groups):
                lanes = slice(g * group, g * group + group)
                s_t = dot_f32(block_rows(k_ref, safe, lanes), qst_ref[g])
                dp_t = dot_f32(block_rows(v_ref, safe, lanes), dost_ref[g])
                p_parts, ds_parts = [], []
                for u in range(halves):
                    t = g * halves + u
                    half = slice(u * 128, u * 128 + 128)
                    lse = lse_ref[0, a, :, t * 128 : t * 128 + 128]
                    p = jnp.exp(jnp.where(allowed, s_t[:, half], NEG) - lse)
                    ds = p * (dp_t[:, half] - delta_ref[t])
                    p_parts.append(p.astype(jnp.bfloat16))
                    ds_parts.append(ds.astype(jnp.bfloat16))
                p_t = jnp.concatenate(p_parts, axis=1) if halves > 1 else p_parts[0]
                ds_t = jnp.concatenate(ds_parts, axis=1) if halves > 1 else ds_parts[0]
                dv = dot_f32(p_t, dos_ref[g])
                dk = dot_f32(ds_t, qs_ref[g])
                dq_t = dot_f32(turned_blocks(kt_ref, safe, lanes), ds_t)
                for j in range(CHUNK):
                    where = pl.ds(pl.multiple_of(safe[j] * BLK, BLK), BLK)
                    part = slice(j * BLK, j * BLK + BLK)
                    dv_acc[where, lanes] += dv[part]
                    dk_acc[where, lanes] += dk[part]
                for u in range(halves):
                    acc_ref[g * halves + u] += pick_diag(dq_t, u)
            return 0

        lax.fori_loop(0, n_ref[row, a], per_chunk, 0)
        for t in range(width // 128):
            dq_ref[0, pl.ds(start, BLK), t * 128 : t * 128 + 128] = (
                head_rows(acc_ref[t]) * 0.125
            ).astype(jnp.bfloat16)
        return 0

    lax.fori_loop(0, nb, per_query, 0)

    def flush(a, _):
        where = pl.ds(pl.multiple_of(a * BLK, BLK), BLK)
        dk_ref[0, where, :] = dk_acc[where, :].astype(jnp.bfloat16)
        dv_ref[0, where, :] = dv_acc[where, :].astype(jnp.bfloat16)
        return 0

    lax.fori_loop(0, nb, flush, 0)


def attention_backward(q, k, v, o, do, lse, plan):
    chunks, listed, seg_cols, seg_rows = plan
    rows, full_len, width = q.shape
    nb, group = full_len // BLK, group_of(width)
    tiles, groups = width // 128, width // group
    pairs = rows * full_len * full_len // 4 * width
    args = (q, k, v, o, do, lse, seg_cols, seg_rows)
    like = jax.ShapeDtypeStruct((rows, full_len, width), jnp.bfloat16)
    square = pltpu.VMEM((groups, group, group), jnp.bfloat16)
    return pl.pallas_call(
        functools.partial(backward_kernel, group),
        out_shape=(like, like, like),
        grid_spec=pltpu.PrefetchScalarGridSpec(
            num_scalar_prefetch=2,
            grid=(rows,),
            in_specs=[one_spec(x.shape) for x in args],
            out_specs=tuple(one_spec(like.shape) for _ in range(3)),
            scratch_shapes=[
                pltpu.VMEM((nb, width, 128), jnp.bfloat16),
                square, square, square, square,
                pltpu.VMEM((tiles, 1, 128), jnp.float32),
                pltpu.VMEM((tiles, HD, 128), jnp.float32),
                pltpu.VMEM((full_len, width), jnp.float32),
                pltpu.VMEM((full_len, width), jnp.float32),
            ],
        ),
        compiler_params=pltpu.CompilerParams(vmem_limit_bytes=58 << 20),
        cost_estimate=pl.CostEstimate(
            flops=100 * pairs, transcendentals=pairs // HD, bytes_accessed=16 * q.size
        ),
        name="attention_backward",
    )(chunks, listed, *args)


def pair_bit(index, bit):
    return lax.rem(index // (1 << bit), 2)


def pair_of(index, bit):
    return index + (1 - 2 * pair_bit(index, bit)) * (1 << bit)


def all_arrived(bits):
    me = lax.axis_index("fsdp")
    barrier = pltpu.get_barrier_semaphore()
    for bit in range(bits):
        pl.semaphore_signal(
            barrier, inc=1, device_id={"fsdp": pair_of(me, bit)},
            device_id_type=pl.DeviceIdType.MESH,
        )
    pl.semaphore_signal(
        barrier, inc=1, device_id={"seq": 1 - lax.axis_index("seq")},
        device_id_type=pl.DeviceIdType.MESH,
    )
    pl.semaphore_wait(barrier, bits + 1)


def qkv_backward_kernel(
    bits, x_in, dq_in, dk_in, dv_in, w_in, res_in, small_in,
    wq_out, wk_out, wv_out, small_out, tok_out,
    x, xt, grads, w, wt, res, tok, kept, sends, lands, final, small, small_land, result,
    in_sem, tok_send, tok_land, own_sem, send_sem, land_sem, x_send, x_land,
    small_send, small_recv, out_sem,
):
    me, side = lax.axis_index("fsdp"), lax.axis_index("seq")
    half = tok.shape[2] * tok.shape[1]
    piece, pieces = tok.shape[2], tok.shape[1]
    own, width = wq_out.shape
    owners = 1 << bits
    sources = (dq_in, dk_in, dv_in)
    loads = [
        pltpu.make_async_copy(w_in, w, in_sem.at[0]),
        pltpu.make_async_copy(res_in, res, in_sem.at[1]),
        pltpu.make_async_copy(small_in, small.at[0], in_sem.at[2]),
        pltpu.make_async_copy(x_in, x, in_sem.at[3]),
    ] + [pltpu.make_async_copy(sources[i], grads.at[i], in_sem.at[4 + i]) for i in range(3)]
    for i in (0, 3, 4, 5, 6, 1, 2):
        loads[i].start()
    all_arrived(bits)
    loads[0].wait()
    for i in range(3):
        first = part_start(width, i)
        wt[i * width : (i + 1) * width, :] = w[:, first : first + width].T
    loads[3].wait()

    def turn(r, _):
        xt[r] = x[pl.ds(pl.multiple_of(r * piece, piece), piece), :].T
        return 0

    lax.fori_loop(0, 2 * pieces, turn, 0)
    for i in (4, 5, 6, 1):
        loads[i].wait()

    def token_rows(start):
        total = res[pl.ds(start, piece), :].astype(jnp.float32)
        for i in range(3):
            total = total + dot_f32(
                grads[i, pl.ds(start, piece), :], wt[i * width : (i + 1) * width, :]
            )
        return total.astype(jnp.bfloat16)

    def sent(i):
        return pltpu.make_async_remote_copy(
            src_ref=tok.at[0, i],
            dst_ref=tok_out.at[side, pl.ds(pl.multiple_of(i * piece, piece), piece)],
            send_sem=tok_send.at[i], recv_sem=tok_land.at[i],
            device_id={"seq": 1 - side}, device_id_type=pl.DeviceIdType.MESH,
        )

    def landed(i):
        return pltpu.make_async_remote_copy(
            src_ref=tok.at[0, i],
            dst_ref=tok_out.at[1 - side, pl.ds(pl.multiple_of(i * piece, piece), piece)],
            send_sem=tok_send.at[i], recv_sem=tok_land.at[i],
            device_id={"seq": 1 - side}, device_id_type=pl.DeviceIdType.MESH,
        )

    def stays(i):
        return pltpu.make_async_copy(
            tok.at[1, i],
            tok_out.at[side, pl.ds(pl.multiple_of(i * piece, piece), piece)],
            own_sem.at[i],
        )

    def send_piece(i, _):
        start = pl.multiple_of((1 - side) * half + i * piece, piece)
        tok[0, i] = token_rows(start)
        sent(i).start()
        return 0

    lax.fori_loop(0, pieces, send_piece, 0)

    def keep_piece(i, _):
        start = pl.multiple_of(side * half + i * piece, piece)
        tok[1, i] = token_rows(start)
        stays(i).start()
        return 0

    low_bit = pair_bit(me, 0) == 0
    tile = 8 if owners % 8 == 0 else owners
    first_of = [0]
    for bit in range(bits):
        first_of.append(first_of[-1] + (owners >> (bit + 1)))

    def weights(i):
        def rows(m, _):
            rows_here = pl.ds(pl.multiple_of(m * tile * own, tile * own), tile * own)
            block = dot_f32(
                jnp.concatenate([xt[r, rows_here, :] for r in range(2 * pieces)], axis=1), grads[i]
            ).reshape(tile // 2, 2, own, width)
            even, odd = block[:, 0], block[:, 1]
            spot = pl.ds(m * (tile // 2), tile // 2)
            kept[i, spot] = jnp.where(low_bit, even, odd)
            sends[i, spot] = jnp.where(low_bit, odd, even).astype(jnp.bfloat16)
            return 0

        lax.fori_loop(0, owners // tile, rows, 0)

    def hop(i, bit):
        count = owners >> (bit + 1)
        spot = pl.ds(first_of[bit], count)
        return pltpu.make_async_remote_copy(
            src_ref=sends.at[i, spot], dst_ref=lands.at[i, spot],
            send_sem=send_sem.at[i, bit], recv_sem=land_sem.at[i, bit],
            device_id={"fsdp": pair_of(me, bit)}, device_id_type=pl.DeviceIdType.MESH,
        )

    def cross(i):
        return pltpu.make_async_remote_copy(
            src_ref=final.at[0, i], dst_ref=final.at[1, i],
            send_sem=x_send.at[i], recv_sem=x_land.at[i],
            device_id={"seq": 1 - side}, device_id_type=pl.DeviceIdType.MESH,
        )

    def advance(i, bit):
        hop(i, bit).wait_recv()
        base = first_of[bit]
        if bit + 1 == bits:
            total = kept[i, base] + lands[i, base].astype(jnp.float32)
            final[0, i] = total.astype(jnp.bfloat16)
            cross(i).start()
            return
        nxt = pair_bit(me, bit + 1)

        def one(j, _):
            stay, go = 2 * j + nxt, 2 * j + 1 - nxt
            kept[i, first_of[bit + 1] + j] = kept[i, base + stay] + lands[
                i, base + stay
            ].astype(jnp.float32)
            sends[i, first_of[bit + 1] + j] = (
                kept[i, base + go] + lands[i, base + go].astype(jnp.float32)
            ).astype(jnp.bfloat16)
            return 0

        lax.fori_loop(0, owners >> (bit + 2), one, 0)
        hop(i, bit + 1).start()

    outs = (wq_out, wk_out, wv_out)

    def written(i):
        return pltpu.make_async_copy(result.at[i], outs[i], out_sem.at[i])

    def finish(i):
        cross(i).wait_recv()
        result[i] = final[0, i].astype(jnp.float32) + final[1, i].astype(jnp.float32)
        written(i).start()

    def small_hop(bit):
        where = {"fsdp": pair_of(me, bit)} if bit < bits else {"seq": 1 - side}
        return pltpu.make_async_remote_copy(
            src_ref=small.at[bit], dst_ref=small_land.at[bit],
            send_sem=small_send.at[bit], recv_sem=small_recv.at[bit],
            device_id=where, device_id_type=pl.DeviceIdType.MESH,
        )

    def small_advance(bit):
        small_hop(bit).wait_recv()
        small[bit + 1] = small[bit] + small_land[bit]
        if bit < bits:
            small_hop(bit + 1).start()

    loads[2].wait()
    weights(0)
    hop(0, 0).start()
    for spot, i in ((0, 0), (1, 2)):
        def column_sums(c, total):
            block = grads[i, pl.ds(pl.multiple_of(c * 128, 128), 128), :].astype(jnp.float32)
            return total + jnp.sum(block.reshape(16, 8, width), axis=0)

        total = lax.fori_loop(
            0, grads.shape[1] // 128, column_sums, jnp.zeros((8, width), jnp.float32)
        )
        small[0, spot : spot + 1] = jnp.sum(total, axis=0, keepdims=True)
    small_hop(0).start()
    weights(1)
    hop(1, 0).start()
    advance(0, 0)
    small_advance(0)
    weights(2)
    hop(2, 0).start()
    plan = []
    for step in range(1, bits + 2):
        todo = []
        for i in range(3):
            bit = step - i
            if 0 <= bit < bits:
                todo.append((i, bit))
        plan.append((todo, step))
    done = 0
    for todo, step in plan:
        for i, bit in todo:
            advance(i, bit)
        if step <= bits:
            small_advance(step)
        if done < pieces:
            keep_piece(done, 0)
            done += 1
    for i in range(3):
        finish(i)
    small_copy = pltpu.make_async_copy(small.at[bits + 1], small_out, out_sem.at[3])
    small_copy.start()
    while done < pieces:
        keep_piece(done, 0)
        done += 1
    for i in range(3):
        written(i).wait()
        cross(i).wait_send()
        for bit in range(bits):
            hop(i, bit).wait_send()
    for bit in range(bits + 1):
        small_hop(bit).wait_send()
    small_copy.wait()
    for i in range(pieces):
        stays(i).wait()
        sent(i).wait_send()
        landed(i).wait_recv()


def qkv_backward(x, dq, dk, dv, w, resid, small, own):
    tokens, width = dq.shape
    bits = lax.axis_size("fsdp").bit_length() - 1
    owners = 1 << bits
    pieces = 4
    piece = tokens // 2 // pieces
    dma = pltpu.SemaphoreType.DMA
    f32, bf16 = jnp.float32, jnp.bfloat16
    shard = jax.ShapeDtypeStruct((own, width), f32)
    anywhere = pl.BlockSpec(memory_space=pl.ANY)
    return pl.pallas_call(
        functools.partial(qkv_backward_kernel, bits),
        out_shape=(
            shard, shard, shard,
            jax.ShapeDtypeStruct(small.shape, f32),
            jax.ShapeDtypeStruct((2, tokens // 2, width), bf16),
        ),
        in_specs=[anywhere] * 7,
        out_specs=(anywhere,) * 5,
        scratch_shapes=[
            pltpu.VMEM((tokens, width), bf16),
            pltpu.VMEM((2 * pieces, width, piece), bf16),
            pltpu.VMEM((3, tokens, width), bf16),
            pltpu.VMEM(w.shape, bf16),
            pltpu.VMEM((3 * width, width), bf16),
            pltpu.VMEM((tokens, width), bf16),
            pltpu.VMEM((2, pieces, piece, width), bf16),
            pltpu.VMEM((3, owners - 1, own, width), f32),
            pltpu.VMEM((3, owners - 1, own, width), bf16),
            pltpu.VMEM((3, owners - 1, own, width), bf16),
            pltpu.VMEM((2, 3, own, width), bf16),
            pltpu.VMEM((bits + 2,) + small.shape, f32),
            pltpu.VMEM((bits + 1,) + small.shape, f32),
            pltpu.VMEM((3, own, width), f32),
            dma((7,)), dma((pieces,)), dma((pieces,)), dma((pieces,)),
            dma((3, bits)), dma((3, bits)), dma((3,)), dma((3,)),
            dma((bits + 1,)), dma((bits + 1,)), dma((4,)),
        ],
        compiler_params=pltpu.CompilerParams(
            collective_id=1, has_side_effects=True, vmem_limit_bytes=60 << 20
        ),
        cost_estimate=pl.CostEstimate(
            flops=40 * tokens * width * width, transcendentals=0,
            bytes_accessed=16 * tokens * width,
        ),
        name="qkv_backward",
    )(x, dq, dk, dv, w, resid, small)


def qkv_forward_kernel(
    bits, tokens_in, own_in,
    x_out, q_out, k_out, v_out, w_out, small_out,
    x, w, qkv, small,
    own_sem, tok_send, tok_land, load_sem, send_sem, land_sem, x_sem, out_sem, w_sem, small_sem,
):
    me, side = lax.axis_index("fsdp"), lax.axis_index("seq")
    pieces, piece, width = x.shape[1], x.shape[2], x.shape[3]
    mine = [pair_bit(me, bit) for bit in range(bits)]
    columns = part_columns(width)
    outs = (q_out, k_out, v_out)

    def slot(bit, part):
        here = [slice(None)] * (bits - 1 - bit) + [mine[b] for b in range(bit, -1, -1)]
        return tuple(here) + (slice(None), columns[part])

    own_tokens = pltpu.make_async_copy(tokens_in.at[side], x.at[side], own_sem.at[0])
    own_tokens.start()

    def load(part):
        spot = tuple(mine[b] for b in range(bits - 1, -1, -1)) + (slice(None), columns[part])
        return pltpu.make_async_copy(
            own_in.at[:, columns[part]], w.at[spot], load_sem.at[part]
        )

    for part in range(3):
        load(part).start()
    all_arrived(bits)

    def sent(i):
        return pltpu.make_async_remote_copy(
            src_ref=tokens_in.at[1 - side, i], dst_ref=x.at[side, i],
            send_sem=tok_send.at[i], recv_sem=tok_land.at[i],
            device_id={"seq": 1 - side}, device_id_type=pl.DeviceIdType.MESH,
        )

    def landed(i):
        return pltpu.make_async_remote_copy(
            src_ref=tokens_in.at[1 - side, i], dst_ref=x.at[1 - side, i],
            send_sem=tok_send.at[i], recv_sem=tok_land.at[i],
            device_id={"seq": 1 - side}, device_id_type=pl.DeviceIdType.MESH,
        )

    def hop(part, turn):
        bit = bits - 1 - turn
        return pltpu.make_async_remote_copy(
            src_ref=w.at[slot(bit, part)], dst_ref=w.at[slot(bit, part)],
            send_sem=send_sem.at[part, turn], recv_sem=land_sem.at[part, turn],
            device_id={"fsdp": pair_of(me, bit)}, device_id_type=pl.DeviceIdType.MESH,
        )

    for part in range(3):
        load(part).wait()
        hop(part, 0).start()
    for i in range(pieces):
        sent(i).start()

    def x_copy(half, i):
        return pltpu.make_async_copy(x.at[half, i], x_out.at[half, i], x_sem.at[half, i])

    def out_copy(part, half, i):
        return pltpu.make_async_copy(
            qkv.at[part, half, i], outs[part].at[half, i], out_sem.at[part, half, i]
        )

    def w_copy(part):
        spot = (slice(None),) * (bits + 1) + (columns[part],)
        return pltpu.make_async_copy(w.at[spot], w_out.at[spot], w_sem.at[part])

    def project(part, half, i):
        first = part_start(width, part)
        spot = (slice(None),) * (bits + 1) + (slice(first, first + width),)
        total = dot_f32(x[half, i], w[spot].reshape(width, width))
        if part == 0:
            total = total + small[0:1, :]
        if part == 2:
            total = total + small[1:2, :]
        qkv[part, half, i] = total.astype(jnp.bfloat16)
        out_copy(part, half, i).start()

    def each_own(part):
        def one(i, _):
            project(part, side, i)
            return 0

        lax.fori_loop(0, pieces, one, 0)

    def arrived(part):
        w_copy(part).start()
        if part == 0:
            spot = (slice(None),) * (bits + 1) + (slice(width, width + 128),)
            turned = w[spot].reshape(width, 128).astype(jnp.float32).T
            small[...] = turned[: small.shape[0]]
            pltpu.make_async_copy(small, small_out, small_sem.at[0]).start()
            own_tokens.wait()
        each_own(part)

    for step in range(bits + 2):
        full = None
        for part in range(3):
            turn = step - part
            if 0 <= turn < bits:
                hop(part, turn).wait_recv()
                if turn + 1 < bits:
                    hop(part, turn + 1).start()
                else:
                    full = part
        if full is not None:
            arrived(full)
    for i in range(pieces):
        x_copy(side, i).start()

    def other(i, _):
        landed(i).wait_recv()
        x_copy(1 - side, i).start()
        for part in range(3):
            project(part, 1 - side, i)
        return 0

    lax.fori_loop(0, pieces, other, 0)
    for i in range(pieces):
        sent(i).wait_send()
    for part in range(3):
        w_copy(part).wait()
        for turn in range(bits):
            hop(part, turn).wait_send()
    pltpu.make_async_copy(small, small_out, small_sem.at[0]).wait()
    for half in range(2):
        for i in range(pieces):
            x_copy(half, i).wait()
            for part in range(3):
                out_copy(part, half, i).wait()


def part_start(width, part):
    return part * width + (128 if part else 0)


def part_columns(width):
    return (
        slice(0, width + 128),
        slice(width + 128, 2 * width + 128),
        slice(2 * width + 128, 3 * width + 128),
    )


def qkv_forward(tokens_in, own_pack):
    rows, local, width = tokens_in.shape
    own, columns = own_pack.shape
    bits = lax.axis_size("fsdp").bit_length() - 1
    pieces = 4
    piece = local // pieces
    dma = pltpu.SemaphoreType.DMA
    bf16 = jnp.bfloat16
    halves = (2, pieces, piece, width)
    gathered = (2,) * bits + (own, columns)
    anywhere = pl.BlockSpec(memory_space=pl.ANY)
    like = jax.ShapeDtypeStruct(halves, bf16)
    x, q, k, v, weights, small = pl.pallas_call(
        functools.partial(qkv_forward_kernel, bits),
        out_shape=(
            like, like, like, like,
            jax.ShapeDtypeStruct(gathered, bf16),
            jax.ShapeDtypeStruct((SMALL_ROWS, width), jnp.float32),
        ),
        in_specs=[anywhere] * 2,
        out_specs=(anywhere,) * 6,
        scratch_shapes=[
            pltpu.VMEM(halves, bf16),
            pltpu.VMEM(gathered, bf16),
            pltpu.VMEM((3,) + halves, bf16),
            pltpu.VMEM((SMALL_ROWS, width), jnp.float32),
            dma((1,)), dma((pieces,)), dma((pieces,)), dma((3,)),
            dma((3, bits)), dma((3, bits)), dma((2, pieces)), dma((3, 2, pieces)),
            dma((3,)), dma((1,)),
        ],
        compiler_params=pltpu.CompilerParams(
            collective_id=2, has_side_effects=True, vmem_limit_bytes=30 << 20
        ),
        cost_estimate=pl.CostEstimate(
            flops=18 * rows * local * width * width, transcendentals=0,
            bytes_accessed=16 * rows * local * width,
        ),
        name="qkv_forward",
    )(tokens_in.reshape(halves), own_pack)
    flat = rows * local, width
    return (
        x.reshape(flat), q.reshape(flat), k.reshape(flat), v.reshape(flat),
        weights.reshape(-1, columns), small,
    )


eps_norm = 1e-06


def dot_rows(left, right):
    return lax.dot_general(
        left, right, (((0,), (0,)), ((), ())), preferred_element_type=jnp.float32
    )


def dot_nt(left, right):
    return lax.dot_general(
        left, right, (((1,), (1,)), ((), ())), preferred_element_type=jnp.float32
    )


def row_mean(values):
    return jnp.mean(values, axis=-1, keepdims=True)


GELU_K = math.sqrt(2.0 / math.pi)
GELU_A = 0.044715


def gelu_pair(u):
    square = u * u
    t = jnp.tanh(u * (GELU_K + (GELU_K * GELU_A) * square))
    half = 0.5 + 0.5 * t
    slope = half + (u * (half * (1.0 - t))) * (GELU_K + (3.0 * GELU_K * GELU_A) * square)
    return u * half, slope


OUT_B, GAIN_1, BIAS_1, OUTER_B, GAIN_2, BIAS_2, INNER_B = 2, 3, 4, 5, 6, 7, 8
STEP_ROWS = 64
SMALL_ROWS = 16


def middle_kernel(
    chunks, weights_in, small, att, tokens, cotangent,
    out, d_attn, d_att, d_weights, sums,
    w, acc, act, slope, z_one, flow, rs_one, normed, normed_t, d_mlp, load_sem, store_sem,
):
    step, steps = pl.program_id(0), pl.num_programs(0)
    rows, width = att.shape
    f32, bf16 = jnp.float32, jnp.bfloat16
    count = 2 * chunks + 1

    def load(i):
        return pltpu.make_async_copy(
            weights_in.at[:, pl.ds(i * width, width)], w.at[i], load_sem.at[i]
        )

    def store(i):
        return pltpu.make_async_copy(
            w.at[i], d_weights.at[:, pl.ds(i * width, width)], store_sem.at[i]
        )

    @pl.when(step == 0)
    def _():
        for i in range(count):
            load(i).start()
        sums[...] = jnp.zeros_like(sums)

        def clear(i, _):
            acc[i] = jnp.zeros_like(acc[i])
            return 0

        lax.fori_loop(0, count, clear, 0)
        for i in range(count):
            load(i).wait()

    def vector(i):
        return small[i : i + 1, :]

    def add_sum(i, values):
        sums[pl.ds(i, 1), :] += jnp.sum(values, axis=0, keepdims=True)

    def by_rows(body):
        def one(r, _):
            body(pl.ds(pl.multiple_of(r * STEP_ROWS, STEP_ROWS), STEP_ROWS))
            return 0

        lax.fori_loop(0, rows // STEP_ROWS, one, 0)

    flow[...] = dot_f32(att[...], w[0])

    def norm_one(r):
        attn = flow[r, :] + vector(OUT_B)
        resid = tokens[r, :].astype(f32) + attn
        add_sum(INNER_B + chunks, resid * resid)
        add_sum(INNER_B + chunks + 1, attn * attn)
        centred = resid - row_mean(resid)
        scale = lax.rsqrt(row_mean(centred * centred) + eps_norm)
        z = centred * scale
        z_one[r, :] = z
        rs_one[r, :] = scale
        normed[r, :] = (z * vector(GAIN_1) + vector(BIAS_1)).astype(bf16)

    by_rows(norm_one)
    normed_t[...] = normed[...].T

    def inner(c, _):
        for n in range(width // 256):
            cols = slice(n * 256, n * 256 + 256)
            pre = dot_f32(normed[...], w[1 + c, :, cols]) + small[pl.ds(INNER_B + c, 1), cols]
            value, grade = gelu_pair(pre)
            act[c, :, cols] = value.astype(bf16)
            slope[c, :, cols] = grade.astype(bf16)
        return 0

    lax.fori_loop(0, chunks, inner, 0)
    flow[...] = dot_f32(act[0], w[1 + chunks])

    def outer(c, _):
        flow[...] += dot_f32(act[c], w[1 + chunks + c])
        return 0

    lax.fori_loop(1, chunks, outer, 0)

    def norm_two(r):
        mlp = flow[r, :] + vector(OUTER_B)
        add_sum(INNER_B + chunks + 2, mlp * mlp)
        resid = z_one[r, :] * vector(GAIN_1) + vector(BIAS_1) + mlp
        centred = resid - row_mean(resid)
        scale = lax.rsqrt(row_mean(centred * centred) + eps_norm)
        z = centred * scale
        out[r, :] = (z * vector(GAIN_2) + vector(BIAS_2)).astype(bf16)
        grad = cotangent[r, :].astype(f32)
        add_sum(GAIN_2, grad * z)
        add_sum(BIAS_2, grad)
        grad = grad * vector(GAIN_2)
        d_resid = scale * (grad - row_mean(grad) - z * row_mean(grad * z))
        low = d_resid.astype(bf16)
        add_sum(OUTER_B, low.astype(f32))
        d_mlp[r, :] = low
        flow[r, :] = d_resid

    by_rows(norm_two)

    def back(c, _):
        for n in range(width // 256):
            cols = slice(n * 256, n * 256 + 256)
            d_act = dot_nt(d_mlp[...], w[1 + chunks + c, cols, :])
            d_pre = (slope[c, :, cols].astype(f32) * d_act).astype(bf16)
            sums[pl.ds(INNER_B + c, 1), cols] += jnp.sum(
                d_pre.astype(f32), axis=0, keepdims=True
            )
            slope[c, :, cols] = d_pre
        acc[1 + chunks + c] += dot_rows(act[c], d_mlp[...])
        acc[1 + c] += dot_f32(normed_t[...], slope[c])
        flow[...] += dot_nt(slope[c], w[1 + c])

        @pl.when(step == steps - 1)
        def _():
            for i in (1 + c, 1 + chunks + c):
                w[i] = acc[i].astype(bf16)
                store(i).start()

        return 0

    lax.fori_loop(0, chunks, back, 0)

    def norm_one_back(r):
        grad = flow[r, :]
        z = z_one[r, :]
        add_sum(GAIN_1, grad * z)
        add_sum(BIAS_1, grad)
        grad = grad * vector(GAIN_1)
        d_resid = rs_one[r, :] * (grad - row_mean(grad) - z * row_mean(grad * z))
        low = d_resid.astype(bf16)
        add_sum(OUT_B, low.astype(f32))
        d_attn[r, :] = low

    by_rows(norm_one_back)
    acc[0] += dot_rows(att[...], d_attn[...])
    d_att[...] = dot_nt(d_attn[...], w[0]).astype(bf16)

    @pl.when(step == steps - 1)
    def _():
        w[0] = acc[0].astype(bf16)
        store(0).start()
        for i in range(count):
            store(i).wait()


def middle(weights, small, att, tokens, cotangent):
    tok_count, width = att.shape
    chunks = (weights.shape[1] // width - 1) // 2
    count = 2 * chunks + 1
    rows = 512
    f32, bf16 = jnp.float32, jnp.bfloat16
    tile = pl.BlockSpec((rows, width), lambda i: (i, 0))
    fixed = pl.BlockSpec(small.shape, lambda i: (0, 0), pipeline_mode=pl.Buffered(1))
    anywhere = pl.BlockSpec(memory_space=pl.ANY)
    like = jax.ShapeDtypeStruct((tok_count, width), bf16)
    flops = 6 * tok_count * width * width * count
    return pl.pallas_call(
        functools.partial(middle_kernel, chunks),
        grid=(tok_count // rows,),
        out_shape=(
            like, like, like,
            jax.ShapeDtypeStruct(weights.shape, bf16),
            jax.ShapeDtypeStruct(small.shape, f32),
        ),
        in_specs=[anywhere, fixed, tile, tile, tile],
        out_specs=(tile, tile, tile, anywhere, pl.BlockSpec(small.shape, lambda i: (0, 0))),
        scratch_shapes=[
            pltpu.VMEM((count, width, width), bf16),
            pltpu.VMEM((count, width, width), f32),
            pltpu.VMEM((chunks, rows, width), bf16),
            pltpu.VMEM((chunks, rows, width), bf16),
            pltpu.VMEM((rows, width), f32),
            pltpu.VMEM((rows, width), f32),
            pltpu.VMEM((rows, 1), f32),
            pltpu.VMEM((rows, width), bf16),
            pltpu.VMEM((width, rows), bf16),
            pltpu.VMEM((rows, width), bf16),
            pltpu.SemaphoreType.DMA((count,)),
            pltpu.SemaphoreType.DMA((count,)),
        ],
        compiler_params=pltpu.CompilerParams(vmem_limit_bytes=62 << 20),
        cost_estimate=pl.CostEstimate(
            flops=2 * flops, transcendentals=tok_count * width * chunks,
            bytes_accessed=12 * tok_count * width + 4 * weights.size,
        ),
        name="middle",
    )(weights, small, att, tokens, cotangent)


def contract_rows(left, right):
    return lax.dot_general(
        left, right, (((0,), (0,)), ((), ())), preferred_element_type=jnp.float32
    )


def times_transpose(left, right):
    return lax.dot_general(
        left, right, (((1,), (1,)), ((), ())), preferred_element_type=jnp.float32
    )


def butterfly_sum(values, axis):
    size = lax.axis_size(axis)
    if size & (size - 1):
        return lax.psum(values, axis)
    step = 1
    while step < size:
        pairs = [(i, i ^ step) for i in range(size)]
        values = values + lax.ppermute(values, axis, pairs)
        step *= 2
    return values


def sum_seq(values):
    if lax.axis_size("seq") == 2:
        other = lax.ppermute(values, "seq", [(0, 1), (1, 0)])
        return values.astype(jnp.float32) + other.astype(jnp.float32)
    return lax.psum(values, "seq").astype(jnp.float32)


class Regroup:
    def __init__(self, row_count):
        self.size = lax.axis_size("seq")
        self.ways = math.gcd(row_count, self.size)
        self.parts = self.size // self.ways
        self.rows = row_count // self.ways
        me = lax.axis_index("seq")
        self.place = lax.rem(me, self.ways)
        self.row_group = me // self.parts

    def targets(self, turn):
        ways, parts = self.ways, self.parts
        return [
            (s, ((s % ways + turn) % ways) * parts + s // ways) for s in range(self.size)
        ]

    def move(self, values, pairs):
        if all(a == b for a, b in pairs):
            return values
        return lax.ppermute(values, "seq", pairs)

    def gather(self, values):
        rows, local, width = self.rows, values.shape[1], values.shape[2]
        out = jnp.zeros((rows, self.ways, local, width), values.dtype)
        for turn in range(self.ways):
            pick = lax.rem(self.place + turn, self.ways)
            chunk = lax.dynamic_slice_in_dim(values, pick * rows, rows, 0)
            chunk = self.move(chunk, self.targets(turn))
            spot = lax.rem(self.row_group - turn + self.ways, self.ways)
            out = lax.dynamic_update_slice_in_dim(out, chunk[:, None], spot, 1)
        return out.reshape(rows, self.ways * local, width)

    def scatter(self, values):
        rows, width = self.rows, values.shape[2]
        local = values.shape[1] // self.ways
        values = values.reshape(rows, self.ways, local, width)
        out = jnp.zeros((rows * self.ways, local, width), values.dtype)
        for turn in range(self.ways):
            spot = lax.rem(self.row_group - turn + self.ways, self.ways)
            chunk = lax.dynamic_slice_in_dim(values, spot, 1, 1)[:, 0]
            chunk = self.move(chunk, [(b, a) for a, b in self.targets(turn)])
            pick = lax.rem(self.place + turn, self.ways)
            out = lax.dynamic_update_slice_in_dim(out, chunk, pick * rows, 0)
        return out

    def pick_rows(self, values):
        return lax.dynamic_slice_in_dim(values, self.row_group * self.rows, self.rows, 0)

    def groups(self):
        return [
            [r * self.parts + j for j in range(self.parts)] for r in range(self.ways)
        ]

    def to_heads(self, values):
        if self.parts == 1:
            return values
        return lax.all_to_all(
            values, "seq", split_axis=2, concat_axis=1, tiled=True,
            axis_index_groups=self.groups(),
        )

    def from_heads(self, values):
        if self.parts == 1:
            return values
        return lax.all_to_all(
            values, "seq", split_axis=1, concat_axis=2, tiled=True,
            axis_index_groups=self.groups(),
        )


def shards(
    tokens_in,
    segment_ids,
    random_blocks,
    global_blocks,
    w_query,
    b_query,
    w_key,
    w_value,
    b_value,
    w_attn_out,
    b_attn_out,
    ln1_gain,
    ln1_bias,
    w_inner,
    b_inner,
    w_outer,
    b_outer,
    ln2_gain,
    ln2_bias,
    out_grad,
):
    row_count, local_len, width = tokens_in.shape
    seq_count = lax.axis_size("seq")
    fsdp_count = lax.axis_size("fsdp")
    tok_count = row_count * local_len
    own = w_query.shape[0]
    chunks = b_inner.shape[0] // own
    regroup = Regroup(row_count)
    paired = row_count == 2 and seq_count == 2 and fsdp_count & (fsdp_count - 1) == 0

    vectors = [b_query, b_value, b_attn_out, ln1_gain, ln1_bias, b_outer, ln2_gain, ln2_bias]
    columns = [x[:, None] for x in vectors] + [b_inner.reshape(own, chunks)]
    used = len(vectors) + chunks
    columns.append(jnp.zeros((own, 128 - used), jnp.bfloat16))
    first = jnp.concatenate([w_query] + columns + [w_key, w_value], axis=1)
    inner_own = w_inner.reshape(own, width, chunks).transpose(0, 2, 1).reshape(own, -1)
    second = jnp.concatenate([w_attn_out, inner_own, w_outer.reshape(own, -1)], axis=1)
    second = lax.all_gather(second, "fsdp", axis=0, tiled=True)
    plan = plan_blocks(
        regroup.pick_rows(segment_ids),
        regroup.pick_rows(random_blocks),
        regroup.pick_rows(global_blocks),
    )

    def split_rows(values):
        return values.reshape(regroup.rows, tok_count // regroup.rows, width)

    def part_of(values, i):
        return values[:, part_start(width, i) : part_start(width, i) + width]

    if paired:
        flat_in, *qkv, first, small = qkv_forward(tokens_in, first)
    else:
        first = lax.all_gather(first, "fsdp", axis=0, tiled=True)
        small = first[:, width : width + SMALL_ROWS].astype(jnp.float32).T
        flat_in = regroup.gather(tokens_in).reshape(tok_count, width)
        biases = (small[0], jnp.zeros_like(small[0]), small[1])
        qkv = [
            (jnp.dot(flat_in, part_of(first, i), preferred_element_type=jnp.float32)
             + biases[i]).astype(jnp.bfloat16)
            for i in range(3)
        ]
    q, out_grad = lax.optimization_barrier((qkv[0], out_grad))
    flat_grad = regroup.gather(out_grad).reshape(tok_count, width)
    q, k, v = (regroup.to_heads(split_rows(x)) for x in (q, qkv[1], qkv[2]))
    att, lse = attention_forward(q, k, v, plan)
    att_flat = regroup.from_heads(att).reshape(tok_count, width)
    out_tokens, d_attn, d_att, d_second, sums = middle(
        second, small, att_flat, flat_in, flat_grad
    )
    out_tokens = regroup.scatter(split_rows(out_tokens))

    def scattered(values):
        return lax.psum_scatter(values, "fsdp", scatter_dimension=0, tiled=True)

    d_second = scattered(d_second)
    dq, dk, dv = attention_backward(
        q, k, v, att, regroup.to_heads(split_rows(d_att)), lse, plan
    )
    dq, dk, dv = (regroup.from_heads(x).reshape(tok_count, width) for x in (dq, dk, dv))
    mine = lax.axis_index("fsdp")
    dq, out_tokens = lax.optimization_barrier((dq, out_tokens))
    if paired:
        d_query_w, d_key_w, d_value_w, sums, d_tokens_in = qkv_backward(
            flat_in, dq, dk, dv, first, d_attn, sums, own
        )
        d_second, sums = lax.optimization_barrier((d_second, sums))
    else:
        for spot, part in ((0, dq), (1, dv)):
            sums = sums.at[spot].set(jnp.sum(part.astype(jnp.float32), axis=0))
        sums = butterfly_sum(butterfly_sum(sums, "fsdp"), "seq")
        d_query_w, d_key_w, d_value_w = (
            sum_seq(scattered(contract_rows(flat_in, x).astype(jnp.bfloat16)))
            for x in (dq, dk, dv)
        )
        d_tokens = d_attn.astype(jnp.float32)
        for i, part in enumerate((dq, dk, dv)):
            d_tokens = d_tokens + times_transpose(part, part_of(first, i))
        d_tokens_in = regroup.scatter(split_rows(d_tokens.astype(jnp.bfloat16)))
    d_second = sum_seq(d_second)
    d_inner_w = (
        d_second[:, width : (1 + chunks) * width]
        .reshape(own, chunks, width)
        .transpose(0, 2, 1)
        .reshape(own, -1)
    )
    d_outer_w = d_second[:, (1 + chunks) * width :].reshape(own * chunks, width)
    d_vec = lax.dynamic_slice_in_dim(sums, mine * own, own, 1)
    entry_total = tok_count * width * seq_count * fsdp_count
    rms_values = jnp.sqrt(
        jnp.sum(sums[INNER_B + chunks : INNER_B + chunks + 3], axis=1) / entry_total
    )
    return (
        out_tokens,
        d_tokens_in,
        d_query_w,
        d_vec[0],
        d_key_w,
        d_value_w,
        d_vec[1],
        d_second[:, :width],
        d_vec[OUT_B],
        d_vec[GAIN_1],
        d_vec[BIAS_1],
        d_inner_w,
        d_vec[INNER_B : INNER_B + chunks].T.reshape(-1),
        d_outer_w,
        d_vec[OUTER_B],
        d_vec[GAIN_2],
        d_vec[BIAS_2],
        rms_values,
    )


def solution(mesh):
    in_specs = (
        P("fsdp", "seq", None),
        P("fsdp", None),
        P("fsdp", None, None),
        P("fsdp", None),
        P("fsdp", None),
        P("fsdp"),
        P("fsdp", None),
        P("fsdp", None),
        P("fsdp"),
        P("fsdp", None),
        P("fsdp"),
        P("fsdp"),
        P("fsdp"),
        P("fsdp", None),
        P("fsdp"),
        P("fsdp", None),
        P("fsdp"),
        P("fsdp"),
        P("fsdp"),
        P("fsdp", "seq", None),
    )
    out_specs = (
        P("fsdp", "seq", None),
        P("fsdp", "seq", None),
        P("fsdp", None),
        P("fsdp"),
        P("fsdp", None),
        P("fsdp", None),
        P("fsdp"),
        P("fsdp", None),
        P("fsdp"),
        P("fsdp"),
        P("fsdp"),
        P("fsdp", None),
        P("fsdp"),
        P("fsdp", None),
        P("fsdp"),
        P("fsdp"),
        P("fsdp"),
        P(),
    )
    return jax.shard_map(shards, mesh=mesh, in_specs=in_specs, out_specs=out_specs, check_vma=False)
```

```python
import functools
import math

import jax
import jax.numpy as jnp
from jax import lax
from jax.experimental import pallas as pl
from jax.experimental.pallas import tpu as pltpu
from jax.sharding import PartitionSpec as P

HD = 64
BLK = 64
CHUNK = 4
NEG = -1e30


def plan_blocks(seg, rand, glob):
    rows, full_len = seg.shape
    nb = full_len // BLK
    ids = jnp.arange(nb, dtype=jnp.int32)
    is_global = jnp.any(ids[None, :, None] == glob[:, None, :], axis=-1)
    picked = jnp.any(rand[:, :, None, :] == ids[None, None, :, None], axis=-1)
    nearby = jnp.abs(ids[:, None] - ids[None, :]) <= 1
    admitted = nearby[None] | picked | is_global[:, :, None] | is_global[:, None, :]
    by_block = seg.reshape(rows, nb, BLK)
    low, high = by_block[:, :, 0], by_block[:, :, BLK - 1]
    meets = (low[:, :, None] <= high[:, None, :]) & (low[:, None, :] <= high[:, :, None])
    active = (admitted & meets).astype(jnp.int32)
    upto = (ids[:, None] <= ids[None, :]).astype(jnp.int32)
    place = jnp.sum(active[:, :, :, None] * upto[None, None], axis=2) - 1
    count = jnp.sum(active, axis=2)
    hit = (place[:, :, :, None] == ids[None, None, None, :]) & (active[:, :, :, None] > 0)
    listed = jnp.sum(jnp.where(hit, ids[None, None, :, None], 0), axis=2)
    listed = jnp.where(ids[None, None, :] < count[:, :, None], listed, nb)
    chunks = (count + (CHUNK - 1)) // CHUNK
    seg_cols = jnp.concatenate([seg, jnp.full((rows, BLK), -1, jnp.int32)], axis=1)
    seg_cols = jnp.broadcast_to(seg_cols[:, :, None], (rows, full_len + BLK, 128))
    seg_rows = jnp.concatenate([by_block, by_block], axis=2)[:, :, None, :]
    return chunks, listed.reshape(rows, nb * nb), jnp.sum(chunks, axis=1), seg_cols, seg_rows


def lane_low(rows):
    return lax.broadcasted_iota(jnp.int32, (rows, 128), 1) < HD


def diag128(dup_t):
    row = lax.broadcasted_iota(jnp.int32, (128, 128), 0) < HD
    col = lax.broadcasted_iota(jnp.int32, (128, 128), 1) < HD
    return jnp.where(row == col, dup_t, jnp.zeros_like(dup_t))


def transposed_twice(tile):
    both = jnp.concatenate([tile, tile], axis=0)
    return both.T


def head_rows(acc):
    turned = jnp.concatenate([acc, acc], axis=0).T
    return jnp.where(lane_low(HD), turned[:HD], turned[HD:])


def pick_diag(full, half):
    lanes = slice(half * 128, half * 128 + 128)
    top = full[half * 128 : half * 128 + HD, lanes]
    low = full[half * 128 + HD : half * 128 + 128, lanes]
    return jnp.where(lane_low(HD), top, low)


def chunk_ids(list_ref, row, base, nb, real):
    base = jnp.minimum(base, nb * nb - CHUNK)
    ids = [jnp.where(real, list_ref[row, base + j], nb) for j in range(CHUNK)]
    safe = [jnp.where(b == nb, 0, b) for b in ids]
    return ids, safe


def block_rows(ref, blocks, lanes):
    return jnp.concatenate(
        [ref[0, pl.ds(pl.multiple_of(b * BLK, BLK), BLK), lanes] for b in blocks], axis=0
    )


def turned_blocks(ref, blocks, rows):
    low = lane_low(rows.stop - rows.start)
    tiles = [ref[b, rows, :] for b in blocks]
    return jnp.concatenate(
        [jnp.where(low, tiles[i], tiles[i + 1]) for i in range(0, CHUNK, 2)], axis=1
    )


def turn_all(src_ref, dst_ref, nb, width):
    def body(b, _):
        start = pl.multiple_of(b * BLK, BLK)
        for t in range(width // 128):
            tile = src_ref[0, pl.ds(start, BLK), t * 128 : t * 128 + 128]
            dst_ref[b, t * 128 : t * 128 + 128, :] = transposed_twice(tile)
        return 0

    lax.fori_loop(0, nb, body, 0, unroll=4)


def dot_f32(left, right):
    return lax.dot_general(
        left, right, (((1,), (0,)), ((), ())), preferred_element_type=jnp.float32
    )


def next_item(n_ref, row, nb, a, c):
    more = c + 1 < n_ref[row, a]
    following = jnp.where(more, a, jnp.minimum(a + 1, nb - 1))
    return following, jnp.where(more, c + 1, 0)


def run_items(n_ref, total_ref, row, nb, ready, item, finish):
    total = total_ref[row]

    def following(a, c):
        return next_item(n_ref, row, nb, a, c)

    def turn(i, carry):
        before, between, a, c = carry
        base = lax.rem(i, 2) * 2
        finish(before)
        finish(between)
        a_two, c_two = following(a, c)
        a_three, c_three = following(a_two, c_two)
        a_four, c_four = following(a_three, c_three)
        ready(a_three, 2 - base)
        ready(a_four, 3 - base)
        real = 2 * i + 1 < total
        a_two, c_two = jnp.where(real, a_two, a), jnp.where(real, c_two, c + 1)
        item(base, a, c, True)
        item(base + 1, a_two, c_two, real)
        return a, a_two, a_three, c_three

    ready(0, 0)
    ready(following(0, 0)[0], 1)
    before, between, _, _ = lax.fori_loop(0, (total + 1) // 2, turn, (0, 0, 0, 0))
    finish(before)
    finish(between)


def forward_kernel(group, n_ref, list_ref, total_ref, q_ref, k_ref, v_ref, segc_ref, segr_ref,
                   o_ref, lse_ref, vt_ref, qst_ref, m_ref, l_ref, acc_ref):
    row = pl.program_id(0)
    width = q_ref.shape[2]
    nb = q_ref.shape[1] // BLK
    groups, halves = width // group, group // 128
    tiles = width // 128
    turn_all(v_ref, vt_ref, nb, width)
    qst_ref[...] = jnp.zeros_like(qst_ref)
    l_ref[...] = jnp.ones_like(l_ref)
    acc_ref[...] = jnp.zeros_like(acc_ref)
    m_ref[...] = jnp.zeros_like(m_ref)

    def ready(a, slot):
        start = pl.multiple_of(a * BLK, BLK)
        for t in range(tiles):
            tile = q_ref[0, pl.ds(start, BLK), t * 128 : t * 128 + 128] * 0.125
            square = slice(t % halves * 128, t % halves * 128 + 128)
            qst_ref[slot, t // halves, square, square] = diag128(
                transposed_twice(tile.astype(jnp.bfloat16))
            )

    def finish(a):
        even = lax.rem(a, 2)
        start = pl.multiple_of(a * BLK, BLK)
        for t in range(tiles):
            lanes = slice(t * 128, t * 128 + 128)
            total = l_ref[even, t]
            o_ref[0, pl.ds(start, BLK), lanes] = head_rows(acc_ref[even, t] / total).astype(
                jnp.bfloat16
            )
            lse_ref[0, a, :, lanes] = m_ref[even, t] + jnp.log(total)

    def item(slot, a, c, real):
        ids, safe = chunk_ids(list_ref, row, a * nb + c * CHUNK, nb, real)
        even = lax.rem(a, 2)
        allowed = block_rows(segc_ref, ids, slice(0, 128)) == segr_ref[0, a]
        first = c == 0
        for g in range(groups):
            lanes = slice(g * group, g * group + group)
            s_t = dot_f32(block_rows(k_ref, safe, lanes), qst_ref[slot, g])
            weights, alphas = [], []
            for u in range(halves):
                t = g * halves + u
                s = jnp.where(allowed, s_t[:, u * 128 : u * 128 + 128], NEG)
                m_old = jnp.where(first, NEG, m_ref[even, t])
                m_new = jnp.maximum(m_old, jnp.max(s, axis=0, keepdims=True))
                p = jnp.exp(s - m_new)
                alpha = jnp.exp(m_old - m_new)
                l_ref[even, t] = alpha * l_ref[even, t] + jnp.sum(p, axis=0, keepdims=True)
                m_ref[even, t] = m_new
                weights.append(p.astype(jnp.bfloat16))
                alphas.append(alpha)
            p_t = jnp.concatenate(weights, axis=1) if halves > 1 else weights[0]
            o_t = dot_f32(turned_blocks(vt_ref, safe, lanes), p_t)
            for u in range(halves):
                t = g * halves + u
                acc_ref[even, t] = alphas[u] * acc_ref[even, t] + pick_diag(o_t, u)

    run_items(n_ref, total_ref, row, nb, ready, item, finish)


def group_of(width):
    return 256 if width % 256 == 0 else 128


def whole_spec(shape):
    rest = (0,) * (len(shape) - 1)
    return pl.BlockSpec((1,) + tuple(shape[1:]), lambda r, *_: (r,) + rest)


def one_spec(shape):
    rest = (0,) * (len(shape) - 1)
    return pl.BlockSpec((1,) + tuple(shape[1:]), lambda r, *_: (r,) + rest,
                        pipeline_mode=pl.Buffered(1))


def attention_forward(q, k, v, plan):
    *tables, seg_cols, seg_rows = plan
    rows, full_len, width = q.shape
    nb, group = full_len // BLK, group_of(width)
    tiles = width // 128
    pairs = rows * full_len * full_len // 4 * width
    args = (q, k, v, seg_cols, seg_rows)
    return pl.pallas_call(
        functools.partial(forward_kernel, group),
        out_shape=(
            jax.ShapeDtypeStruct((rows, full_len, width), jnp.bfloat16),
            jax.ShapeDtypeStruct((rows, nb, 1, width), jnp.float32),
        ),
        grid_spec=pltpu.PrefetchScalarGridSpec(
            num_scalar_prefetch=3,
            grid=(rows,),
            in_specs=[one_spec(x.shape) for x in args],
            out_specs=(one_spec((rows, full_len, width)), one_spec((rows, nb, 1, width))),
            scratch_shapes=[
                pltpu.VMEM((nb, width, 128), jnp.bfloat16),
                pltpu.VMEM((4, width // group, group, group), jnp.bfloat16),
                pltpu.VMEM((2, tiles, 1, 128), jnp.float32),
                pltpu.VMEM((2, tiles, 1, 128), jnp.float32),
                pltpu.VMEM((2, tiles, HD, 128), jnp.float32),
            ],
        ),
        compiler_params=pltpu.CompilerParams(vmem_limit_bytes=62 << 20),
        cost_estimate=pl.CostEstimate(
            flops=4 * pairs, transcendentals=pairs // HD, bytes_accessed=8 * q.size
        ),
        name="attention_forward",
    )(*tables, *args)


def backward_kernel(group, n_ref, list_ref, total_ref, q_ref, k_ref, v_ref, o_ref, do_ref,
                    lse_ref, segc_ref, segr_ref, dq_ref, dk_ref, dv_ref,
                    kt_ref, qst_ref, qs_ref, dost_ref, dos_ref, delta_ref, acc_ref,
                    dk_acc, dv_acc):
    row = pl.program_id(0)
    full_len, width = q_ref.shape[1], q_ref.shape[2]
    nb = full_len // BLK
    groups, halves = width // group, group // 128
    tiles = width // 128
    turn_all(k_ref, kt_ref, nb, width)
    for ref in (qst_ref, qs_ref, dost_ref, dos_ref, dk_acc, dv_acc, acc_ref):
        ref[...] = jnp.zeros_like(ref)
    low = lane_low(1)

    def ready(a, slot):
        start = pl.multiple_of(a * BLK, BLK)
        for t in range(tiles):
            g, u = t // halves, t % halves
            lanes = slice(t * 128, t * 128 + 128)
            square = slice(u * 128, u * 128 + 128)
            q_tile = (q_ref[0, pl.ds(start, BLK), lanes] * 0.125).astype(jnp.bfloat16)
            g_tile = do_ref[0, pl.ds(start, BLK), lanes]
            o_tile = o_ref[0, pl.ds(start, BLK), lanes]
            g_turn = transposed_twice(g_tile)
            qst_ref[slot, g, square, square] = diag128(transposed_twice(q_tile))
            dost_ref[slot, g, square, square] = diag128(g_turn)
            qs_ref[slot, g, square, square] = diag128(jnp.concatenate([q_tile, q_tile], axis=0))
            dos_ref[slot, g, square, square] = diag128(
                jnp.concatenate([g_tile, g_tile], axis=0)
            )
            product = g_turn.astype(jnp.float32) * transposed_twice(o_tile).astype(jnp.float32)
            delta_ref[slot, t] = jnp.where(
                low,
                jnp.sum(product[:HD], axis=0, keepdims=True),
                jnp.sum(product[HD:], axis=0, keepdims=True),
            )

    def finish(a):
        even = lax.rem(a, 2)
        start = pl.multiple_of(a * BLK, BLK)
        for t in range(tiles):
            dq_ref[0, pl.ds(start, BLK), t * 128 : t * 128 + 128] = (
                head_rows(acc_ref[even, t]) * 0.125
            ).astype(jnp.bfloat16)

    def item(slot, a, c, real):
        ids, safe = chunk_ids(list_ref, row, a * nb + c * CHUNK, nb, real)
        even = lax.rem(a, 2)
        allowed = block_rows(segc_ref, ids, slice(0, 128)) == segr_ref[0, a]
        first = c == 0
        for g in range(groups):
            lanes = slice(g * group, g * group + group)
            s_t = dot_f32(block_rows(k_ref, safe, lanes), qst_ref[slot, g])
            dp_t = dot_f32(block_rows(v_ref, safe, lanes), dost_ref[slot, g])
            p_parts, ds_parts = [], []
            for u in range(halves):
                t = g * halves + u
                half = slice(u * 128, u * 128 + 128)
                lse = lse_ref[0, a, :, t * 128 : t * 128 + 128]
                p = jnp.exp(jnp.where(allowed, s_t[:, half], NEG) - lse)
                ds = p * (dp_t[:, half] - delta_ref[slot, t])
                p_parts.append(p.astype(jnp.bfloat16))
                ds_parts.append(ds.astype(jnp.bfloat16))
            p_t = jnp.concatenate(p_parts, axis=1) if halves > 1 else p_parts[0]
            ds_t = jnp.concatenate(ds_parts, axis=1) if halves > 1 else ds_parts[0]
            dv = dot_f32(p_t, dos_ref[slot, g])
            dk = dot_f32(ds_t, qs_ref[slot, g])
            dq_t = dot_f32(turned_blocks(kt_ref, safe, lanes), ds_t)
            for j in range(CHUNK):
                where = pl.ds(pl.multiple_of(safe[j] * BLK, BLK), BLK)
                part = slice(j * BLK, j * BLK + BLK)
                dv_acc[where, lanes] += dv[part]
                dk_acc[where, lanes] += dk[part]
            for u in range(halves):
                t = g * halves + u
                acc_ref[even, t] = jnp.where(first, 0.0, acc_ref[even, t]) + pick_diag(dq_t, u)

    run_items(n_ref, total_ref, row, nb, ready, item, finish)

    def flush(a, _):
        where = pl.ds(pl.multiple_of(a * BLK, BLK), BLK)
        dk_ref[0, where, :] = dk_acc[where, :].astype(jnp.bfloat16)
        dv_ref[0, where, :] = dv_acc[where, :].astype(jnp.bfloat16)
        return 0

    lax.fori_loop(0, nb, flush, 0, unroll=2)


def attention_backward(q, k, v, o, do, lse, plan):
    *tables, seg_cols, seg_rows = plan
    rows, full_len, width = q.shape
    nb, group = full_len // BLK, group_of(width)
    tiles, groups = width // 128, width // group
    pairs = rows * full_len * full_len // 4 * width
    args = (q, k, v, o, do, lse, seg_cols, seg_rows)
    like = jax.ShapeDtypeStruct((rows, full_len, width), jnp.bfloat16)
    square = pltpu.VMEM((4, groups, group, group), jnp.bfloat16)
    return pl.pallas_call(
        functools.partial(backward_kernel, group),
        out_shape=(like, like, like),
        grid_spec=pltpu.PrefetchScalarGridSpec(
            num_scalar_prefetch=3,
            grid=(rows,),
            in_specs=[one_spec(x.shape) for x in args],
            out_specs=tuple(one_spec(like.shape) for _ in range(3)),
            scratch_shapes=[
                pltpu.VMEM((nb, width, 128), jnp.bfloat16),
                square, square, square, square,
                pltpu.VMEM((4, tiles, 1, 128), jnp.float32),
                pltpu.VMEM((2, tiles, HD, 128), jnp.float32),
                pltpu.VMEM((full_len, width), jnp.float32),
                pltpu.VMEM((full_len, width), jnp.float32),
            ],
        ),
        compiler_params=pltpu.CompilerParams(vmem_limit_bytes=62 << 20),
        cost_estimate=pl.CostEstimate(
            flops=10 * pairs, transcendentals=pairs // HD, bytes_accessed=16 * q.size
        ),
        name="attention_backward",
    )(*tables, *args)


def pair_bit(index, bit):
    return lax.rem(index // (1 << bit), 2)


def pair_of(index, bit):
    return index + (1 - 2 * pair_bit(index, bit)) * (1 << bit)


def all_arrived(bits):
    me = lax.axis_index("fsdp")
    barrier = pltpu.get_barrier_semaphore()
    for bit in range(bits):
        pl.semaphore_signal(
            barrier, inc=1, device_id={"fsdp": pair_of(me, bit)},
            device_id_type=pl.DeviceIdType.MESH,
        )
    pl.semaphore_signal(
        barrier, inc=1, device_id={"seq": 1 - lax.axis_index("seq")},
        device_id_type=pl.DeviceIdType.MESH,
    )
    pl.semaphore_wait(barrier, bits + 1)


def qkv_backward_kernel(
    bits, xt_in, dq_in, dk_in, dv_in, wt_in, res_in, small_in,
    wq_out, wk_out, wv_out, small_out, tok_out,
    xt, grads, wt, res, tok, kept, sends, lands, final, small, small_land, result,
    in_sem, tok_send, tok_land, own_sem, send_sem, land_sem, x_send, x_land,
    small_send, small_recv, out_sem,
):
    me, side = lax.axis_index("fsdp"), lax.axis_index("seq")
    half = tok.shape[2] * tok.shape[1]
    piece, pieces = tok.shape[2], tok.shape[1]
    own, width = wq_out.shape
    owners = 1 << bits
    sources = (dq_in, dk_in, dv_in)
    loads = [
        pltpu.make_async_copy(wt_in, wt, in_sem.at[0]),
        pltpu.make_async_copy(res_in, res, in_sem.at[1]),
        pltpu.make_async_copy(small_in, small.at[0], in_sem.at[2]),
        pltpu.make_async_copy(xt_in, xt, in_sem.at[3]),
    ] + [pltpu.make_async_copy(sources[i], grads.at[i], in_sem.at[4 + i]) for i in range(3)]
    for i in (3, 4, 5, 6, 0, 1, 2):
        loads[i].start()
    all_arrived(bits)

    def token_rows(start):
        total = res[pl.ds(start, piece), :].astype(jnp.float32)
        for i in range(3):
            total = total + dot_f32(
                grads[i, pl.ds(start, piece), :], wt[i]
            )
        return total.astype(jnp.bfloat16)

    def sent(i):
        return pltpu.make_async_remote_copy(
            src_ref=tok.at[0, i],
            dst_ref=tok_out.at[side, pl.ds(pl.multiple_of(i * piece, piece), piece)],
            send_sem=tok_send.at[i], recv_sem=tok_land.at[i],
            device_id={"seq": 1 - side}, device_id_type=pl.DeviceIdType.MESH,
        )

    def landed(i):
        return pltpu.make_async_remote_copy(
            src_ref=tok.at[0, i],
            dst_ref=tok_out.at[1 - side, pl.ds(pl.multiple_of(i * piece, piece), piece)],
            send_sem=tok_send.at[i], recv_sem=tok_land.at[i],
            device_id={"seq": 1 - side}, device_id_type=pl.DeviceIdType.MESH,
        )

    def stays(i):
        return pltpu.make_async_copy(
            tok.at[1, i],
            tok_out.at[side, pl.ds(pl.multiple_of(i * piece, piece), piece)],
            own_sem.at[i],
        )

    def send_piece(i, _):
        start = pl.multiple_of((1 - side) * half + i * piece, piece)
        tok[0, i] = token_rows(start)
        sent(i).start()
        return 0

    def keep_piece(i, _):
        start = pl.multiple_of(side * half + i * piece, piece)
        tok[1, i] = token_rows(start)
        stays(i).start()
        return 0

    low_bit = pair_bit(me, 0) == 0
    tile = 8 if owners % 8 == 0 else owners
    first_of = [0]
    for bit in range(bits):
        first_of.append(first_of[-1] + (owners >> (bit + 1)))

    def weights(i):
        def rows(m, _):
            rows_here = pl.ds(pl.multiple_of(m * tile * own, tile * own), tile * own)
            block = dot_f32(
                jnp.concatenate(
                    [xt[h, r, rows_here, :] for h in range(2) for r in range(pieces)], axis=1
                ),
                grads[i],
            ).reshape(tile // 2, 2, own, width)
            even, odd = block[:, 0], block[:, 1]
            spot = pl.ds(m * (tile // 2), tile // 2)
            kept[i, spot] = jnp.where(low_bit, even, odd)
            sends[i, spot] = jnp.where(low_bit, odd, even).astype(jnp.bfloat16)
            return 0

        lax.fori_loop(0, owners // tile, rows, 0)

    def hop(i, bit):
        count = owners >> (bit + 1)
        spot = pl.ds(first_of[bit], count)
        return pltpu.make_async_remote_copy(
            src_ref=sends.at[i, spot], dst_ref=lands.at[i, spot],
            send_sem=send_sem.at[i, bit], recv_sem=land_sem.at[i, bit],
            device_id={"fsdp": pair_of(me, bit)}, device_id_type=pl.DeviceIdType.MESH,
        )

    def cross(i):
        return pltpu.make_async_remote_copy(
            src_ref=final.at[0, i], dst_ref=final.at[1, i],
            send_sem=x_send.at[i], recv_sem=x_land.at[i],
            device_id={"seq": 1 - side}, device_id_type=pl.DeviceIdType.MESH,
        )

    def advance(i, bit):
        hop(i, bit).wait_recv()
        base = first_of[bit]
        if bit + 1 == bits:
            total = kept[i, base] + lands[i, base].astype(jnp.float32)
            final[0, i] = total.astype(jnp.bfloat16)
            cross(i).start()
            return
        nxt = pair_bit(me, bit + 1)

        def one(j, _):
            stay, go = 2 * j + nxt, 2 * j + 1 - nxt
            kept[i, first_of[bit + 1] + j] = kept[i, base + stay] + lands[
                i, base + stay
            ].astype(jnp.float32)
            sends[i, first_of[bit + 1] + j] = (
                kept[i, base + go] + lands[i, base + go].astype(jnp.float32)
            ).astype(jnp.bfloat16)
            return 0

        lax.fori_loop(0, owners >> (bit + 2), one, 0)
        hop(i, bit + 1).start()

    outs = (wq_out, wk_out, wv_out)

    def written(i):
        return pltpu.make_async_copy(result.at[i], outs[i], out_sem.at[i])

    def finish(i):
        cross(i).wait_recv()
        result[i] = final[0, i].astype(jnp.float32) + final[1, i].astype(jnp.float32)
        written(i).start()

    def small_hop(bit):
        where = {"fsdp": pair_of(me, bit)} if bit < bits else {"seq": 1 - side}
        return pltpu.make_async_remote_copy(
            src_ref=small.at[bit], dst_ref=small_land.at[bit],
            send_sem=small_send.at[bit], recv_sem=small_recv.at[bit],
            device_id=where, device_id_type=pl.DeviceIdType.MESH,
        )

    def small_advance(bit):
        small_hop(bit).wait_recv()
        small[bit + 1] = small[bit] + small_land[bit]
        if bit < bits:
            small_hop(bit + 1).start()

    for i in (3, 4):
        loads[i].wait()
    weights(0)
    hop(0, 0).start()
    for i in (5, 6, 0, 1):
        loads[i].wait()
    lax.fori_loop(0, pieces, send_piece, 0)
    advance(0, 0)
    weights(1)
    hop(1, 0).start()
    loads[2].wait()
    for spot, i in ((0, 0), (1, 2)):
        def column_sums(c, total):
            block = grads[i, pl.ds(pl.multiple_of(c * 128, 128), 128), :].astype(jnp.float32)
            return total + jnp.sum(block.reshape(16, 8, width), axis=0)

        total = lax.fori_loop(
            0, grads.shape[1] // 128, column_sums, jnp.zeros((8, width), jnp.float32)
        )
        small[0, spot : spot + 1] = jnp.sum(total, axis=0, keepdims=True)
    small_hop(0).start()
    weights(2)
    hop(2, 0).start()
    small_advance(0)
    plan = []
    for step in range(1, bits + 2):
        todo = []
        for i in range(3):
            bit = step - i
            if 0 <= bit < bits:
                todo.append((i, bit))
        plan.append((todo, step))
    done = 0
    for todo, step in plan:
        for i, bit in todo:
            advance(i, bit)
        if step <= bits:
            small_advance(step)
        if done < pieces:
            keep_piece(done, 0)
            done += 1
    for i in range(3):
        finish(i)
    small_copy = pltpu.make_async_copy(small.at[bits + 1], small_out, out_sem.at[3])
    small_copy.start()
    while done < pieces:
        keep_piece(done, 0)
        done += 1
    for i in range(3):
        written(i).wait()
        cross(i).wait_send()
        for bit in range(bits):
            hop(i, bit).wait_send()
    for bit in range(bits + 1):
        small_hop(bit).wait_send()
    small_copy.wait()
    for i in range(pieces):
        stays(i).wait()
        sent(i).wait_send()
        landed(i).wait_recv()


def qkv_backward(xt, dq, dk, dv, wt, resid, small, own):
    tokens, width = dq.shape
    bits = lax.axis_size("fsdp").bit_length() - 1
    owners = 1 << bits
    pieces = 4
    piece = tokens // 2 // pieces
    dma = pltpu.SemaphoreType.DMA
    f32, bf16 = jnp.float32, jnp.bfloat16
    shard = jax.ShapeDtypeStruct((own, width), f32)
    anywhere = pl.BlockSpec(memory_space=pltpu.HBM)
    return pl.pallas_call(
        functools.partial(qkv_backward_kernel, bits),
        out_shape=(
            shard, shard, shard,
            jax.ShapeDtypeStruct(small.shape, f32),
            jax.ShapeDtypeStruct((2, tokens // 2, width), bf16),
        ),
        in_specs=[anywhere] * 7,
        out_specs=(anywhere,) * 5,
        scratch_shapes=[
            pltpu.VMEM(xt.shape, bf16),
            pltpu.VMEM((3, tokens, width), bf16),
            pltpu.VMEM(wt.shape, bf16),
            pltpu.VMEM((tokens, width), bf16),
            pltpu.VMEM((2, pieces, piece, width), bf16),
            pltpu.VMEM((3, owners - 1, own, width), f32),
            pltpu.VMEM((3, owners - 1, own, width), bf16),
            pltpu.VMEM((3, owners - 1, own, width), bf16),
            pltpu.VMEM((2, 3, own, width), bf16),
            pltpu.VMEM((bits + 2,) + small.shape, f32),
            pltpu.VMEM((bits + 1,) + small.shape, f32),
            pltpu.VMEM((3, own, width), f32),
            dma((7,)), dma((pieces,)), dma((pieces,)), dma((pieces,)),
            dma((3, bits)), dma((3, bits)), dma((3,)), dma((3,)),
            dma((bits + 1,)), dma((bits + 1,)), dma((4,)),
        ],
        compiler_params=pltpu.CompilerParams(
            collective_id=1, has_side_effects=True, vmem_limit_bytes=62 << 20
        ),
        cost_estimate=pl.CostEstimate(
            flops=40 * tokens * width * width, transcendentals=0,
            bytes_accessed=16 * tokens * width,
        ),
        name="qkv_backward",
    )(xt, dq, dk, dv, wt, resid, small)


def qkv_forward_kernel(
    bits, tokens_in, own_in,
    x_out, xt_out, q_out, k_out, v_out, wt_out, small_out,
    x, xt, w, wt, qkv, small,
    own_sem, tok_send, tok_land, load_sem, send_sem, land_sem, x_sem, xt_sem, out_sem, w_sem,
    small_sem,
):
    me, side = lax.axis_index("fsdp"), lax.axis_index("seq")
    pieces, piece, width = x.shape[1], x.shape[2], x.shape[3]
    mine = [pair_bit(me, bit) for bit in range(bits)]
    columns = part_columns(width)
    outs = (q_out, k_out, v_out)

    def slot(bit, part):
        here = [slice(None)] * (bits - 1 - bit) + [mine[b] for b in range(bit, -1, -1)]
        return tuple(here) + (slice(None), columns[part])

    own_tokens = pltpu.make_async_copy(tokens_in.at[side], x.at[side], own_sem.at[0])
    own_tokens.start()

    def load(part):
        spot = tuple(mine[b] for b in range(bits - 1, -1, -1)) + (slice(None), columns[part])
        return pltpu.make_async_copy(
            own_in.at[:, columns[part]], w.at[spot], load_sem.at[part]
        )

    for part in range(3):
        load(part).start()
    all_arrived(bits)

    def sent(i):
        return pltpu.make_async_remote_copy(
            src_ref=tokens_in.at[1 - side, i], dst_ref=x.at[side, i],
            send_sem=tok_send.at[i], recv_sem=tok_land.at[i],
            device_id={"seq": 1 - side}, device_id_type=pl.DeviceIdType.MESH,
        )

    def landed(i):
        return pltpu.make_async_remote_copy(
            src_ref=tokens_in.at[1 - side, i], dst_ref=x.at[1 - side, i],
            send_sem=tok_send.at[i], recv_sem=tok_land.at[i],
            device_id={"seq": 1 - side}, device_id_type=pl.DeviceIdType.MESH,
        )

    def hop(part, turn):
        bit = bits - 1 - turn
        return pltpu.make_async_remote_copy(
            src_ref=w.at[slot(bit, part)], dst_ref=w.at[slot(bit, part)],
            send_sem=send_sem.at[part, turn], recv_sem=land_sem.at[part, turn],
            device_id={"fsdp": pair_of(me, bit)}, device_id_type=pl.DeviceIdType.MESH,
        )

    for part in range(3):
        load(part).wait()
        hop(part, 0).start()
    for i in range(pieces):
        sent(i).start()

    def x_copy(half, i):
        return pltpu.make_async_copy(x.at[half, i], x_out.at[half, i], x_sem.at[half, i])

    def out_copy(part, half, i):
        return pltpu.make_async_copy(
            qkv.at[part, half, i], outs[part].at[half, i], out_sem.at[part, half, i]
        )

    def xt_copy(half, i):
        return pltpu.make_async_copy(xt.at[half, i], xt_out.at[half, i], xt_sem.at[half, i])

    def w_copy(part):
        return pltpu.make_async_copy(wt.at[part], wt_out.at[part], w_sem.at[part])

    def whole(part):
        first = part_start(width, part)
        spot = (slice(None),) * (bits + 1) + (slice(first, first + width),)
        return w[spot].reshape(width, width)

    def turn(half, i):
        x_copy(half, i).start()
        xt[half, i] = x[half, i].T
        xt_copy(half, i).start()

    def project(part, half, i):
        total = dot_f32(x[half, i], whole(part))
        if part == 0:
            total = total + small[0:1, :]
        if part == 2:
            total = total + small[1:2, :]
        qkv[part, half, i] = total.astype(jnp.bfloat16)
        out_copy(part, half, i).start()

    def over(body):
        def one(i, _):
            body(i)
            return 0

        lax.fori_loop(0, pieces, one, 0)

    def turn_weights(part):
        wt[part] = whole(part).T
        w_copy(part).start()

    def other(i):
        landed(i).wait_recv()
        turn(1 - side, i)
        project(0, 1 - side, i)
        project(1, 1 - side, i)

    own_tokens.wait()
    over(lambda i: turn(side, i))
    for step in range(bits + 2):
        full = None
        for part in range(3):
            hops = step - part
            if 0 <= hops < bits:
                hop(part, hops).wait_recv()
                if hops + 1 < bits:
                    hop(part, hops + 1).start()
                else:
                    full = part
        if full == 0:
            spot = (slice(None),) * (bits + 1) + (slice(width, width + 128),)
            turned = w[spot].reshape(width, 128).astype(jnp.float32).T
            small[...] = turned[: small.shape[0]]
            pltpu.make_async_copy(small, small_out, small_sem.at[0]).start()
        if full is not None:
            over(lambda i: project(full, side, i))
        if full == 1:
            turn_weights(0)
            turn_weights(1)
            over(other)
        if full == 2:
            over(lambda i: project(2, 1 - side, i))
            turn_weights(2)
    for i in range(pieces):
        sent(i).wait_send()
    for part in range(3):
        w_copy(part).wait()
        for hops in range(bits):
            hop(part, hops).wait_send()
    pltpu.make_async_copy(small, small_out, small_sem.at[0]).wait()
    for half in range(2):
        for i in range(pieces):
            x_copy(half, i).wait()
            xt_copy(half, i).wait()
            for part in range(3):
                out_copy(part, half, i).wait()


def part_start(width, part):
    return part * width + (128 if part else 0)


def part_columns(width):
    return (
        slice(0, width + 128),
        slice(width + 128, 2 * width + 128),
        slice(2 * width + 128, 3 * width + 128),
    )


def qkv_forward(tokens_in, own_pack):
    rows, local, width = tokens_in.shape
    own, columns = own_pack.shape
    bits = lax.axis_size("fsdp").bit_length() - 1
    pieces = 4
    piece = local // pieces
    dma = pltpu.SemaphoreType.DMA
    bf16 = jnp.bfloat16
    halves = (2, pieces, piece, width)
    gathered = (2,) * bits + (own, columns)
    anywhere = pl.BlockSpec(memory_space=pltpu.HBM)
    like = jax.ShapeDtypeStruct(halves, bf16)
    turned = (2, pieces, width, piece)
    x, xt, q, k, v, weights_t, small = pl.pallas_call(
        functools.partial(qkv_forward_kernel, bits),
        out_shape=(
            like, jax.ShapeDtypeStruct(turned, bf16), like, like, like,
            jax.ShapeDtypeStruct((3, width, width), bf16),
            jax.ShapeDtypeStruct((SMALL_ROWS, width), jnp.float32),
        ),
        in_specs=[anywhere] * 2,
        out_specs=(anywhere,) * 7,
        scratch_shapes=[
            pltpu.VMEM(halves, bf16),
            pltpu.VMEM(turned, bf16),
            pltpu.VMEM(gathered, bf16),
            pltpu.VMEM((3, width, width), bf16),
            pltpu.VMEM((3,) + halves, bf16),
            pltpu.VMEM((SMALL_ROWS, width), jnp.float32),
            dma((1,)), dma((pieces,)), dma((pieces,)), dma((3,)),
            dma((3, bits)), dma((3, bits)), dma((2, pieces)), dma((2, pieces)),
            dma((3, 2, pieces)), dma((3,)), dma((1,)),
        ],
        compiler_params=pltpu.CompilerParams(
            collective_id=2, has_side_effects=True, vmem_limit_bytes=62 << 20
        ),
        cost_estimate=pl.CostEstimate(
            flops=18 * rows * local * width * width, transcendentals=0,
            bytes_accessed=16 * rows * local * width,
        ),
        name="qkv_forward",
    )(tokens_in.reshape(halves), own_pack)
    flat = rows * local, width
    return x.reshape(flat), q.reshape(flat), k.reshape(flat), v.reshape(flat), xt, weights_t, small


eps_norm = 1e-06


def dot_rows(left, right):
    return lax.dot_general(
        left, right, (((0,), (0,)), ((), ())), preferred_element_type=jnp.float32
    )


def dot_nt(left, right):
    return lax.dot_general(
        left, right, (((1,), (1,)), ((), ())), preferred_element_type=jnp.float32
    )


def row_mean(values):
    return jnp.mean(values, axis=-1, keepdims=True)


GELU_K = math.sqrt(2.0 / math.pi)
GELU_A = 0.044715


def gelu_pair(u):
    square = u * u
    t = jnp.tanh(u * (GELU_K + (GELU_K * GELU_A) * square))
    half = 0.5 + 0.5 * t
    slope = half + (u * (half * (1.0 - t))) * (GELU_K + (3.0 * GELU_K * GELU_A) * square)
    return u * half, slope


OUT_B, GAIN_1, BIAS_1, OUTER_B, GAIN_2, BIAS_2, INNER_B = 2, 3, 4, 5, 6, 7, 8
STEP_ROWS = 512
SMALL_ROWS = 16


def middle_kernel(
    chunks, weights_in, small, att, tokens, cotangent,
    out, d_attn, d_att, d_weights, sums,
    w, acc, act, slope, z_one, flow, rs_one, normed, normed_t, d_mlp, part, load_sem, store_sem,
):
    step, steps = pl.program_id(0), pl.num_programs(0)
    rows, width = att.shape
    f32, bf16 = jnp.float32, jnp.bfloat16
    count = 2 * chunks + 1

    def load(i):
        return pltpu.make_async_copy(
            weights_in.at[:, pl.ds(i * width, width)], w.at[i], load_sem.at[i]
        )

    def store(i):
        return pltpu.make_async_copy(
            w.at[i], d_weights.at[:, pl.ds(i * width, width)], store_sem.at[i]
        )

    @pl.when(step == 0)
    def _():
        for i in range(count):
            load(i).start()
        part[...] = jnp.zeros_like(part)

        def clear(i, _):
            acc[i] = jnp.zeros_like(acc[i])
            return 0

        lax.fori_loop(0, count, clear, 0)
        for i in range(count):
            load(i).wait()

    def vector(i):
        return small[i : i + 1, :]

    def eights(values):
        return jnp.sum(values.reshape(-1, 8, values.shape[-1]), axis=0)

    def add_sum(i, values):
        part[i] += eights(values)

    def by_rows(body):
        def one(r, _):
            body(pl.ds(pl.multiple_of(r * STEP_ROWS, STEP_ROWS), STEP_ROWS))
            return 0

        lax.fori_loop(0, rows // STEP_ROWS, one, 0)

    flow[...] = dot_f32(att[...], w[0])

    def norm_one(r):
        attn = flow[r, :] + vector(OUT_B)
        resid = tokens[r, :].astype(f32) + attn
        add_sum(INNER_B + chunks, resid * resid)
        add_sum(INNER_B + chunks + 1, attn * attn)
        centred = resid - row_mean(resid)
        scale = lax.rsqrt(row_mean(centred * centred) + eps_norm)
        z = centred * scale
        z_one[r, :] = z
        rs_one[r, :] = scale
        normed[r, :] = (z * vector(GAIN_1) + vector(BIAS_1)).astype(bf16)

    by_rows(norm_one)
    normed_t[...] = normed[...].T

    def inner(c, _):
        for n in range(width // 256):
            cols = slice(n * 256, n * 256 + 256)
            pre = dot_f32(normed[...], w[1 + c, :, cols]) + small[pl.ds(INNER_B + c, 1), cols]
            value, grade = gelu_pair(pre)
            act[c, :, cols] = value.astype(bf16)
            slope[c, :, cols] = grade.astype(bf16)
        return 0

    lax.fori_loop(0, chunks, inner, 0)
    flow[...] = dot_f32(act[0], w[1 + chunks])

    def outer(c, _):
        flow[...] += dot_f32(act[c], w[1 + chunks + c])
        return 0

    lax.fori_loop(1, chunks, outer, 0)

    def norm_two(r):
        mlp = flow[r, :] + vector(OUTER_B)
        add_sum(INNER_B + chunks + 2, mlp * mlp)
        resid = z_one[r, :] * vector(GAIN_1) + vector(BIAS_1) + mlp
        centred = resid - row_mean(resid)
        scale = lax.rsqrt(row_mean(centred * centred) + eps_norm)
        z = centred * scale
        out[r, :] = (z * vector(GAIN_2) + vector(BIAS_2)).astype(bf16)
        grad = cotangent[r, :].astype(f32)
        add_sum(GAIN_2, grad * z)
        add_sum(BIAS_2, grad)
        grad = grad * vector(GAIN_2)
        d_resid = scale * (grad - row_mean(grad) - z * row_mean(grad * z))
        low = d_resid.astype(bf16)
        add_sum(OUTER_B, low.astype(f32))
        d_mlp[r, :] = low
        flow[r, :] = d_resid

    by_rows(norm_two)

    def back(c, _):
        for n in range(width // 256):
            cols = slice(n * 256, n * 256 + 256)
            d_act = dot_nt(d_mlp[...], w[1 + chunks + c, cols, :])
            d_pre = (slope[c, :, cols].astype(f32) * d_act).astype(bf16)
            part[INNER_B + c, :, cols] += eights(d_pre.astype(f32))
            slope[c, :, cols] = d_pre
        acc[1 + chunks + c] += dot_rows(act[c], d_mlp[...])
        acc[1 + c] += dot_f32(normed_t[...], slope[c])
        flow[...] += dot_nt(slope[c], w[1 + c])

        @pl.when(step == steps - 1)
        def _():
            for i in (1 + c, 1 + chunks + c):
                w[i] = acc[i].astype(bf16)
                store(i).start()

        return 0

    lax.fori_loop(0, chunks, back, 0)

    def norm_one_back(r):
        grad = flow[r, :]
        z = z_one[r, :]
        add_sum(GAIN_1, grad * z)
        add_sum(BIAS_1, grad)
        grad = grad * vector(GAIN_1)
        d_resid = rs_one[r, :] * (grad - row_mean(grad) - z * row_mean(grad * z))
        low = d_resid.astype(bf16)
        add_sum(OUT_B, low.astype(f32))
        d_attn[r, :] = low

    by_rows(norm_one_back)
    acc[0] += dot_rows(att[...], d_attn[...])
    d_att[...] = dot_nt(d_attn[...], w[0]).astype(bf16)

    @pl.when(step == steps - 1)
    def _():
        w[0] = acc[0].astype(bf16)
        store(0).start()
        sums[...] = jnp.sum(part[...], axis=1)
        for i in range(count):
            store(i).wait()


def middle(weights, small, att, tokens, cotangent):
    tok_count, width = att.shape
    chunks = (weights.shape[1] // width - 1) // 2
    count = 2 * chunks + 1
    rows = 512
    f32, bf16 = jnp.float32, jnp.bfloat16
    tile = pl.BlockSpec((rows, width), lambda i: (i, 0))
    fixed = pl.BlockSpec(small.shape, lambda i: (0, 0), pipeline_mode=pl.Buffered(1))
    anywhere = pl.BlockSpec(memory_space=pl.ANY)
    like = jax.ShapeDtypeStruct((tok_count, width), bf16)
    flops = 6 * tok_count * width * width * count
    return pl.pallas_call(
        functools.partial(middle_kernel, chunks),
        grid=(tok_count // rows,),
        out_shape=(
            like, like, like,
            jax.ShapeDtypeStruct(weights.shape, bf16),
            jax.ShapeDtypeStruct(small.shape, f32),
        ),
        in_specs=[anywhere, fixed, tile, tile, tile],
        out_specs=(tile, tile, tile, anywhere, pl.BlockSpec(small.shape, lambda i: (0, 0))),
        scratch_shapes=[
            pltpu.VMEM((count, width, width), bf16),
            pltpu.VMEM((count, width, width), f32),
            pltpu.VMEM((chunks, rows, width), bf16),
            pltpu.VMEM((chunks, rows, width), bf16),
            pltpu.VMEM((rows, width), f32),
            pltpu.VMEM((rows, width), f32),
            pltpu.VMEM((rows, 1), f32),
            pltpu.VMEM((rows, width), bf16),
            pltpu.VMEM((width, rows), bf16),
            pltpu.VMEM((rows, width), bf16),
            pltpu.VMEM((small.shape[0], 8, width), f32),
            pltpu.SemaphoreType.DMA((count,)),
            pltpu.SemaphoreType.DMA((count,)),
        ],
        compiler_params=pltpu.CompilerParams(vmem_limit_bytes=62 << 20),
        cost_estimate=pl.CostEstimate(
            flops=2 * flops, transcendentals=tok_count * width * chunks,
            bytes_accessed=12 * tok_count * width + 4 * weights.size,
        ),
        name="middle",
    )(weights, small, att, tokens, cotangent)


def contract_rows(left, right):
    return lax.dot_general(
        left, right, (((0,), (0,)), ((), ())), preferred_element_type=jnp.float32
    )


def times_transpose(left, right):
    return lax.dot_general(
        left, right, (((1,), (1,)), ((), ())), preferred_element_type=jnp.float32
    )


def butterfly_sum(values, axis):
    size = lax.axis_size(axis)
    if size & (size - 1):
        return lax.psum(values, axis)
    step = 1
    while step < size:
        pairs = [(i, i ^ step) for i in range(size)]
        values = values + lax.ppermute(values, axis, pairs)
        step *= 2
    return values


def sum_seq(values):
    if lax.axis_size("seq") == 2:
        other = lax.ppermute(values, "seq", [(0, 1), (1, 0)])
        return values.astype(jnp.float32) + other.astype(jnp.float32)
    return lax.psum(values, "seq").astype(jnp.float32)


class Regroup:
    def __init__(self, row_count):
        self.size = lax.axis_size("seq")
        self.ways = math.gcd(row_count, self.size)
        self.parts = self.size // self.ways
        self.rows = row_count // self.ways
        me = lax.axis_index("seq")
        self.place = lax.rem(me, self.ways)
        self.row_group = me // self.parts

    def targets(self, turn):
        ways, parts = self.ways, self.parts
        return [
            (s, ((s % ways + turn) % ways) * parts + s // ways) for s in range(self.size)
        ]

    def move(self, values, pairs):
        if all(a == b for a, b in pairs):
            return values
        return lax.ppermute(values, "seq", pairs)

    def gather(self, values):
        rows, local, width = self.rows, values.shape[1], values.shape[2]
        out = jnp.zeros((rows, self.ways, local, width), values.dtype)
        for turn in range(self.ways):
            pick = lax.rem(self.place + turn, self.ways)
            chunk = lax.dynamic_slice_in_dim(values, pick * rows, rows, 0)
            chunk = self.move(chunk, self.targets(turn))
            spot = lax.rem(self.row_group - turn + self.ways, self.ways)
            out = lax.dynamic_update_slice_in_dim(out, chunk[:, None], spot, 1)
        return out.reshape(rows, self.ways * local, width)

    def scatter(self, values):
        rows, width = self.rows, values.shape[2]
        local = values.shape[1] // self.ways
        values = values.reshape(rows, self.ways, local, width)
        out = jnp.zeros((rows * self.ways, local, width), values.dtype)
        for turn in range(self.ways):
            spot = lax.rem(self.row_group - turn + self.ways, self.ways)
            chunk = lax.dynamic_slice_in_dim(values, spot, 1, 1)[:, 0]
            chunk = self.move(chunk, [(b, a) for a, b in self.targets(turn)])
            pick = lax.rem(self.place + turn, self.ways)
            out = lax.dynamic_update_slice_in_dim(out, chunk, pick * rows, 0)
        return out

    def pick_rows(self, values):
        return lax.dynamic_slice_in_dim(values, self.row_group * self.rows, self.rows, 0)

    def groups(self):
        return [
            [r * self.parts + j for j in range(self.parts)] for r in range(self.ways)
        ]

    def to_heads(self, values):
        if self.parts == 1:
            return values
        return lax.all_to_all(
            values, "seq", split_axis=2, concat_axis=1, tiled=True,
            axis_index_groups=self.groups(),
        )

    def from_heads(self, values):
        if self.parts == 1:
            return values
        return lax.all_to_all(
            values, "seq", split_axis=1, concat_axis=2, tiled=True,
            axis_index_groups=self.groups(),
        )


def shards(
    tokens_in,
    segment_ids,
    random_blocks,
    global_blocks,
    w_query,
    b_query,
    w_key,
    w_value,
    b_value,
    w_attn_out,
    b_attn_out,
    ln1_gain,
    ln1_bias,
    w_inner,
    b_inner,
    w_outer,
    b_outer,
    ln2_gain,
    ln2_bias,
    out_grad,
):
    row_count, local_len, width = tokens_in.shape
    seq_count = lax.axis_size("seq")
    fsdp_count = lax.axis_size("fsdp")
    tok_count = row_count * local_len
    own = w_query.shape[0]
    chunks = b_inner.shape[0] // own
    regroup = Regroup(row_count)
    paired = row_count == 2 and seq_count == 2 and fsdp_count & (fsdp_count - 1) == 0

    vectors = [b_query, b_value, b_attn_out, ln1_gain, ln1_bias, b_outer, ln2_gain, ln2_bias]
    columns = [x[:, None] for x in vectors] + [b_inner.reshape(own, chunks)]
    used = len(vectors) + chunks
    columns.append(jnp.zeros((own, 128 - used), jnp.bfloat16))
    first = jnp.concatenate([w_query] + columns + [w_key, w_value], axis=1)
    inner_own = w_inner.reshape(own, width, chunks).transpose(0, 2, 1).reshape(own, -1)
    second = jnp.concatenate([w_attn_out, inner_own, w_outer.reshape(own, -1)], axis=1)
    second = lax.all_gather(second, "fsdp", axis=0, tiled=True)
    plan = plan_blocks(
        regroup.pick_rows(segment_ids),
        regroup.pick_rows(random_blocks),
        regroup.pick_rows(global_blocks),
    )

    def split_rows(values):
        return values.reshape(regroup.rows, tok_count // regroup.rows, width)

    def part_of(values, i):
        return values[:, part_start(width, i) : part_start(width, i) + width]

    if paired:
        flat_in, *qkv, turned_in, turned_w, small = qkv_forward(tokens_in, first)
    else:
        first = lax.all_gather(first, "fsdp", axis=0, tiled=True)
        small = first[:, width : width + SMALL_ROWS].astype(jnp.float32).T
        flat_in = regroup.gather(tokens_in).reshape(tok_count, width)
        biases = (small[0], jnp.zeros_like(small[0]), small[1])
        qkv = [
            (jnp.dot(flat_in, part_of(first, i), preferred_element_type=jnp.float32)
             + biases[i]).astype(jnp.bfloat16)
            for i in range(3)
        ]
    q, out_grad = lax.optimization_barrier((qkv[0], out_grad))
    flat_grad = regroup.gather(out_grad).reshape(tok_count, width)
    q, k, v = (regroup.to_heads(split_rows(x)) for x in (q, qkv[1], qkv[2]))
    att, lse = attention_forward(q, k, v, plan)
    att_flat = regroup.from_heads(att).reshape(tok_count, width)
    out_tokens, d_attn, d_att, d_second, sums = middle(
        second, small, att_flat, flat_in, flat_grad
    )
    out_tokens = regroup.scatter(split_rows(out_tokens))

    def scattered(values):
        return lax.psum_scatter(values, "fsdp", scatter_dimension=0, tiled=True)

    d_second = scattered(d_second)
    dq, dk, dv = attention_backward(
        q, k, v, att, regroup.to_heads(split_rows(d_att)), lse, plan
    )
    dq, dk, dv = (regroup.from_heads(x).reshape(tok_count, width) for x in (dq, dk, dv))
    mine = lax.axis_index("fsdp")
    dq, out_tokens = lax.optimization_barrier((dq, out_tokens))
    if paired:
        d_query_w, d_key_w, d_value_w, sums, d_tokens_in = qkv_backward(
            turned_in, dq, dk, dv, turned_w, d_attn, sums, own
        )
        d_second, sums = lax.optimization_barrier((d_second, sums))
    else:
        for spot, part in ((0, dq), (1, dv)):
            sums = sums.at[spot].set(jnp.sum(part.astype(jnp.float32), axis=0))
        sums = butterfly_sum(butterfly_sum(sums, "fsdp"), "seq")
        d_query_w, d_key_w, d_value_w = (
            sum_seq(scattered(contract_rows(flat_in, x).astype(jnp.bfloat16)))
            for x in (dq, dk, dv)
        )
        d_tokens = d_attn.astype(jnp.float32)
        for i, part in enumerate((dq, dk, dv)):
            d_tokens = d_tokens + times_transpose(part, part_of(first, i))
        d_tokens_in = regroup.scatter(split_rows(d_tokens.astype(jnp.bfloat16)))
    d_second = sum_seq(d_second)
    d_inner_w = (
        d_second[:, width : (1 + chunks) * width]
        .reshape(own, chunks, width)
        .transpose(0, 2, 1)
        .reshape(own, -1)
    )
    d_outer_w = d_second[:, (1 + chunks) * width :].reshape(own * chunks, width)
    d_vec = lax.dynamic_slice_in_dim(sums, mine * own, own, 1)
    entry_total = tok_count * width * seq_count * fsdp_count
    rms_values = jnp.sqrt(
        jnp.sum(sums[INNER_B + chunks : INNER_B + chunks + 3], axis=1) / entry_total
    )
    return (
        out_tokens,
        d_tokens_in,
        d_query_w,
        d_vec[0],
        d_key_w,
        d_value_w,
        d_vec[1],
        d_second[:, :width],
        d_vec[OUT_B],
        d_vec[GAIN_1],
        d_vec[BIAS_1],
        d_inner_w,
        d_vec[INNER_B : INNER_B + chunks].T.reshape(-1),
        d_outer_w,
        d_vec[OUTER_B],
        d_vec[GAIN_2],
        d_vec[BIAS_2],
        rms_values,
    )


def solution(mesh):
    in_specs = (
        P("fsdp", "seq", None),
        P("fsdp", None),
        P("fsdp", None, None),
        P("fsdp", None),
        P("fsdp", None),
        P("fsdp"),
        P("fsdp", None),
        P("fsdp", None),
        P("fsdp"),
        P("fsdp", None),
        P("fsdp"),
        P("fsdp"),
        P("fsdp"),
        P("fsdp", None),
        P("fsdp"),
        P("fsdp", None),
        P("fsdp"),
        P("fsdp"),
        P("fsdp"),
        P("fsdp", "seq", None),
    )
    out_specs = (
        P("fsdp", "seq", None),
        P("fsdp", "seq", None),
        P("fsdp", None),
        P("fsdp"),
        P("fsdp", None),
        P("fsdp", None),
        P("fsdp"),
        P("fsdp", None),
        P("fsdp"),
        P("fsdp"),
        P("fsdp"),
        P("fsdp", None),
        P("fsdp"),
        P("fsdp", None),
        P("fsdp"),
        P("fsdp"),
        P("fsdp"),
        P(),
    )
    return jax.shard_map(shards, mesh=mesh, in_specs=in_specs, out_specs=out_specs, check_vma=False)
```

```python
import functools
import math

import jax
import jax.numpy as jnp
from jax import lax
from jax.experimental import pallas as pl
from jax.experimental.pallas import tpu as pltpu
from jax.sharding import PartitionSpec as P

HD = 64
BLK = 64
CHUNK = 4
NEG = -1e30


def plan_blocks(seg, rand, glob):
    rows, full_len = seg.shape
    nb = full_len // BLK
    ids = jnp.arange(nb, dtype=jnp.int32)
    is_global = jnp.any(ids[None, :, None] == glob[:, None, :], axis=-1)
    picked = jnp.any(rand[:, :, None, :] == ids[None, None, :, None], axis=-1)
    nearby = jnp.abs(ids[:, None] - ids[None, :]) <= 1
    admitted = nearby[None] | picked | is_global[:, :, None] | is_global[:, None, :]
    by_block = seg.reshape(rows, nb, BLK)
    low, high = by_block[:, :, 0], by_block[:, :, BLK - 1]
    meets = (low[:, :, None] <= high[:, None, :]) & (low[:, None, :] <= high[:, :, None])
    active = (admitted & meets).astype(jnp.int32)
    upto = (ids[:, None] <= ids[None, :]).astype(jnp.int32)
    place = jnp.sum(active[:, :, :, None] * upto[None, None], axis=2) - 1
    count = jnp.sum(active, axis=2)
    hit = (place[:, :, :, None] == ids[None, None, None, :]) & (active[:, :, :, None] > 0)
    listed = jnp.sum(jnp.where(hit, ids[None, None, :, None], 0), axis=2)
    listed = jnp.where(ids[None, None, :] < count[:, :, None], listed, nb)
    chunks = (count + (CHUNK - 1)) // CHUNK
    seg_cols = jnp.concatenate([seg, jnp.full((rows, BLK), -1, jnp.int32)], axis=1)
    seg_cols = jnp.broadcast_to(seg_cols[:, :, None], (rows, full_len + BLK, 128))
    seg_rows = jnp.concatenate([by_block, by_block], axis=2)[:, :, None, :]
    return chunks, listed.reshape(rows, nb * nb), jnp.sum(chunks, axis=1), seg_cols, seg_rows


def lane_low(rows):
    return lax.broadcasted_iota(jnp.int32, (rows, 128), 1) < HD


def diag128(dup_t):
    row = lax.broadcasted_iota(jnp.int32, (128, 128), 0) < HD
    col = lax.broadcasted_iota(jnp.int32, (128, 128), 1) < HD
    return jnp.where(row == col, dup_t, jnp.zeros_like(dup_t))


def transposed_twice(tile):
    both = jnp.concatenate([tile, tile], axis=0)
    return both.T


def head_rows(acc):
    turned = jnp.concatenate([acc, acc], axis=0).T
    return jnp.where(lane_low(HD), turned[:HD], turned[HD:])


def pick_diag(full, half):
    lanes = slice(half * 128, half * 128 + 128)
    top = full[half * 128 : half * 128 + HD, lanes]
    low = full[half * 128 + HD : half * 128 + 128, lanes]
    return jnp.where(lane_low(HD), top, low)


def chunk_ids(list_ref, row, base, nb, real):
    base = jnp.minimum(base, nb * nb - CHUNK)
    ids = [jnp.where(real, list_ref[row, base + j], nb) for j in range(CHUNK)]
    safe = [jnp.where(b == nb, 0, b) for b in ids]
    return ids, safe


def block_rows(ref, blocks, lanes):
    return jnp.concatenate(
        [ref[0, pl.ds(pl.multiple_of(b * BLK, BLK), BLK), lanes] for b in blocks], axis=0
    )


def turned_blocks(ref, blocks, rows):
    low = lane_low(rows.stop - rows.start)
    tiles = [ref[b, rows, :] for b in blocks]
    return jnp.concatenate(
        [jnp.where(low, tiles[i], tiles[i + 1]) for i in range(0, CHUNK, 2)], axis=1
    )


def turn_all(src_ref, dst_ref, nb, width):
    def body(b, _):
        start = pl.multiple_of(b * BLK, BLK)
        for t in range(width // 128):
            tile = src_ref[0, pl.ds(start, BLK), t * 128 : t * 128 + 128]
            dst_ref[b, t * 128 : t * 128 + 128, :] = transposed_twice(tile)
        return 0

    lax.fori_loop(0, nb, body, 0, unroll=4)


def dot_f32(left, right):
    return lax.dot_general(
        left, right, (((1,), (0,)), ((), ())), preferred_element_type=jnp.float32
    )


def next_item(n_ref, row, nb, a, c):
    more = c + 1 < n_ref[row, a]
    following = jnp.where(more, a, jnp.minimum(a + 1, nb - 1))
    return following, jnp.where(more, c + 1, 0)


def run_items(n_ref, total_ref, row, nb, ready, item, finish):
    total = total_ref[row]

    def following(a, c):
        return next_item(n_ref, row, nb, a, c)

    def turn(i, carry):
        before, between, a, c = carry
        base = lax.rem(i, 2) * 2
        finish(before)
        finish(between)
        a_two, c_two = following(a, c)
        a_three, c_three = following(a_two, c_two)
        a_four, c_four = following(a_three, c_three)
        ready(a_three, 2 - base)
        ready(a_four, 3 - base)
        real = 2 * i + 1 < total
        a_two, c_two = jnp.where(real, a_two, a), jnp.where(real, c_two, c + 1)
        item(base, a, c, True)
        item(base + 1, a_two, c_two, real)
        return a, a_two, a_three, c_three

    ready(0, 0)
    ready(following(0, 0)[0], 1)
    before, between, _, _ = lax.fori_loop(0, (total + 1) // 2, turn, (0, 0, 0, 0))
    finish(before)
    finish(between)


def forward_kernel(group, n_ref, list_ref, total_ref, q_ref, k_ref, v_ref, segc_ref, segr_ref,
                   o_ref, lse_ref, vt_ref, qst_ref, m_ref, l_ref, acc_ref):
    row = pl.program_id(0)
    width = q_ref.shape[2]
    nb = q_ref.shape[1] // BLK
    groups, halves = width // group, group // 128
    tiles = width // 128
    turn_all(v_ref, vt_ref, nb, width)
    qst_ref[...] = jnp.zeros_like(qst_ref)
    l_ref[...] = jnp.ones_like(l_ref)
    acc_ref[...] = jnp.zeros_like(acc_ref)
    m_ref[...] = jnp.zeros_like(m_ref)

    def ready(a, slot):
        start = pl.multiple_of(a * BLK, BLK)
        for t in range(tiles):
            tile = q_ref[0, pl.ds(start, BLK), t * 128 : t * 128 + 128] * 0.125
            square = slice(t % halves * 128, t % halves * 128 + 128)
            qst_ref[slot, t // halves, square, square] = diag128(
                transposed_twice(tile.astype(jnp.bfloat16))
            )

    def finish(a):
        even = lax.rem(a, 2)
        start = pl.multiple_of(a * BLK, BLK)
        for t in range(tiles):
            lanes = slice(t * 128, t * 128 + 128)
            total = l_ref[even, t]
            o_ref[0, pl.ds(start, BLK), lanes] = head_rows(acc_ref[even, t] / total).astype(
                jnp.bfloat16
            )
            lse_ref[0, a, :, lanes] = m_ref[even, t] + jnp.log(total)

    def item(slot, a, c, real):
        ids, safe = chunk_ids(list_ref, row, a * nb + c * CHUNK, nb, real)
        even = lax.rem(a, 2)
        allowed = block_rows(segc_ref, ids, slice(0, 128)) == segr_ref[0, a]
        first = c == 0
        for g in range(groups):
            lanes = slice(g * group, g * group + group)
            s_t = dot_f32(block_rows(k_ref, safe, lanes), qst_ref[slot, g])
            weights, alphas = [], []
            for u in range(halves):
                t = g * halves + u
                s = jnp.where(allowed, s_t[:, u * 128 : u * 128 + 128], NEG)
                m_old = jnp.where(first, NEG, m_ref[even, t])
                m_new = jnp.maximum(m_old, jnp.max(s, axis=0, keepdims=True))
                p = jnp.exp(s - m_new)
                alpha = jnp.exp(m_old - m_new)
                l_ref[even, t] = alpha * l_ref[even, t] + jnp.sum(p, axis=0, keepdims=True)
                m_ref[even, t] = m_new
                weights.append(p.astype(jnp.bfloat16))
                alphas.append(alpha)
            p_t = jnp.concatenate(weights, axis=1) if halves > 1 else weights[0]
            o_t = dot_f32(turned_blocks(vt_ref, safe, lanes), p_t)
            for u in range(halves):
                t = g * halves + u
                acc_ref[even, t] = alphas[u] * acc_ref[even, t] + pick_diag(o_t, u)

    run_items(n_ref, total_ref, row, nb, ready, item, finish)


def group_of(width):
    return 256 if width % 256 == 0 else 128


def whole_spec(shape):
    rest = (0,) * (len(shape) - 1)
    return pl.BlockSpec((1,) + tuple(shape[1:]), lambda r, *_: (r,) + rest)


def one_spec(shape):
    rest = (0,) * (len(shape) - 1)
    return pl.BlockSpec((1,) + tuple(shape[1:]), lambda r, *_: (r,) + rest,
                        pipeline_mode=pl.Buffered(1))


def attention_forward(q, k, v, plan):
    *tables, seg_cols, seg_rows = plan
    rows, full_len, width = q.shape
    nb, group = full_len // BLK, group_of(width)
    tiles = width // 128
    pairs = rows * full_len * full_len // 4 * width
    args = (q, k, v, seg_cols, seg_rows)
    return pl.pallas_call(
        functools.partial(forward_kernel, group),
        out_shape=(
            jax.ShapeDtypeStruct((rows, full_len, width), jnp.bfloat16),
            jax.ShapeDtypeStruct((rows, nb, 1, width), jnp.float32),
        ),
        grid_spec=pltpu.PrefetchScalarGridSpec(
            num_scalar_prefetch=3,
            grid=(rows,),
            in_specs=[one_spec(x.shape) for x in args],
            out_specs=(one_spec((rows, full_len, width)), one_spec((rows, nb, 1, width))),
            scratch_shapes=[
                pltpu.VMEM((nb, width, 128), jnp.bfloat16),
                pltpu.VMEM((4, width // group, group, group), jnp.bfloat16),
                pltpu.VMEM((2, tiles, 1, 128), jnp.float32),
                pltpu.VMEM((2, tiles, 1, 128), jnp.float32),
                pltpu.VMEM((2, tiles, HD, 128), jnp.float32),
            ],
        ),
        compiler_params=pltpu.CompilerParams(vmem_limit_bytes=62 << 20),
        cost_estimate=pl.CostEstimate(
            flops=4 * pairs, transcendentals=pairs // HD, bytes_accessed=8 * q.size
        ),
        name="attention_forward",
    )(*tables, *args)


def backward_kernel(group, n_ref, list_ref, total_ref, q_ref, k_ref, v_ref, o_ref, do_ref,
                    lse_ref, segc_ref, segr_ref, dq_ref, dk_ref, dv_ref,
                    kt_ref, qst_ref, qs_ref, dost_ref, dos_ref, delta_ref, acc_ref,
                    dk_acc, dv_acc):
    row = pl.program_id(0)
    full_len, width = q_ref.shape[1], q_ref.shape[2]
    nb = full_len // BLK
    groups, halves = width // group, group // 128
    tiles = width // 128
    turn_all(k_ref, kt_ref, nb, width)
    for ref in (qst_ref, qs_ref, dost_ref, dos_ref, dk_acc, dv_acc, acc_ref):
        ref[...] = jnp.zeros_like(ref)
    low = lane_low(1)

    def ready(a, slot):
        start = pl.multiple_of(a * BLK, BLK)
        for t in range(tiles):
            g, u = t // halves, t % halves
            lanes = slice(t * 128, t * 128 + 128)
            square = slice(u * 128, u * 128 + 128)
            q_tile = (q_ref[0, pl.ds(start, BLK), lanes] * 0.125).astype(jnp.bfloat16)
            g_tile = do_ref[0, pl.ds(start, BLK), lanes]
            o_tile = o_ref[0, pl.ds(start, BLK), lanes]
            g_turn = transposed_twice(g_tile)
            qst_ref[slot, g, square, square] = diag128(transposed_twice(q_tile))
            dost_ref[slot, g, square, square] = diag128(g_turn)
            qs_ref[slot, g, square, square] = diag128(jnp.concatenate([q_tile, q_tile], axis=0))
            dos_ref[slot, g, square, square] = diag128(
                jnp.concatenate([g_tile, g_tile], axis=0)
            )
            product = g_turn.astype(jnp.float32) * transposed_twice(o_tile).astype(jnp.float32)
            delta_ref[slot, t] = jnp.where(
                low,
                jnp.sum(product[:HD], axis=0, keepdims=True),
                jnp.sum(product[HD:], axis=0, keepdims=True),
            )

    def finish(a):
        even = lax.rem(a, 2)
        start = pl.multiple_of(a * BLK, BLK)
        for t in range(tiles):
            dq_ref[0, pl.ds(start, BLK), t * 128 : t * 128 + 128] = (
                head_rows(acc_ref[even, t]) * 0.125
            ).astype(jnp.bfloat16)

    def item(slot, a, c, real):
        ids, safe = chunk_ids(list_ref, row, a * nb + c * CHUNK, nb, real)
        even = lax.rem(a, 2)
        allowed = block_rows(segc_ref, ids, slice(0, 128)) == segr_ref[0, a]
        first = c == 0
        for g in range(groups):
            lanes = slice(g * group, g * group + group)
            s_t = dot_f32(block_rows(k_ref, safe, lanes), qst_ref[slot, g])
            dp_t = dot_f32(block_rows(v_ref, safe, lanes), dost_ref[slot, g])
            p_parts, ds_parts = [], []
            for u in range(halves):
                t = g * halves + u
                half = slice(u * 128, u * 128 + 128)
                lse = lse_ref[0, a, :, t * 128 : t * 128 + 128]
                p = jnp.exp(jnp.where(allowed, s_t[:, half], NEG) - lse)
                ds = p * (dp_t[:, half] - delta_ref[slot, t])
                p_parts.append(p.astype(jnp.bfloat16))
                ds_parts.append(ds.astype(jnp.bfloat16))
            p_t = jnp.concatenate(p_parts, axis=1) if halves > 1 else p_parts[0]
            ds_t = jnp.concatenate(ds_parts, axis=1) if halves > 1 else ds_parts[0]
            dv = dot_f32(p_t, dos_ref[slot, g])
            dk = dot_f32(ds_t, qs_ref[slot, g])
            dq_t = dot_f32(turned_blocks(kt_ref, safe, lanes), ds_t)
            for j in range(CHUNK):
                where = pl.ds(pl.multiple_of(safe[j] * BLK, BLK), BLK)
                part = slice(j * BLK, j * BLK + BLK)
                dv_acc[where, lanes] += dv[part]
                dk_acc[where, lanes] += dk[part]
            for u in range(halves):
                t = g * halves + u
                acc_ref[even, t] = jnp.where(first, 0.0, acc_ref[even, t]) + pick_diag(dq_t, u)

    run_items(n_ref, total_ref, row, nb, ready, item, finish)

    def flush(a, _):
        where = pl.ds(pl.multiple_of(a * BLK, BLK), BLK)
        dk_ref[0, where, :] = dk_acc[where, :].astype(jnp.bfloat16)
        dv_ref[0, where, :] = dv_acc[where, :].astype(jnp.bfloat16)
        return 0

    lax.fori_loop(0, nb, flush, 0, unroll=2)


def attention_backward(q, k, v, o, do, lse, plan):
    *tables, seg_cols, seg_rows = plan
    rows, full_len, width = q.shape
    nb, group = full_len // BLK, group_of(width)
    tiles, groups = width // 128, width // group
    pairs = rows * full_len * full_len // 4 * width
    args = (q, k, v, o, do, lse, seg_cols, seg_rows)
    like = jax.ShapeDtypeStruct((rows, full_len, width), jnp.bfloat16)
    square = pltpu.VMEM((4, groups, group, group), jnp.bfloat16)
    return pl.pallas_call(
        functools.partial(backward_kernel, group),
        out_shape=(like, like, like),
        grid_spec=pltpu.PrefetchScalarGridSpec(
            num_scalar_prefetch=3,
            grid=(rows,),
            in_specs=[one_spec(x.shape) for x in args],
            out_specs=tuple(one_spec(like.shape) for _ in range(3)),
            scratch_shapes=[
                pltpu.VMEM((nb, width, 128), jnp.bfloat16),
                square, square, square, square,
                pltpu.VMEM((4, tiles, 1, 128), jnp.float32),
                pltpu.VMEM((2, tiles, HD, 128), jnp.float32),
                pltpu.VMEM((full_len, width), jnp.float32),
                pltpu.VMEM((full_len, width), jnp.float32),
            ],
        ),
        compiler_params=pltpu.CompilerParams(vmem_limit_bytes=62 << 20),
        cost_estimate=pl.CostEstimate(
            flops=10 * pairs, transcendentals=pairs // HD, bytes_accessed=16 * q.size
        ),
        name="attention_backward",
    )(*tables, *args)


def pair_bit(index, bit):
    return lax.rem(index // (1 << bit), 2)


def pair_of(index, bit):
    return index + (1 - 2 * pair_bit(index, bit)) * (1 << bit)


def all_arrived(bits):
    me = lax.axis_index("fsdp")
    barrier = pltpu.get_barrier_semaphore()
    for bit in range(bits):
        pl.semaphore_signal(
            barrier, inc=1, device_id={"fsdp": pair_of(me, bit)},
            device_id_type=pl.DeviceIdType.MESH,
        )
    pl.semaphore_signal(
        barrier, inc=1, device_id={"seq": 1 - lax.axis_index("seq")},
        device_id_type=pl.DeviceIdType.MESH,
    )
    pl.semaphore_wait(barrier, bits + 1)


def qkv_backward_kernel(
    bits, xt_in, dq_in, dk_in, dv_in, wt_in, res_in, small_in,
    wq_out, wk_out, wv_out, small_out, tok_out,
    xt, grads, wt, res, tok, kept, sends, lands, final, small, small_land, result,
    in_sem, tok_send, tok_land, own_sem, send_sem, land_sem, x_send, x_land,
    small_send, small_recv, out_sem,
):
    me, side = lax.axis_index("fsdp"), lax.axis_index("seq")
    half = tok.shape[2] * tok.shape[1]
    piece, pieces = tok.shape[2], tok.shape[1]
    own, width = wq_out.shape
    owners = 1 << bits
    sources = (dq_in, dk_in, dv_in)
    rows_of = [pl.ds(pl.multiple_of(p * half, half), half) for p in (1 - side, side)]
    loads = [pltpu.make_async_copy(wt_in, wt, in_sem.at[0])]
    for p in range(2):
        for i in range(3):
            loads.append(
                pltpu.make_async_copy(
                    sources[i].at[rows_of[p]], grads.at[i, rows_of[p]], in_sem.at[1 + 4 * p + i]
                )
            )
        loads.append(
            pltpu.make_async_copy(res_in.at[rows_of[p]], res.at[rows_of[p]], in_sem.at[4 + 4 * p])
        )
    loads.append(pltpu.make_async_copy(xt_in, xt, in_sem.at[9]))
    loads.append(pltpu.make_async_copy(small_in, small.at[0], in_sem.at[10]))
    for i in (0, 1, 2, 3, 4, 9, 5, 6, 7, 8, 10):
        loads[i].start()
    all_arrived(bits)

    def token_rows(start):
        total = res[pl.ds(start, piece), :].astype(jnp.float32)
        for i in range(3):
            total = total + dot_f32(
                grads[i, pl.ds(start, piece), :], wt[i]
            )
        return total.astype(jnp.bfloat16)

    def sent(i):
        return pltpu.make_async_remote_copy(
            src_ref=tok.at[0, i],
            dst_ref=tok_out.at[side, pl.ds(pl.multiple_of(i * piece, piece), piece)],
            send_sem=tok_send.at[i], recv_sem=tok_land.at[i],
            device_id={"seq": 1 - side}, device_id_type=pl.DeviceIdType.MESH,
        )

    def landed(i):
        return pltpu.make_async_remote_copy(
            src_ref=tok.at[0, i],
            dst_ref=tok_out.at[1 - side, pl.ds(pl.multiple_of(i * piece, piece), piece)],
            send_sem=tok_send.at[i], recv_sem=tok_land.at[i],
            device_id={"seq": 1 - side}, device_id_type=pl.DeviceIdType.MESH,
        )

    def stays(i):
        return pltpu.make_async_copy(
            tok.at[1, i],
            tok_out.at[side, pl.ds(pl.multiple_of(i * piece, piece), piece)],
            own_sem.at[i],
        )

    def send_piece(i, _):
        start = pl.multiple_of((1 - side) * half + i * piece, piece)
        tok[0, i] = token_rows(start)
        sent(i).start()
        return 0

    def keep_piece(i, _):
        start = pl.multiple_of(side * half + i * piece, piece)
        tok[1, i] = token_rows(start)
        stays(i).start()
        return 0

    low_bit = pair_bit(me, 0) == 0
    tile = 8 if owners % 8 == 0 else owners
    first_of = [0]
    for bit in range(bits):
        first_of.append(first_of[-1] + (owners >> (bit + 1)))

    def weights(i):
        def rows(m, _):
            rows_here = pl.ds(pl.multiple_of(m * tile * own, tile * own), tile * own)
            block = dot_f32(
                jnp.concatenate(
                    [xt[h, r, rows_here, :] for h in range(2) for r in range(pieces)], axis=1
                ),
                grads[i],
            ).reshape(tile // 2, 2, own, width)
            even, odd = block[:, 0], block[:, 1]
            spot = pl.ds(m * (tile // 2), tile // 2)
            kept[i, spot] = jnp.where(low_bit, even, odd)
            sends[i, spot] = jnp.where(low_bit, odd, even).astype(jnp.bfloat16)
            return 0

        lax.fori_loop(0, owners // tile, rows, 0)

    def hop(i, bit):
        count = owners >> (bit + 1)
        spot = pl.ds(first_of[bit], count)
        return pltpu.make_async_remote_copy(
            src_ref=sends.at[i, spot], dst_ref=lands.at[i, spot],
            send_sem=send_sem.at[i, bit], recv_sem=land_sem.at[i, bit],
            device_id={"fsdp": pair_of(me, bit)}, device_id_type=pl.DeviceIdType.MESH,
        )

    def cross(i):
        return pltpu.make_async_remote_copy(
            src_ref=final.at[0, i], dst_ref=final.at[1, i],
            send_sem=x_send.at[i], recv_sem=x_land.at[i],
            device_id={"seq": 1 - side}, device_id_type=pl.DeviceIdType.MESH,
        )

    def advance(i, bit):
        hop(i, bit).wait_recv()
        base = first_of[bit]
        if bit + 1 == bits:
            total = kept[i, base] + lands[i, base].astype(jnp.float32)
            final[0, i] = total.astype(jnp.bfloat16)
            cross(i).start()
            return
        nxt = pair_bit(me, bit + 1)

        def one(j, _):
            stay, go = 2 * j + nxt, 2 * j + 1 - nxt
            kept[i, first_of[bit + 1] + j] = kept[i, base + stay] + lands[
                i, base + stay
            ].astype(jnp.float32)
            sends[i, first_of[bit + 1] + j] = (
                kept[i, base + go] + lands[i, base + go].astype(jnp.float32)
            ).astype(jnp.bfloat16)
            return 0

        lax.fori_loop(0, owners >> (bit + 2), one, 0)
        hop(i, bit + 1).start()

    outs = (wq_out, wk_out, wv_out)

    def written(i):
        return pltpu.make_async_copy(result.at[i], outs[i], out_sem.at[i])

    def finish(i):
        cross(i).wait_recv()
        result[i] = final[0, i].astype(jnp.float32) + final[1, i].astype(jnp.float32)
        written(i).start()

    def small_hop(bit):
        where = {"fsdp": pair_of(me, bit)} if bit < bits else {"seq": 1 - side}
        return pltpu.make_async_remote_copy(
            src_ref=small.at[bit], dst_ref=small_land.at[bit],
            send_sem=small_send.at[bit], recv_sem=small_recv.at[bit],
            device_id=where, device_id_type=pl.DeviceIdType.MESH,
        )

    def small_advance(bit):
        small_hop(bit).wait_recv()
        small[bit + 1] = small[bit] + small_land[bit]
        if bit < bits:
            small_hop(bit + 1).start()

    def column_sums(i, spot):
        def one(c, total):
            block = grads[i, pl.ds(pl.multiple_of(c * 256, 256), 256), :].astype(jnp.float32)
            return total + jnp.sum(block.reshape(32, 8, width), axis=0)

        total = lax.fori_loop(
            0, grads.shape[1] // 256, one, jnp.zeros((8, width), jnp.float32)
        )
        small[0, spot : spot + 1] = jnp.sum(total, axis=0, keepdims=True)

    for i in range(5):
        loads[i].wait()
    send_piece(0, 0)
    for i in range(5, 11):
        loads[i].wait()

    def begin(i, _):
        weights(i)
        hop(i, 0).start()
        send_piece(i + 1, 0)
        advance(i, 0)
        return 0

    lax.fori_loop(0, 3, begin, 0)
    column_sums(0, 0)
    column_sums(2, 1)
    small_hop(0).start()

    def second(i, _):
        keep_piece(i, 0)
        advance(i, 1)
        return 0

    lax.fori_loop(0, 3, second, 0)
    small_advance(0)
    keep_piece(3, 0)
    for bit in range(2, bits):
        for i in range(3):
            advance(i, bit)
        small_advance(bit - 1)
    for bit in range(bits - 1, bits + 1):
        small_advance(bit)
    for i in range(3):
        finish(i)
    small_copy = pltpu.make_async_copy(small.at[bits + 1], small_out, out_sem.at[3])
    small_copy.start()
    for i in range(3):
        written(i).wait()
        cross(i).wait_send()
        for bit in range(bits):
            hop(i, bit).wait_send()
    for bit in range(bits + 1):
        small_hop(bit).wait_send()
    small_copy.wait()
    for i in range(pieces):
        stays(i).wait()
        sent(i).wait_send()
        landed(i).wait_recv()


def qkv_backward(xt, dq, dk, dv, wt, resid, small, own):
    tokens, width = dq.shape
    bits = lax.axis_size("fsdp").bit_length() - 1
    owners = 1 << bits
    pieces = 4
    piece = tokens // 2 // pieces
    dma = pltpu.SemaphoreType.DMA
    f32, bf16 = jnp.float32, jnp.bfloat16
    shard = jax.ShapeDtypeStruct((own, width), f32)
    anywhere = pl.BlockSpec(memory_space=pltpu.HBM)
    return pl.pallas_call(
        functools.partial(qkv_backward_kernel, bits),
        out_shape=(
            shard, shard, shard,
            jax.ShapeDtypeStruct(small.shape, f32),
            jax.ShapeDtypeStruct((2, tokens // 2, width), bf16),
        ),
        in_specs=[anywhere] * 7,
        out_specs=(anywhere,) * 5,
        scratch_shapes=[
            pltpu.VMEM(xt.shape, bf16),
            pltpu.VMEM((3, tokens, width), bf16),
            pltpu.VMEM(wt.shape, bf16),
            pltpu.VMEM((tokens, width), bf16),
            pltpu.VMEM((2, pieces, piece, width), bf16),
            pltpu.VMEM((3, owners - 1, own, width), f32),
            pltpu.VMEM((3, owners - 1, own, width), bf16),
            pltpu.VMEM((3, owners - 1, own, width), bf16),
            pltpu.VMEM((2, 3, own, width), bf16),
            pltpu.VMEM((bits + 2,) + small.shape, f32),
            pltpu.VMEM((bits + 1,) + small.shape, f32),
            pltpu.VMEM((3, own, width), f32),
            dma((11,)), dma((pieces,)), dma((pieces,)), dma((pieces,)),
            dma((3, bits)), dma((3, bits)), dma((3,)), dma((3,)),
            dma((bits + 1,)), dma((bits + 1,)), dma((4,)),
        ],
        compiler_params=pltpu.CompilerParams(
            collective_id=1, has_side_effects=True, vmem_limit_bytes=62 << 20
        ),
        cost_estimate=pl.CostEstimate(
            flops=40 * tokens * width * width, transcendentals=0,
            bytes_accessed=16 * tokens * width,
        ),
        name="qkv_backward",
    )(xt, dq, dk, dv, wt, resid, small)


def qkv_forward_kernel(
    bits, tokens_in, own_in, grad_in,
    grad_out, x_out, xt_out, q_out, k_out, v_out, wt_out, small_out,
    x, xt, w, wt, qkv, small,
    own_sem, tok_send, tok_land, load_sem, send_sem, land_sem, x_sem, xt_sem, out_sem, w_sem,
    small_sem,
):
    me, side = lax.axis_index("fsdp"), lax.axis_index("seq")
    pieces, piece, width = x.shape[1], x.shape[2], x.shape[3]
    mine = [pair_bit(me, bit) for bit in range(bits)]
    columns = part_columns(width)
    outs = (q_out, k_out, v_out)

    def slot(bit, part):
        here = [slice(None)] * (bits - 1 - bit) + [mine[b] for b in range(bit, -1, -1)]
        return tuple(here) + (slice(None), columns[part])

    own_tokens = pltpu.make_async_copy(tokens_in.at[side], x.at[side], own_sem.at[0])
    own_tokens.start()
    grad_rows = pltpu.make_async_copy(grad_in.at[1 - side], grad_out, own_sem.at[1])
    grad_rows.start()

    def load(part):
        spot = tuple(mine[b] for b in range(bits - 1, -1, -1)) + (slice(None), columns[part])
        return pltpu.make_async_copy(
            own_in.at[:, columns[part]], w.at[spot], load_sem.at[part]
        )

    for part in range(3):
        load(part).start()
    all_arrived(bits)

    def sent(i):
        return pltpu.make_async_remote_copy(
            src_ref=tokens_in.at[1 - side, i], dst_ref=x.at[side, i],
            send_sem=tok_send.at[i], recv_sem=tok_land.at[i],
            device_id={"seq": 1 - side}, device_id_type=pl.DeviceIdType.MESH,
        )

    def landed(i):
        return pltpu.make_async_remote_copy(
            src_ref=tokens_in.at[1 - side, i], dst_ref=x.at[1 - side, i],
            send_sem=tok_send.at[i], recv_sem=tok_land.at[i],
            device_id={"seq": 1 - side}, device_id_type=pl.DeviceIdType.MESH,
        )

    def hop(part, turn):
        bit = bits - 1 - turn
        return pltpu.make_async_remote_copy(
            src_ref=w.at[slot(bit, part)], dst_ref=w.at[slot(bit, part)],
            send_sem=send_sem.at[part, turn], recv_sem=land_sem.at[part, turn],
            device_id={"fsdp": pair_of(me, bit)}, device_id_type=pl.DeviceIdType.MESH,
        )

    for part in range(3):
        load(part).wait()
        hop(part, 0).start()
    for i in range(pieces):
        sent(i).start()

    def x_copy(half, i):
        return pltpu.make_async_copy(x.at[half, i], x_out.at[half, i], x_sem.at[half, i])

    def out_copy(part, half, i):
        return pltpu.make_async_copy(
            qkv.at[part, half, i], outs[part].at[half, i], out_sem.at[part, half, i]
        )

    def xt_copy(half, i):
        return pltpu.make_async_copy(xt.at[half, i], xt_out.at[half, i], xt_sem.at[half, i])

    def w_copy(part):
        return pltpu.make_async_copy(wt.at[part], wt_out.at[part], w_sem.at[part])

    def whole(part):
        first = part_start(width, part)
        spot = (slice(None),) * (bits + 1) + (slice(first, first + width),)
        return w[spot].reshape(width, width)

    def turn(half, i):
        x_copy(half, i).start()
        xt[half, i] = x[half, i].T
        xt_copy(half, i).start()

    def project(part, half, i):
        total = dot_f32(x[half, i], whole(part))
        if part == 0:
            total = total + small[0:1, :]
        if part == 2:
            total = total + small[1:2, :]
        qkv[part, half, i] = total.astype(jnp.bfloat16)
        out_copy(part, half, i).start()

    def over(body):
        def one(i, _):
            body(i)
            return 0

        lax.fori_loop(0, pieces, one, 0)

    def turn_weights(part):
        wt[part] = whole(part).T
        w_copy(part).start()

    def other(i):
        landed(i).wait_recv()
        turn(1 - side, i)
        project(0, 1 - side, i)
        project(1, 1 - side, i)

    own_tokens.wait()
    over(lambda i: turn(side, i))
    for step in range(bits + 2):
        full = None
        for part in range(3):
            hops = step - part
            if 0 <= hops < bits:
                hop(part, hops).wait_recv()
                if hops + 1 < bits:
                    hop(part, hops + 1).start()
                else:
                    full = part
        if full == 0:
            spot = (slice(None),) * (bits + 1) + (slice(width, width + 128),)
            turned = w[spot].reshape(width, 128).astype(jnp.float32).T
            small[...] = turned[: small.shape[0]]
            pltpu.make_async_copy(small, small_out, small_sem.at[0]).start()
        if full is not None:
            over(lambda i: project(full, side, i))
        if full == 1:
            turn_weights(0)
            turn_weights(1)
            over(other)
        if full == 2:
            over(lambda i: project(2, 1 - side, i))
            turn_weights(2)
    for i in range(pieces):
        sent(i).wait_send()
    for part in range(3):
        w_copy(part).wait()
        for hops in range(bits):
            hop(part, hops).wait_send()
    grad_rows.wait()
    pltpu.make_async_copy(small, small_out, small_sem.at[0]).wait()
    for half in range(2):
        for i in range(pieces):
            x_copy(half, i).wait()
            xt_copy(half, i).wait()
            for part in range(3):
                out_copy(part, half, i).wait()


def part_start(width, part):
    return part * width + (128 if part else 0)


def part_columns(width):
    return (
        slice(0, width + 128),
        slice(width + 128, 2 * width + 128),
        slice(2 * width + 128, 3 * width + 128),
    )


def qkv_forward(tokens_in, own_pack, out_grad):
    rows, local, width = tokens_in.shape
    own, columns = own_pack.shape
    bits = lax.axis_size("fsdp").bit_length() - 1
    pieces = 4
    piece = local // pieces
    dma = pltpu.SemaphoreType.DMA
    bf16 = jnp.bfloat16
    halves = (2, pieces, piece, width)
    gathered = (2,) * bits + (own, columns)
    anywhere = pl.BlockSpec(memory_space=pltpu.HBM)
    like = jax.ShapeDtypeStruct(halves, bf16)
    turned = (2, pieces, width, piece)
    grad, x, xt, q, k, v, weights_t, small = pl.pallas_call(
        functools.partial(qkv_forward_kernel, bits),
        out_shape=(
            jax.ShapeDtypeStruct((local, width), bf16),
            like, jax.ShapeDtypeStruct(turned, bf16), like, like, like,
            jax.ShapeDtypeStruct((3, width, width), bf16),
            jax.ShapeDtypeStruct((SMALL_ROWS, width), jnp.float32),
        ),
        in_specs=[anywhere] * 3,
        out_specs=(anywhere,) * 8,
        scratch_shapes=[
            pltpu.VMEM(halves, bf16),
            pltpu.VMEM(turned, bf16),
            pltpu.VMEM(gathered, bf16),
            pltpu.VMEM((3, width, width), bf16),
            pltpu.VMEM((3,) + halves, bf16),
            pltpu.VMEM((SMALL_ROWS, width), jnp.float32),
            dma((2,)), dma((pieces,)), dma((pieces,)), dma((3,)),
            dma((3, bits)), dma((3, bits)), dma((2, pieces)), dma((2, pieces)),
            dma((3, 2, pieces)), dma((3,)), dma((1,)),
        ],
        compiler_params=pltpu.CompilerParams(
            collective_id=2, has_side_effects=True, vmem_limit_bytes=62 << 20
        ),
        cost_estimate=pl.CostEstimate(
            flops=18 * rows * local * width * width, transcendentals=0,
            bytes_accessed=16 * rows * local * width,
        ),
        name="qkv_forward",
    )(tokens_in.reshape(halves), own_pack, out_grad)
    flat = rows * local, width
    return (
        x.reshape(flat), q.reshape(flat), k.reshape(flat), v.reshape(flat), xt, weights_t, small, grad
    )


eps_norm = 1e-06


def dot_rows(left, right):
    return lax.dot_general(
        left, right, (((0,), (0,)), ((), ())), preferred_element_type=jnp.float32
    )


def dot_nt(left, right):
    return lax.dot_general(
        left, right, (((1,), (1,)), ((), ())), preferred_element_type=jnp.float32
    )


def row_mean(values):
    return jnp.mean(values, axis=-1, keepdims=True)


GELU_K = math.sqrt(2.0 / math.pi)
GELU_A = 0.044715


def gelu_pair(u):
    square = u * u
    t = jnp.tanh(u * (GELU_K + (GELU_K * GELU_A) * square))
    half = 0.5 + 0.5 * t
    slope = half + (u * (half * (1.0 - t))) * (GELU_K + (3.0 * GELU_K * GELU_A) * square)
    return u * half, slope


OUT_B, GAIN_1, BIAS_1, OUTER_B, GAIN_2, BIAS_2, INNER_B = 2, 3, 4, 5, 6, 7, 8
STEP_ROWS = 512
SMALL_ROWS = 16


def middle_kernel(
    chunks, side, weights_in, small, att, tokens, grad_own, grad_other,
    out_keep, out_send, d_attn, d_att, d_weights, sums,
    w, acc, act, slope, z_one, flow, rs_one, normed, normed_t, d_mlp, part, load_sem, store_sem,
):
    step, steps = pl.program_id(0), pl.num_programs(0)
    rows, width = att.shape
    f32, bf16 = jnp.float32, jnp.bfloat16
    count = 2 * chunks + 1
    staying = step // (steps // 2) == side[0]

    def load(i):
        return pltpu.make_async_copy(
            weights_in.at[:, pl.ds(i * width, width)], w.at[i], load_sem.at[i]
        )

    def store(i):
        return pltpu.make_async_copy(
            w.at[i], d_weights.at[:, pl.ds(i * width, width)], store_sem.at[i]
        )

    @pl.when(step == 0)
    def _():
        for i in range(count):
            load(i).start()
        part[...] = jnp.zeros_like(part)

        def clear(i, _):
            acc[i] = jnp.zeros_like(acc[i])
            return 0

        lax.fori_loop(0, count, clear, 0)
        load(0).wait()

    def vector(i):
        return small[i : i + 1, :]

    def eights(values):
        return jnp.sum(values.reshape(-1, 8, values.shape[-1]), axis=0)

    def add_sum(i, values):
        part[i] += eights(values)

    def by_rows(body):
        def one(r, _):
            body(pl.ds(pl.multiple_of(r * STEP_ROWS, STEP_ROWS), STEP_ROWS))
            return 0

        lax.fori_loop(0, rows // STEP_ROWS, one, 0)

    flow[...] = dot_f32(att[...], w[0])

    def norm_one(r):
        attn = flow[r, :] + vector(OUT_B)
        resid = tokens[r, :].astype(f32) + attn
        add_sum(INNER_B + chunks, resid * resid)
        add_sum(INNER_B + chunks + 1, attn * attn)
        centred = resid - row_mean(resid)
        scale = lax.rsqrt(row_mean(centred * centred) + eps_norm)
        z = centred * scale
        z_one[r, :] = z
        rs_one[r, :] = scale
        normed[r, :] = (z * vector(GAIN_1) + vector(BIAS_1)).astype(bf16)

    by_rows(norm_one)
    normed_t[...] = normed[...].T

    def inner(c, _):
        @pl.when(step == 0)
        def _():
            load(1 + c).wait()

        for n in range(width // 256):
            cols = slice(n * 256, n * 256 + 256)
            pre = dot_f32(normed[...], w[1 + c, :, cols]) + small[pl.ds(INNER_B + c, 1), cols]
            value, grade = gelu_pair(pre)
            act[c, :, cols] = value.astype(bf16)
            slope[c, :, cols] = grade.astype(bf16)
        return 0

    lax.fori_loop(0, chunks, inner, 0)

    @pl.when(step == 0)
    def _():
        for i in range(1 + chunks, count):
            load(i).wait()

    flow[...] = dot_f32(act[0], w[1 + chunks])

    def outer(c, _):
        flow[...] += dot_f32(act[c], w[1 + chunks + c])
        return 0

    lax.fori_loop(1, chunks, outer, 0)

    def norm_two(r):
        mlp = flow[r, :] + vector(OUTER_B)
        add_sum(INNER_B + chunks + 2, mlp * mlp)
        resid = z_one[r, :] * vector(GAIN_1) + vector(BIAS_1) + mlp
        centred = resid - row_mean(resid)
        scale = lax.rsqrt(row_mean(centred * centred) + eps_norm)
        z = centred * scale
        result = (z * vector(GAIN_2) + vector(BIAS_2)).astype(bf16)

        @pl.when(staying)
        def _():
            out_keep[r, :] = result

        @pl.when(jnp.logical_not(staying))
        def _():
            out_send[r, :] = result

        grad = jnp.where(staying, grad_own[r, :], grad_other[r, :]).astype(f32)
        add_sum(GAIN_2, grad * z)
        add_sum(BIAS_2, grad)
        grad = grad * vector(GAIN_2)
        d_resid = scale * (grad - row_mean(grad) - z * row_mean(grad * z))
        low = d_resid.astype(bf16)
        add_sum(OUTER_B, low.astype(f32))
        d_mlp[r, :] = low
        flow[r, :] = d_resid

    by_rows(norm_two)

    def back(c, _):
        for n in range(width // 256):
            cols = slice(n * 256, n * 256 + 256)
            d_act = dot_nt(d_mlp[...], w[1 + chunks + c, cols, :])
            d_pre = (slope[c, :, cols].astype(f32) * d_act).astype(bf16)
            part[INNER_B + c, :, cols] += eights(d_pre.astype(f32))
            slope[c, :, cols] = d_pre
        acc[1 + chunks + c] += dot_rows(act[c], d_mlp[...])
        acc[1 + c] += dot_f32(normed_t[...], slope[c])
        flow[...] += dot_nt(slope[c], w[1 + c])

        @pl.when(step == steps - 1)
        def _():
            for i in (1 + c, 1 + chunks + c):
                w[i] = acc[i].astype(bf16)
                store(i).start()

        return 0

    lax.fori_loop(0, chunks, back, 0)

    def norm_one_back(r):
        grad = flow[r, :]
        z = z_one[r, :]
        add_sum(GAIN_1, grad * z)
        add_sum(BIAS_1, grad)
        grad = grad * vector(GAIN_1)
        d_resid = rs_one[r, :] * (grad - row_mean(grad) - z * row_mean(grad * z))
        low = d_resid.astype(bf16)
        add_sum(OUT_B, low.astype(f32))
        d_attn[r, :] = low

    by_rows(norm_one_back)
    acc[0] += dot_rows(att[...], d_attn[...])
    d_att[...] = dot_nt(d_attn[...], w[0]).astype(bf16)

    @pl.when(step == steps - 1)
    def _():
        w[0] = acc[0].astype(bf16)
        store(0).start()
        sums[...] = jnp.sum(part[...], axis=1)
        for i in range(count):
            store(i).wait()


def middle(side, weights, small, att, tokens, grad_own, grad_other):
    tok_count, width = att.shape
    chunks = (weights.shape[1] // width - 1) // 2
    count = 2 * chunks + 1
    rows = 512
    f32, bf16 = jnp.float32, jnp.bfloat16
    half = tok_count // rows // 2

    def early(i):
        return jnp.minimum(i, half - 1)

    def late(i):
        return jnp.maximum(i - half, 0)

    tile = pl.BlockSpec((rows, width), lambda i, s: (i, 0))
    keep = pl.BlockSpec((rows, width), lambda i, s: (jnp.where(s[0] == 0, early(i), late(i)), 0))
    send = pl.BlockSpec((rows, width), lambda i, s: (jnp.where(s[0] == 0, late(i), early(i)), 0))
    fixed = pl.BlockSpec(small.shape, lambda i, s: (0, 0), pipeline_mode=pl.Buffered(1))
    anywhere = pl.BlockSpec(memory_space=pl.ANY)
    like = jax.ShapeDtypeStruct((tok_count, width), bf16)
    part = jax.ShapeDtypeStruct((tok_count // 2, width), bf16)
    flops = 6 * tok_count * width * width * count
    return pl.pallas_call(
        functools.partial(middle_kernel, chunks),
        out_shape=(
            part, part, like, like,
            jax.ShapeDtypeStruct(weights.shape, bf16),
            jax.ShapeDtypeStruct(small.shape, f32),
        ),
        grid_spec=pltpu.PrefetchScalarGridSpec(
          num_scalar_prefetch=1,
          grid=(tok_count // rows,),
          in_specs=[anywhere, fixed, tile, tile, keep, send],
          out_specs=(
            keep, send, tile, tile, anywhere, pl.BlockSpec(small.shape, lambda i, s: (0, 0))
          ),
          scratch_shapes=[
            pltpu.VMEM((count, width, width), bf16),
            pltpu.VMEM((count, width, width), f32),
            pltpu.VMEM((chunks, rows, width), bf16),
            pltpu.VMEM((chunks, rows, width), bf16),
            pltpu.VMEM((rows, width), f32),
            pltpu.VMEM((rows, width), f32),
            pltpu.VMEM((rows, 1), f32),
            pltpu.VMEM((rows, width), bf16),
            pltpu.VMEM((width, rows), bf16),
            pltpu.VMEM((rows, width), bf16),
            pltpu.VMEM((small.shape[0], 8, width), f32),
            pltpu.SemaphoreType.DMA((count,)),
            pltpu.SemaphoreType.DMA((count,)),
          ],
        ),
        compiler_params=pltpu.CompilerParams(vmem_limit_bytes=62 << 20),
        cost_estimate=pl.CostEstimate(
            flops=2 * flops, transcendentals=tok_count * width * chunks,
            bytes_accessed=12 * tok_count * width + 4 * weights.size,
        ),
        name="middle",
    )(side.reshape(1), weights, small, att, tokens, grad_own, grad_other)


def contract_rows(left, right):
    return lax.dot_general(
        left, right, (((0,), (0,)), ((), ())), preferred_element_type=jnp.float32
    )


def times_transpose(left, right):
    return lax.dot_general(
        left, right, (((1,), (1,)), ((), ())), preferred_element_type=jnp.float32
    )


def butterfly_sum(values, axis):
    size = lax.axis_size(axis)
    if size & (size - 1):
        return lax.psum(values, axis)
    step = 1
    while step < size:
        pairs = [(i, i ^ step) for i in range(size)]
        values = values + lax.ppermute(values, axis, pairs)
        step *= 2
    return values


def sum_seq(values):
    if lax.axis_size("seq") == 2:
        other = lax.ppermute(values, "seq", [(0, 1), (1, 0)])
        return values.astype(jnp.float32) + other.astype(jnp.float32)
    return lax.psum(values, "seq").astype(jnp.float32)


class Regroup:
    def __init__(self, row_count):
        self.size = lax.axis_size("seq")
        self.ways = math.gcd(row_count, self.size)
        self.parts = self.size // self.ways
        self.rows = row_count // self.ways
        me = lax.axis_index("seq")
        self.place = lax.rem(me, self.ways)
        self.row_group = me // self.parts

    def targets(self, turn):
        ways, parts = self.ways, self.parts
        return [
            (s, ((s % ways + turn) % ways) * parts + s // ways) for s in range(self.size)
        ]

    def move(self, values, pairs):
        if all(a == b for a, b in pairs):
            return values
        return lax.ppermute(values, "seq", pairs)

    def gather(self, values):
        rows, local, width = self.rows, values.shape[1], values.shape[2]
        out = jnp.zeros((rows, self.ways, local, width), values.dtype)
        for turn in range(self.ways):
            pick = lax.rem(self.place + turn, self.ways)
            chunk = lax.dynamic_slice_in_dim(values, pick * rows, rows, 0)
            chunk = self.move(chunk, self.targets(turn))
            spot = lax.rem(self.row_group - turn + self.ways, self.ways)
            out = lax.dynamic_update_slice_in_dim(out, chunk[:, None], spot, 1)
        return out.reshape(rows, self.ways * local, width)

    def scatter(self, values):
        rows, width = self.rows, values.shape[2]
        local = values.shape[1] // self.ways
        values = values.reshape(rows, self.ways, local, width)
        out = jnp.zeros((rows * self.ways, local, width), values.dtype)
        for turn in range(self.ways):
            spot = lax.rem(self.row_group - turn + self.ways, self.ways)
            chunk = lax.dynamic_slice_in_dim(values, spot, 1, 1)[:, 0]
            chunk = self.move(chunk, [(b, a) for a, b in self.targets(turn)])
            pick = lax.rem(self.place + turn, self.ways)
            out = lax.dynamic_update_slice_in_dim(out, chunk, pick * rows, 0)
        return out

    def pick_rows(self, values):
        return lax.dynamic_slice_in_dim(values, self.row_group * self.rows, self.rows, 0)

    def groups(self):
        return [
            [r * self.parts + j for j in range(self.parts)] for r in range(self.ways)
        ]

    def to_heads(self, values):
        if self.parts == 1:
            return values
        return lax.all_to_all(
            values, "seq", split_axis=2, concat_axis=1, tiled=True,
            axis_index_groups=self.groups(),
        )

    def from_heads(self, values):
        if self.parts == 1:
            return values
        return lax.all_to_all(
            values, "seq", split_axis=1, concat_axis=2, tiled=True,
            axis_index_groups=self.groups(),
        )


def shards(
    tokens_in,
    segment_ids,
    random_blocks,
    global_blocks,
    w_query,
    b_query,
    w_key,
    w_value,
    b_value,
    w_attn_out,
    b_attn_out,
    ln1_gain,
    ln1_bias,
    w_inner,
    b_inner,
    w_outer,
    b_outer,
    ln2_gain,
    ln2_bias,
    out_grad,
):
    row_count, local_len, width = tokens_in.shape
    seq_count = lax.axis_size("seq")
    fsdp_count = lax.axis_size("fsdp")
    tok_count = row_count * local_len
    own = w_query.shape[0]
    chunks = b_inner.shape[0] // own
    regroup = Regroup(row_count)
    paired = row_count == 2 and seq_count == 2 and fsdp_count in (4, 8, 16, 32)

    vectors = [b_query, b_value, b_attn_out, ln1_gain, ln1_bias, b_outer, ln2_gain, ln2_bias]
    columns = [x[:, None] for x in vectors] + [b_inner.reshape(own, chunks)]
    used = len(vectors) + chunks
    columns.append(jnp.zeros((own, 128 - used), jnp.bfloat16))
    first = jnp.concatenate([w_query] + columns + [w_key, w_value], axis=1)
    inner_own = w_inner.reshape(own, width, chunks).transpose(0, 2, 1).reshape(own, -1)
    second = jnp.concatenate([w_attn_out, inner_own, w_outer.reshape(own, -1)], axis=1)
    second = lax.all_gather(second, "fsdp", axis=0, tiled=True)
    plan = plan_blocks(
        regroup.pick_rows(segment_ids),
        regroup.pick_rows(random_blocks),
        regroup.pick_rows(global_blocks),
    )

    def split_rows(values):
        return values.reshape(regroup.rows, tok_count // regroup.rows, width)

    def part_of(values, i):
        return values[:, part_start(width, i) : part_start(width, i) + width]

    side = lax.axis_index("seq") if paired else jnp.int32(0)
    swap = [(0, 1), (1, 0)]
    if paired:
        flat_in, *qkv, turned_in, turned_w, small, leaving = qkv_forward(
            tokens_in, first, out_grad
        )
        grad_other = lax.ppermute(leaving, "seq", swap)
        grad_own = lax.dynamic_index_in_dim(out_grad, side, 0, keepdims=False)
    else:
        first = lax.all_gather(first, "fsdp", axis=0, tiled=True)
        small = first[:, width : width + SMALL_ROWS].astype(jnp.float32).T
        flat_in = regroup.gather(tokens_in).reshape(tok_count, width)
        biases = (small[0], jnp.zeros_like(small[0]), small[1])
        qkv = [
            (jnp.dot(flat_in, part_of(first, i), preferred_element_type=jnp.float32)
             + biases[i]).astype(jnp.bfloat16)
            for i in range(3)
        ]
        flat_grad = regroup.gather(out_grad).reshape(tok_count, width)
        grad_own, grad_other = flat_grad[: tok_count // 2], flat_grad[tok_count // 2 :]
    q, k, v = (regroup.to_heads(split_rows(x)) for x in qkv)
    att, lse = attention_forward(q, k, v, plan)
    att_flat = regroup.from_heads(att).reshape(tok_count, width)
    kept, sent, d_attn, d_att, d_second, sums = middle(
        side, second, small, att_flat, flat_in, grad_own, grad_other
    )
    if paired:
        sent = lax.ppermute(sent, "seq", swap)

    def scattered(values):
        return lax.psum_scatter(values, "fsdp", scatter_dimension=0, tiled=True)

    d_second = scattered(d_second)
    dq, dk, dv = attention_backward(
        q, k, v, att, regroup.to_heads(split_rows(d_att)), lse, plan
    )
    dq, dk, dv = (regroup.from_heads(x).reshape(tok_count, width) for x in (dq, dk, dv))
    mine = lax.axis_index("fsdp")
    dq, sent = lax.optimization_barrier((dq, sent))
    if paired:
        d_query_w, d_key_w, d_value_w, sums, d_tokens_in = qkv_backward(
            turned_in, dq, dk, dv, turned_w, d_attn, sums, own
        )
        d_second, sums = lax.optimization_barrier((d_second, sums))
        place = jnp.arange(2, dtype=jnp.int32)[:, None, None]
        out_tokens = jnp.where(place == side, kept[None], sent[None])
        d_tokens_in = jnp.where(place >= -side, d_tokens_in, jnp.zeros_like(d_tokens_in))
    else:
        for spot, part in ((0, dq), (1, dv)):
            sums = sums.at[spot].set(jnp.sum(part.astype(jnp.float32), axis=0))
        sums = butterfly_sum(butterfly_sum(sums, "fsdp"), "seq")
        d_query_w, d_key_w, d_value_w = (
            sum_seq(scattered(contract_rows(flat_in, x).astype(jnp.bfloat16)))
            for x in (dq, dk, dv)
        )
        d_tokens = d_attn.astype(jnp.float32)
        for i, part in enumerate((dq, dk, dv)):
            d_tokens = d_tokens + times_transpose(part, part_of(first, i))
        d_tokens_in = regroup.scatter(split_rows(d_tokens.astype(jnp.bfloat16)))
        out_tokens = regroup.scatter(split_rows(jnp.concatenate([kept, sent])))
    d_second = sum_seq(d_second)
    d_inner_w = (
        d_second[:, width : (1 + chunks) * width]
        .reshape(own, chunks, width)
        .transpose(0, 2, 1)
        .reshape(own, -1)
    )
    d_outer_w = d_second[:, (1 + chunks) * width :].reshape(own * chunks, width)
    d_vec = lax.dynamic_slice_in_dim(sums, mine * own, own, 1)
    entry_total = tok_count * width * seq_count * fsdp_count
    rms_values = jnp.sqrt(
        jnp.sum(sums[INNER_B + chunks : INNER_B + chunks + 3], axis=1) / entry_total
    )
    return (
        out_tokens,
        d_tokens_in,
        d_query_w,
        d_vec[0],
        d_key_w,
        d_value_w,
        d_vec[1],
        d_second[:, :width],
        d_vec[OUT_B],
        d_vec[GAIN_1],
        d_vec[BIAS_1],
        d_inner_w,
        d_vec[INNER_B : INNER_B + chunks].T.reshape(-1),
        d_outer_w,
        d_vec[OUTER_B],
        d_vec[GAIN_2],
        d_vec[BIAS_2],
        rms_values,
    )


def solution(mesh):
    in_specs = (
        P("fsdp", "seq", None),
        P("fsdp", None),
        P("fsdp", None, None),
        P("fsdp", None),
        P("fsdp", None),
        P("fsdp"),
        P("fsdp", None),
        P("fsdp", None),
        P("fsdp"),
        P("fsdp", None),
        P("fsdp"),
        P("fsdp"),
        P("fsdp"),
        P("fsdp", None),
        P("fsdp"),
        P("fsdp", None),
        P("fsdp"),
        P("fsdp"),
        P("fsdp"),
        P("fsdp", "seq", None),
    )
    out_specs = (
        P("fsdp", "seq", None),
        P("fsdp", "seq", None),
        P("fsdp", None),
        P("fsdp"),
        P("fsdp", None),
        P("fsdp", None),
        P("fsdp"),
        P("fsdp", None),
        P("fsdp"),
        P("fsdp"),
        P("fsdp"),
        P("fsdp", None),
        P("fsdp"),
        P("fsdp", None),
        P("fsdp"),
        P("fsdp"),
        P("fsdp"),
        P(),
    )
    return jax.shard_map(shards, mesh=mesh, in_specs=in_specs, out_specs=out_specs, check_vma=False)
```

```python
import functools
import math

import jax
import jax.numpy as jnp
from jax import lax
from jax.experimental import pallas as pl
from jax.experimental.pallas import tpu as pltpu
from jax.sharding import PartitionSpec as P

HD = 64
BLK = 64
CHUNK = 4
NEG = -1e30


def plan_blocks(seg, rand, glob):
    rows, full_len = seg.shape
    nb = full_len // BLK
    ids = jnp.arange(nb, dtype=jnp.int32)
    is_global = jnp.any(ids[None, :, None] == glob[:, None, :], axis=-1)
    picked = jnp.any(rand[:, :, None, :] == ids[None, None, :, None], axis=-1)
    nearby = jnp.abs(ids[:, None] - ids[None, :]) <= 1
    admitted = nearby[None] | picked | is_global[:, :, None] | is_global[:, None, :]
    by_block = seg.reshape(rows, nb, BLK)
    low, high = by_block[:, :, 0], by_block[:, :, BLK - 1]
    meets = (low[:, :, None] <= high[:, None, :]) & (low[:, None, :] <= high[:, :, None])
    active = (admitted & meets).astype(jnp.int32)
    upto = (ids[:, None] <= ids[None, :]).astype(jnp.int32)
    place = jnp.sum(active[:, :, :, None] * upto[None, None], axis=2) - 1
    count = jnp.sum(active, axis=2)
    hit = (place[:, :, :, None] == ids[None, None, None, :]) & (active[:, :, :, None] > 0)
    listed = jnp.sum(jnp.where(hit, ids[None, None, :, None], 0), axis=2)
    listed = jnp.where(ids[None, None, :] < count[:, :, None], listed, nb)
    chunks = (count + (CHUNK - 1)) // CHUNK
    seg_cols = jnp.concatenate([seg, jnp.full((rows, BLK), -1, jnp.int32)], axis=1)
    seg_cols = jnp.broadcast_to(seg_cols[:, :, None], (rows, full_len + BLK, 128))
    seg_rows = jnp.concatenate([by_block, by_block], axis=2)[:, :, None, :]
    return chunks, listed.reshape(rows, nb * nb), jnp.sum(chunks, axis=1), seg_cols, seg_rows


def lane_low(rows):
    return lax.broadcasted_iota(jnp.int32, (rows, 128), 1) < HD


def diag128(dup_t):
    row = lax.broadcasted_iota(jnp.int32, (128, 128), 0) < HD
    col = lax.broadcasted_iota(jnp.int32, (128, 128), 1) < HD
    return jnp.where(row == col, dup_t, jnp.zeros_like(dup_t))


def transposed_twice(tile):
    both = jnp.concatenate([tile, tile], axis=0)
    return both.T


def head_rows(acc):
    turned = jnp.concatenate([acc, acc], axis=0).T
    return jnp.where(lane_low(HD), turned[:HD], turned[HD:])


def pick_diag(full, half):
    lanes = slice(half * 128, half * 128 + 128)
    top = full[half * 128 : half * 128 + HD, lanes]
    low = full[half * 128 + HD : half * 128 + 128, lanes]
    return jnp.where(lane_low(HD), top, low)


def chunk_ids(list_ref, row, base, nb, real):
    base = jnp.minimum(base, nb * nb - CHUNK)
    ids = [jnp.where(real, list_ref[row, base + j], nb) for j in range(CHUNK)]
    safe = [jnp.where(b == nb, 0, b) for b in ids]
    return ids, safe


def block_rows(ref, blocks, lanes):
    return jnp.concatenate(
        [ref[0, pl.ds(pl.multiple_of(b * BLK, BLK), BLK), lanes] for b in blocks], axis=0
    )


def turned_blocks(ref, blocks, rows):
    low = lane_low(rows.stop - rows.start)
    tiles = [ref[b, rows, :] for b in blocks]
    return jnp.concatenate(
        [jnp.where(low, tiles[i], tiles[i + 1]) for i in range(0, CHUNK, 2)], axis=1
    )


def turn_all(src_ref, dst_ref, nb, width):
    def body(b, _):
        start = pl.multiple_of(b * BLK, BLK)
        for t in range(width // 128):
            tile = src_ref[0, pl.ds(start, BLK), t * 128 : t * 128 + 128]
            dst_ref[b, t * 128 : t * 128 + 128, :] = transposed_twice(tile)
        return 0

    lax.fori_loop(0, nb, body, 0, unroll=4)


def dot_f32(left, right):
    return lax.dot_general(
        left, right, (((1,), (0,)), ((), ())), preferred_element_type=jnp.float32
    )


def next_item(n_ref, row, nb, a, c):
    more = c + 1 < n_ref[row, a]
    following = jnp.where(more, a, jnp.minimum(a + 1, nb - 1))
    return following, jnp.where(more, c + 1, 0)


def run_items(n_ref, total_ref, row, nb, ready, item, finish):
    total = total_ref[row]

    def following(a, c):
        return next_item(n_ref, row, nb, a, c)

    def turn(i, carry):
        before, between, a, c = carry
        base = lax.rem(i, 2) * 2
        finish(before)
        finish(between)
        a_two, c_two = following(a, c)
        a_three, c_three = following(a_two, c_two)
        a_four, c_four = following(a_three, c_three)
        ready(a_three, 2 - base)
        ready(a_four, 3 - base)
        real = 2 * i + 1 < total
        a_two, c_two = jnp.where(real, a_two, a), jnp.where(real, c_two, c + 1)
        item(base, a, c, True)
        item(base + 1, a_two, c_two, real)
        return a, a_two, a_three, c_three

    ready(0, 0)
    ready(following(0, 0)[0], 1)
    before, between, _, _ = lax.fori_loop(0, (total + 1) // 2, turn, (0, 0, 0, 0))
    finish(before)
    finish(between)


def forward_kernel(group, n_ref, list_ref, total_ref, q_ref, k_ref, v_ref, segc_ref, segr_ref,
                   o_ref, lse_ref, vt_ref, qst_ref, m_ref, l_ref, acc_ref):
    row = pl.program_id(0)
    width = q_ref.shape[2]
    nb = q_ref.shape[1] // BLK
    groups, halves = width // group, group // 128
    tiles = width // 128
    turn_all(v_ref, vt_ref, nb, width)
    qst_ref[...] = jnp.zeros_like(qst_ref)
    l_ref[...] = jnp.ones_like(l_ref)
    acc_ref[...] = jnp.zeros_like(acc_ref)
    m_ref[...] = jnp.zeros_like(m_ref)

    def ready(a, slot):
        start = pl.multiple_of(a * BLK, BLK)
        for t in range(tiles):
            tile = q_ref[0, pl.ds(start, BLK), t * 128 : t * 128 + 128] * 0.125
            square = slice(t % halves * 128, t % halves * 128 + 128)
            qst_ref[slot, t // halves, square, square] = diag128(
                transposed_twice(tile.astype(jnp.bfloat16))
            )

    def finish(a):
        even = lax.rem(a, 2)
        start = pl.multiple_of(a * BLK, BLK)
        for t in range(tiles):
            lanes = slice(t * 128, t * 128 + 128)
            total = l_ref[even, t]
            o_ref[0, pl.ds(start, BLK), lanes] = head_rows(acc_ref[even, t] / total).astype(
                jnp.bfloat16
            )
            lse_ref[0, a, :, lanes] = m_ref[even, t] + jnp.log(total)

    def item(slot, a, c, real):
        ids, safe = chunk_ids(list_ref, row, a * nb + c * CHUNK, nb, real)
        even = lax.rem(a, 2)
        allowed = block_rows(segc_ref, ids, slice(0, 128)) == segr_ref[0, a]
        first = c == 0
        for g in range(groups):
            lanes = slice(g * group, g * group + group)
            s_t = dot_f32(block_rows(k_ref, safe, lanes), qst_ref[slot, g])
            weights, alphas = [], []
            for u in range(halves):
                t = g * halves + u
                s = jnp.where(allowed, s_t[:, u * 128 : u * 128 + 128], NEG)
                m_old = jnp.where(first, NEG, m_ref[even, t])
                m_new = jnp.maximum(m_old, jnp.max(s, axis=0, keepdims=True))
                p = jnp.exp(s - m_new)
                alpha = jnp.exp(m_old - m_new)
                l_ref[even, t] = alpha * l_ref[even, t] + jnp.sum(p, axis=0, keepdims=True)
                m_ref[even, t] = m_new
                weights.append(p.astype(jnp.bfloat16))
                alphas.append(alpha)
            p_t = jnp.concatenate(weights, axis=1) if halves > 1 else weights[0]
            o_t = dot_f32(turned_blocks(vt_ref, safe, lanes), p_t)
            for u in range(halves):
                t = g * halves + u
                acc_ref[even, t] = alphas[u] * acc_ref[even, t] + pick_diag(o_t, u)

    run_items(n_ref, total_ref, row, nb, ready, item, finish)


def group_of(width):
    return 256 if width % 256 == 0 else 128


def whole_spec(shape):
    rest = (0,) * (len(shape) - 1)
    return pl.BlockSpec((1,) + tuple(shape[1:]), lambda r, *_: (r,) + rest)


def one_spec(shape):
    rest = (0,) * (len(shape) - 1)
    return pl.BlockSpec((1,) + tuple(shape[1:]), lambda r, *_: (r,) + rest,
                        pipeline_mode=pl.Buffered(1))


def attention_forward(q, k, v, plan):
    *tables, seg_cols, seg_rows = plan
    rows, full_len, width = q.shape
    nb, group = full_len // BLK, group_of(width)
    tiles = width // 128
    pairs = rows * full_len * full_len // 4 * width
    args = (q, k, v, seg_cols, seg_rows)
    return pl.pallas_call(
        functools.partial(forward_kernel, group),
        out_shape=(
            jax.ShapeDtypeStruct((rows, full_len, width), jnp.bfloat16),
            jax.ShapeDtypeStruct((rows, nb, 1, width), jnp.float32),
        ),
        grid_spec=pltpu.PrefetchScalarGridSpec(
            num_scalar_prefetch=3,
            grid=(rows,),
            in_specs=[one_spec(x.shape) for x in args],
            out_specs=(one_spec((rows, full_len, width)), one_spec((rows, nb, 1, width))),
            scratch_shapes=[
                pltpu.VMEM((nb, width, 128), jnp.bfloat16),
                pltpu.VMEM((4, width // group, group, group), jnp.bfloat16),
                pltpu.VMEM((2, tiles, 1, 128), jnp.float32),
                pltpu.VMEM((2, tiles, 1, 128), jnp.float32),
                pltpu.VMEM((2, tiles, HD, 128), jnp.float32),
            ],
        ),
        compiler_params=pltpu.CompilerParams(vmem_limit_bytes=62 << 20),
        cost_estimate=pl.CostEstimate(
            flops=4 * pairs, transcendentals=pairs // HD, bytes_accessed=8 * q.size
        ),
        name="attention_forward",
    )(*tables, *args)


def backward_kernel(group, n_ref, list_ref, total_ref, q_ref, k_ref, v_ref, o_ref, do_ref,
                    lse_ref, segc_ref, segr_ref, dq_ref, dk_ref, dv_ref,
                    kt_ref, qst_ref, qs_ref, dost_ref, dos_ref, delta_ref, acc_ref,
                    dk_acc, dv_acc):
    row = pl.program_id(0)
    full_len, width = q_ref.shape[1], q_ref.shape[2]
    nb = full_len // BLK
    groups, halves = width // group, group // 128
    tiles = width // 128
    turn_all(k_ref, kt_ref, nb, width)
    for ref in (qst_ref, qs_ref, dost_ref, dos_ref, dk_acc, dv_acc, acc_ref):
        ref[...] = jnp.zeros_like(ref)
    low = lane_low(1)

    def ready(a, slot):
        start = pl.multiple_of(a * BLK, BLK)
        for t in range(tiles):
            g, u = t // halves, t % halves
            lanes = slice(t * 128, t * 128 + 128)
            square = slice(u * 128, u * 128 + 128)
            q_tile = (q_ref[0, pl.ds(start, BLK), lanes] * 0.125).astype(jnp.bfloat16)
            g_tile = do_ref[0, pl.ds(start, BLK), lanes]
            o_tile = o_ref[0, pl.ds(start, BLK), lanes]
            g_turn = transposed_twice(g_tile)
            qst_ref[slot, g, square, square] = diag128(transposed_twice(q_tile))
            dost_ref[slot, g, square, square] = diag128(g_turn)
            qs_ref[slot, g, square, square] = diag128(jnp.concatenate([q_tile, q_tile], axis=0))
            dos_ref[slot, g, square, square] = diag128(
                jnp.concatenate([g_tile, g_tile], axis=0)
            )
            product = g_turn.astype(jnp.float32) * transposed_twice(o_tile).astype(jnp.float32)
            delta_ref[slot, t] = jnp.where(
                low,
                jnp.sum(product[:HD], axis=0, keepdims=True),
                jnp.sum(product[HD:], axis=0, keepdims=True),
            )

    def finish(a):
        even = lax.rem(a, 2)
        start = pl.multiple_of(a * BLK, BLK)
        for t in range(tiles):
            dq_ref[0, pl.ds(start, BLK), t * 128 : t * 128 + 128] = (
                head_rows(acc_ref[even, t]) * 0.125
            ).astype(jnp.bfloat16)

    def item(slot, a, c, real):
        ids, safe = chunk_ids(list_ref, row, a * nb + c * CHUNK, nb, real)
        even = lax.rem(a, 2)
        allowed = block_rows(segc_ref, ids, slice(0, 128)) == segr_ref[0, a]
        first = c == 0
        for g in range(groups):
            lanes = slice(g * group, g * group + group)
            s_t = dot_f32(block_rows(k_ref, safe, lanes), qst_ref[slot, g])
            dp_t = dot_f32(block_rows(v_ref, safe, lanes), dost_ref[slot, g])
            p_parts, ds_parts = [], []
            for u in range(halves):
                t = g * halves + u
                half = slice(u * 128, u * 128 + 128)
                lse = lse_ref[0, a, :, t * 128 : t * 128 + 128]
                p = jnp.exp(jnp.where(allowed, s_t[:, half], NEG) - lse)
                ds = p * (dp_t[:, half] - delta_ref[slot, t])
                p_parts.append(p.astype(jnp.bfloat16))
                ds_parts.append(ds.astype(jnp.bfloat16))
            p_t = jnp.concatenate(p_parts, axis=1) if halves > 1 else p_parts[0]
            ds_t = jnp.concatenate(ds_parts, axis=1) if halves > 1 else ds_parts[0]
            dv = dot_f32(p_t, dos_ref[slot, g])
            dk = dot_f32(ds_t, qs_ref[slot, g])
            dq_t = dot_f32(turned_blocks(kt_ref, safe, lanes), ds_t)
            for j in range(CHUNK):
                where = pl.ds(pl.multiple_of(safe[j] * BLK, BLK), BLK)
                part = slice(j * BLK, j * BLK + BLK)
                dv_acc[where, lanes] += dv[part]
                dk_acc[where, lanes] += dk[part]
            for u in range(halves):
                t = g * halves + u
                acc_ref[even, t] = jnp.where(first, 0.0, acc_ref[even, t]) + pick_diag(dq_t, u)

    run_items(n_ref, total_ref, row, nb, ready, item, finish)

    def flush(a, _):
        where = pl.ds(pl.multiple_of(a * BLK, BLK), BLK)
        dk_ref[0, where, :] = dk_acc[where, :].astype(jnp.bfloat16)
        dv_ref[0, where, :] = dv_acc[where, :].astype(jnp.bfloat16)
        return 0

    lax.fori_loop(0, nb, flush, 0, unroll=2)


def attention_backward(q, k, v, o, do, lse, plan):
    *tables, seg_cols, seg_rows = plan
    rows, full_len, width = q.shape
    nb, group = full_len // BLK, group_of(width)
    tiles, groups = width // 128, width // group
    pairs = rows * full_len * full_len // 4 * width
    args = (q, k, v, o, do, lse, seg_cols, seg_rows)
    like = jax.ShapeDtypeStruct((rows, full_len, width), jnp.bfloat16)
    square = pltpu.VMEM((4, groups, group, group), jnp.bfloat16)
    return pl.pallas_call(
        functools.partial(backward_kernel, group),
        out_shape=(like, like, like),
        grid_spec=pltpu.PrefetchScalarGridSpec(
            num_scalar_prefetch=3,
            grid=(rows,),
            in_specs=[one_spec(x.shape) for x in args],
            out_specs=tuple(one_spec(like.shape) for _ in range(3)),
            scratch_shapes=[
                pltpu.VMEM((nb, width, 128), jnp.bfloat16),
                square, square, square, square,
                pltpu.VMEM((4, tiles, 1, 128), jnp.float32),
                pltpu.VMEM((2, tiles, HD, 128), jnp.float32),
                pltpu.VMEM((full_len, width), jnp.float32),
                pltpu.VMEM((full_len, width), jnp.float32),
            ],
        ),
        compiler_params=pltpu.CompilerParams(vmem_limit_bytes=62 << 20),
        cost_estimate=pl.CostEstimate(
            flops=10 * pairs, transcendentals=pairs // HD, bytes_accessed=16 * q.size
        ),
        name="attention_backward",
    )(*tables, *args)


def pair_bit(index, bit):
    return lax.rem(index // (1 << bit), 2)


def pair_of(index, bit):
    return index + (1 - 2 * pair_bit(index, bit)) * (1 << bit)


def all_arrived(bits):
    me = lax.axis_index("fsdp")
    barrier = pltpu.get_barrier_semaphore()
    for bit in range(bits):
        pl.semaphore_signal(
            barrier, inc=1, device_id={"fsdp": pair_of(me, bit)},
            device_id_type=pl.DeviceIdType.MESH,
        )
    pl.semaphore_signal(
        barrier, inc=1, device_id={"seq": 1 - lax.axis_index("seq")},
        device_id_type=pl.DeviceIdType.MESH,
    )
    pl.semaphore_wait(barrier, bits + 1)


def qkv_backward_kernel(
    bits, xt_in, dq_in, dk_in, dv_in, wt_in, res_in, small_in,
    wq_out, wk_out, wv_out, small_out, tok_out,
    xt, grads, wt, res, tok, kept, sends, lands, final, small, small_land, result,
    in_sem, tok_send, tok_land, own_sem, send_sem, land_sem, x_send, x_land,
    small_send, small_recv, out_sem,
):
    me, side = lax.axis_index("fsdp"), lax.axis_index("seq")
    half = tok.shape[2] * tok.shape[1]
    piece, pieces = tok.shape[2], tok.shape[1]
    own, width = wq_out.shape
    owners = 1 << bits
    sources = (dq_in, dk_in, dv_in)
    rows_of = [pl.ds(pl.multiple_of(p * half, half), half) for p in (1 - side, side)]
    loads = [pltpu.make_async_copy(wt_in, wt, in_sem.at[0])]
    for p in range(2):
        for i in range(3):
            loads.append(
                pltpu.make_async_copy(
                    sources[i].at[rows_of[p]], grads.at[i, rows_of[p]], in_sem.at[1 + 4 * p + i]
                )
            )
        loads.append(
            pltpu.make_async_copy(res_in.at[rows_of[p]], res.at[rows_of[p]], in_sem.at[4 + 4 * p])
        )
    loads.append(pltpu.make_async_copy(xt_in, xt, in_sem.at[9]))
    loads.append(pltpu.make_async_copy(small_in, small.at[0], in_sem.at[10]))
    for i in (0, 1, 2, 3, 4, 9, 5, 6, 7, 8, 10):
        loads[i].start()
    all_arrived(bits)

    def token_rows(start):
        total = res[pl.ds(start, piece), :].astype(jnp.float32)
        for i in range(3):
            total = total + dot_f32(
                grads[i, pl.ds(start, piece), :], wt[i]
            )
        return total.astype(jnp.bfloat16)

    def sent(i):
        return pltpu.make_async_remote_copy(
            src_ref=tok.at[0, i],
            dst_ref=tok_out.at[side, pl.ds(pl.multiple_of(i * piece, piece), piece)],
            send_sem=tok_send.at[i], recv_sem=tok_land.at[i],
            device_id={"seq": 1 - side}, device_id_type=pl.DeviceIdType.MESH,
        )

    def landed(i):
        return pltpu.make_async_remote_copy(
            src_ref=tok.at[0, i],
            dst_ref=tok_out.at[1 - side, pl.ds(pl.multiple_of(i * piece, piece), piece)],
            send_sem=tok_send.at[i], recv_sem=tok_land.at[i],
            device_id={"seq": 1 - side}, device_id_type=pl.DeviceIdType.MESH,
        )

    def stays(i):
        return pltpu.make_async_copy(
            tok.at[1, i],
            tok_out.at[side, pl.ds(pl.multiple_of(i * piece, piece), piece)],
            own_sem.at[i],
        )

    def send_piece(i, _):
        start = pl.multiple_of((1 - side) * half + i * piece, piece)
        tok[0, i] = token_rows(start)
        sent(i).start()
        return 0

    def keep_piece(i, _):
        start = pl.multiple_of(side * half + i * piece, piece)
        tok[1, i] = token_rows(start)
        stays(i).start()
        return 0

    low_bit = pair_bit(me, 0) == 0
    tile = 8 if owners % 8 == 0 else owners
    first_of = [0]
    for bit in range(bits):
        first_of.append(first_of[-1] + (owners >> (bit + 1)))

    def weights(i):
        def rows(m, _):
            rows_here = pl.ds(pl.multiple_of(m * tile * own, tile * own), tile * own)
            block = dot_f32(
                jnp.concatenate(
                    [xt[h, r, rows_here, :] for h in range(2) for r in range(pieces)], axis=1
                ),
                grads[i],
            ).reshape(tile // 2, 2, own, width)
            even, odd = block[:, 0], block[:, 1]
            spot = pl.ds(m * (tile // 2), tile // 2)
            kept[i, spot] = jnp.where(low_bit, even, odd)
            sends[i, spot] = jnp.where(low_bit, odd, even).astype(jnp.bfloat16)
            return 0

        lax.fori_loop(0, owners // tile, rows, 0)

    def hop(i, bit):
        count = owners >> (bit + 1)
        spot = pl.ds(first_of[bit], count)
        return pltpu.make_async_remote_copy(
            src_ref=sends.at[i, spot], dst_ref=lands.at[i, spot],
            send_sem=send_sem.at[i, bit], recv_sem=land_sem.at[i, bit],
            device_id={"fsdp": pair_of(me, bit)}, device_id_type=pl.DeviceIdType.MESH,
        )

    def cross(i):
        return pltpu.make_async_remote_copy(
            src_ref=final.at[0, i], dst_ref=final.at[1, i],
            send_sem=x_send.at[i], recv_sem=x_land.at[i],
            device_id={"seq": 1 - side}, device_id_type=pl.DeviceIdType.MESH,
        )

    def advance(i, bit):
        hop(i, bit).wait_recv()
        base = first_of[bit]
        if bit + 1 == bits:
            total = kept[i, base] + lands[i, base].astype(jnp.float32)
            final[0, i] = total.astype(jnp.bfloat16)
            cross(i).start()
            return
        nxt = pair_bit(me, bit + 1)

        def one(j, _):
            stay, go = 2 * j + nxt, 2 * j + 1 - nxt
            kept[i, first_of[bit + 1] + j] = kept[i, base + stay] + lands[
                i, base + stay
            ].astype(jnp.float32)
            sends[i, first_of[bit + 1] + j] = (
                kept[i, base + go] + lands[i, base + go].astype(jnp.float32)
            ).astype(jnp.bfloat16)
            return 0

        lax.fori_loop(0, owners >> (bit + 2), one, 0)
        hop(i, bit + 1).start()

    outs = (wq_out, wk_out, wv_out)

    def written(i):
        return pltpu.make_async_copy(result.at[i], outs[i], out_sem.at[i])

    def finish(i):
        cross(i).wait_recv()
        result[i] = final[0, i].astype(jnp.float32) + final[1, i].astype(jnp.float32)
        written(i).start()

    def small_hop(bit):
        where = {"fsdp": pair_of(me, bit)} if bit < bits else {"seq": 1 - side}
        return pltpu.make_async_remote_copy(
            src_ref=small.at[bit], dst_ref=small_land.at[bit],
            send_sem=small_send.at[bit], recv_sem=small_recv.at[bit],
            device_id=where, device_id_type=pl.DeviceIdType.MESH,
        )

    def small_advance(bit):
        small_hop(bit).wait_recv()
        small[bit + 1] = small[bit] + small_land[bit]
        if bit < bits:
            small_hop(bit + 1).start()

    def column_sums(i, spot):
        def one(c, total):
            block = grads[i, pl.ds(pl.multiple_of(c * 256, 256), 256), :].astype(jnp.float32)
            return total + jnp.sum(block.reshape(32, 8, width), axis=0)

        total = lax.fori_loop(
            0, grads.shape[1] // 256, one, jnp.zeros((8, width), jnp.float32)
        )
        small[0, spot : spot + 1] = jnp.sum(total, axis=0, keepdims=True)

    for i in range(5):
        loads[i].wait()
    send_piece(0, 0)
    for i in range(5, 11):
        loads[i].wait()

    def begin(i, _):
        weights(i)
        hop(i, 0).start()
        send_piece(i + 1, 0)
        advance(i, 0)
        return 0

    lax.fori_loop(0, 3, begin, 0)
    column_sums(0, 0)
    column_sums(2, 1)
    small_hop(0).start()

    def second(i, _):
        keep_piece(i, 0)
        advance(i, 1)
        return 0

    lax.fori_loop(0, 3, second, 0)
    small_advance(0)
    keep_piece(3, 0)
    for bit in range(2, bits):
        for i in range(3):
            advance(i, bit)
        small_advance(bit - 1)
    for bit in range(bits - 1, bits + 1):
        small_advance(bit)
    for i in range(3):
        finish(i)
    small_copy = pltpu.make_async_copy(small.at[bits + 1], small_out, out_sem.at[3])
    small_copy.start()
    for i in range(3):
        written(i).wait()
        cross(i).wait_send()
        for bit in range(bits):
            hop(i, bit).wait_send()
    for bit in range(bits + 1):
        small_hop(bit).wait_send()
    small_copy.wait()
    for i in range(pieces):
        stays(i).wait()
        sent(i).wait_send()
        landed(i).wait_recv()


def qkv_backward(xt, dq, dk, dv, wt, resid, small, own):
    tokens, width = dq.shape
    bits = lax.axis_size("fsdp").bit_length() - 1
    owners = 1 << bits
    pieces = 4
    piece = tokens // 2 // pieces
    dma = pltpu.SemaphoreType.DMA
    f32, bf16 = jnp.float32, jnp.bfloat16
    shard = jax.ShapeDtypeStruct((own, width), f32)
    anywhere = pl.BlockSpec(memory_space=pltpu.HBM)
    return pl.pallas_call(
        functools.partial(qkv_backward_kernel, bits),
        out_shape=(
            shard, shard, shard,
            jax.ShapeDtypeStruct(small.shape, f32),
            jax.ShapeDtypeStruct((2, tokens // 2, width), bf16),
        ),
        in_specs=[anywhere] * 7,
        out_specs=(anywhere,) * 5,
        scratch_shapes=[
            pltpu.VMEM(xt.shape, bf16),
            pltpu.VMEM((3, tokens, width), bf16),
            pltpu.VMEM(wt.shape, bf16),
            pltpu.VMEM((tokens, width), bf16),
            pltpu.VMEM((2, pieces, piece, width), bf16),
            pltpu.VMEM((3, owners - 1, own, width), f32),
            pltpu.VMEM((3, owners - 1, own, width), bf16),
            pltpu.VMEM((3, owners - 1, own, width), bf16),
            pltpu.VMEM((2, 3, own, width), bf16),
            pltpu.VMEM((bits + 2,) + small.shape, f32),
            pltpu.VMEM((bits + 1,) + small.shape, f32),
            pltpu.VMEM((3, own, width), f32),
            dma((11,)), dma((pieces,)), dma((pieces,)), dma((pieces,)),
            dma((3, bits)), dma((3, bits)), dma((3,)), dma((3,)),
            dma((bits + 1,)), dma((bits + 1,)), dma((4,)),
        ],
        compiler_params=pltpu.CompilerParams(
            collective_id=1, has_side_effects=True, vmem_limit_bytes=62 << 20
        ),
        cost_estimate=pl.CostEstimate(
            flops=40 * tokens * width * width, transcendentals=0,
            bytes_accessed=16 * tokens * width,
        ),
        name="qkv_backward",
    )(xt, dq, dk, dv, wt, resid, small)


def qkv_forward_kernel(
    bits, tokens_in, own_in, grad_in,
    grad_out, x_out, xt_out, q_out, k_out, v_out, wt_out, small_out,
    x, xt, w, wt, qkv, small,
    own_sem, tok_send, tok_land, load_sem, send_sem, land_sem, x_sem, xt_sem, out_sem, w_sem,
    small_sem,
):
    me, side = lax.axis_index("fsdp"), lax.axis_index("seq")
    pieces, piece, width = x.shape[1], x.shape[2], x.shape[3]
    mine = [pair_bit(me, bit) for bit in range(bits)]
    columns = part_columns(width)
    outs = (q_out, k_out, v_out)

    def slot(bit, part):
        here = [slice(None)] * (bits - 1 - bit) + [mine[b] for b in range(bit, -1, -1)]
        return tuple(here) + (slice(None), columns[part])

    own_tokens = pltpu.make_async_copy(tokens_in.at[side], x.at[side], own_sem.at[0])
    own_tokens.start()
    grad_rows = pltpu.make_async_copy(grad_in.at[1 - side], grad_out, own_sem.at[1])
    grad_rows.start()

    def load(part):
        spot = tuple(mine[b] for b in range(bits - 1, -1, -1)) + (slice(None), columns[part])
        return pltpu.make_async_copy(
            own_in.at[:, columns[part]], w.at[spot], load_sem.at[part]
        )

    for part in range(3):
        load(part).start()
    all_arrived(bits)

    def sent(i):
        return pltpu.make_async_remote_copy(
            src_ref=tokens_in.at[1 - side, i], dst_ref=x.at[side, i],
            send_sem=tok_send.at[i], recv_sem=tok_land.at[i],
            device_id={"seq": 1 - side}, device_id_type=pl.DeviceIdType.MESH,
        )

    def landed(i):
        return pltpu.make_async_remote_copy(
            src_ref=tokens_in.at[1 - side, i], dst_ref=x.at[1 - side, i],
            send_sem=tok_send.at[i], recv_sem=tok_land.at[i],
            device_id={"seq": 1 - side}, device_id_type=pl.DeviceIdType.MESH,
        )

    def hop(part, turn):
        bit = bits - 1 - turn
        return pltpu.make_async_remote_copy(
            src_ref=w.at[slot(bit, part)], dst_ref=w.at[slot(bit, part)],
            send_sem=send_sem.at[part, turn], recv_sem=land_sem.at[part, turn],
            device_id={"fsdp": pair_of(me, bit)}, device_id_type=pl.DeviceIdType.MESH,
        )

    for part in range(3):
        load(part).wait()
        hop(part, 0).start()
    for i in range(pieces):
        sent(i).start()

    def x_copy(half, i):
        return pltpu.make_async_copy(x.at[half, i], x_out.at[half, i], x_sem.at[half, i])

    def out_copy(part, half, i):
        return pltpu.make_async_copy(
            qkv.at[part, half, i], outs[part].at[half, i], out_sem.at[part, half, i]
        )

    def xt_copy(half, i):
        return pltpu.make_async_copy(xt.at[half, i], xt_out.at[half, i], xt_sem.at[half, i])

    def w_copy(part):
        return pltpu.make_async_copy(wt.at[part], wt_out.at[part], w_sem.at[part])

    def whole(part):
        first = part_start(width, part)
        spot = (slice(None),) * (bits + 1) + (slice(first, first + width),)
        return w[spot].reshape(width, width)

    def turn(half, i):
        x_copy(half, i).start()
        xt[half, i] = x[half, i].T
        xt_copy(half, i).start()

    def project(part, half, i):
        total = dot_f32(x[half, i], whole(part))
        if part == 0:
            total = total + small[0:1, :]
        if part == 2:
            total = total + small[1:2, :]
        qkv[part, half, i] = total.astype(jnp.bfloat16)
        out_copy(part, half, i).start()

    def over(body):
        def one(i, _):
            body(i)
            return 0

        lax.fori_loop(0, pieces, one, 0)

    def turn_weights(part):
        wt[part] = whole(part).T
        w_copy(part).start()

    def other(i):
        landed(i).wait_recv()
        turn(1 - side, i)
        project(0, 1 - side, i)
        project(1, 1 - side, i)

    own_tokens.wait()
    over(lambda i: turn(side, i))
    for step in range(bits + 2):
        full = None
        for part in range(3):
            hops = step - part
            if 0 <= hops < bits:
                hop(part, hops).wait_recv()
                if hops + 1 < bits:
                    hop(part, hops + 1).start()
                else:
                    full = part
        if full == 0:
            spot = (slice(None),) * (bits + 1) + (slice(width, width + 128),)
            turned = w[spot].reshape(width, 128).astype(jnp.float32).T
            small[...] = turned[: small.shape[0]]
            pltpu.make_async_copy(small, small_out, small_sem.at[0]).start()
        if full is not None:
            over(lambda i: project(full, side, i))
        if full == 1:
            turn_weights(0)
            turn_weights(1)
            over(other)
        if full == 2:
            over(lambda i: project(2, 1 - side, i))
            turn_weights(2)
    for i in range(pieces):
        sent(i).wait_send()
    for part in range(3):
        w_copy(part).wait()
        for hops in range(bits):
            hop(part, hops).wait_send()
    grad_rows.wait()
    pltpu.make_async_copy(small, small_out, small_sem.at[0]).wait()
    for half in range(2):
        for i in range(pieces):
            x_copy(half, i).wait()
            xt_copy(half, i).wait()
            for part in range(3):
                out_copy(part, half, i).wait()


def part_start(width, part):
    return part * width + (128 if part else 0)


def part_columns(width):
    return (
        slice(0, width + 128),
        slice(width + 128, 2 * width + 128),
        slice(2 * width + 128, 3 * width + 128),
    )


def qkv_forward(tokens_in, own_pack, out_grad):
    rows, local, width = tokens_in.shape
    own, columns = own_pack.shape
    bits = lax.axis_size("fsdp").bit_length() - 1
    pieces = 4
    piece = local // pieces
    dma = pltpu.SemaphoreType.DMA
    bf16 = jnp.bfloat16
    halves = (2, pieces, piece, width)
    gathered = (2,) * bits + (own, columns)
    anywhere = pl.BlockSpec(memory_space=pltpu.HBM)
    like = jax.ShapeDtypeStruct(halves, bf16)
    turned = (2, pieces, width, piece)
    grad, x, xt, q, k, v, weights_t, small = pl.pallas_call(
        functools.partial(qkv_forward_kernel, bits),
        out_shape=(
            jax.ShapeDtypeStruct((local, width), bf16),
            like, jax.ShapeDtypeStruct(turned, bf16), like, like, like,
            jax.ShapeDtypeStruct((3, width, width), bf16),
            jax.ShapeDtypeStruct((SMALL_ROWS, width), jnp.float32),
        ),
        in_specs=[anywhere] * 3,
        out_specs=(anywhere,) * 8,
        scratch_shapes=[
            pltpu.VMEM(halves, bf16),
            pltpu.VMEM(turned, bf16),
            pltpu.VMEM(gathered, bf16),
            pltpu.VMEM((3, width, width), bf16),
            pltpu.VMEM((3,) + halves, bf16),
            pltpu.VMEM((SMALL_ROWS, width), jnp.float32),
            dma((2,)), dma((pieces,)), dma((pieces,)), dma((3,)),
            dma((3, bits)), dma((3, bits)), dma((2, pieces)), dma((2, pieces)),
            dma((3, 2, pieces)), dma((3,)), dma((1,)),
        ],
        compiler_params=pltpu.CompilerParams(
            collective_id=2, has_side_effects=True, vmem_limit_bytes=62 << 20
        ),
        cost_estimate=pl.CostEstimate(
            flops=18 * rows * local * width * width, transcendentals=0,
            bytes_accessed=16 * rows * local * width,
        ),
        name="qkv_forward",
    )(tokens_in.reshape(halves), own_pack, out_grad)
    flat = rows * local, width
    return (
        x.reshape(flat), q.reshape(flat), k.reshape(flat), v.reshape(flat), xt, weights_t, small, grad
    )


eps_norm = 1e-06


def dot_rows(left, right):
    return lax.dot_general(
        left, right, (((0,), (0,)), ((), ())), preferred_element_type=jnp.float32
    )


def dot_nt(left, right):
    return lax.dot_general(
        left, right, (((1,), (1,)), ((), ())), preferred_element_type=jnp.float32
    )


def row_mean(values):
    return jnp.mean(values, axis=-1, keepdims=True)


GELU_K = math.sqrt(2.0 / math.pi)
GELU_A = 0.044715


def gelu_pair(u):
    square = u * u
    t = jnp.tanh(u * (GELU_K + (GELU_K * GELU_A) * square))
    half = 0.5 + 0.5 * t
    slope = half + (u * (half * (1.0 - t))) * (GELU_K + (3.0 * GELU_K * GELU_A) * square)
    return u * half, slope


OUT_B, GAIN_1, BIAS_1, OUTER_B, GAIN_2, BIAS_2, INNER_B = 2, 3, 4, 5, 6, 7, 8
SMALL_ROWS = 16


def eights(values):
    return jnp.sum(values.reshape(-1, 8, values.shape[-1]), axis=0)


def middle_forward_kernel(
    chunks, side, weights_in, small, att, tokens, grad_own, grad_other,
    out_keep, out_send, d_mlp, normed, z_one, rs_one, slope, d_weights, sums,
    w, acc, act, flow, part, load_sem, store_sem,
):
    step, steps = pl.program_id(0), pl.num_programs(0)
    rows, width = att.shape
    f32, bf16 = jnp.float32, jnp.bfloat16
    count = 2 * chunks + 1
    staying = step // (steps // 2) == side[0]

    def load(i):
        return pltpu.make_async_copy(
            weights_in.at[:, pl.ds(i * width, width)], w.at[i], load_sem.at[i]
        )

    def store(c):
        return pltpu.make_async_copy(
            w.at[1 + chunks + c], d_weights.at[:, pl.ds(c * width, width)], store_sem.at[c]
        )

    @pl.when(step == 0)
    def _():
        for i in range(count):
            load(i).start()
        part[...] = jnp.zeros_like(part)

        def clear(i, _):
            acc[i] = jnp.zeros_like(acc[i])
            return 0

        lax.fori_loop(0, chunks, clear, 0)
        load(0).wait()

    def vector(i):
        return small[i : i + 1, :]

    def add_sum(i, values):
        part[i] += eights(values)

    attn = dot_f32(att[...], w[0]) + vector(OUT_B)
    resid = tokens[...].astype(f32) + attn
    add_sum(INNER_B + chunks, resid * resid)
    add_sum(INNER_B + chunks + 1, attn * attn)
    centred = resid - row_mean(resid)
    scale = lax.rsqrt(row_mean(centred * centred) + eps_norm)
    z = centred * scale
    rs_one[...] = scale
    z_one[...] = z.astype(bf16)
    full = z * vector(GAIN_1) + vector(BIAS_1)
    flow[...] = full
    normed[...] = full.astype(bf16)

    def inner(c, _):
        @pl.when(step == 0)
        def _():
            load(1 + c).wait()

        for n in range(width // 256):
            cols = slice(n * 256, n * 256 + 256)
            pre = dot_f32(normed[...], w[1 + c, :, cols]) + small[pl.ds(INNER_B + c, 1), cols]
            value, grade = gelu_pair(pre)
            act[c, :, cols] = value.astype(bf16)
            slope[c, :, cols] = grade.astype(bf16)
        return 0

    lax.fori_loop(0, chunks, inner, 0)

    @pl.when(step == 0)
    def _():
        for i in range(1 + chunks, count):
            load(i).wait()

    mlp = dot_f32(act[0], w[1 + chunks])
    for c in range(1, chunks):
        mlp = mlp + dot_f32(act[c], w[1 + chunks + c])
    mlp = mlp + vector(OUTER_B)
    add_sum(INNER_B + chunks + 2, mlp * mlp)
    resid = flow[...] + mlp
    centred = resid - row_mean(resid)
    scale = lax.rsqrt(row_mean(centred * centred) + eps_norm)
    z = centred * scale
    result = (z * vector(GAIN_2) + vector(BIAS_2)).astype(bf16)

    @pl.when(staying)
    def _():
        out_keep[...] = result

    @pl.when(jnp.logical_not(staying))
    def _():
        out_send[...] = result

    grad = jnp.where(staying, grad_own[...], grad_other[...]).astype(f32)
    add_sum(GAIN_2, grad * z)
    add_sum(BIAS_2, grad)
    grad = grad * vector(GAIN_2)
    low = (scale * (grad - row_mean(grad) - z * row_mean(grad * z))).astype(bf16)
    add_sum(OUTER_B, low.astype(f32))
    d_mlp[...] = low

    def back(c, _):
        acc[c] += dot_rows(act[c], d_mlp[...])

        @pl.when(step == steps - 1)
        def _():
            w[1 + chunks + c] = acc[c].astype(bf16)
            store(c).start()

        return 0

    lax.fori_loop(0, chunks, back, 0)

    @pl.when(step == steps - 1)
    def _():
        sums[...] = jnp.sum(part[...], axis=1)
        for c in range(chunks):
            store(c).wait()


def middle_backward_kernel(
    chunks, weights_in, small, sums_in, att, d_mlp, normed, z_one, rs_one, slope,
    d_attn, d_att, d_weights, sums,
    w, acc, d_pre, flow, part, load_sem, store_sem,
):
    step, steps = pl.program_id(0), pl.num_programs(0)
    rows, width = att.shape
    f32, bf16 = jnp.float32, jnp.bfloat16
    count = 2 * chunks + 1

    def load(i):
        return pltpu.make_async_copy(
            weights_in.at[:, pl.ds(i * width, width)], w.at[i], load_sem.at[i]
        )

    def store(i):
        return pltpu.make_async_copy(
            w.at[i], d_weights.at[:, pl.ds(i * width, width)], store_sem.at[i]
        )

    @pl.when(step == 0)
    def _():
        for c in range(chunks):
            load(1 + chunks + c).start()
            load(1 + c).start()
        load(0).start()
        part[...] = jnp.zeros_like(part)

        def clear(i, _):
            acc[i] = jnp.zeros_like(acc[i])
            return 0

        lax.fori_loop(0, chunks + 1, clear, 0)

    def vector(i):
        return small[i : i + 1, :]

    def add_sum(i, values):
        part[i] += eights(values)

    turned = normed[...].T
    flow[...] = d_mlp[...].astype(f32)

    def back(c, _):
        @pl.when(step == 0)
        def _():
            load(1 + chunks + c).wait()
            load(1 + c).wait()

        for n in range(width // 256):
            cols = slice(n * 256, n * 256 + 256)
            d_act = dot_nt(d_mlp[...], w[1 + chunks + c, cols, :])
            low = (slope[c, :, cols].astype(f32) * d_act).astype(bf16)
            part[INNER_B + c, :, cols] += eights(low.astype(f32))
            d_pre[:, cols] = low
        acc[1 + c] += dot_f32(turned, d_pre[...])
        flow[...] += dot_nt(d_pre[...], w[1 + c])

        @pl.when(step == steps - 1)
        def _():
            w[1 + c] = acc[1 + c].astype(bf16)
            store(1 + c).start()

        return 0

    lax.fori_loop(0, chunks, back, 0)

    @pl.when(step == 0)
    def _():
        load(0).wait()

    grad = flow[...]
    z = z_one[...].astype(f32)
    add_sum(GAIN_1, grad * z)
    add_sum(BIAS_1, grad)
    grad = grad * vector(GAIN_1)
    low = (rs_one[...] * (grad - row_mean(grad) - z * row_mean(grad * z))).astype(bf16)
    add_sum(OUT_B, low.astype(f32))
    d_attn[...] = low
    acc[0] += dot_rows(att[...], d_attn[...])
    d_att[...] = dot_nt(d_attn[...], w[0]).astype(bf16)

    @pl.when(step == steps - 1)
    def _():
        w[0] = acc[0].astype(bf16)
        store(0).start()
        sums[...] = sums_in[...] + jnp.sum(part[...], axis=1)
        for i in range(chunks + 1):
            store(i).wait()


def middle_parts(weights, small, tok_count, width):
    chunks = (weights.shape[1] // width - 1) // 2
    rows = 512
    return chunks, rows, tok_count // rows


def middle_forward(side, weights, small, att, tokens, grad_own, grad_other):
    tok_count, width = att.shape
    chunks, rows, steps = middle_parts(weights, small, tok_count, width)
    count = 2 * chunks + 1
    f32, bf16 = jnp.float32, jnp.bfloat16
    half = steps // 2

    def early(i):
        return jnp.minimum(i, half - 1)

    def late(i):
        return jnp.maximum(i - half, 0)

    tile = pl.BlockSpec((rows, width), lambda i, s: (i, 0))
    thin = pl.BlockSpec((rows, 1), lambda i, s: (i, 0))
    deep = pl.BlockSpec((chunks, rows, width), lambda i, s: (0, i, 0))
    keep = pl.BlockSpec((rows, width), lambda i, s: (jnp.where(s[0] == 0, early(i), late(i)), 0))
    send = pl.BlockSpec((rows, width), lambda i, s: (jnp.where(s[0] == 0, late(i), early(i)), 0))
    fixed = pl.BlockSpec(small.shape, lambda i, s: (0, 0), pipeline_mode=pl.Buffered(1))
    anywhere = pl.BlockSpec(memory_space=pl.ANY)
    like = jax.ShapeDtypeStruct((tok_count, width), bf16)
    part = jax.ShapeDtypeStruct((tok_count // 2, width), bf16)
    return pl.pallas_call(
        functools.partial(middle_forward_kernel, chunks),
        out_shape=(
            part, part, like, like, like,
            jax.ShapeDtypeStruct((tok_count, 1), f32),
            jax.ShapeDtypeStruct((chunks, tok_count, width), bf16),
            jax.ShapeDtypeStruct((width, chunks * width), bf16),
            jax.ShapeDtypeStruct(small.shape, f32),
        ),
        grid_spec=pltpu.PrefetchScalarGridSpec(
            num_scalar_prefetch=1,
            grid=(steps,),
            in_specs=[anywhere, fixed, tile, tile, keep, send],
            out_specs=(keep, send, tile, tile, tile, thin, deep, anywhere, fixed),
            scratch_shapes=[
                pltpu.VMEM((count, width, width), bf16),
                pltpu.VMEM((chunks, width, width), f32),
                pltpu.VMEM((chunks, rows, width), bf16),
                pltpu.VMEM((rows, width), f32),
                pltpu.VMEM((small.shape[0], 8, width), f32),
                pltpu.SemaphoreType.DMA((count,)),
                pltpu.SemaphoreType.DMA((chunks,)),
            ],
        ),
        compiler_params=pltpu.CompilerParams(vmem_limit_bytes=62 << 20),
        cost_estimate=pl.CostEstimate(
            flops=12 * tok_count * width * width * (count + 1) // 2,
            transcendentals=tok_count * width * chunks,
            bytes_accessed=30 * tok_count * width + 4 * weights.size,
        ),
        name="middle_forward",
    )(side.reshape(1), weights, small, att, tokens, grad_own, grad_other)


def middle_backward(weights, small, sums, att, d_mlp, normed, z_one, rs_one, slope):
    tok_count, width = att.shape
    chunks, rows, steps = middle_parts(weights, small, tok_count, width)
    count = 2 * chunks + 1
    f32, bf16 = jnp.float32, jnp.bfloat16
    tile = pl.BlockSpec((rows, width), lambda i: (i, 0))
    thin = pl.BlockSpec((rows, 1), lambda i: (i, 0))
    deep = pl.BlockSpec((chunks, rows, width), lambda i: (0, i, 0))
    fixed = pl.BlockSpec(small.shape, lambda i: (0, 0), pipeline_mode=pl.Buffered(1))
    anywhere = pl.BlockSpec(memory_space=pl.ANY)
    like = jax.ShapeDtypeStruct((tok_count, width), bf16)
    return pl.pallas_call(
        functools.partial(middle_backward_kernel, chunks),
        grid=(steps,),
        out_shape=(
            like, like,
            jax.ShapeDtypeStruct((width, (chunks + 1) * width), bf16),
            jax.ShapeDtypeStruct(small.shape, f32),
        ),
        in_specs=[anywhere, fixed, fixed, tile, tile, tile, tile, thin, deep],
        out_specs=(tile, tile, anywhere, fixed),
        scratch_shapes=[
            pltpu.VMEM((count, width, width), bf16),
            pltpu.VMEM((chunks + 1, width, width), f32),
            pltpu.VMEM((rows, width), bf16),
            pltpu.VMEM((rows, width), f32),
            pltpu.VMEM((small.shape[0], 8, width), f32),
            pltpu.SemaphoreType.DMA((count,)),
            pltpu.SemaphoreType.DMA((chunks + 1,)),
        ],
        compiler_params=pltpu.CompilerParams(vmem_limit_bytes=62 << 20),
        cost_estimate=pl.CostEstimate(
            flops=12 * tok_count * width * width * (count + 1) // 2, transcendentals=0,
            bytes_accessed=30 * tok_count * width + 4 * weights.size,
        ),
        name="middle_backward",
    )(weights, small, sums, att, d_mlp, normed, z_one, rs_one, slope)


def contract_rows(left, right):
    return lax.dot_general(
        left, right, (((0,), (0,)), ((), ())), preferred_element_type=jnp.float32
    )


def times_transpose(left, right):
    return lax.dot_general(
        left, right, (((1,), (1,)), ((), ())), preferred_element_type=jnp.float32
    )


def butterfly_sum(values, axis):
    size = lax.axis_size(axis)
    if size & (size - 1):
        return lax.psum(values, axis)
    step = 1
    while step < size:
        pairs = [(i, i ^ step) for i in range(size)]
        values = values + lax.ppermute(values, axis, pairs)
        step *= 2
    return values


def sum_seq(values):
    if lax.axis_size("seq") == 2:
        other = lax.ppermute(values, "seq", [(0, 1), (1, 0)])
        return values.astype(jnp.float32) + other.astype(jnp.float32)
    return lax.psum(values, "seq").astype(jnp.float32)


class Regroup:
    def __init__(self, row_count):
        self.size = lax.axis_size("seq")
        self.ways = math.gcd(row_count, self.size)
        self.parts = self.size // self.ways
        self.rows = row_count // self.ways
        me = lax.axis_index("seq")
        self.place = lax.rem(me, self.ways)
        self.row_group = me // self.parts

    def targets(self, turn):
        ways, parts = self.ways, self.parts
        return [
            (s, ((s % ways + turn) % ways) * parts + s // ways) for s in range(self.size)
        ]

    def move(self, values, pairs):
        if all(a == b for a, b in pairs):
            return values
        return lax.ppermute(values, "seq", pairs)

    def gather(self, values):
        rows, local, width = self.rows, values.shape[1], values.shape[2]
        out = jnp.zeros((rows, self.ways, local, width), values.dtype)
        for turn in range(self.ways):
            pick = lax.rem(self.place + turn, self.ways)
            chunk = lax.dynamic_slice_in_dim(values, pick * rows, rows, 0)
            chunk = self.move(chunk, self.targets(turn))
            spot = lax.rem(self.row_group - turn + self.ways, self.ways)
            out = lax.dynamic_update_slice_in_dim(out, chunk[:, None], spot, 1)
        return out.reshape(rows, self.ways * local, width)

    def scatter(self, values):
        rows, width = self.rows, values.shape[2]
        local = values.shape[1] // self.ways
        values = values.reshape(rows, self.ways, local, width)
        out = jnp.zeros((rows * self.ways, local, width), values.dtype)
        for turn in range(self.ways):
            spot = lax.rem(self.row_group - turn + self.ways, self.ways)
            chunk = lax.dynamic_slice_in_dim(values, spot, 1, 1)[:, 0]
            chunk = self.move(chunk, [(b, a) for a, b in self.targets(turn)])
            pick = lax.rem(self.place + turn, self.ways)
            out = lax.dynamic_update_slice_in_dim(out, chunk, pick * rows, 0)
        return out

    def pick_rows(self, values):
        return lax.dynamic_slice_in_dim(values, self.row_group * self.rows, self.rows, 0)

    def groups(self):
        return [
            [r * self.parts + j for j in range(self.parts)] for r in range(self.ways)
        ]

    def to_heads(self, values):
        if self.parts == 1:
            return values
        return lax.all_to_all(
            values, "seq", split_axis=2, concat_axis=1, tiled=True,
            axis_index_groups=self.groups(),
        )

    def from_heads(self, values):
        if self.parts == 1:
            return values
        return lax.all_to_all(
            values, "seq", split_axis=1, concat_axis=2, tiled=True,
            axis_index_groups=self.groups(),
        )


def shards(
    tokens_in,
    segment_ids,
    random_blocks,
    global_blocks,
    w_query,
    b_query,
    w_key,
    w_value,
    b_value,
    w_attn_out,
    b_attn_out,
    ln1_gain,
    ln1_bias,
    w_inner,
    b_inner,
    w_outer,
    b_outer,
    ln2_gain,
    ln2_bias,
    out_grad,
):
    row_count, local_len, width = tokens_in.shape
    seq_count = lax.axis_size("seq")
    fsdp_count = lax.axis_size("fsdp")
    tok_count = row_count * local_len
    own = w_query.shape[0]
    chunks = b_inner.shape[0] // own
    regroup = Regroup(row_count)
    paired = row_count == 2 and seq_count == 2 and fsdp_count in (4, 8, 16, 32)

    vectors = [b_query, b_value, b_attn_out, ln1_gain, ln1_bias, b_outer, ln2_gain, ln2_bias]
    columns = [x[:, None] for x in vectors] + [b_inner.reshape(own, chunks)]
    used = len(vectors) + chunks
    columns.append(jnp.zeros((own, 128 - used), jnp.bfloat16))
    first = jnp.concatenate([w_query] + columns + [w_key, w_value], axis=1)
    inner_own = w_inner.reshape(own, width, chunks).transpose(0, 2, 1).reshape(own, -1)
    second = jnp.concatenate([w_attn_out, inner_own, w_outer.reshape(own, -1)], axis=1)
    second = lax.all_gather(second, "fsdp", axis=0, tiled=True)
    plan = plan_blocks(
        regroup.pick_rows(segment_ids),
        regroup.pick_rows(random_blocks),
        regroup.pick_rows(global_blocks),
    )

    def split_rows(values):
        return values.reshape(regroup.rows, tok_count // regroup.rows, width)

    def part_of(values, i):
        return values[:, part_start(width, i) : part_start(width, i) + width]

    side = lax.axis_index("seq") if paired else jnp.int32(0)
    swap = [(0, 1), (1, 0)]
    if paired:
        flat_in, *qkv, turned_in, turned_w, small, leaving = qkv_forward(
            tokens_in, first, out_grad
        )
        grad_other = lax.ppermute(leaving, "seq", swap)
        grad_own = lax.dynamic_index_in_dim(out_grad, side, 0, keepdims=False)
    else:
        first = lax.all_gather(first, "fsdp", axis=0, tiled=True)
        small = first[:, width : width + SMALL_ROWS].astype(jnp.float32).T
        flat_in = regroup.gather(tokens_in).reshape(tok_count, width)
        biases = (small[0], jnp.zeros_like(small[0]), small[1])
        qkv = [
            (jnp.dot(flat_in, part_of(first, i), preferred_element_type=jnp.float32)
             + biases[i]).astype(jnp.bfloat16)
            for i in range(3)
        ]
        flat_grad = regroup.gather(out_grad).reshape(tok_count, width)
        grad_own, grad_other = flat_grad[: tok_count // 2], flat_grad[tok_count // 2 :]
    q, k, v = (regroup.to_heads(split_rows(x)) for x in qkv)
    att, lse = attention_forward(q, k, v, plan)
    att_flat = regroup.from_heads(att).reshape(tok_count, width)
    kept, sent, *saved, d_outer, sums = middle_forward(
        side, second, small, att_flat, flat_in, grad_own, grad_other
    )
    if paired:
        sent = lax.ppermute(sent, "seq", swap)
    d_attn, d_att, d_second, sums = middle_backward(second, small, sums, att_flat, *saved)

    def scattered(values):
        return lax.psum_scatter(values, "fsdp", scatter_dimension=0, tiled=True)

    d_outer = scattered(d_outer)
    d_second = scattered(d_second)
    dq, dk, dv = attention_backward(
        q, k, v, att, regroup.to_heads(split_rows(d_att)), lse, plan
    )
    dq, dk, dv = (regroup.from_heads(x).reshape(tok_count, width) for x in (dq, dk, dv))
    mine = lax.axis_index("fsdp")
    dq, sent, d_outer = lax.optimization_barrier((dq, sent, d_outer))
    d_outer = sum_seq(d_outer)
    if paired:
        d_query_w, d_key_w, d_value_w, sums, d_tokens_in = qkv_backward(
            turned_in, dq, dk, dv, turned_w, d_attn, sums, own
        )
        d_second, sums = lax.optimization_barrier((d_second, sums))
        place = jnp.arange(2, dtype=jnp.int32)[:, None, None]
        out_tokens = jnp.where(place == side, kept[None], sent[None])
        d_tokens_in = jnp.where(place >= -side, d_tokens_in, jnp.zeros_like(d_tokens_in))
    else:
        for spot, part in ((0, dq), (1, dv)):
            sums = sums.at[spot].set(jnp.sum(part.astype(jnp.float32), axis=0))
        sums = butterfly_sum(butterfly_sum(sums, "fsdp"), "seq")
        d_query_w, d_key_w, d_value_w = (
            sum_seq(scattered(contract_rows(flat_in, x).astype(jnp.bfloat16)))
            for x in (dq, dk, dv)
        )
        d_tokens = d_attn.astype(jnp.float32)
        for i, part in enumerate((dq, dk, dv)):
            d_tokens = d_tokens + times_transpose(part, part_of(first, i))
        d_tokens_in = regroup.scatter(split_rows(d_tokens.astype(jnp.bfloat16)))
        out_tokens = regroup.scatter(split_rows(jnp.concatenate([kept, sent])))
    d_second = sum_seq(d_second)
    d_inner_w = (
        d_second[:, width:]
        .reshape(own, chunks, width)
        .transpose(0, 2, 1)
        .reshape(own, -1)
    )
    d_outer_w = d_outer.reshape(own * chunks, width)
    d_vec = lax.dynamic_slice_in_dim(sums, mine * own, own, 1)
    entry_total = tok_count * width * seq_count * fsdp_count
    rms_values = jnp.sqrt(
        jnp.sum(sums[INNER_B + chunks : INNER_B + chunks + 3], axis=1) / entry_total
    )
    return (
        out_tokens,
        d_tokens_in,
        d_query_w,
        d_vec[0],
        d_key_w,
        d_value_w,
        d_vec[1],
        d_second[:, :width],
        d_vec[OUT_B],
        d_vec[GAIN_1],
        d_vec[BIAS_1],
        d_inner_w,
        d_vec[INNER_B : INNER_B + chunks].T.reshape(-1),
        d_outer_w,
        d_vec[OUTER_B],
        d_vec[GAIN_2],
        d_vec[BIAS_2],
        rms_values,
    )


def solution(mesh):
    in_specs = (
        P("fsdp", "seq", None),
        P("fsdp", None),
        P("fsdp", None, None),
        P("fsdp", None),
        P("fsdp", None),
        P("fsdp"),
        P("fsdp", None),
        P("fsdp", None),
        P("fsdp"),
        P("fsdp", None),
        P("fsdp"),
        P("fsdp"),
        P("fsdp"),
        P("fsdp", None),
        P("fsdp"),
        P("fsdp", None),
        P("fsdp"),
        P("fsdp"),
        P("fsdp"),
        P("fsdp", "seq", None),
    )
    out_specs = (
        P("fsdp", "seq", None),
        P("fsdp", "seq", None),
        P("fsdp", None),
        P("fsdp"),
        P("fsdp", None),
        P("fsdp", None),
        P("fsdp"),
        P("fsdp", None),
        P("fsdp"),
        P("fsdp"),
        P("fsdp"),
        P("fsdp", None),
        P("fsdp"),
        P("fsdp", None),
        P("fsdp"),
        P("fsdp"),
        P("fsdp"),
        P(),
    )
    return jax.shard_map(shards, mesh=mesh, in_specs=in_specs, out_specs=out_specs, check_vma=False)
```

```python
import functools
import math

import jax
import jax.numpy as jnp
from jax import lax
from jax.experimental import pallas as pl
from jax.experimental.pallas import tpu as pltpu
from jax.sharding import PartitionSpec as P

HD = 64
BLK = 64
CHUNK = 4
ITEMS = 3
NEG = -1e30


def plan_blocks(seg, rand, glob):
    rows, full_len = seg.shape
    nb = full_len // BLK
    ids = jnp.arange(nb, dtype=jnp.int32)
    is_global = jnp.any(ids[None, :, None] == glob[:, None, :], axis=-1)
    picked = jnp.any(rand[:, :, None, :] == ids[None, None, :, None], axis=-1)
    nearby = jnp.abs(ids[:, None] - ids[None, :]) <= 1
    admitted = nearby[None] | picked | is_global[:, :, None] | is_global[:, None, :]
    by_block = seg.reshape(rows, nb, BLK)
    low, high = by_block[:, :, 0], by_block[:, :, BLK - 1]
    meets = (low[:, :, None] <= high[:, None, :]) & (low[:, None, :] <= high[:, :, None])
    active = (admitted & meets).astype(jnp.int32)
    upto = (ids[:, None] <= ids[None, :]).astype(jnp.int32)
    place = jnp.sum(active[:, :, :, None] * upto[None, None], axis=2) - 1
    count = jnp.sum(active, axis=2)
    hit = (place[:, :, :, None] == ids[None, None, None, :]) & (active[:, :, :, None] > 0)
    listed = jnp.sum(jnp.where(hit, ids[None, None, :, None], 0), axis=2)
    listed = jnp.where(ids[None, None, :] < count[:, :, None], listed, nb)
    chunks = (count + (CHUNK - 1)) // CHUNK
    seg_cols = jnp.concatenate([seg, jnp.full((rows, BLK), -1, jnp.int32)], axis=1)
    seg_cols = jnp.broadcast_to(seg_cols[:, :, None], (rows, full_len + BLK, 128))
    seg_rows = jnp.concatenate([by_block, by_block], axis=2)[:, :, None, :]
    return chunks, listed.reshape(rows, nb * nb), jnp.sum(chunks, axis=1), seg_cols, seg_rows


def lane_low(rows):
    return lax.broadcasted_iota(jnp.int32, (rows, 128), 1) < HD


def diag128(dup_t):
    row = lax.broadcasted_iota(jnp.int32, (128, 128), 0) < HD
    col = lax.broadcasted_iota(jnp.int32, (128, 128), 1) < HD
    return jnp.where(row == col, dup_t, jnp.zeros_like(dup_t))


def transposed_twice(tile):
    both = jnp.concatenate([tile, tile], axis=0)
    return both.T


def head_rows(acc):
    turned = jnp.concatenate([acc, acc], axis=0).T
    return jnp.where(lane_low(HD), turned[:HD], turned[HD:])


def pick_diag(full, half):
    lanes = slice(half * 128, half * 128 + 128)
    top = full[half * 128 : half * 128 + HD, lanes]
    low = full[half * 128 + HD : half * 128 + 128, lanes]
    return jnp.where(lane_low(HD), top, low)


def chunk_ids(list_ref, row, base, nb, real):
    base = jnp.minimum(base, nb * nb - CHUNK)
    ids = [jnp.where(real, list_ref[row, base + j], nb) for j in range(CHUNK)]
    safe = [jnp.where(b == nb, 0, b) for b in ids]
    return ids, safe


def block_rows(ref, blocks, lanes):
    return jnp.concatenate(
        [ref[0, pl.ds(pl.multiple_of(b * BLK, BLK), BLK), lanes] for b in blocks], axis=0
    )


def turned_blocks(ref, blocks, rows):
    low = lane_low(rows.stop - rows.start)
    tiles = [ref[b, rows, :] for b in blocks]
    return jnp.concatenate(
        [jnp.where(low, tiles[i], tiles[i + 1]) for i in range(0, CHUNK, 2)], axis=1
    )


def turn_all(src_ref, dst_ref, nb, width):
    def body(b, _):
        start = pl.multiple_of(b * BLK, BLK)
        for t in range(width // 128):
            tile = src_ref[0, pl.ds(start, BLK), t * 128 : t * 128 + 128]
            dst_ref[b, t * 128 : t * 128 + 128, :] = transposed_twice(tile)
        return 0

    lax.fori_loop(0, nb, body, 0, unroll=4)


def dot_f32(left, right):
    return lax.dot_general(
        left, right, (((1,), (0,)), ((), ())), preferred_element_type=jnp.float32
    )


def fetch(row, pairs, sem):
    loads = [
        pltpu.make_async_copy(src.at[pl.ds(row, 1)], dst, sem.at[i])
        for i, (src, dst) in enumerate(pairs)
    ]
    for load in loads:
        load.start()
    return loads


def next_item(n_ref, row, nb, a, c):
    more = c + 1 < n_ref[row, a]
    following = jnp.where(more, a, jnp.minimum(a + 1, nb - 1))
    return following, jnp.where(more, c + 1, 0)


def run_items(n_ref, total_ref, row, nb, ready, item, finish):
    total = total_ref[row]

    def walk(a, c):
        places = [(a, c)]
        for _ in range(2 * ITEMS - 1):
            places.append(next_item(n_ref, row, nb, *places[-1]))
        return places

    def turn(i, carry):
        before, a, c = carry
        base = lax.rem(i, 2) * ITEMS
        for past in before:
            finish(past)
        places = walk(a, c)
        for k in range(ITEMS):
            ready(places[ITEMS + k][0], ITEMS - base + k)
        here = [places[0]]
        item(base, *here[0], True)
        for k in range(1, ITEMS):
            real = ITEMS * i + k < total
            here.append(
                (
                    jnp.where(real, places[k][0], here[-1][0]),
                    jnp.where(real, places[k][1], here[-1][1] + 1),
                )
            )
            item(base + k, *here[k], real)
        return (tuple(place[0] for place in here), *places[ITEMS])

    for k, place in enumerate(walk(0, 0)[:ITEMS]):
        ready(place[0], k)
    before, _, _ = lax.fori_loop(
        0, (total + ITEMS - 1) // ITEMS, turn, ((0,) * ITEMS, 0, 0)
    )
    for past in before:
        finish(past)


def forward_kernel(group, n_ref, list_ref, total_ref, q_in, k_in, v_in, segc_ref, segr_ref,
                   o_ref, lse_ref, q_ref, k_ref, v_ref, vt_ref, qst_ref, m_ref, l_ref, acc_ref,
                   sem):
    row = pl.program_id(0)
    width = q_ref.shape[2]
    nb = q_ref.shape[1] // BLK
    groups, halves = width // group, group // 128
    tiles = width // 128
    loads = fetch(row, ((v_in, v_ref), (q_in, q_ref), (k_in, k_ref)), sem)
    qst_ref[...] = jnp.zeros_like(qst_ref)
    l_ref[...] = jnp.ones_like(l_ref)
    acc_ref[...] = jnp.zeros_like(acc_ref)
    m_ref[...] = jnp.zeros_like(m_ref)
    loads[0].wait()
    turn_all(v_ref, vt_ref, nb, width)
    for load in loads[1:]:
        load.wait()

    def ready(a, slot):
        start = pl.multiple_of(a * BLK, BLK)
        for t in range(tiles):
            tile = q_ref[0, pl.ds(start, BLK), t * 128 : t * 128 + 128] * 0.125
            square = slice(t % halves * 128, t % halves * 128 + 128)
            qst_ref[slot, t // halves, square, square] = diag128(
                transposed_twice(tile.astype(jnp.bfloat16))
            )

    def finish(a):
        even = lax.rem(a, ITEMS)
        start = pl.multiple_of(a * BLK, BLK)
        for t in range(tiles):
            lanes = slice(t * 128, t * 128 + 128)
            total = l_ref[even, t]
            o_ref[0, pl.ds(start, BLK), lanes] = head_rows(acc_ref[even, t] / total).astype(
                jnp.bfloat16
            )
            lse_ref[0, a, :, lanes] = m_ref[even, t] + jnp.log(total)

    def item(slot, a, c, real):
        ids, safe = chunk_ids(list_ref, row, a * nb + c * CHUNK, nb, real)
        even = lax.rem(a, ITEMS)
        allowed = block_rows(segc_ref, ids, slice(0, 128)) == segr_ref[0, a]
        first = c == 0
        for g in range(groups):
            lanes = slice(g * group, g * group + group)
            s_t = dot_f32(block_rows(k_ref, safe, lanes), qst_ref[slot, g])
            weights, alphas = [], []
            for u in range(halves):
                t = g * halves + u
                s = jnp.where(allowed, s_t[:, u * 128 : u * 128 + 128], NEG)
                m_old = jnp.where(first, NEG, m_ref[even, t])
                m_new = jnp.maximum(m_old, jnp.max(s, axis=0, keepdims=True))
                p = jnp.exp(s - m_new)
                alpha = jnp.exp(m_old - m_new)
                l_ref[even, t] = alpha * l_ref[even, t] + jnp.sum(p, axis=0, keepdims=True)
                m_ref[even, t] = m_new
                weights.append(p.astype(jnp.bfloat16))
                alphas.append(alpha)
            p_t = jnp.concatenate(weights, axis=1) if halves > 1 else weights[0]
            o_t = dot_f32(turned_blocks(vt_ref, safe, lanes), p_t)
            for u in range(halves):
                t = g * halves + u
                acc_ref[even, t] = alphas[u] * acc_ref[even, t] + pick_diag(o_t, u)

    run_items(n_ref, total_ref, row, nb, ready, item, finish)


def group_of(width):
    return 256 if width % 256 == 0 else 128


def whole_spec(shape):
    rest = (0,) * (len(shape) - 1)
    return pl.BlockSpec((1,) + tuple(shape[1:]), lambda r, *_: (r,) + rest)


def one_spec(shape):
    rest = (0,) * (len(shape) - 1)
    return pl.BlockSpec((1,) + tuple(shape[1:]), lambda r, *_: (r,) + rest,
                        pipeline_mode=pl.Buffered(1))


def attention_forward(q, k, v, plan):
    *tables, seg_cols, seg_rows = plan
    rows, full_len, width = q.shape
    nb, group = full_len // BLK, group_of(width)
    tiles = width // 128
    pairs = rows * full_len * full_len // 4 * width
    args = (q, k, v, seg_cols, seg_rows)
    anywhere = pl.BlockSpec(memory_space=pl.ANY)
    stretch = pltpu.VMEM((1, full_len, width), jnp.bfloat16)
    return pl.pallas_call(
        functools.partial(forward_kernel, group),
        out_shape=(
            jax.ShapeDtypeStruct((rows, full_len, width), jnp.bfloat16),
            jax.ShapeDtypeStruct((rows, nb, 1, width), jnp.float32),
        ),
        grid_spec=pltpu.PrefetchScalarGridSpec(
            num_scalar_prefetch=3,
            grid=(rows,),
            in_specs=[anywhere] * 3 + [one_spec(x.shape) for x in args[3:]],
            out_specs=(one_spec((rows, full_len, width)), one_spec((rows, nb, 1, width))),
            scratch_shapes=[
                stretch, stretch, stretch,
                pltpu.VMEM((nb, width, 128), jnp.bfloat16),
                pltpu.VMEM((2 * ITEMS, width // group, group, group), jnp.bfloat16),
                pltpu.VMEM((ITEMS, tiles, 1, 128), jnp.float32),
                pltpu.VMEM((ITEMS, tiles, 1, 128), jnp.float32),
                pltpu.VMEM((ITEMS, tiles, HD, 128), jnp.float32),
                pltpu.SemaphoreType.DMA((3,)),
            ],
        ),
        compiler_params=pltpu.CompilerParams(vmem_limit_bytes=62 << 20),
        cost_estimate=pl.CostEstimate(
            flops=4 * pairs, transcendentals=pairs // HD, bytes_accessed=8 * q.size
        ),
        name="attention_forward",
    )(*tables, *args)


def backward_kernel(group, n_ref, list_ref, total_ref, q_in, k_in, v_in, o_in, do_in,
                    lse_ref, segc_ref, segr_ref, dq_out, dk_out, dv_out,
                    q_ref, k_ref, v_ref, o_ref, do_ref, dq_ref, kt_ref, qst_ref, qs_ref, dost_ref, dos_ref, delta_ref, acc_ref,
                    dk_acc, dv_acc, sem, out_sem):
    row = pl.program_id(0)
    full_len, width = q_ref.shape[1], q_ref.shape[2]
    nb = full_len // BLK
    groups, halves = width // group, group // 128
    tiles = width // 128
    loads = fetch(
        row,
        ((k_in, k_ref), (q_in, q_ref), (do_in, do_ref), (o_in, o_ref), (v_in, v_ref)),
        sem,
    )
    for ref in (qst_ref, qs_ref, dost_ref, dos_ref, acc_ref):
        ref[...] = jnp.zeros_like(ref)
    loads[0].wait()
    turn_all(k_ref, kt_ref, nb, width)
    for ref in (dk_acc, dv_acc):
        ref[...] = jnp.zeros_like(ref)
    for load in loads[1:]:
        load.wait()
    low = lane_low(1)

    def ready(a, slot):
        start = pl.multiple_of(a * BLK, BLK)
        for t in range(tiles):
            g, u = t // halves, t % halves
            lanes = slice(t * 128, t * 128 + 128)
            square = slice(u * 128, u * 128 + 128)
            q_tile = (q_ref[0, pl.ds(start, BLK), lanes] * 0.125).astype(jnp.bfloat16)
            g_tile = do_ref[0, pl.ds(start, BLK), lanes]
            o_tile = o_ref[0, pl.ds(start, BLK), lanes]
            g_turn = transposed_twice(g_tile)
            qst_ref[slot, g, square, square] = diag128(transposed_twice(q_tile))
            dost_ref[slot, g, square, square] = diag128(g_turn)
            qs_ref[slot, g, square, square] = diag128(jnp.concatenate([q_tile, q_tile], axis=0))
            dos_ref[slot, g, square, square] = diag128(
                jnp.concatenate([g_tile, g_tile], axis=0)
            )
            product = g_turn.astype(jnp.float32) * transposed_twice(o_tile).astype(jnp.float32)
            delta_ref[slot, t] = jnp.where(
                low,
                jnp.sum(product[:HD], axis=0, keepdims=True),
                jnp.sum(product[HD:], axis=0, keepdims=True),
            )

    def finish(a):
        even = lax.rem(a, ITEMS)
        start = pl.multiple_of(a * BLK, BLK)
        for t in range(tiles):
            dq_ref[0, pl.ds(start, BLK), t * 128 : t * 128 + 128] = (
                head_rows(acc_ref[even, t]) * 0.125
            ).astype(jnp.bfloat16)

    def item(slot, a, c, real):
        ids, safe = chunk_ids(list_ref, row, a * nb + c * CHUNK, nb, real)
        even = lax.rem(a, ITEMS)
        allowed = block_rows(segc_ref, ids, slice(0, 128)) == segr_ref[0, a]
        first = c == 0
        for g in range(groups):
            lanes = slice(g * group, g * group + group)
            s_t = dot_f32(block_rows(k_ref, safe, lanes), qst_ref[slot, g])
            dp_t = dot_f32(block_rows(v_ref, safe, lanes), dost_ref[slot, g])
            p_parts, ds_parts = [], []
            for u in range(halves):
                t = g * halves + u
                half = slice(u * 128, u * 128 + 128)
                lse = lse_ref[0, a, :, t * 128 : t * 128 + 128]
                p = jnp.exp(jnp.where(allowed, s_t[:, half], NEG) - lse)
                ds = p * (dp_t[:, half] - delta_ref[slot, t])
                p_parts.append(p.astype(jnp.bfloat16))
                ds_parts.append(ds.astype(jnp.bfloat16))
            p_t = jnp.concatenate(p_parts, axis=1) if halves > 1 else p_parts[0]
            ds_t = jnp.concatenate(ds_parts, axis=1) if halves > 1 else ds_parts[0]
            dv = dot_f32(p_t, dos_ref[slot, g])
            dk = dot_f32(ds_t, qs_ref[slot, g])
            dq_t = dot_f32(turned_blocks(kt_ref, safe, lanes), ds_t)
            for j in range(CHUNK):
                where = pl.ds(pl.multiple_of(safe[j] * BLK, BLK), BLK)
                part = slice(j * BLK, j * BLK + BLK)
                dv_acc[where, lanes] += dv[part]
                dk_acc[where, lanes] += dk[part]
            for u in range(halves):
                t = g * halves + u
                acc_ref[even, t] = jnp.where(first, 0.0, acc_ref[even, t]) + pick_diag(dq_t, u)

    run_items(n_ref, total_ref, row, nb, ready, item, finish)

    def leave(i, src, dst):
        return pltpu.make_async_copy(src, dst.at[pl.ds(row, 1)], out_sem.at[i])

    leaving = [leave(0, dq_ref, dq_out)]
    leaving[0].start()
    for i, (total, low, out) in enumerate(((dk_acc, q_ref, dk_out), (dv_acc, o_ref, dv_out))):
        def flush(a, _):
            where = pl.ds(pl.multiple_of(a * BLK, BLK), BLK)
            low[0, where, :] = total[where, :].astype(jnp.bfloat16)
            return 0

        lax.fori_loop(0, nb, flush, 0, unroll=2)
        leaving.append(leave(1 + i, low, out))
        leaving[-1].start()
    for copy in leaving:
        copy.wait()


def attention_backward(q, k, v, o, do, lse, plan):
    *tables, seg_cols, seg_rows = plan
    rows, full_len, width = q.shape
    nb, group = full_len // BLK, group_of(width)
    tiles, groups = width // 128, width // group
    pairs = rows * full_len * full_len // 4 * width
    args = (q, k, v, o, do, lse, seg_cols, seg_rows)
    anywhere = pl.BlockSpec(memory_space=pl.ANY)
    stretch = pltpu.VMEM((1, full_len, width), jnp.bfloat16)
    like = jax.ShapeDtypeStruct((rows, full_len, width), jnp.bfloat16)
    square = pltpu.VMEM((2 * ITEMS, groups, group, group), jnp.bfloat16)
    return pl.pallas_call(
        functools.partial(backward_kernel, group),
        out_shape=(like, like, like),
        grid_spec=pltpu.PrefetchScalarGridSpec(
            num_scalar_prefetch=3,
            grid=(rows,),
            in_specs=[anywhere] * 5 + [one_spec(x.shape) for x in args[5:]],
            out_specs=(anywhere,) * 3,
            scratch_shapes=[
                stretch, stretch, stretch, stretch, stretch, stretch,
                pltpu.VMEM((nb, width, 128), jnp.bfloat16),
                square, square, square, square,
                pltpu.VMEM((2 * ITEMS, tiles, 1, 128), jnp.float32),
                pltpu.VMEM((ITEMS, tiles, HD, 128), jnp.float32),
                pltpu.VMEM((full_len, width), jnp.float32),
                pltpu.VMEM((full_len, width), jnp.float32),
                pltpu.SemaphoreType.DMA((5,)),
                pltpu.SemaphoreType.DMA((3,)),
            ],
        ),
        compiler_params=pltpu.CompilerParams(vmem_limit_bytes=62 << 20),
        cost_estimate=pl.CostEstimate(
            flops=10 * pairs, transcendentals=pairs // HD, bytes_accessed=16 * q.size
        ),
        name="attention_backward",
    )(*tables, *args)


def pair_bit(index, bit):
    return lax.rem(index // (1 << bit), 2)


def pair_of(index, bit):
    return index + (1 - 2 * pair_bit(index, bit)) * (1 << bit)


def all_arrived(bits):
    me = lax.axis_index("fsdp")
    barrier = pltpu.get_barrier_semaphore()
    for bit in range(bits):
        pl.semaphore_signal(
            barrier, inc=1, device_id={"fsdp": pair_of(me, bit)},
            device_id_type=pl.DeviceIdType.MESH,
        )
    pl.semaphore_signal(
        barrier, inc=1, device_id={"seq": 1 - lax.axis_index("seq")},
        device_id_type=pl.DeviceIdType.MESH,
    )
    pl.semaphore_wait(barrier, bits + 1)


def qkv_backward_kernel(
    bits, xt_in, dq_in, dk_in, dv_in, wt_in, res_in, small_in,
    wq_out, wk_out, wv_out, small_out, tok_out,
    xt, grads, wt, res, tok, kept, sends, lands, final, small, small_land, result,
    in_sem, tok_send, tok_land, own_sem, send_sem, land_sem, x_send, x_land,
    small_send, small_recv, out_sem,
):
    me, side = lax.axis_index("fsdp"), lax.axis_index("seq")
    half = tok.shape[2] * tok.shape[1]
    piece, pieces = tok.shape[2], tok.shape[1]
    own, width = wq_out.shape
    owners = 1 << bits
    sources = (dq_in, dk_in, dv_in)
    rows_of = [pl.ds(pl.multiple_of(p * half, half), half) for p in (1 - side, side)]
    loads = [pltpu.make_async_copy(wt_in, wt, in_sem.at[0])]
    for p in range(2):
        for i in range(3):
            loads.append(
                pltpu.make_async_copy(
                    sources[i].at[rows_of[p]], grads.at[i, rows_of[p]], in_sem.at[1 + 4 * p + i]
                )
            )
        loads.append(
            pltpu.make_async_copy(res_in.at[rows_of[p]], res.at[rows_of[p]], in_sem.at[4 + 4 * p])
        )
    loads.append(pltpu.make_async_copy(xt_in, xt, in_sem.at[9]))
    loads.append(pltpu.make_async_copy(small_in, small.at[0], in_sem.at[10]))
    for i in (0, 1, 2, 3, 4, 9, 5, 6, 7, 8, 10):
        loads[i].start()
    all_arrived(bits)

    def token_rows(start):
        total = res[pl.ds(start, piece), :].astype(jnp.float32)
        for i in range(3):
            total = total + dot_f32(
                grads[i, pl.ds(start, piece), :], wt[i]
            )
        return total.astype(jnp.bfloat16)

    def sent(i):
        return pltpu.make_async_remote_copy(
            src_ref=tok.at[0, i],
            dst_ref=tok_out.at[side, pl.ds(pl.multiple_of(i * piece, piece), piece)],
            send_sem=tok_send.at[i], recv_sem=tok_land.at[i],
            device_id={"seq": 1 - side}, device_id_type=pl.DeviceIdType.MESH,
        )

    def landed(i):
        return pltpu.make_async_remote_copy(
            src_ref=tok.at[0, i],
            dst_ref=tok_out.at[1 - side, pl.ds(pl.multiple_of(i * piece, piece), piece)],
            send_sem=tok_send.at[i], recv_sem=tok_land.at[i],
            device_id={"seq": 1 - side}, device_id_type=pl.DeviceIdType.MESH,
        )

    def stays(i):
        return pltpu.make_async_copy(
            tok.at[1, i],
            tok_out.at[side, pl.ds(pl.multiple_of(i * piece, piece), piece)],
            own_sem.at[i],
        )

    def send_piece(i, _):
        start = pl.multiple_of((1 - side) * half + i * piece, piece)
        tok[0, i] = token_rows(start)
        sent(i).start()
        return 0

    def keep_piece(i, _):
        start = pl.multiple_of(side * half + i * piece, piece)
        tok[1, i] = token_rows(start)
        stays(i).start()
        return 0

    low_bit = pair_bit(me, 0) == 0
    tile = 8 if owners % 8 == 0 else owners
    first_of = [0]
    for bit in range(bits):
        first_of.append(first_of[-1] + (owners >> (bit + 1)))

    def weights(i):
        def rows(m, _):
            rows_here = pl.ds(pl.multiple_of(m * tile * own, tile * own), tile * own)
            block = dot_f32(
                jnp.concatenate(
                    [xt[h, r, rows_here, :] for h in range(2) for r in range(pieces)], axis=1
                ),
                grads[i],
            ).reshape(tile // 2, 2, own, width)
            even, odd = block[:, 0], block[:, 1]
            spot = pl.ds(m * (tile // 2), tile // 2)
            kept[i, spot] = jnp.where(low_bit, even, odd)
            sends[i, spot] = jnp.where(low_bit, odd, even).astype(jnp.bfloat16)
            return 0

        lax.fori_loop(0, owners // tile, rows, 0)

    def hop(i, bit):
        count = owners >> (bit + 1)
        spot = pl.ds(first_of[bit], count)
        return pltpu.make_async_remote_copy(
            src_ref=sends.at[i, spot], dst_ref=lands.at[i, spot],
            send_sem=send_sem.at[i, bit], recv_sem=land_sem.at[i, bit],
            device_id={"fsdp": pair_of(me, bit)}, device_id_type=pl.DeviceIdType.MESH,
        )

    def cross(i):
        return pltpu.make_async_remote_copy(
            src_ref=final.at[0, i], dst_ref=final.at[1, i],
            send_sem=x_send.at[i], recv_sem=x_land.at[i],
            device_id={"seq": 1 - side}, device_id_type=pl.DeviceIdType.MESH,
        )

    def advance(i, bit):
        hop(i, bit).wait_recv()
        base = first_of[bit]
        if bit + 1 == bits:
            total = kept[i, base] + lands[i, base].astype(jnp.float32)
            final[0, i] = total.astype(jnp.bfloat16)
            cross(i).start()
            return
        nxt = pair_bit(me, bit + 1)

        def one(j, _):
            stay, go = 2 * j + nxt, 2 * j + 1 - nxt
            kept[i, first_of[bit + 1] + j] = kept[i, base + stay] + lands[
                i, base + stay
            ].astype(jnp.float32)
            sends[i, first_of[bit + 1] + j] = (
                kept[i, base + go] + lands[i, base + go].astype(jnp.float32)
            ).astype(jnp.bfloat16)
            return 0

        lax.fori_loop(0, owners >> (bit + 2), one, 0)
        hop(i, bit + 1).start()

    outs = (wq_out, wk_out, wv_out)

    def written(i):
        return pltpu.make_async_copy(result.at[i], outs[i], out_sem.at[i])

    def finish(i):
        cross(i).wait_recv()
        result[i] = final[0, i].astype(jnp.float32) + final[1, i].astype(jnp.float32)
        written(i).start()

    def small_hop(bit):
        where = {"fsdp": pair_of(me, bit)} if bit < bits else {"seq": 1 - side}
        return pltpu.make_async_remote_copy(
            src_ref=small.at[bit], dst_ref=small_land.at[bit],
            send_sem=small_send.at[bit], recv_sem=small_recv.at[bit],
            device_id=where, device_id_type=pl.DeviceIdType.MESH,
        )

    def small_advance(bit):
        small_hop(bit).wait_recv()
        small[bit + 1] = small[bit] + small_land[bit]
        if bit < bits:
            small_hop(bit + 1).start()

    def column_sums(i, spot):
        def one(c, total):
            block = grads[i, pl.ds(pl.multiple_of(c * 256, 256), 256), :].astype(jnp.float32)
            return total + jnp.sum(block.reshape(32, 8, width), axis=0)

        total = lax.fori_loop(
            0, grads.shape[1] // 256, one, jnp.zeros((8, width), jnp.float32)
        )
        small[0, spot : spot + 1] = jnp.sum(total, axis=0, keepdims=True)

    for i in range(5):
        loads[i].wait()
    send_piece(0, 0)
    for i in range(5, 11):
        loads[i].wait()

    def begin(i, _):
        weights(i)
        hop(i, 0).start()
        send_piece(i + 1, 0)
        advance(i, 0)
        return 0

    lax.fori_loop(0, 3, begin, 0)
    column_sums(0, 0)
    column_sums(2, 1)
    small_hop(0).start()

    def second(i, _):
        keep_piece(i, 0)
        advance(i, 1)
        return 0

    lax.fori_loop(0, 3, second, 0)
    small_advance(0)
    keep_piece(3, 0)
    for bit in range(2, bits):
        for i in range(3):
            advance(i, bit)
        small_advance(bit - 1)
    for bit in range(bits - 1, bits + 1):
        small_advance(bit)
    for i in range(3):
        finish(i)
    small_copy = pltpu.make_async_copy(small.at[bits + 1], small_out, out_sem.at[3])
    small_copy.start()
    for i in range(3):
        written(i).wait()
        cross(i).wait_send()
        for bit in range(bits):
            hop(i, bit).wait_send()
    for bit in range(bits + 1):
        small_hop(bit).wait_send()
    small_copy.wait()
    for i in range(pieces):
        stays(i).wait()
        sent(i).wait_send()
        landed(i).wait_recv()


def qkv_backward(xt, dq, dk, dv, wt, resid, small, own):
    tokens, width = dq.shape
    bits = lax.axis_size("fsdp").bit_length() - 1
    owners = 1 << bits
    pieces = 4
    piece = tokens // 2 // pieces
    dma = pltpu.SemaphoreType.DMA
    f32, bf16 = jnp.float32, jnp.bfloat16
    shard = jax.ShapeDtypeStruct((own, width), f32)
    anywhere = pl.BlockSpec(memory_space=pltpu.HBM)
    return pl.pallas_call(
        functools.partial(qkv_backward_kernel, bits),
        out_shape=(
            shard, shard, shard,
            jax.ShapeDtypeStruct(small.shape, f32),
            jax.ShapeDtypeStruct((2, tokens // 2, width), bf16),
        ),
        in_specs=[anywhere] * 7,
        out_specs=(anywhere,) * 5,
        scratch_shapes=[
            pltpu.VMEM(xt.shape, bf16),
            pltpu.VMEM((3, tokens, width), bf16),
            pltpu.VMEM(wt.shape, bf16),
            pltpu.VMEM((tokens, width), bf16),
            pltpu.VMEM((2, pieces, piece, width), bf16),
            pltpu.VMEM((3, owners - 1, own, width), f32),
            pltpu.VMEM((3, owners - 1, own, width), bf16),
            pltpu.VMEM((3, owners - 1, own, width), bf16),
            pltpu.VMEM((2, 3, own, width), bf16),
            pltpu.VMEM((bits + 2,) + small.shape, f32),
            pltpu.VMEM((bits + 1,) + small.shape, f32),
            pltpu.VMEM((3, own, width), f32),
            dma((11,)), dma((pieces,)), dma((pieces,)), dma((pieces,)),
            dma((3, bits)), dma((3, bits)), dma((3,)), dma((3,)),
            dma((bits + 1,)), dma((bits + 1,)), dma((4,)),
        ],
        compiler_params=pltpu.CompilerParams(
            collective_id=1, has_side_effects=True, vmem_limit_bytes=62 << 20
        ),
        cost_estimate=pl.CostEstimate(
            flops=40 * tokens * width * width, transcendentals=0,
            bytes_accessed=16 * tokens * width,
        ),
        name="qkv_backward",
    )(xt, dq, dk, dv, wt, resid, small)


def qkv_forward_kernel(
    bits, tokens_in, own_in, grad_in,
    grad_out, x_out, xt_out, q_out, k_out, v_out, wt_out, small_out,
    x, xt, w, wt, qkv, small,
    own_sem, tok_send, tok_land, load_sem, send_sem, land_sem, x_sem, xt_sem, out_sem, w_sem,
    small_sem,
):
    me, side = lax.axis_index("fsdp"), lax.axis_index("seq")
    pieces, piece, width = x.shape[1], x.shape[2], x.shape[3]
    mine = [pair_bit(me, bit) for bit in range(bits)]
    columns = part_columns(width)
    outs = (q_out, k_out, v_out)

    def slot(bit, part):
        here = [slice(None)] * (bits - 1 - bit) + [mine[b] for b in range(bit, -1, -1)]
        return tuple(here) + (slice(None), columns[part])

    own_tokens = pltpu.make_async_copy(tokens_in.at[side], x.at[side], own_sem.at[0])
    own_tokens.start()
    grad_rows = pltpu.make_async_copy(grad_in.at[1 - side], grad_out, own_sem.at[1])
    grad_rows.start()

    def load(part):
        spot = tuple(mine[b] for b in range(bits - 1, -1, -1)) + (slice(None), columns[part])
        return pltpu.make_async_copy(
            own_in.at[:, columns[part]], w.at[spot], load_sem.at[part]
        )

    for part in range(3):
        load(part).start()
    all_arrived(bits)

    def sent(i):
        return pltpu.make_async_remote_copy(
            src_ref=tokens_in.at[1 - side, i], dst_ref=x.at[side, i],
            send_sem=tok_send.at[i], recv_sem=tok_land.at[i],
            device_id={"seq": 1 - side}, device_id_type=pl.DeviceIdType.MESH,
        )

    def landed(i):
        return pltpu.make_async_remote_copy(
            src_ref=tokens_in.at[1 - side, i], dst_ref=x.at[1 - side, i],
            send_sem=tok_send.at[i], recv_sem=tok_land.at[i],
            device_id={"seq": 1 - side}, device_id_type=pl.DeviceIdType.MESH,
        )

    def hop(part, turn):
        bit = bits - 1 - turn
        return pltpu.make_async_remote_copy(
            src_ref=w.at[slot(bit, part)], dst_ref=w.at[slot(bit, part)],
            send_sem=send_sem.at[part, turn], recv_sem=land_sem.at[part, turn],
            device_id={"fsdp": pair_of(me, bit)}, device_id_type=pl.DeviceIdType.MESH,
        )

    for part in range(3):
        load(part).wait()
        hop(part, 0).start()
    for i in range(pieces):
        sent(i).start()

    def x_copy(half, i):
        return pltpu.make_async_copy(x.at[half, i], x_out.at[half, i], x_sem.at[half, i])

    def out_copy(part, half, i):
        return pltpu.make_async_copy(
            qkv.at[part, half, i], outs[part].at[half, i], out_sem.at[part, half, i]
        )

    def xt_copy(half, i):
        return pltpu.make_async_copy(xt.at[half, i], xt_out.at[half, i], xt_sem.at[half, i])

    def w_copy(part):
        return pltpu.make_async_copy(wt.at[part], wt_out.at[part], w_sem.at[part])

    def whole(part):
        first = part_start(width, part)
        spot = (slice(None),) * (bits + 1) + (slice(first, first + width),)
        return w[spot].reshape(width, width)

    def turn(half, i):
        x_copy(half, i).start()
        xt[half, i] = x[half, i].T
        xt_copy(half, i).start()

    def project(part, half, i):
        total = dot_f32(x[half, i], whole(part))
        if part == 0:
            total = total + small[0:1, :]
        if part == 2:
            total = total + small[1:2, :]
        qkv[part, half, i] = total.astype(jnp.bfloat16)
        out_copy(part, half, i).start()

    def over(body):
        def one(i, _):
            body(i)
            return 0

        lax.fori_loop(0, pieces, one, 0)

    def turn_weights(part):
        wt[part] = whole(part).T
        w_copy(part).start()

    def other(i):
        landed(i).wait_recv()
        turn(1 - side, i)
        project(0, 1 - side, i)
        project(1, 1 - side, i)

    own_tokens.wait()
    over(lambda i: turn(side, i))
    for step in range(bits + 2):
        full = None
        for part in range(3):
            hops = step - part
            if 0 <= hops < bits:
                hop(part, hops).wait_recv()
                if hops + 1 < bits:
                    hop(part, hops + 1).start()
                else:
                    full = part
        if full == 0:
            spot = (slice(None),) * (bits + 1) + (slice(width, width + 128),)
            turned = w[spot].reshape(width, 128).astype(jnp.float32).T
            small[...] = turned[: small.shape[0]]
            pltpu.make_async_copy(small, small_out, small_sem.at[0]).start()
        if full is not None:
            over(lambda i: project(full, side, i))
        if full == 1:
            turn_weights(0)
            turn_weights(1)
            over(other)
        if full == 2:
            over(lambda i: project(2, 1 - side, i))
            turn_weights(2)
    for i in range(pieces):
        sent(i).wait_send()
    for part in range(3):
        w_copy(part).wait()
        for hops in range(bits):
            hop(part, hops).wait_send()
    grad_rows.wait()
    pltpu.make_async_copy(small, small_out, small_sem.at[0]).wait()
    for half in range(2):
        for i in range(pieces):
            x_copy(half, i).wait()
            xt_copy(half, i).wait()
            for part in range(3):
                out_copy(part, half, i).wait()


def part_start(width, part):
    return part * width + (128 if part else 0)


def part_columns(width):
    return (
        slice(0, width + 128),
        slice(width + 128, 2 * width + 128),
        slice(2 * width + 128, 3 * width + 128),
    )


def qkv_forward(tokens_in, own_pack, out_grad):
    rows, local, width = tokens_in.shape
    own, columns = own_pack.shape
    bits = lax.axis_size("fsdp").bit_length() - 1
    pieces = 4
    piece = local // pieces
    dma = pltpu.SemaphoreType.DMA
    bf16 = jnp.bfloat16
    halves = (2, pieces, piece, width)
    gathered = (2,) * bits + (own, columns)
    anywhere = pl.BlockSpec(memory_space=pltpu.HBM)
    like = jax.ShapeDtypeStruct(halves, bf16)
    turned = (2, pieces, width, piece)
    grad, x, xt, q, k, v, weights_t, small = pl.pallas_call(
        functools.partial(qkv_forward_kernel, bits),
        out_shape=(
            jax.ShapeDtypeStruct((local, width), bf16),
            like, jax.ShapeDtypeStruct(turned, bf16), like, like, like,
            jax.ShapeDtypeStruct((3, width, width), bf16),
            jax.ShapeDtypeStruct((SMALL_ROWS, width), jnp.float32),
        ),
        in_specs=[anywhere] * 3,
        out_specs=(anywhere,) * 8,
        scratch_shapes=[
            pltpu.VMEM(halves, bf16),
            pltpu.VMEM(turned, bf16),
            pltpu.VMEM(gathered, bf16),
            pltpu.VMEM((3, width, width), bf16),
            pltpu.VMEM((3,) + halves, bf16),
            pltpu.VMEM((SMALL_ROWS, width), jnp.float32),
            dma((2,)), dma((pieces,)), dma((pieces,)), dma((3,)),
            dma((3, bits)), dma((3, bits)), dma((2, pieces)), dma((2, pieces)),
            dma((3, 2, pieces)), dma((3,)), dma((1,)),
        ],
        compiler_params=pltpu.CompilerParams(
            collective_id=2, has_side_effects=True, vmem_limit_bytes=62 << 20
        ),
        cost_estimate=pl.CostEstimate(
            flops=18 * rows * local * width * width, transcendentals=0,
            bytes_accessed=16 * rows * local * width,
        ),
        name="qkv_forward",
    )(tokens_in.reshape(halves), own_pack, out_grad)
    flat = rows * local, width
    return (
        x.reshape(flat), q.reshape(flat), k.reshape(flat), v.reshape(flat), xt, weights_t, small, grad
    )


eps_norm = 1e-06


def dot_rows(left, right):
    return lax.dot_general(
        left, right, (((0,), (0,)), ((), ())), preferred_element_type=jnp.float32
    )


def dot_nt(left, right):
    return lax.dot_general(
        left, right, (((1,), (1,)), ((), ())), preferred_element_type=jnp.float32
    )


def row_mean(values):
    return jnp.mean(values, axis=-1, keepdims=True)


GELU_K = math.sqrt(2.0 / math.pi)
GELU_A = 0.044715


def gelu_pair(u):
    square = u * u
    t = jnp.tanh(u * (GELU_K + (GELU_K * GELU_A) * square))
    half = 0.5 + 0.5 * t
    slope = half + (u * (half * (1.0 - t))) * (GELU_K + (3.0 * GELU_K * GELU_A) * square)
    return u * half, slope


OUT_B, GAIN_1, BIAS_1, OUTER_B, GAIN_2, BIAS_2, INNER_B = 2, 3, 4, 5, 6, 7, 8
SMALL_ROWS = 16


def eights(values):
    return jnp.sum(values.reshape(-1, 8, values.shape[-1]), axis=0)


def middle_forward_kernel(
    chunks, side, weights_in, small, att, tokens, grad_own, grad_other,
    out_keep, out_send, d_mlp, normed, z_one, rs_one, slope, d_weights, sums,
    w, acc, act, flow, part, load_sem, store_sem,
):
    step, steps = pl.program_id(0), pl.num_programs(0)
    rows, width = att.shape
    f32, bf16 = jnp.float32, jnp.bfloat16
    count = 2 * chunks + 1
    staying = step // (steps // 2) == side[0]

    def load(i):
        return pltpu.make_async_copy(
            weights_in.at[:, pl.ds(i * width, width)], w.at[i], load_sem.at[i]
        )

    def store(c):
        return pltpu.make_async_copy(
            w.at[1 + chunks + c], d_weights.at[:, pl.ds(c * width, width)], store_sem.at[c]
        )

    @pl.when(step == 0)
    def _():
        for i in range(count):
            load(i).start()
        part[...] = jnp.zeros_like(part)

        def clear(i, _):
            acc[i] = jnp.zeros_like(acc[i])
            return 0

        lax.fori_loop(0, chunks, clear, 0)
        load(0).wait()

    def vector(i):
        return small[i : i + 1, :]

    def add_sum(i, values):
        part[i] += eights(values)

    attn = dot_f32(att[...], w[0]) + vector(OUT_B)
    resid = tokens[...].astype(f32) + attn
    add_sum(INNER_B + chunks, resid * resid)
    add_sum(INNER_B + chunks + 1, attn * attn)
    centred = resid - row_mean(resid)
    scale = lax.rsqrt(row_mean(centred * centred) + eps_norm)
    z = centred * scale
    rs_one[...] = scale
    z_one[...] = z.astype(bf16)
    full = z * vector(GAIN_1) + vector(BIAS_1)
    flow[...] = full
    normed[...] = full.astype(bf16)

    def inner(c, _):
        @pl.when(step == 0)
        def _():
            load(1 + c).wait()

        for n in range(width // 256):
            cols = slice(n * 256, n * 256 + 256)
            pre = dot_f32(normed[...], w[1 + c, :, cols]) + small[pl.ds(INNER_B + c, 1), cols]
            value, grade = gelu_pair(pre)
            act[c, :, cols] = value.astype(bf16)
            slope[c, :, cols] = grade.astype(bf16)
        return 0

    lax.fori_loop(0, chunks, inner, 0)

    @pl.when(step == 0)
    def _():
        for i in range(1 + chunks, count):
            load(i).wait()

    mlp = dot_f32(act[0], w[1 + chunks])
    for c in range(1, chunks):
        mlp = mlp + dot_f32(act[c], w[1 + chunks + c])
    mlp = mlp + vector(OUTER_B)
    add_sum(INNER_B + chunks + 2, mlp * mlp)
    resid = flow[...] + mlp
    centred = resid - row_mean(resid)
    scale = lax.rsqrt(row_mean(centred * centred) + eps_norm)
    z = centred * scale
    result = (z * vector(GAIN_2) + vector(BIAS_2)).astype(bf16)

    @pl.when(staying)
    def _():
        out_keep[...] = result

    @pl.when(jnp.logical_not(staying))
    def _():
        out_send[...] = result

    grad = jnp.where(staying, grad_own[...], grad_other[...]).astype(f32)
    add_sum(GAIN_2, grad * z)
    add_sum(BIAS_2, grad)
    grad = grad * vector(GAIN_2)
    low = (scale * (grad - row_mean(grad) - z * row_mean(grad * z))).astype(bf16)
    add_sum(OUTER_B, low.astype(f32))
    d_mlp[...] = low

    def back(c, _):
        acc[c] += dot_rows(act[c], d_mlp[...])

        @pl.when(step == steps - 1)
        def _():
            w[1 + chunks + c] = acc[c].astype(bf16)
            store(c).start()

        return 0

    lax.fori_loop(0, chunks, back, 0)

    @pl.when(step == steps - 1)
    def _():
        sums[...] = jnp.sum(part[...], axis=1)
        for c in range(chunks):
            store(c).wait()


def middle_backward_kernel(
    chunks, weights_in, small, sums_in, att, d_mlp, normed, z_one, rs_one, slope,
    d_attn, d_att, d_weights, sums,
    w, acc, d_pre, flow, part, load_sem, store_sem,
):
    step, steps = pl.program_id(0), pl.num_programs(0)
    rows, width = att.shape
    f32, bf16 = jnp.float32, jnp.bfloat16
    count = 2 * chunks + 1

    def load(i):
        return pltpu.make_async_copy(
            weights_in.at[:, pl.ds(i * width, width)], w.at[i], load_sem.at[i]
        )

    def store(i):
        return pltpu.make_async_copy(
            w.at[i], d_weights.at[:, pl.ds(i * width, width)], store_sem.at[i]
        )

    @pl.when(step == 0)
    def _():
        for c in range(chunks):
            load(1 + chunks + c).start()
            load(1 + c).start()
        load(0).start()
        part[...] = jnp.zeros_like(part)

        def clear(i, _):
            acc[i] = jnp.zeros_like(acc[i])
            return 0

        lax.fori_loop(0, chunks + 1, clear, 0)

    def vector(i):
        return small[i : i + 1, :]

    def add_sum(i, values):
        part[i] += eights(values)

    turned = normed[...].T
    flow[...] = d_mlp[...].astype(f32)

    def back(c, _):
        @pl.when(step == 0)
        def _():
            load(1 + chunks + c).wait()
            load(1 + c).wait()

        for n in range(width // 256):
            cols = slice(n * 256, n * 256 + 256)
            d_act = dot_nt(d_mlp[...], w[1 + chunks + c, cols, :])
            low = (slope[c, :, cols].astype(f32) * d_act).astype(bf16)
            part[INNER_B + c, :, cols] += eights(low.astype(f32))
            d_pre[:, cols] = low
        acc[1 + c] += dot_f32(turned, d_pre[...])
        flow[...] += dot_nt(d_pre[...], w[1 + c])

        @pl.when(step == steps - 1)
        def _():
            w[1 + c] = acc[1 + c].astype(bf16)
            store(1 + c).start()

        return 0

    lax.fori_loop(0, chunks, back, 0)

    @pl.when(step == 0)
    def _():
        load(0).wait()

    grad = flow[...]
    z = z_one[...].astype(f32)
    add_sum(GAIN_1, grad * z)
    add_sum(BIAS_1, grad)
    grad = grad * vector(GAIN_1)
    low = (rs_one[...] * (grad - row_mean(grad) - z * row_mean(grad * z))).astype(bf16)
    add_sum(OUT_B, low.astype(f32))
    d_attn[...] = low
    acc[0] += dot_rows(att[...], d_attn[...])
    d_att[...] = dot_nt(d_attn[...], w[0]).astype(bf16)

    @pl.when(step == steps - 1)
    def _():
        w[0] = acc[0].astype(bf16)
        store(0).start()
        sums[...] = sums_in[...] + jnp.sum(part[...], axis=1)
        for i in range(chunks + 1):
            store(i).wait()


def middle_parts(weights, small, tok_count, width):
    chunks = (weights.shape[1] // width - 1) // 2
    rows = 512
    return chunks, rows, tok_count // rows


def middle_forward(side, weights, small, att, tokens, grad_own, grad_other):
    tok_count, width = att.shape
    chunks, rows, steps = middle_parts(weights, small, tok_count, width)
    count = 2 * chunks + 1
    f32, bf16 = jnp.float32, jnp.bfloat16
    half = steps // 2

    def early(i):
        return jnp.minimum(i, half - 1)

    def late(i):
        return jnp.maximum(i - half, 0)

    tile = pl.BlockSpec((rows, width), lambda i, s: (i, 0))
    thin = pl.BlockSpec((rows, 1), lambda i, s: (i, 0))
    deep = pl.BlockSpec((chunks, rows, width), lambda i, s: (0, i, 0))
    keep = pl.BlockSpec((rows, width), lambda i, s: (jnp.where(s[0] == 0, early(i), late(i)), 0))
    send = pl.BlockSpec((rows, width), lambda i, s: (jnp.where(s[0] == 0, late(i), early(i)), 0))
    own = pl.BlockSpec(
        (None, rows, width), lambda i, s: (s[0], jnp.where(s[0] == 0, early(i), late(i)), 0)
    )
    fixed = pl.BlockSpec(small.shape, lambda i, s: (0, 0), pipeline_mode=pl.Buffered(1))
    anywhere = pl.BlockSpec(memory_space=pl.ANY)
    like = jax.ShapeDtypeStruct((tok_count, width), bf16)
    part = jax.ShapeDtypeStruct((tok_count // 2, width), bf16)
    return pl.pallas_call(
        functools.partial(middle_forward_kernel, chunks),
        out_shape=(
            part, part, like, like, like,
            jax.ShapeDtypeStruct((tok_count, 1), f32),
            jax.ShapeDtypeStruct((chunks, tok_count, width), bf16),
            jax.ShapeDtypeStruct((width, chunks * width), bf16),
            jax.ShapeDtypeStruct(small.shape, f32),
        ),
        grid_spec=pltpu.PrefetchScalarGridSpec(
            num_scalar_prefetch=1,
            grid=(steps,),
            in_specs=[anywhere, fixed, tile, tile, own, send],
            out_specs=(keep, send, tile, tile, tile, thin, deep, anywhere, fixed),
            scratch_shapes=[
                pltpu.VMEM((count, width, width), bf16),
                pltpu.VMEM((chunks, width, width), f32),
                pltpu.VMEM((chunks, rows, width), bf16),
                pltpu.VMEM((rows, width), f32),
                pltpu.VMEM((small.shape[0], 8, width), f32),
                pltpu.SemaphoreType.DMA((count,)),
                pltpu.SemaphoreType.DMA((chunks,)),
            ],
        ),
        compiler_params=pltpu.CompilerParams(vmem_limit_bytes=62 << 20),
        cost_estimate=pl.CostEstimate(
            flops=12 * tok_count * width * width * (count + 1) // 2,
            transcendentals=tok_count * width * chunks,
            bytes_accessed=30 * tok_count * width + 4 * weights.size,
        ),
        name="middle_forward",
    )(side.reshape(1), weights, small, att, tokens, grad_own, grad_other)


def middle_backward(weights, small, sums, att, d_mlp, normed, z_one, rs_one, slope):
    tok_count, width = att.shape
    chunks, rows, steps = middle_parts(weights, small, tok_count, width)
    count = 2 * chunks + 1
    f32, bf16 = jnp.float32, jnp.bfloat16
    tile = pl.BlockSpec((rows, width), lambda i: (i, 0))
    thin = pl.BlockSpec((rows, 1), lambda i: (i, 0))
    deep = pl.BlockSpec((chunks, rows, width), lambda i: (0, i, 0))
    fixed = pl.BlockSpec(small.shape, lambda i: (0, 0), pipeline_mode=pl.Buffered(1))
    anywhere = pl.BlockSpec(memory_space=pl.ANY)
    like = jax.ShapeDtypeStruct((tok_count, width), bf16)
    return pl.pallas_call(
        functools.partial(middle_backward_kernel, chunks),
        grid=(steps,),
        out_shape=(
            like, like,
            jax.ShapeDtypeStruct((width, (chunks + 1) * width), bf16),
            jax.ShapeDtypeStruct(small.shape, f32),
        ),
        in_specs=[anywhere, fixed, fixed, tile, tile, tile, tile, thin, deep],
        out_specs=(tile, tile, anywhere, fixed),
        scratch_shapes=[
            pltpu.VMEM((count, width, width), bf16),
            pltpu.VMEM((chunks + 1, width, width), f32),
            pltpu.VMEM((rows, width), bf16),
            pltpu.VMEM((rows, width), f32),
            pltpu.VMEM((small.shape[0], 8, width), f32),
            pltpu.SemaphoreType.DMA((count,)),
            pltpu.SemaphoreType.DMA((chunks + 1,)),
        ],
        compiler_params=pltpu.CompilerParams(vmem_limit_bytes=62 << 20),
        cost_estimate=pl.CostEstimate(
            flops=12 * tok_count * width * width * (count + 1) // 2, transcendentals=0,
            bytes_accessed=30 * tok_count * width + 4 * weights.size,
        ),
        name="middle_backward",
    )(weights, small, sums, att, d_mlp, normed, z_one, rs_one, slope)


def contract_rows(left, right):
    return lax.dot_general(
        left, right, (((0,), (0,)), ((), ())), preferred_element_type=jnp.float32
    )


def times_transpose(left, right):
    return lax.dot_general(
        left, right, (((1,), (1,)), ((), ())), preferred_element_type=jnp.float32
    )


def butterfly_sum(values, axis):
    size = lax.axis_size(axis)
    if size & (size - 1):
        return lax.psum(values, axis)
    step = 1
    while step < size:
        pairs = [(i, i ^ step) for i in range(size)]
        values = values + lax.ppermute(values, axis, pairs)
        step *= 2
    return values


def sum_seq(values):
    if lax.axis_size("seq") == 2:
        other = lax.ppermute(values, "seq", [(0, 1), (1, 0)])
        return values.astype(jnp.float32) + other.astype(jnp.float32)
    return lax.psum(values, "seq").astype(jnp.float32)


class Regroup:
    def __init__(self, row_count):
        self.size = lax.axis_size("seq")
        self.ways = math.gcd(row_count, self.size)
        self.parts = self.size // self.ways
        self.rows = row_count // self.ways
        me = lax.axis_index("seq")
        self.place = lax.rem(me, self.ways)
        self.row_group = me // self.parts

    def targets(self, turn):
        ways, parts = self.ways, self.parts
        return [
            (s, ((s % ways + turn) % ways) * parts + s // ways) for s in range(self.size)
        ]

    def move(self, values, pairs):
        if all(a == b for a, b in pairs):
            return values
        return lax.ppermute(values, "seq", pairs)

    def gather(self, values):
        rows, local, width = self.rows, values.shape[1], values.shape[2]
        out = jnp.zeros((rows, self.ways, local, width), values.dtype)
        for turn in range(self.ways):
            pick = lax.rem(self.place + turn, self.ways)
            chunk = lax.dynamic_slice_in_dim(values, pick * rows, rows, 0)
            chunk = self.move(chunk, self.targets(turn))
            spot = lax.rem(self.row_group - turn + self.ways, self.ways)
            out = lax.dynamic_update_slice_in_dim(out, chunk[:, None], spot, 1)
        return out.reshape(rows, self.ways * local, width)

    def scatter(self, values):
        rows, width = self.rows, values.shape[2]
        local = values.shape[1] // self.ways
        values = values.reshape(rows, self.ways, local, width)
        out = jnp.zeros((rows * self.ways, local, width), values.dtype)
        for turn in range(self.ways):
            spot = lax.rem(self.row_group - turn + self.ways, self.ways)
            chunk = lax.dynamic_slice_in_dim(values, spot, 1, 1)[:, 0]
            chunk = self.move(chunk, [(b, a) for a, b in self.targets(turn)])
            pick = lax.rem(self.place + turn, self.ways)
            out = lax.dynamic_update_slice_in_dim(out, chunk, pick * rows, 0)
        return out

    def pick_rows(self, values):
        return lax.dynamic_slice_in_dim(values, self.row_group * self.rows, self.rows, 0)

    def groups(self):
        return [
            [r * self.parts + j for j in range(self.parts)] for r in range(self.ways)
        ]

    def to_heads(self, values):
        if self.parts == 1:
            return values
        return lax.all_to_all(
            values, "seq", split_axis=2, concat_axis=1, tiled=True,
            axis_index_groups=self.groups(),
        )

    def from_heads(self, values):
        if self.parts == 1:
            return values
        return lax.all_to_all(
            values, "seq", split_axis=1, concat_axis=2, tiled=True,
            axis_index_groups=self.groups(),
        )


def shards(
    tokens_in,
    segment_ids,
    random_blocks,
    global_blocks,
    w_query,
    b_query,
    w_key,
    w_value,
    b_value,
    w_attn_out,
    b_attn_out,
    ln1_gain,
    ln1_bias,
    w_inner,
    b_inner,
    w_outer,
    b_outer,
    ln2_gain,
    ln2_bias,
    out_grad,
):
    row_count, local_len, width = tokens_in.shape
    seq_count = lax.axis_size("seq")
    fsdp_count = lax.axis_size("fsdp")
    tok_count = row_count * local_len
    own = w_query.shape[0]
    chunks = b_inner.shape[0] // own
    regroup = Regroup(row_count)
    paired = row_count == 2 and seq_count == 2 and fsdp_count in (4, 8, 16, 32)

    vectors = [b_query, b_value, b_attn_out, ln1_gain, ln1_bias, b_outer, ln2_gain, ln2_bias]
    columns = [x[:, None] for x in vectors] + [b_inner.reshape(own, chunks)]
    used = len(vectors) + chunks
    columns.append(jnp.zeros((own, 128 - used), jnp.bfloat16))
    first = jnp.concatenate([w_query] + columns + [w_key, w_value], axis=1)
    inner_own = w_inner.reshape(own, width, chunks).transpose(0, 2, 1).reshape(own, -1)
    second = jnp.concatenate([w_attn_out, inner_own, w_outer.reshape(own, -1)], axis=1)
    second = lax.all_gather(second, "fsdp", axis=0, tiled=True)
    plan = plan_blocks(
        regroup.pick_rows(segment_ids),
        regroup.pick_rows(random_blocks),
        regroup.pick_rows(global_blocks),
    )

    def split_rows(values):
        return values.reshape(regroup.rows, tok_count // regroup.rows, width)

    def part_of(values, i):
        return values[:, part_start(width, i) : part_start(width, i) + width]

    side = lax.axis_index("seq") if paired else jnp.int32(0)
    swap = [(0, 1), (1, 0)]
    if paired:
        flat_in, *qkv, turned_in, turned_w, small, leaving = qkv_forward(
            tokens_in, first, out_grad
        )
        grad_other = lax.ppermute(leaving, "seq", swap)
        grad_own = out_grad
    else:
        first = lax.all_gather(first, "fsdp", axis=0, tiled=True)
        small = first[:, width : width + SMALL_ROWS].astype(jnp.float32).T
        flat_in = regroup.gather(tokens_in).reshape(tok_count, width)
        biases = (small[0], jnp.zeros_like(small[0]), small[1])
        qkv = [
            (jnp.dot(flat_in, part_of(first, i), preferred_element_type=jnp.float32)
             + biases[i]).astype(jnp.bfloat16)
            for i in range(3)
        ]
        flat_grad = regroup.gather(out_grad).reshape(tok_count, width)
        grad_own = flat_grad.reshape(2, tok_count // 2, width)
        grad_other = grad_own[1]
    q, k, v = (regroup.to_heads(split_rows(x)) for x in qkv)
    att, lse = attention_forward(q, k, v, plan)
    att_flat = regroup.from_heads(att).reshape(tok_count, width)
    kept, sent, *saved, d_outer, sums = middle_forward(
        side, second, small, att_flat, flat_in, grad_own, grad_other
    )
    if paired:
        sent = lax.ppermute(sent, "seq", swap)
    d_attn, d_att, d_second, sums = middle_backward(second, small, sums, att_flat, *saved)

    def scattered(values):
        return lax.psum_scatter(values, "fsdp", scatter_dimension=0, tiled=True)

    d_outer = scattered(d_outer)
    d_second = scattered(d_second)
    dq, dk, dv = attention_backward(
        q, k, v, att, regroup.to_heads(split_rows(d_att)), lse, plan
    )
    dq, dk, dv = (regroup.from_heads(x).reshape(tok_count, width) for x in (dq, dk, dv))
    mine = lax.axis_index("fsdp")
    dq, sent, d_outer = lax.optimization_barrier((dq, sent, d_outer))
    d_outer = sum_seq(d_outer)
    if paired:
        d_query_w, d_key_w, d_value_w, sums, d_tokens_in = qkv_backward(
            turned_in, dq, dk, dv, turned_w, d_attn, sums, own
        )
        d_second, sums = lax.optimization_barrier((d_second, sums))
        place = jnp.arange(2, dtype=jnp.int32)[:, None, None]
        out_tokens = jnp.where(place == side, kept[None], sent[None])
        d_tokens_in = jnp.where(place >= -side, d_tokens_in, jnp.zeros_like(d_tokens_in))
    else:
        for spot, part in ((0, dq), (1, dv)):
            sums = sums.at[spot].set(jnp.sum(part.astype(jnp.float32), axis=0))
        sums = butterfly_sum(butterfly_sum(sums, "fsdp"), "seq")
        d_query_w, d_key_w, d_value_w = (
            sum_seq(scattered(contract_rows(flat_in, x).astype(jnp.bfloat16)))
            for x in (dq, dk, dv)
        )
        d_tokens = d_attn.astype(jnp.float32)
        for i, part in enumerate((dq, dk, dv)):
            d_tokens = d_tokens + times_transpose(part, part_of(first, i))
        d_tokens_in = regroup.scatter(split_rows(d_tokens.astype(jnp.bfloat16)))
        out_tokens = regroup.scatter(split_rows(jnp.concatenate([kept, sent])))
    d_second = sum_seq(d_second)
    d_inner_w = (
        d_second[:, width:]
        .reshape(own, chunks, width)
        .transpose(0, 2, 1)
        .reshape(own, -1)
    )
    d_outer_w = d_outer.reshape(own * chunks, width)
    d_vec = lax.dynamic_slice_in_dim(sums, mine * own, own, 1)
    entry_total = tok_count * width * seq_count * fsdp_count
    rms_values = jnp.sqrt(
        jnp.sum(sums[INNER_B + chunks : INNER_B + chunks + 3], axis=1) / entry_total
    )
    return (
        out_tokens,
        d_tokens_in,
        d_query_w,
        d_vec[0],
        d_key_w,
        d_value_w,
        d_vec[1],
        d_second[:, :width],
        d_vec[OUT_B],
        d_vec[GAIN_1],
        d_vec[BIAS_1],
        d_inner_w,
        d_vec[INNER_B : INNER_B + chunks].T.reshape(-1),
        d_outer_w,
        d_vec[OUTER_B],
        d_vec[GAIN_2],
        d_vec[BIAS_2],
        rms_values,
    )


def solution(mesh):
    in_specs = (
        P("fsdp", "seq", None),
        P("fsdp", None),
        P("fsdp", None, None),
        P("fsdp", None),
        P("fsdp", None),
        P("fsdp"),
        P("fsdp", None),
        P("fsdp", None),
        P("fsdp"),
        P("fsdp", None),
        P("fsdp"),
        P("fsdp"),
        P("fsdp"),
        P("fsdp", None),
        P("fsdp"),
        P("fsdp", None),
        P("fsdp"),
        P("fsdp"),
        P("fsdp"),
        P("fsdp", "seq", None),
    )
    out_specs = (
        P("fsdp", "seq", None),
        P("fsdp", "seq", None),
        P("fsdp", None),
        P("fsdp"),
        P("fsdp", None),
        P("fsdp", None),
        P("fsdp"),
        P("fsdp", None),
        P("fsdp"),
        P("fsdp"),
        P("fsdp"),
        P("fsdp", None),
        P("fsdp"),
        P("fsdp", None),
        P("fsdp"),
        P("fsdp"),
        P("fsdp"),
        P(),
    )
    return jax.shard_map(shards, mesh=mesh, in_specs=in_specs, out_specs=out_specs, check_vma=False)
```

```python
import functools
import math

import jax
import jax.numpy as jnp
from jax import lax
from jax.experimental import pallas as pl
from jax.experimental.pallas import tpu as pltpu
from jax.sharding import PartitionSpec as P

HD = 64
BLK = 64
CHUNK = 4
ITEMS = 3
NEG = -1e30


def plan_blocks(seg, rand, glob):
    rows, full_len = seg.shape
    nb = full_len // BLK
    ids = jnp.arange(nb, dtype=jnp.int32)
    is_global = jnp.any(ids[None, :, None] == glob[:, None, :], axis=-1)
    picked = jnp.any(rand[:, :, None, :] == ids[None, None, :, None], axis=-1)
    nearby = jnp.abs(ids[:, None] - ids[None, :]) <= 1
    admitted = nearby[None] | picked | is_global[:, :, None] | is_global[:, None, :]
    by_block = seg.reshape(rows, nb, BLK)
    low, high = by_block[:, :, 0], by_block[:, :, BLK - 1]
    meets = (low[:, :, None] <= high[:, None, :]) & (low[:, None, :] <= high[:, :, None])
    active = (admitted & meets).astype(jnp.int32)
    upto = (ids[:, None] <= ids[None, :]).astype(jnp.int32)
    place = jnp.sum(active[:, :, :, None] * upto[None, None], axis=2) - 1
    count = jnp.sum(active, axis=2)
    hit = (place[:, :, :, None] == ids[None, None, None, :]) & (active[:, :, :, None] > 0)
    listed = jnp.sum(jnp.where(hit, ids[None, None, :, None], 0), axis=2)
    listed = jnp.where(ids[None, None, :] < count[:, :, None], listed, nb)
    chunks = (count + (CHUNK - 1)) // CHUNK
    seg_cols = jnp.concatenate([seg, jnp.full((rows, BLK), -1, jnp.int32)], axis=1)
    seg_cols = jnp.broadcast_to(seg_cols[:, :, None], (rows, full_len + BLK, 128))
    seg_rows = jnp.concatenate([by_block, by_block], axis=2)[:, :, None, :]
    return chunks, listed.reshape(rows, nb * nb), jnp.sum(chunks, axis=1), seg_cols, seg_rows


def lane_low(rows):
    return lax.broadcasted_iota(jnp.int32, (rows, 128), 1) < HD


def diag128(dup_t):
    row = lax.broadcasted_iota(jnp.int32, (128, 128), 0) < HD
    col = lax.broadcasted_iota(jnp.int32, (128, 128), 1) < HD
    return jnp.where(row == col, dup_t, jnp.zeros_like(dup_t))


def transposed_twice(tile):
    both = jnp.concatenate([tile, tile], axis=0)
    return both.T


def head_rows(acc):
    turned = jnp.concatenate([acc, acc], axis=0).T
    return jnp.where(lane_low(HD), turned[:HD], turned[HD:])


def pick_diag(full, half):
    lanes = slice(half * 128, half * 128 + 128)
    top = full[half * 128 : half * 128 + HD, lanes]
    low = full[half * 128 + HD : half * 128 + 128, lanes]
    return jnp.where(lane_low(HD), top, low)


def chunk_ids(list_ref, row, base, nb, real):
    base = jnp.minimum(base, nb * nb - CHUNK)
    ids = [jnp.where(real, list_ref[row, base + j], nb) for j in range(CHUNK)]
    safe = [jnp.where(b == nb, 0, b) for b in ids]
    return ids, safe


def block_rows(ref, blocks, lanes):
    return jnp.concatenate(
        [ref[0, pl.ds(pl.multiple_of(b * BLK, BLK), BLK), lanes] for b in blocks], axis=0
    )


def turned_blocks(ref, blocks, rows):
    low = lane_low(rows.stop - rows.start)
    tiles = [ref[b, rows, :] for b in blocks]
    return jnp.concatenate(
        [jnp.where(low, tiles[i], tiles[i + 1]) for i in range(0, CHUNK, 2)], axis=1
    )


def turn_all(src_ref, dst_ref, nb, width):
    def body(b, _):
        start = pl.multiple_of(b * BLK, BLK)
        for t in range(width // 128):
            tile = src_ref[0, pl.ds(start, BLK), t * 128 : t * 128 + 128]
            dst_ref[b, t * 128 : t * 128 + 128, :] = transposed_twice(tile)
        return 0

    lax.fori_loop(0, nb, body, 0, unroll=4)


def dot_f32(left, right):
    return lax.dot_general(
        left, right, (((1,), (0,)), ((), ())), preferred_element_type=jnp.float32
    )


def fetch(row, pairs, sem):
    loads = [
        pltpu.make_async_copy(src.at[pl.ds(row, 1)], dst, sem.at[i])
        for i, (src, dst) in enumerate(pairs)
    ]
    for load in loads:
        load.start()
    return loads


def next_item(n_ref, row, nb, a, c):
    more = c + 1 < n_ref[row, a]
    following = jnp.where(more, a, jnp.minimum(a + 1, nb - 1))
    return following, jnp.where(more, c + 1, 0)


def run_items(n_ref, total_ref, row, nb, ready, item, finish):
    total = total_ref[row]

    def walk(a, c):
        places = [(a, c)]
        for _ in range(2 * ITEMS - 1):
            places.append(next_item(n_ref, row, nb, *places[-1]))
        return places

    def turn(i, carry):
        before, a, c = carry
        base = lax.rem(i, 2) * ITEMS
        for past in before:
            finish(past)
        places = walk(a, c)
        for k in range(ITEMS):
            ready(places[ITEMS + k][0], ITEMS - base + k)
        here = [places[0]]
        item(base, *here[0], True)
        for k in range(1, ITEMS):
            real = ITEMS * i + k < total
            here.append(
                (
                    jnp.where(real, places[k][0], here[-1][0]),
                    jnp.where(real, places[k][1], here[-1][1] + 1),
                )
            )
            item(base + k, *here[k], real)
        return (tuple(place[0] for place in here), *places[ITEMS])

    for k, place in enumerate(walk(0, 0)[:ITEMS]):
        ready(place[0], k)
    before, _, _ = lax.fori_loop(
        0, (total + ITEMS - 1) // ITEMS, turn, ((0,) * ITEMS, 0, 0)
    )
    for past in before:
        finish(past)


def forward_kernel(group, n_ref, list_ref, total_ref, q_in, k_in, v_in, segc_ref, segr_ref,
                   o_ref, lse_ref, q_ref, k_ref, v_ref, vt_ref, qst_ref, m_ref, l_ref, acc_ref,
                   sem):
    row = pl.program_id(0)
    width = q_ref.shape[2]
    nb = q_ref.shape[1] // BLK
    groups, halves = width // group, group // 128
    tiles = width // 128
    loads = fetch(row, ((v_in, v_ref), (q_in, q_ref), (k_in, k_ref)), sem)
    qst_ref[...] = jnp.zeros_like(qst_ref)
    l_ref[...] = jnp.ones_like(l_ref)
    acc_ref[...] = jnp.zeros_like(acc_ref)
    m_ref[...] = jnp.zeros_like(m_ref)
    loads[0].wait()
    turn_all(v_ref, vt_ref, nb, width)
    for load in loads[1:]:
        load.wait()

    def ready(a, slot):
        start = pl.multiple_of(a * BLK, BLK)
        for t in range(tiles):
            tile = q_ref[0, pl.ds(start, BLK), t * 128 : t * 128 + 128] * 0.125
            square = slice(t % halves * 128, t % halves * 128 + 128)
            qst_ref[slot, t // halves, square, square] = diag128(
                transposed_twice(tile.astype(jnp.bfloat16))
            )

    def finish(a):
        even = lax.rem(a, ITEMS)
        start = pl.multiple_of(a * BLK, BLK)
        for t in range(tiles):
            lanes = slice(t * 128, t * 128 + 128)
            total = l_ref[even, t]
            o_ref[0, pl.ds(start, BLK), lanes] = head_rows(acc_ref[even, t] / total).astype(
                jnp.bfloat16
            )
            lse_ref[0, a, :, lanes] = m_ref[even, t] + jnp.log(total)

    def item(slot, a, c, real):
        ids, safe = chunk_ids(list_ref, row, a * nb + c * CHUNK, nb, real)
        even = lax.rem(a, ITEMS)
        allowed = block_rows(segc_ref, ids, slice(0, 128)) == segr_ref[0, a]
        first = c == 0
        for g in range(groups):
            lanes = slice(g * group, g * group + group)
            s_t = dot_f32(block_rows(k_ref, safe, lanes), qst_ref[slot, g])
            weights, alphas = [], []
            for u in range(halves):
                t = g * halves + u
                s = jnp.where(allowed, s_t[:, u * 128 : u * 128 + 128], NEG)
                m_old = jnp.where(first, NEG, m_ref[even, t])
                m_new = jnp.maximum(m_old, jnp.max(s, axis=0, keepdims=True))
                p = jnp.exp(s - m_new)
                alpha = jnp.exp(m_old - m_new)
                l_ref[even, t] = alpha * l_ref[even, t] + jnp.sum(p, axis=0, keepdims=True)
                m_ref[even, t] = m_new
                weights.append(p.astype(jnp.bfloat16))
                alphas.append(alpha)
            p_t = jnp.concatenate(weights, axis=1) if halves > 1 else weights[0]
            o_t = dot_f32(turned_blocks(vt_ref, safe, lanes), p_t)
            for u in range(halves):
                t = g * halves + u
                acc_ref[even, t] = alphas[u] * acc_ref[even, t] + pick_diag(o_t, u)

    run_items(n_ref, total_ref, row, nb, ready, item, finish)


def group_of(width):
    return 256 if width % 256 == 0 else 128


def whole_spec(shape):
    rest = (0,) * (len(shape) - 1)
    return pl.BlockSpec((1,) + tuple(shape[1:]), lambda r, *_: (r,) + rest)


def one_spec(shape):
    rest = (0,) * (len(shape) - 1)
    return pl.BlockSpec((1,) + tuple(shape[1:]), lambda r, *_: (r,) + rest,
                        pipeline_mode=pl.Buffered(1))


def attention_forward(q, k, v, plan):
    *tables, seg_cols, seg_rows = plan
    rows, full_len, width = q.shape
    nb, group = full_len // BLK, group_of(width)
    tiles = width // 128
    pairs = rows * full_len * full_len // 4 * width
    args = (q, k, v, seg_cols, seg_rows)
    anywhere = pl.BlockSpec(memory_space=pl.ANY)
    stretch = pltpu.VMEM((1, full_len, width), jnp.bfloat16)
    return pl.pallas_call(
        functools.partial(forward_kernel, group),
        out_shape=(
            jax.ShapeDtypeStruct((rows, full_len, width), jnp.bfloat16),
            jax.ShapeDtypeStruct((rows, nb, 1, width), jnp.float32),
        ),
        grid_spec=pltpu.PrefetchScalarGridSpec(
            num_scalar_prefetch=3,
            grid=(rows,),
            in_specs=[anywhere] * 3 + [one_spec(x.shape) for x in args[3:]],
            out_specs=(one_spec((rows, full_len, width)), one_spec((rows, nb, 1, width))),
            scratch_shapes=[
                stretch, stretch, stretch,
                pltpu.VMEM((nb, width, 128), jnp.bfloat16),
                pltpu.VMEM((2 * ITEMS, width // group, group, group), jnp.bfloat16),
                pltpu.VMEM((ITEMS, tiles, 1, 128), jnp.float32),
                pltpu.VMEM((ITEMS, tiles, 1, 128), jnp.float32),
                pltpu.VMEM((ITEMS, tiles, HD, 128), jnp.float32),
                pltpu.SemaphoreType.DMA((3,)),
            ],
        ),
        compiler_params=pltpu.CompilerParams(vmem_limit_bytes=62 << 20),
        cost_estimate=pl.CostEstimate(
            flops=4 * pairs, transcendentals=pairs // HD, bytes_accessed=8 * q.size
        ),
        name="attention_forward",
    )(*tables, *args)


def backward_kernel(group, n_ref, list_ref, total_ref, q_in, k_in, v_in, o_in, do_in,
                    lse_ref, segc_ref, segr_ref, dq_out, dk_out, dv_out,
                    q_ref, k_ref, v_ref, o_ref, do_ref, dq_ref, kt_ref, qst_ref, qs_ref, dost_ref, dos_ref, delta_ref, acc_ref,
                    dk_acc, dv_acc, sem, out_sem):
    row = pl.program_id(0)
    full_len, width = q_ref.shape[1], q_ref.shape[2]
    nb = full_len // BLK
    groups, halves = width // group, group // 128
    tiles = width // 128
    loads = fetch(
        row,
        ((k_in, k_ref), (q_in, q_ref), (do_in, do_ref), (o_in, o_ref), (v_in, v_ref)),
        sem,
    )
    for ref in (qst_ref, qs_ref, dost_ref, dos_ref, acc_ref):
        ref[...] = jnp.zeros_like(ref)
    loads[0].wait()
    turn_all(k_ref, kt_ref, nb, width)
    for ref in (dk_acc, dv_acc):
        ref[...] = jnp.zeros_like(ref)
    for load in loads[1:]:
        load.wait()
    low = lane_low(1)

    def ready(a, slot):
        start = pl.multiple_of(a * BLK, BLK)
        for t in range(tiles):
            g, u = t // halves, t % halves
            lanes = slice(t * 128, t * 128 + 128)
            square = slice(u * 128, u * 128 + 128)
            q_tile = (q_ref[0, pl.ds(start, BLK), lanes] * 0.125).astype(jnp.bfloat16)
            g_tile = do_ref[0, pl.ds(start, BLK), lanes]
            o_tile = o_ref[0, pl.ds(start, BLK), lanes]
            g_turn = transposed_twice(g_tile)
            qst_ref[slot, g, square, square] = diag128(transposed_twice(q_tile))
            dost_ref[slot, g, square, square] = diag128(g_turn)
            qs_ref[slot, g, square, square] = diag128(jnp.concatenate([q_tile, q_tile], axis=0))
            dos_ref[slot, g, square, square] = diag128(
                jnp.concatenate([g_tile, g_tile], axis=0)
            )
            product = g_turn.astype(jnp.float32) * transposed_twice(o_tile).astype(jnp.float32)
            delta_ref[slot, t] = jnp.where(
                low,
                jnp.sum(product[:HD], axis=0, keepdims=True),
                jnp.sum(product[HD:], axis=0, keepdims=True),
            )

    def finish(a):
        even = lax.rem(a, ITEMS)
        start = pl.multiple_of(a * BLK, BLK)
        for t in range(tiles):
            dq_ref[0, pl.ds(start, BLK), t * 128 : t * 128 + 128] = (
                head_rows(acc_ref[even, t]) * 0.125
            ).astype(jnp.bfloat16)

    def item(slot, a, c, real):
        ids, safe = chunk_ids(list_ref, row, a * nb + c * CHUNK, nb, real)
        even = lax.rem(a, ITEMS)
        allowed = block_rows(segc_ref, ids, slice(0, 128)) == segr_ref[0, a]
        first = c == 0
        for g in range(groups):
            lanes = slice(g * group, g * group + group)
            s_t = dot_f32(block_rows(k_ref, safe, lanes), qst_ref[slot, g])
            dp_t = dot_f32(block_rows(v_ref, safe, lanes), dost_ref[slot, g])
            p_parts, ds_parts = [], []
            for u in range(halves):
                t = g * halves + u
                half = slice(u * 128, u * 128 + 128)
                lse = lse_ref[0, a, :, t * 128 : t * 128 + 128]
                p = jnp.exp(jnp.where(allowed, s_t[:, half], NEG) - lse)
                ds = p * (dp_t[:, half] - delta_ref[slot, t])
                p_parts.append(p.astype(jnp.bfloat16))
                ds_parts.append(ds.astype(jnp.bfloat16))
            p_t = jnp.concatenate(p_parts, axis=1) if halves > 1 else p_parts[0]
            ds_t = jnp.concatenate(ds_parts, axis=1) if halves > 1 else ds_parts[0]
            dv = dot_f32(p_t, dos_ref[slot, g])
            dk = dot_f32(ds_t, qs_ref[slot, g])
            dq_t = dot_f32(turned_blocks(kt_ref, safe, lanes), ds_t)
            for j in range(CHUNK):
                where = pl.ds(pl.multiple_of(safe[j] * BLK, BLK), BLK)
                part = slice(j * BLK, j * BLK + BLK)
                dv_acc[where, lanes] += dv[part]
                dk_acc[where, lanes] += dk[part]
            for u in range(halves):
                t = g * halves + u
                acc_ref[even, t] = jnp.where(first, 0.0, acc_ref[even, t]) + pick_diag(dq_t, u)

    run_items(n_ref, total_ref, row, nb, ready, item, finish)

    def leave(i, src, dst):
        return pltpu.make_async_copy(src, dst.at[pl.ds(row, 1)], out_sem.at[i])

    leaving = [leave(0, dq_ref, dq_out)]
    leaving[0].start()
    for i, (total, low, out) in enumerate(((dk_acc, q_ref, dk_out), (dv_acc, o_ref, dv_out))):
        def flush(a, _):
            where = pl.ds(pl.multiple_of(a * BLK, BLK), BLK)
            low[0, where, :] = total[where, :].astype(jnp.bfloat16)
            return 0

        lax.fori_loop(0, nb, flush, 0, unroll=2)
        leaving.append(leave(1 + i, low, out))
        leaving[-1].start()
    for copy in leaving:
        copy.wait()


def attention_backward(q, k, v, o, do, lse, plan):
    *tables, seg_cols, seg_rows = plan
    rows, full_len, width = q.shape
    nb, group = full_len // BLK, group_of(width)
    tiles, groups = width // 128, width // group
    pairs = rows * full_len * full_len // 4 * width
    args = (q, k, v, o, do, lse, seg_cols, seg_rows)
    anywhere = pl.BlockSpec(memory_space=pl.ANY)
    stretch = pltpu.VMEM((1, full_len, width), jnp.bfloat16)
    like = jax.ShapeDtypeStruct((rows, full_len, width), jnp.bfloat16)
    square = pltpu.VMEM((2 * ITEMS, groups, group, group), jnp.bfloat16)
    return pl.pallas_call(
        functools.partial(backward_kernel, group),
        out_shape=(like, like, like),
        grid_spec=pltpu.PrefetchScalarGridSpec(
            num_scalar_prefetch=3,
            grid=(rows,),
            in_specs=[anywhere] * 5 + [one_spec(x.shape) for x in args[5:]],
            out_specs=(anywhere,) * 3,
            scratch_shapes=[
                stretch, stretch, stretch, stretch, stretch, stretch,
                pltpu.VMEM((nb, width, 128), jnp.bfloat16),
                square, square, square, square,
                pltpu.VMEM((2 * ITEMS, tiles, 1, 128), jnp.float32),
                pltpu.VMEM((ITEMS, tiles, HD, 128), jnp.float32),
                pltpu.VMEM((full_len, width), jnp.float32),
                pltpu.VMEM((full_len, width), jnp.float32),
                pltpu.SemaphoreType.DMA((5,)),
                pltpu.SemaphoreType.DMA((3,)),
            ],
        ),
        compiler_params=pltpu.CompilerParams(vmem_limit_bytes=62 << 20),
        cost_estimate=pl.CostEstimate(
            flops=10 * pairs, transcendentals=pairs // HD, bytes_accessed=16 * q.size
        ),
        name="attention_backward",
    )(*tables, *args)


def pair_bit(index, bit):
    return lax.rem(index // (1 << bit), 2)


def pair_of(index, bit):
    return index + (1 - 2 * pair_bit(index, bit)) * (1 << bit)


def all_arrived(bits):
    me = lax.axis_index("fsdp")
    barrier = pltpu.get_barrier_semaphore()
    for bit in range(bits):
        pl.semaphore_signal(
            barrier, inc=1, device_id={"fsdp": pair_of(me, bit)},
            device_id_type=pl.DeviceIdType.MESH,
        )
    pl.semaphore_signal(
        barrier, inc=1, device_id={"seq": 1 - lax.axis_index("seq")},
        device_id_type=pl.DeviceIdType.MESH,
    )
    pl.semaphore_wait(barrier, bits + 1)


def qkv_backward_kernel(
    bits, xt_in, dq_in, dk_in, dv_in, wt_in, res_in, small_in, outer_in,
    wq_out, wk_out, wv_out, small_out, tok_out, outer_out,
    xt, grads, wt, res, tok, kept, sends, lands, final, small, small_land, result,
    in_sem, tok_send, tok_land, own_sem, send_sem, land_sem, x_send, x_land,
    small_send, small_recv, out_sem, outer_sem,
):
    me, side = lax.axis_index("fsdp"), lax.axis_index("seq")
    half = tok.shape[2] * tok.shape[1]
    piece, pieces = tok.shape[2], tok.shape[1]
    own, width = wq_out.shape
    owners = 1 << bits
    sources = (dq_in, dk_in, dv_in)
    rows_of = [pl.ds(pl.multiple_of(p * half, half), half) for p in (1 - side, side)]
    loads = [pltpu.make_async_copy(wt_in, wt, in_sem.at[0])]
    for p in range(2):
        for i in range(3):
            loads.append(
                pltpu.make_async_copy(
                    sources[i].at[rows_of[p]], grads.at[i, rows_of[p]], in_sem.at[1 + 4 * p + i]
                )
            )
        loads.append(
            pltpu.make_async_copy(res_in.at[rows_of[p]], res.at[rows_of[p]], in_sem.at[4 + 4 * p])
        )
    loads.append(pltpu.make_async_copy(xt_in, xt, in_sem.at[9]))
    loads.append(pltpu.make_async_copy(small_in, small.at[0], in_sem.at[10]))
    for i in (0, 1, 2, 3, 4, 9, 5, 6, 7, 8, 10):
        loads[i].start()
    all_arrived(bits)

    def token_rows(start):
        total = res[pl.ds(start, piece), :].astype(jnp.float32)
        for i in range(3):
            total = total + dot_f32(
                grads[i, pl.ds(start, piece), :], wt[i]
            )
        return total.astype(jnp.bfloat16)

    def sent(i):
        return pltpu.make_async_remote_copy(
            src_ref=tok.at[0, i],
            dst_ref=tok_out.at[side, pl.ds(pl.multiple_of(i * piece, piece), piece)],
            send_sem=tok_send.at[i], recv_sem=tok_land.at[i],
            device_id={"seq": 1 - side}, device_id_type=pl.DeviceIdType.MESH,
        )

    def landed(i):
        return pltpu.make_async_remote_copy(
            src_ref=tok.at[0, i],
            dst_ref=tok_out.at[1 - side, pl.ds(pl.multiple_of(i * piece, piece), piece)],
            send_sem=tok_send.at[i], recv_sem=tok_land.at[i],
            device_id={"seq": 1 - side}, device_id_type=pl.DeviceIdType.MESH,
        )

    def stays(i):
        return pltpu.make_async_copy(
            tok.at[1, i],
            tok_out.at[side, pl.ds(pl.multiple_of(i * piece, piece), piece)],
            own_sem.at[i],
        )

    def send_piece(i, _):
        start = pl.multiple_of((1 - side) * half + i * piece, piece)
        tok[0, i] = token_rows(start)
        sent(i).start()
        return 0

    def keep_piece(i, _):
        start = pl.multiple_of(side * half + i * piece, piece)
        tok[1, i] = token_rows(start)
        stays(i).start()
        return 0

    low_bit = pair_bit(me, 0) == 0
    tile = 8 if owners % 8 == 0 else owners
    first_of = [0]
    for bit in range(bits):
        first_of.append(first_of[-1] + (owners >> (bit + 1)))

    def weights(i):
        def rows(m, _):
            rows_here = pl.ds(pl.multiple_of(m * tile * own, tile * own), tile * own)
            block = dot_f32(
                jnp.concatenate(
                    [xt[h, r, rows_here, :] for h in range(2) for r in range(pieces)], axis=1
                ),
                grads[i],
            ).reshape(tile // 2, 2, own, width)
            even, odd = block[:, 0], block[:, 1]
            spot = pl.ds(m * (tile // 2), tile // 2)
            kept[i, spot] = jnp.where(low_bit, even, odd)
            sends[i, spot] = jnp.where(low_bit, odd, even).astype(jnp.bfloat16)
            return 0

        lax.fori_loop(0, owners // tile, rows, 0)

    def hop(i, bit):
        count = owners >> (bit + 1)
        spot = pl.ds(first_of[bit], count)
        return pltpu.make_async_remote_copy(
            src_ref=sends.at[i, spot], dst_ref=lands.at[i, spot],
            send_sem=send_sem.at[i, bit], recv_sem=land_sem.at[i, bit],
            device_id={"fsdp": pair_of(me, bit)}, device_id_type=pl.DeviceIdType.MESH,
        )

    def cross(i):
        return pltpu.make_async_remote_copy(
            src_ref=final.at[0, i], dst_ref=final.at[1, i],
            send_sem=x_send.at[i], recv_sem=x_land.at[i],
            device_id={"seq": 1 - side}, device_id_type=pl.DeviceIdType.MESH,
        )

    def advance(i, bit):
        hop(i, bit).wait_recv()
        base = first_of[bit]
        if bit + 1 == bits:
            total = kept[i, base] + lands[i, base].astype(jnp.float32)
            final[0, i] = total.astype(jnp.bfloat16)
            cross(i).start()
            return
        nxt = pair_bit(me, bit + 1)

        def one(j, _):
            stay, go = 2 * j + nxt, 2 * j + 1 - nxt
            kept[i, first_of[bit + 1] + j] = kept[i, base + stay] + lands[
                i, base + stay
            ].astype(jnp.float32)
            sends[i, first_of[bit + 1] + j] = (
                kept[i, base + go] + lands[i, base + go].astype(jnp.float32)
            ).astype(jnp.bfloat16)
            return 0

        lax.fori_loop(0, owners >> (bit + 2), one, 0)
        hop(i, bit + 1).start()

    outs = (wq_out, wk_out, wv_out)

    def written(i):
        return pltpu.make_async_copy(result.at[i], outs[i], out_sem.at[i])

    def finish(i):
        cross(i).wait_recv()
        result[i] = final[0, i].astype(jnp.float32) + final[1, i].astype(jnp.float32)
        written(i).start()

    def small_hop(bit):
        where = {"fsdp": pair_of(me, bit)} if bit < bits else {"seq": 1 - side}
        return pltpu.make_async_remote_copy(
            src_ref=small.at[bit], dst_ref=small_land.at[bit],
            send_sem=small_send.at[bit], recv_sem=small_recv.at[bit],
            device_id=where, device_id_type=pl.DeviceIdType.MESH,
        )

    def small_advance(bit):
        small_hop(bit).wait_recv()
        small[bit + 1] = small[bit] + small_land[bit]
        if bit < bits:
            small_hop(bit + 1).start()

    def column_sums(i, spot):
        def one(c, total):
            block = grads[i, pl.ds(pl.multiple_of(c * 256, 256), 256), :].astype(jnp.float32)
            return total + jnp.sum(block.reshape(32, 8, width), axis=0)

        total = lax.fori_loop(
            0, grads.shape[1] // 256, one, jnp.zeros((8, width), jnp.float32)
        )
        small[0, spot : spot + 1] = jnp.sum(total, axis=0, keepdims=True)

    for i in range(5):
        loads[i].wait()
    send_piece(0, 0)
    for i in range(5, 11):
        loads[i].wait()

    def begin(i, _):
        weights(i)
        hop(i, 0).start()
        send_piece(i + 1, 0)
        advance(i, 0)
        return 0

    lax.fori_loop(0, 3, begin, 0)
    outer = pltpu.make_async_remote_copy(
        src_ref=outer_in, dst_ref=outer_out, send_sem=outer_sem.at[0], recv_sem=outer_sem.at[1],
        device_id={"seq": 1 - side}, device_id_type=pl.DeviceIdType.MESH,
    )
    outer.start()
    column_sums(0, 0)
    column_sums(2, 1)
    small_hop(0).start()

    def second(i, _):
        keep_piece(i, 0)
        advance(i, 1)
        return 0

    lax.fori_loop(0, 3, second, 0)
    small_advance(0)
    keep_piece(3, 0)
    for bit in range(2, bits):
        for i in range(3):
            advance(i, bit)
        small_advance(bit - 1)
    for bit in range(bits - 1, bits + 1):
        small_advance(bit)
    for i in range(3):
        finish(i)
    small_copy = pltpu.make_async_copy(small.at[bits + 1], small_out, out_sem.at[3])
    small_copy.start()
    for i in range(3):
        written(i).wait()
        cross(i).wait_send()
        for bit in range(bits):
            hop(i, bit).wait_send()
    for bit in range(bits + 1):
        small_hop(bit).wait_send()
    small_copy.wait()
    outer.wait_send()
    outer.wait_recv()
    for i in range(pieces):
        stays(i).wait()
        sent(i).wait_send()
        landed(i).wait_recv()


def qkv_backward(xt, dq, dk, dv, wt, resid, small, outer, own):
    tokens, width = dq.shape
    bits = lax.axis_size("fsdp").bit_length() - 1
    owners = 1 << bits
    pieces = 4
    piece = tokens // 2 // pieces
    dma = pltpu.SemaphoreType.DMA
    f32, bf16 = jnp.float32, jnp.bfloat16
    shard = jax.ShapeDtypeStruct((own, width), f32)
    anywhere = pl.BlockSpec(memory_space=pltpu.HBM)
    return pl.pallas_call(
        functools.partial(qkv_backward_kernel, bits),
        out_shape=(
            shard, shard, shard,
            jax.ShapeDtypeStruct(small.shape, f32),
            jax.ShapeDtypeStruct((2, tokens // 2, width), bf16),
            jax.ShapeDtypeStruct(outer.shape, bf16),
        ),
        in_specs=[anywhere] * 8,
        out_specs=(anywhere,) * 6,
        scratch_shapes=[
            pltpu.VMEM(xt.shape, bf16),
            pltpu.VMEM((3, tokens, width), bf16),
            pltpu.VMEM(wt.shape, bf16),
            pltpu.VMEM((tokens, width), bf16),
            pltpu.VMEM((2, pieces, piece, width), bf16),
            pltpu.VMEM((3, owners - 1, own, width), f32),
            pltpu.VMEM((3, owners - 1, own, width), bf16),
            pltpu.VMEM((3, owners - 1, own, width), bf16),
            pltpu.VMEM((2, 3, own, width), bf16),
            pltpu.VMEM((bits + 2,) + small.shape, f32),
            pltpu.VMEM((bits + 1,) + small.shape, f32),
            pltpu.VMEM((3, own, width), f32),
            dma((11,)), dma((pieces,)), dma((pieces,)), dma((pieces,)),
            dma((3, bits)), dma((3, bits)), dma((3,)), dma((3,)),
            dma((bits + 1,)), dma((bits + 1,)), dma((4,)), dma((2,)),
        ],
        compiler_params=pltpu.CompilerParams(
            collective_id=1, has_side_effects=True, vmem_limit_bytes=62 << 20
        ),
        cost_estimate=pl.CostEstimate(
            flops=40 * tokens * width * width, transcendentals=0,
            bytes_accessed=16 * tokens * width,
        ),
        name="qkv_backward",
    )(xt, dq, dk, dv, wt, resid, small, outer)


def qkv_forward_kernel(
    bits, tokens_in, own_in, grad_in,
    grad_out, x_out, xt_out, q_out, k_out, v_out, wt_out, small_out,
    x, xt, w, wt, qkv, small,
    own_sem, tok_send, tok_land, load_sem, send_sem, land_sem, x_sem, xt_sem, out_sem, w_sem,
    small_sem,
):
    me, side = lax.axis_index("fsdp"), lax.axis_index("seq")
    pieces, piece, width = x.shape[1], x.shape[2], x.shape[3]
    mine = [pair_bit(me, bit) for bit in range(bits)]
    columns = part_columns(width)
    outs = (q_out, k_out, v_out)

    def slot(bit, part):
        here = [slice(None)] * (bits - 1 - bit) + [mine[b] for b in range(bit, -1, -1)]
        return tuple(here) + (slice(None), columns[part])

    own_tokens = pltpu.make_async_copy(tokens_in.at[side], x.at[side], own_sem.at[0])
    own_tokens.start()
    grad_rows = pltpu.make_async_copy(grad_in.at[1 - side], grad_out, own_sem.at[1])
    grad_rows.start()

    def load(part):
        spot = tuple(mine[b] for b in range(bits - 1, -1, -1)) + (slice(None), columns[part])
        return pltpu.make_async_copy(
            own_in.at[:, columns[part]], w.at[spot], load_sem.at[part]
        )

    for part in range(3):
        load(part).start()
    all_arrived(bits)

    def sent(i):
        return pltpu.make_async_remote_copy(
            src_ref=tokens_in.at[1 - side, i], dst_ref=x.at[side, i],
            send_sem=tok_send.at[i], recv_sem=tok_land.at[i],
            device_id={"seq": 1 - side}, device_id_type=pl.DeviceIdType.MESH,
        )

    def landed(i):
        return pltpu.make_async_remote_copy(
            src_ref=tokens_in.at[1 - side, i], dst_ref=x.at[1 - side, i],
            send_sem=tok_send.at[i], recv_sem=tok_land.at[i],
            device_id={"seq": 1 - side}, device_id_type=pl.DeviceIdType.MESH,
        )

    def hop(part, turn):
        bit = bits - 1 - turn
        return pltpu.make_async_remote_copy(
            src_ref=w.at[slot(bit, part)], dst_ref=w.at[slot(bit, part)],
            send_sem=send_sem.at[part, turn], recv_sem=land_sem.at[part, turn],
            device_id={"fsdp": pair_of(me, bit)}, device_id_type=pl.DeviceIdType.MESH,
        )

    for part in range(3):
        load(part).wait()
        hop(part, 0).start()
    for i in range(pieces):
        sent(i).start()

    def x_copy(half, i):
        return pltpu.make_async_copy(x.at[half, i], x_out.at[half, i], x_sem.at[half, i])

    def out_copy(part, half, i):
        return pltpu.make_async_copy(
            qkv.at[part, half, i], outs[part].at[half, i], out_sem.at[part, half, i]
        )

    def xt_copy(half, i):
        return pltpu.make_async_copy(xt.at[half, i], xt_out.at[half, i], xt_sem.at[half, i])

    def w_copy(part):
        return pltpu.make_async_copy(wt.at[part], wt_out.at[part], w_sem.at[part])

    def whole(part):
        first = part_start(width, part)
        spot = (slice(None),) * (bits + 1) + (slice(first, first + width),)
        return w[spot].reshape(width, width)

    def turn(half, i):
        x_copy(half, i).start()
        xt[half, i] = x[half, i].T
        xt_copy(half, i).start()

    def project(part, half, i):
        total = dot_f32(x[half, i], whole(part))
        if part == 0:
            total = total + small[0:1, :]
        if part == 2:
            total = total + small[1:2, :]
        qkv[part, half, i] = total.astype(jnp.bfloat16)
        out_copy(part, half, i).start()

    def over(body):
        def one(i, _):
            body(i)
            return 0

        lax.fori_loop(0, pieces, one, 0)

    def turn_weights(part):
        wt[part] = whole(part).T
        w_copy(part).start()

    def other(i):
        landed(i).wait_recv()
        turn(1 - side, i)
        project(0, 1 - side, i)
        project(1, 1 - side, i)

    own_tokens.wait()
    over(lambda i: turn(side, i))
    for step in range(bits + 2):
        full = None
        for part in range(3):
            hops = step - part
            if 0 <= hops < bits:
                hop(part, hops).wait_recv()
                if hops + 1 < bits:
                    hop(part, hops + 1).start()
                else:
                    full = part
        if full == 0:
            spot = (slice(None),) * (bits + 1) + (slice(width, width + 128),)
            turned = w[spot].reshape(width, 128).astype(jnp.float32).T
            small[...] = turned[: small.shape[0]]
            pltpu.make_async_copy(small, small_out, small_sem.at[0]).start()
        if full is not None:
            over(lambda i: project(full, side, i))
        if full == 1:
            turn_weights(0)
            turn_weights(1)
            over(other)
        if full == 2:
            over(lambda i: project(2, 1 - side, i))
            turn_weights(2)
    for i in range(pieces):
        sent(i).wait_send()
    for part in range(3):
        w_copy(part).wait()
        for hops in range(bits):
            hop(part, hops).wait_send()
    grad_rows.wait()
    pltpu.make_async_copy(small, small_out, small_sem.at[0]).wait()
    for half in range(2):
        for i in range(pieces):
            x_copy(half, i).wait()
            xt_copy(half, i).wait()
            for part in range(3):
                out_copy(part, half, i).wait()


def part_start(width, part):
    return part * width + (128 if part else 0)


def part_columns(width):
    return (
        slice(0, width + 128),
        slice(width + 128, 2 * width + 128),
        slice(2 * width + 128, 3 * width + 128),
    )


def qkv_forward(tokens_in, own_pack, out_grad):
    rows, local, width = tokens_in.shape
    own, columns = own_pack.shape
    bits = lax.axis_size("fsdp").bit_length() - 1
    pieces = 4
    piece = local // pieces
    dma = pltpu.SemaphoreType.DMA
    bf16 = jnp.bfloat16
    halves = (2, pieces, piece, width)
    gathered = (2,) * bits + (own, columns)
    anywhere = pl.BlockSpec(memory_space=pltpu.HBM)
    like = jax.ShapeDtypeStruct(halves, bf16)
    turned = (2, pieces, width, piece)
    grad, x, xt, q, k, v, weights_t, small = pl.pallas_call(
        functools.partial(qkv_forward_kernel, bits),
        out_shape=(
            jax.ShapeDtypeStruct((local, width), bf16),
            like, jax.ShapeDtypeStruct(turned, bf16), like, like, like,
            jax.ShapeDtypeStruct((3, width, width), bf16),
            jax.ShapeDtypeStruct((SMALL_ROWS, width), jnp.float32),
        ),
        in_specs=[anywhere] * 3,
        out_specs=(anywhere,) * 8,
        scratch_shapes=[
            pltpu.VMEM(halves, bf16),
            pltpu.VMEM(turned, bf16),
            pltpu.VMEM(gathered, bf16),
            pltpu.VMEM((3, width, width), bf16),
            pltpu.VMEM((3,) + halves, bf16),
            pltpu.VMEM((SMALL_ROWS, width), jnp.float32),
            dma((2,)), dma((pieces,)), dma((pieces,)), dma((3,)),
            dma((3, bits)), dma((3, bits)), dma((2, pieces)), dma((2, pieces)),
            dma((3, 2, pieces)), dma((3,)), dma((1,)),
        ],
        compiler_params=pltpu.CompilerParams(
            collective_id=2, has_side_effects=True, vmem_limit_bytes=62 << 20
        ),
        cost_estimate=pl.CostEstimate(
            flops=18 * rows * local * width * width, transcendentals=0,
            bytes_accessed=16 * rows * local * width,
        ),
        name="qkv_forward",
    )(tokens_in.reshape(halves), own_pack, out_grad)
    flat = rows * local, width
    return (
        x.reshape(flat), q.reshape(flat), k.reshape(flat), v.reshape(flat), xt, weights_t, small, grad
    )


eps_norm = 1e-06


def dot_rows(left, right):
    return lax.dot_general(
        left, right, (((0,), (0,)), ((), ())), preferred_element_type=jnp.float32
    )


def dot_nt(left, right):
    return lax.dot_general(
        left, right, (((1,), (1,)), ((), ())), preferred_element_type=jnp.float32
    )


def row_mean(values):
    return jnp.mean(values, axis=-1, keepdims=True)


GELU_K = math.sqrt(2.0 / math.pi)
GELU_A = 0.044715


def gelu_pair(u):
    square = u * u
    t = jnp.tanh(u * (GELU_K + (GELU_K * GELU_A) * square))
    half = 0.5 + 0.5 * t
    slope = half + (u * (half * (1.0 - t))) * (GELU_K + (3.0 * GELU_K * GELU_A) * square)
    return u * half, slope


OUT_B, GAIN_1, BIAS_1, OUTER_B, GAIN_2, BIAS_2, INNER_B = 2, 3, 4, 5, 6, 7, 8
SMALL_ROWS = 16


def eights(values):
    return jnp.sum(values.reshape(-1, 8, values.shape[-1]), axis=0)


def middle_forward_kernel(
    chunks, side, weights_in, small, att, tokens, grad_own, grad_other,
    out_keep, out_send, d_mlp, normed, z_one, rs_one, slope, d_weights, sums,
    w, acc, act, flow, part, load_sem, store_sem,
):
    step, steps = pl.program_id(0), pl.num_programs(0)
    rows, width = att.shape
    f32, bf16 = jnp.float32, jnp.bfloat16
    count = 2 * chunks + 1
    staying = step // (steps // 2) == side[0]

    def load(i):
        return pltpu.make_async_copy(
            weights_in.at[:, pl.ds(i * width, width)], w.at[i], load_sem.at[i]
        )

    def store(c):
        return pltpu.make_async_copy(
            w.at[1 + chunks + c], d_weights.at[:, pl.ds(c * width, width)], store_sem.at[c]
        )

    @pl.when(step == 0)
    def _():
        for i in range(count):
            load(i).start()
        part[...] = jnp.zeros_like(part)

        def clear(i, _):
            acc[i] = jnp.zeros_like(acc[i])
            return 0

        lax.fori_loop(0, chunks, clear, 0)
        load(0).wait()

    def vector(i):
        return small[i : i + 1, :]

    def add_sum(i, values):
        part[i] += eights(values)

    attn = dot_f32(att[...], w[0]) + vector(OUT_B)
    resid = tokens[...].astype(f32) + attn
    add_sum(INNER_B + chunks, resid * resid)
    add_sum(INNER_B + chunks + 1, attn * attn)
    centred = resid - row_mean(resid)
    scale = lax.rsqrt(row_mean(centred * centred) + eps_norm)
    z = centred * scale
    rs_one[...] = scale
    z_one[...] = z.astype(bf16)
    full = z * vector(GAIN_1) + vector(BIAS_1)
    flow[...] = full
    normed[...] = full.astype(bf16)

    def inner(c, _):
        @pl.when(step == 0)
        def _():
            load(1 + c).wait()

        for n in range(width // 256):
            cols = slice(n * 256, n * 256 + 256)
            pre = dot_f32(normed[...], w[1 + c, :, cols]) + small[pl.ds(INNER_B + c, 1), cols]
            value, grade = gelu_pair(pre)
            act[c, :, cols] = value.astype(bf16)
            slope[c, :, cols] = grade.astype(bf16)
        return 0

    lax.fori_loop(0, chunks, inner, 0)

    @pl.when(step == 0)
    def _():
        for i in range(1 + chunks, count):
            load(i).wait()

    mlp = dot_f32(act[0], w[1 + chunks])
    for c in range(1, chunks):
        mlp = mlp + dot_f32(act[c], w[1 + chunks + c])
    mlp = mlp + vector(OUTER_B)
    add_sum(INNER_B + chunks + 2, mlp * mlp)
    resid = flow[...] + mlp
    centred = resid - row_mean(resid)
    scale = lax.rsqrt(row_mean(centred * centred) + eps_norm)
    z = centred * scale
    result = (z * vector(GAIN_2) + vector(BIAS_2)).astype(bf16)

    @pl.when(staying)
    def _():
        out_keep[...] = result

    @pl.when(jnp.logical_not(staying))
    def _():
        out_send[...] = result

    grad = jnp.where(staying, grad_own[...], grad_other[...]).astype(f32)
    add_sum(GAIN_2, grad * z)
    add_sum(BIAS_2, grad)
    grad = grad * vector(GAIN_2)
    low = (scale * (grad - row_mean(grad) - z * row_mean(grad * z))).astype(bf16)
    add_sum(OUTER_B, low.astype(f32))
    d_mlp[...] = low

    def back(c, _):
        acc[c] += dot_rows(act[c], d_mlp[...])

        @pl.when(step == steps - 1)
        def _():
            w[1 + chunks + c] = acc[c].astype(bf16)
            store(c).start()

        return 0

    lax.fori_loop(0, chunks, back, 0)

    @pl.when(step == steps - 1)
    def _():
        sums[...] = jnp.sum(part[...], axis=1)
        for c in range(chunks):
            store(c).wait()


def middle_backward_kernel(
    chunks, weights_in, small, sums_in, att, d_mlp, normed, z_one, rs_one, slope,
    d_attn, d_att, d_weights, sums,
    w, acc, d_pre, flow, part, load_sem, store_sem,
):
    step, steps = pl.program_id(0), pl.num_programs(0)
    rows, width = att.shape
    f32, bf16 = jnp.float32, jnp.bfloat16
    count = 2 * chunks + 1

    def load(i):
        return pltpu.make_async_copy(
            weights_in.at[:, pl.ds(i * width, width)], w.at[i], load_sem.at[i]
        )

    def store(i):
        return pltpu.make_async_copy(
            w.at[i], d_weights.at[:, pl.ds(i * width, width)], store_sem.at[i]
        )

    @pl.when(step == 0)
    def _():
        for c in range(chunks):
            load(1 + chunks + c).start()
            load(1 + c).start()
        load(0).start()
        part[...] = jnp.zeros_like(part)

        def clear(i, _):
            acc[i] = jnp.zeros_like(acc[i])
            return 0

        lax.fori_loop(0, chunks + 1, clear, 0)

    def vector(i):
        return small[i : i + 1, :]

    def add_sum(i, values):
        part[i] += eights(values)

    turned = normed[...].T
    flow[...] = d_mlp[...].astype(f32)

    def back(c, _):
        @pl.when(step == 0)
        def _():
            load(1 + chunks + c).wait()
            load(1 + c).wait()

        for n in range(width // 256):
            cols = slice(n * 256, n * 256 + 256)
            d_act = dot_nt(d_mlp[...], w[1 + chunks + c, cols, :])
            low = (slope[c, :, cols].astype(f32) * d_act).astype(bf16)
            part[INNER_B + c, :, cols] += eights(low.astype(f32))
            d_pre[:, cols] = low
        acc[1 + c] += dot_f32(turned, d_pre[...])
        flow[...] += dot_nt(d_pre[...], w[1 + c])

        @pl.when(step == steps - 1)
        def _():
            w[1 + c] = acc[1 + c].astype(bf16)
            store(1 + c).start()

        return 0

    lax.fori_loop(0, chunks, back, 0)

    @pl.when(step == 0)
    def _():
        load(0).wait()

    grad = flow[...]
    z = z_one[...].astype(f32)
    add_sum(GAIN_1, grad * z)
    add_sum(BIAS_1, grad)
    grad = grad * vector(GAIN_1)
    low = (rs_one[...] * (grad - row_mean(grad) - z * row_mean(grad * z))).astype(bf16)
    add_sum(OUT_B, low.astype(f32))
    d_attn[...] = low
    acc[0] += dot_rows(att[...], d_attn[...])
    d_att[...] = dot_nt(d_attn[...], w[0]).astype(bf16)

    @pl.when(step == steps - 1)
    def _():
        w[0] = acc[0].astype(bf16)
        store(0).start()
        sums[...] = sums_in[...] + jnp.sum(part[...], axis=1)
        for i in range(chunks + 1):
            store(i).wait()


def middle_parts(weights, small, tok_count, width):
    chunks = (weights.shape[1] // width - 1) // 2
    rows = 512
    return chunks, rows, tok_count // rows


def middle_forward(side, weights, small, att, tokens, grad_own, grad_other):
    tok_count, width = att.shape
    chunks, rows, steps = middle_parts(weights, small, tok_count, width)
    count = 2 * chunks + 1
    f32, bf16 = jnp.float32, jnp.bfloat16
    half = steps // 2

    def early(i):
        return jnp.minimum(i, half - 1)

    def late(i):
        return jnp.maximum(i - half, 0)

    tile = pl.BlockSpec((rows, width), lambda i, s: (i, 0))
    thin = pl.BlockSpec((rows, 1), lambda i, s: (i, 0))
    deep = pl.BlockSpec((chunks, rows, width), lambda i, s: (0, i, 0))
    keep = pl.BlockSpec((rows, width), lambda i, s: (jnp.where(s[0] == 0, early(i), late(i)), 0))
    send = pl.BlockSpec((rows, width), lambda i, s: (jnp.where(s[0] == 0, late(i), early(i)), 0))
    own = pl.BlockSpec(
        (None, rows, width), lambda i, s: (s[0], jnp.where(s[0] == 0, early(i), late(i)), 0)
    )
    fixed = pl.BlockSpec(small.shape, lambda i, s: (0, 0), pipeline_mode=pl.Buffered(1))
    anywhere = pl.BlockSpec(memory_space=pl.ANY)
    like = jax.ShapeDtypeStruct((tok_count, width), bf16)
    part = jax.ShapeDtypeStruct((tok_count // 2, width), bf16)
    return pl.pallas_call(
        functools.partial(middle_forward_kernel, chunks),
        out_shape=(
            part, part, like, like, like,
            jax.ShapeDtypeStruct((tok_count, 1), f32),
            jax.ShapeDtypeStruct((chunks, tok_count, width), bf16),
            jax.ShapeDtypeStruct((width, chunks * width), bf16),
            jax.ShapeDtypeStruct(small.shape, f32),
        ),
        grid_spec=pltpu.PrefetchScalarGridSpec(
            num_scalar_prefetch=1,
            grid=(steps,),
            in_specs=[anywhere, fixed, tile, tile, own, send],
            out_specs=(keep, send, tile, tile, tile, thin, deep, anywhere, fixed),
            scratch_shapes=[
                pltpu.VMEM((count, width, width), bf16),
                pltpu.VMEM((chunks, width, width), f32),
                pltpu.VMEM((chunks, rows, width), bf16),
                pltpu.VMEM((rows, width), f32),
                pltpu.VMEM((small.shape[0], 8, width), f32),
                pltpu.SemaphoreType.DMA((count,)),
                pltpu.SemaphoreType.DMA((chunks,)),
            ],
        ),
        compiler_params=pltpu.CompilerParams(vmem_limit_bytes=62 << 20),
        cost_estimate=pl.CostEstimate(
            flops=12 * tok_count * width * width * (count + 1) // 2,
            transcendentals=tok_count * width * chunks,
            bytes_accessed=30 * tok_count * width + 4 * weights.size,
        ),
        name="middle_forward",
    )(side.reshape(1), weights, small, att, tokens, grad_own, grad_other)


def middle_backward(weights, small, sums, att, d_mlp, normed, z_one, rs_one, slope):
    tok_count, width = att.shape
    chunks, rows, steps = middle_parts(weights, small, tok_count, width)
    count = 2 * chunks + 1
    f32, bf16 = jnp.float32, jnp.bfloat16
    tile = pl.BlockSpec((rows, width), lambda i: (i, 0))
    thin = pl.BlockSpec((rows, 1), lambda i: (i, 0))
    deep = pl.BlockSpec((chunks, rows, width), lambda i: (0, i, 0))
    fixed = pl.BlockSpec(small.shape, lambda i: (0, 0), pipeline_mode=pl.Buffered(1))
    anywhere = pl.BlockSpec(memory_space=pl.ANY)
    like = jax.ShapeDtypeStruct((tok_count, width), bf16)
    return pl.pallas_call(
        functools.partial(middle_backward_kernel, chunks),
        grid=(steps,),
        out_shape=(
            like, like,
            jax.ShapeDtypeStruct((width, (chunks + 1) * width), bf16),
            jax.ShapeDtypeStruct(small.shape, f32),
        ),
        in_specs=[anywhere, fixed, fixed, tile, tile, tile, tile, thin, deep],
        out_specs=(tile, tile, anywhere, fixed),
        scratch_shapes=[
            pltpu.VMEM((count, width, width), bf16),
            pltpu.VMEM((chunks + 1, width, width), f32),
            pltpu.VMEM((rows, width), bf16),
            pltpu.VMEM((rows, width), f32),
            pltpu.VMEM((small.shape[0], 8, width), f32),
            pltpu.SemaphoreType.DMA((count,)),
            pltpu.SemaphoreType.DMA((chunks + 1,)),
        ],
        compiler_params=pltpu.CompilerParams(vmem_limit_bytes=62 << 20),
        cost_estimate=pl.CostEstimate(
            flops=12 * tok_count * width * width * (count + 1) // 2, transcendentals=0,
            bytes_accessed=30 * tok_count * width + 4 * weights.size,
        ),
        name="middle_backward",
    )(weights, small, sums, att, d_mlp, normed, z_one, rs_one, slope)


def contract_rows(left, right):
    return lax.dot_general(
        left, right, (((0,), (0,)), ((), ())), preferred_element_type=jnp.float32
    )


def times_transpose(left, right):
    return lax.dot_general(
        left, right, (((1,), (1,)), ((), ())), preferred_element_type=jnp.float32
    )


def butterfly_sum(values, axis):
    size = lax.axis_size(axis)
    if size & (size - 1):
        return lax.psum(values, axis)
    step = 1
    while step < size:
        pairs = [(i, i ^ step) for i in range(size)]
        values = values + lax.ppermute(values, axis, pairs)
        step *= 2
    return values


def sum_seq(values):
    if lax.axis_size("seq") == 2:
        other = lax.ppermute(values, "seq", [(0, 1), (1, 0)])
        return values.astype(jnp.float32) + other.astype(jnp.float32)
    return lax.psum(values, "seq").astype(jnp.float32)


class Regroup:
    def __init__(self, row_count):
        self.size = lax.axis_size("seq")
        self.ways = math.gcd(row_count, self.size)
        self.parts = self.size // self.ways
        self.rows = row_count // self.ways
        me = lax.axis_index("seq")
        self.place = lax.rem(me, self.ways)
        self.row_group = me // self.parts

    def targets(self, turn):
        ways, parts = self.ways, self.parts
        return [
            (s, ((s % ways + turn) % ways) * parts + s // ways) for s in range(self.size)
        ]

    def move(self, values, pairs):
        if all(a == b for a, b in pairs):
            return values
        return lax.ppermute(values, "seq", pairs)

    def gather(self, values):
        rows, local, width = self.rows, values.shape[1], values.shape[2]
        out = jnp.zeros((rows, self.ways, local, width), values.dtype)
        for turn in range(self.ways):
            pick = lax.rem(self.place + turn, self.ways)
            chunk = lax.dynamic_slice_in_dim(values, pick * rows, rows, 0)
            chunk = self.move(chunk, self.targets(turn))
            spot = lax.rem(self.row_group - turn + self.ways, self.ways)
            out = lax.dynamic_update_slice_in_dim(out, chunk[:, None], spot, 1)
        return out.reshape(rows, self.ways * local, width)

    def scatter(self, values):
        rows, width = self.rows, values.shape[2]
        local = values.shape[1] // self.ways
        values = values.reshape(rows, self.ways, local, width)
        out = jnp.zeros((rows * self.ways, local, width), values.dtype)
        for turn in range(self.ways):
            spot = lax.rem(self.row_group - turn + self.ways, self.ways)
            chunk = lax.dynamic_slice_in_dim(values, spot, 1, 1)[:, 0]
            chunk = self.move(chunk, [(b, a) for a, b in self.targets(turn)])
            pick = lax.rem(self.place + turn, self.ways)
            out = lax.dynamic_update_slice_in_dim(out, chunk, pick * rows, 0)
        return out

    def pick_rows(self, values):
        return lax.dynamic_slice_in_dim(values, self.row_group * self.rows, self.rows, 0)

    def groups(self):
        return [
            [r * self.parts + j for j in range(self.parts)] for r in range(self.ways)
        ]

    def to_heads(self, values):
        if self.parts == 1:
            return values
        return lax.all_to_all(
            values, "seq", split_axis=2, concat_axis=1, tiled=True,
            axis_index_groups=self.groups(),
        )

    def from_heads(self, values):
        if self.parts == 1:
            return values
        return lax.all_to_all(
            values, "seq", split_axis=1, concat_axis=2, tiled=True,
            axis_index_groups=self.groups(),
        )


def shards(
    tokens_in,
    segment_ids,
    random_blocks,
    global_blocks,
    w_query,
    b_query,
    w_key,
    w_value,
    b_value,
    w_attn_out,
    b_attn_out,
    ln1_gain,
    ln1_bias,
    w_inner,
    b_inner,
    w_outer,
    b_outer,
    ln2_gain,
    ln2_bias,
    out_grad,
):
    row_count, local_len, width = tokens_in.shape
    seq_count = lax.axis_size("seq")
    fsdp_count = lax.axis_size("fsdp")
    tok_count = row_count * local_len
    own = w_query.shape[0]
    chunks = b_inner.shape[0] // own
    regroup = Regroup(row_count)
    paired = row_count == 2 and seq_count == 2 and fsdp_count in (4, 8, 16, 32)

    vectors = [b_query, b_value, b_attn_out, ln1_gain, ln1_bias, b_outer, ln2_gain, ln2_bias]
    columns = [x[:, None] for x in vectors] + [b_inner.reshape(own, chunks)]
    used = len(vectors) + chunks
    columns.append(jnp.zeros((own, 128 - used), jnp.bfloat16))
    first = jnp.concatenate([w_query] + columns + [w_key, w_value], axis=1)
    inner_own = w_inner.reshape(own, width, chunks).transpose(0, 2, 1).reshape(own, -1)
    second = jnp.concatenate([w_attn_out, inner_own, w_outer.reshape(own, -1)], axis=1)
    second = lax.all_gather(second, "fsdp", axis=0, tiled=True)
    plan = plan_blocks(
        regroup.pick_rows(segment_ids),
        regroup.pick_rows(random_blocks),
        regroup.pick_rows(global_blocks),
    )

    def split_rows(values):
        return values.reshape(regroup.rows, tok_count // regroup.rows, width)

    def part_of(values, i):
        return values[:, part_start(width, i) : part_start(width, i) + width]

    side = lax.axis_index("seq") if paired else jnp.int32(0)
    swap = [(0, 1), (1, 0)]
    if paired:
        flat_in, *qkv, turned_in, turned_w, small, leaving = qkv_forward(
            tokens_in, first, out_grad
        )
        grad_other = lax.ppermute(leaving, "seq", swap)
        grad_own = out_grad
    else:
        first = lax.all_gather(first, "fsdp", axis=0, tiled=True)
        small = first[:, width : width + SMALL_ROWS].astype(jnp.float32).T
        flat_in = regroup.gather(tokens_in).reshape(tok_count, width)
        biases = (small[0], jnp.zeros_like(small[0]), small[1])
        qkv = [
            (jnp.dot(flat_in, part_of(first, i), preferred_element_type=jnp.float32)
             + biases[i]).astype(jnp.bfloat16)
            for i in range(3)
        ]
        flat_grad = regroup.gather(out_grad).reshape(tok_count, width)
        grad_own = flat_grad.reshape(2, tok_count // 2, width)
        grad_other = grad_own[1]
    q, k, v = (regroup.to_heads(split_rows(x)) for x in qkv)
    att, lse = attention_forward(q, k, v, plan)
    att_flat = regroup.from_heads(att).reshape(tok_count, width)
    kept, sent, *saved, d_outer, sums = middle_forward(
        side, second, small, att_flat, flat_in, grad_own, grad_other
    )
    if paired:
        sent = lax.ppermute(sent, "seq", swap)
    d_attn, d_att, d_second, sums = middle_backward(second, small, sums, att_flat, *saved)

    def scattered(values):
        return lax.psum_scatter(values, "fsdp", scatter_dimension=0, tiled=True)

    d_outer = scattered(d_outer)
    d_second = scattered(d_second)
    dq, dk, dv = attention_backward(
        q, k, v, att, regroup.to_heads(split_rows(d_att)), lse, plan
    )
    dq, dk, dv = (regroup.from_heads(x).reshape(tok_count, width) for x in (dq, dk, dv))
    mine = lax.axis_index("fsdp")
    dq, sent, d_outer = lax.optimization_barrier((dq, sent, d_outer))
    if paired:
        d_query_w, d_key_w, d_value_w, sums, d_tokens_in, other = qkv_backward(
            turned_in, dq, dk, dv, turned_w, d_attn, sums, d_outer, own
        )
        d_outer = d_outer.astype(jnp.float32) + other.astype(jnp.float32)
        d_second, sums, d_tokens_in, sent = lax.optimization_barrier(
            (d_second, sums, d_tokens_in, sent)
        )
        place = jnp.arange(2, dtype=jnp.int32)[:, None, None]
        out_tokens = jnp.where(place == side, kept[None], sent[None])
        d_tokens_in = jnp.where(place >= -side, d_tokens_in, jnp.zeros_like(d_tokens_in))
    else:
        d_outer = sum_seq(d_outer)
        for spot, part in ((0, dq), (1, dv)):
            sums = sums.at[spot].set(jnp.sum(part.astype(jnp.float32), axis=0))
        sums = butterfly_sum(butterfly_sum(sums, "fsdp"), "seq")
        d_query_w, d_key_w, d_value_w = (
            sum_seq(scattered(contract_rows(flat_in, x).astype(jnp.bfloat16)))
            for x in (dq, dk, dv)
        )
        d_tokens = d_attn.astype(jnp.float32)
        for i, part in enumerate((dq, dk, dv)):
            d_tokens = d_tokens + times_transpose(part, part_of(first, i))
        d_tokens_in = regroup.scatter(split_rows(d_tokens.astype(jnp.bfloat16)))
        out_tokens = regroup.scatter(split_rows(jnp.concatenate([kept, sent])))
    d_second = sum_seq(d_second)
    d_inner_w = (
        d_second[:, width:]
        .reshape(own, chunks, width)
        .transpose(0, 2, 1)
        .reshape(own, -1)
    )
    d_outer_w = d_outer.reshape(own * chunks, width)
    d_vec = lax.dynamic_slice_in_dim(sums, mine * own, own, 1)
    entry_total = tok_count * width * seq_count * fsdp_count
    rms_values = jnp.sqrt(
        jnp.sum(sums[INNER_B + chunks : INNER_B + chunks + 3], axis=1) / entry_total
    )
    return (
        out_tokens,
        d_tokens_in,
        d_query_w,
        d_vec[0],
        d_key_w,
        d_value_w,
        d_vec[1],
        d_second[:, :width],
        d_vec[OUT_B],
        d_vec[GAIN_1],
        d_vec[BIAS_1],
        d_inner_w,
        d_vec[INNER_B : INNER_B + chunks].T.reshape(-1),
        d_outer_w,
        d_vec[OUTER_B],
        d_vec[GAIN_2],
        d_vec[BIAS_2],
        rms_values,
    )


def solution(mesh):
    in_specs = (
        P("fsdp", "seq", None),
        P("fsdp", None),
        P("fsdp", None, None),
        P("fsdp", None),
        P("fsdp", None),
        P("fsdp"),
        P("fsdp", None),
        P("fsdp", None),
        P("fsdp"),
        P("fsdp", None),
        P("fsdp"),
        P("fsdp"),
        P("fsdp"),
        P("fsdp", None),
        P("fsdp"),
        P("fsdp", None),
        P("fsdp"),
        P("fsdp"),
        P("fsdp"),
        P("fsdp", "seq", None),
    )
    out_specs = (
        P("fsdp", "seq", None),
        P("fsdp", "seq", None),
        P("fsdp", None),
        P("fsdp"),
        P("fsdp", None),
        P("fsdp", None),
        P("fsdp"),
        P("fsdp", None),
        P("fsdp"),
        P("fsdp"),
        P("fsdp"),
        P("fsdp", None),
        P("fsdp"),
        P("fsdp", None),
        P("fsdp"),
        P("fsdp"),
        P("fsdp"),
        P(),
    )
    return jax.shard_map(shards, mesh=mesh, in_specs=in_specs, out_specs=out_specs, check_vma=False)
```
